32 devices in a mesh: expert: 4 (over y, x), shard: 8 (over z, core).
Axes of the slice: x: 2, y: 2, z: 4, core: 2. Of those that a mesh axis runs over, the one named last changes fastest.
Arguments:
- tokens_in: bfloat16 [4096, 1536], P(('expert', 'shard')), may hold values from -6 to 6
- output_cotangent: bfloat16 [4096, 1536], P(('expert', 'shard')), may hold values from -6 to 6
- routes: int32 [4096, 8], P(('expert', 'shard')), may hold values from 0 to 39, all different within a row
- doc_ids: int32 [4, 1024], P('expert'), may hold values from 0 to 2, never falling along the last dimension, each value on 1 to 512 neighbouring positions
- picture_starts: int32 [4, 2], P('expert'), may hold values from 0 to 768, as said below
- qkv_weight: bfloat16 [1536, 2560], P('shard'), may hold values from -0.15625 to 0.15625
- out_weight: bfloat16 [1536, 1536], P('shard'), may hold values from -1.5 to 1.5
- router_weight: bfloat16 [1536, 40], P('shard'), may hold values from -0.078125 to 0.078125
- attn_gain: bfloat16 [1536], P('shard'), may hold values from 0.099609375 to 1.8984375
- moe_gain: bfloat16 [1536], P('shard'), may hold values from 0.099609375 to 1.8984375
- gate_up_weight: bfloat16 [1536, 40960], P('shard', 'expert'), may hold values from -0.15625 to 0.15625
- down_weight: bfloat16 [1536, 20480], P('shard', 'expert'), may hold values from -1 to 1
Outputs:
- output: bfloat16 [4096, 1536], P(('expert', 'shard'))
- input_grad: bfloat16 [4096, 1536], P(('expert', 'shard'))
- qkv_weight_grad: float32 [1536, 2560], P('shard')
- out_weight_grad: float32 [1536, 1536], P('shard')
- router_grad: float32 [1536, 40], P('shard')
- attn_gain_grad: float32 [1536], P('shard')
- moe_gain_grad: float32 [1536], P('shard')
- gate_up_grad: float32 [1536, 40960], P('shard', 'expert')
- down_grad: float32 [1536, 20480], P('shard', 'expert')
The draws below stay inside these ranges and needn't reach their ends.
Inputs may be any that keep to these rules, and one draw needn't show every extreme that they name: `routes`: each token names 8 different experts. `doc_ids`: ids never fall along a sequence; each of the 3 documents holds one position or more. `picture_starts`: piece k of a sequence starts between k * 512 and k * 512 + 256.
All inputs are finite; a program needn't handle non-finite values.
Results may differ from the reference program's by a relative error of at most 0.023.
Values may be sent and summed in bfloat16 or wider, within the bound.
No kernel may reach another device: no remote copies, remote signals or barrier semaphores. Data moves between devices by JAX's collectives and lax.ppermute only.
A program may use at most 384 MiB of HBM per device.

```python
import math
import jax
import jax.numpy as jnp
import numpy as np
from jax import lax

D = 1536
HEADS = 24
KV_HEADS = 8
HEAD_DIM = 64
H = 512
EXPERTS = 40
TOP = 8
TOK_DEV = 128
DOCS = 3
PIECE = 256
SLOT = 512
SEQS = 4
SEQ = 1024
TOKENS = 4096
PIECES = 2
QW = 1536
KW = 512
CAP = 32
N_EXPERT = 4
N_SHARD = 8


def draw_picture_starts(key, part):
    offsets = jax.random.randint(key, (SEQS, PIECES), 0, SLOT - PIECE + 1)
    offsets = offsets.at[0, 0].set(0).at[SEQS - 1, PIECES - 1].set(SLOT - PIECE)
    return (offsets + SLOT * jnp.arange(PIECES, dtype=jnp.int32)[None, :]).astype(jnp.int32)


def levels(rng, dims, pieces, least, largest):
    def one(dim, parts):
        draws = jax.random.uniform(jax.random.fold_in(jax.random.fold_in(rng, 6), dim), (parts,), jnp.float32, least / len(pieces), largest / len(pieces))
        return jnp.repeat(jnp.exp(draws), dims[dim] // parts).reshape((-1,) + (1,) * (len(dims) - dim - 1))

    factor_of = one(*pieces[0])
    for cut in pieces[1:]:
        factor_of = factor_of * one(*cut)
    return factor_of


def different_ones(stream_key, rows, amount, top, lift):
    order = jax.random.permutation(jax.random.fold_in(stream_key, 1), amount)
    boost = order
    for power in range(3):
        boost = boost * boost // amount
    boost = boost * lift // amount
    lots = jax.random.randint(jax.random.fold_in(stream_key, 2), (rows, amount), 0, 4096) + boost
    sure = jax.random.permutation(jax.random.fold_in(stream_key, 3), rows)[jnp.arange(amount) % rows]
    lots = jnp.where(jnp.arange(rows)[:, None] == sure[None, :], 1 << 14, lots)
    priority = lots * amount + jnp.arange(amount)
    return lax.top_k(priority.astype(jnp.int32), top)[1].astype(jnp.int32)


def split_up(amount, total, bound, slope):
    weights = [(1 << 20) // math.isqrt(standing ** slope) + 1 for standing in range(2, amount + 1)]
    spare, holding = total - bound - (amount - 1), [1] * (amount - 1)
    while spare > 0:
        free = [i for i in range(amount - 1) if holding[i] < bound]
        pool, left = sum([weights[i] for i in free]), spare
        for i in free:
            extra = min(bound - holding[i], max(1, left * weights[i] // pool), spare)
            holding[i] = holding[i] + extra
            spare = spare - extra
    return np.array([bound] + holding)


def ragged(key, count, total, most, lean):
    if count == 2:
        one = jax.random.randint(key, (), max(1, total - most), min(most, total - 1) + 1)
        return jnp.stack([one, total - one])
    sizes = jnp.asarray(split_up(count, total, most, lean), jnp.int32)
    pairs = (count - 1) // 2
    giver, sink = sizes[1:1 + 2 * pairs:2], sizes[2:2 + 2 * pairs:2]
    room = jnp.minimum(giver - 1, most - sink)
    moved = jax.random.randint(jax.random.fold_in(key, 1), (pairs,), 0, 1 << 20) % (room + 1)
    sizes = sizes.at[1:1 + 2 * pairs:2].set(giver - moved).at[2:2 + 2 * pairs:2].set(sink + moved)
    return sizes[jax.random.permutation(jax.random.fold_in(key, 2), count)]


def bell_draw(key, shape, scale, limit, split=(), held_as=jnp.bfloat16):
    values = scale * jax.random.normal(key, shape, jnp.float32)
    if split:
        values = values * levels(key, shape, split, -0.22, 0.18)
    return jnp.clip(values, -limit, limit).astype(held_as)


def setup_inputs(seed: int = 0) -> dict:
    keys = jax.random.split(jax.random.key(seed), 13)
    tokens_in = bell_draw(keys[0], (TOKENS, D), 1.0, 6.0, ((0, 32),))
    output_cotangent = bell_draw(keys[1], (TOKENS, D), 1.0, 6.0, ((0, 32),))
    routes = different_ones(keys[2], TOKENS, EXPERTS, TOP, 1638)
    doc_ids = jax.vmap(lambda own: jnp.searchsorted(jnp.cumsum(ragged(own, DOCS, SEQ, SEQ // 2, 0)), jnp.arange(SEQ), side="right"))(jax.random.split(keys[3], SEQS)).reshape((SEQS, SEQ)).astype(jnp.int32)
    picture_starts = draw_picture_starts(jax.random.fold_in(keys[12], 71), 0)
    qkv_weight = bell_draw(keys[5], (D, QW + 2 * KW), D ** -0.5, 0.15625, ((0, 8),))
    out_weight = bell_draw(keys[6], (D, QW), (max(4 * QW * DOCS // SEQ, 1)) ** -0.5, 1.5, ((0, 8),))
    router_weight = bell_draw(keys[7], (D, EXPERTS), (4 * D) ** -0.5, 0.078125, ((0, 8),))
    attn_gain = jnp.clip(1.0 + 0.18 * jax.random.normal(keys[8], (D,), jnp.float32), 0.099609375, 1.8984375).astype(jnp.bfloat16)
    moe_gain = jnp.clip(1.0 + 0.18 * jax.random.normal(keys[9], (D,), jnp.float32), 0.099609375, 1.8984375).astype(jnp.bfloat16)
    gate_up_weight = bell_draw(keys[10], (D, EXPERTS * 2 * H), D ** -0.5, 0.15625, ((0, 8), (1, 4)))
    down_weight = bell_draw(keys[11], (D, EXPERTS * H), (max(H // 16, 1)) ** -0.5, 1.0, ((0, 8), (1, 4)))
    return {"tokens_in": tokens_in, "output_cotangent": output_cotangent, "routes": routes, "doc_ids": doc_ids, "picture_starts": picture_starts, "qkv_weight": qkv_weight, "out_weight": out_weight, "router_weight": router_weight, "attn_gain": attn_gain, "moe_gain": moe_gain, "gate_up_weight": gate_up_weight, "down_weight": down_weight}


norm_eps = 1e-06
rope_base = 10000.0
masked_score = -1e+30
full_precision = lax.Precision.HIGHEST

@jax.custom_vjp
def low(v):
    return lax.optimization_barrier(v.astype(jnp.bfloat16)).astype(jnp.float32)

@jax.custom_vjp
def low_back(v):
    return v

def low_keep(v):
    return (low(v), None)

def low_pass(kept, grad):
    return (grad,)

def back_keep(v):
    return (v, None)

def back_low(kept, grad):
    return (low(grad),)
low.defvjp(low_keep, low_pass)
low_back.defvjp(back_keep, back_low)

def rope_tables(positions, head_dim):
    half_dim = head_dim // 2
    frequency = rope_base ** (-2.0 * jnp.arange(half_dim, dtype=jnp.float32) / head_dim)
    angles = positions.astype(jnp.float32)[:, None] * frequency[None, :]
    return (jnp.cos(angles)[:, None, :], jnp.sin(angles)[:, None, :])

def rotate(values, cosine, sine_table):
    half_dim = values.shape[-1] // 2
    first_half = values[..., :half_dim]
    second = values[..., half_dim:]
    return jnp.concatenate([first_half * cosine - second * sine_table, second * cosine + first_half * sine_table], -1)

def rms_norm(values, gain):
    inverse = lax.rsqrt(lax.optimization_barrier(jnp.mean(values * values, -1, keepdims=True)) + norm_eps)
    return values * inverse * gain

def picture_ids(positions, starts, slot_len, piece_len):
    slot_index = positions // slot_len
    picked_slot = slot_index[:, None] == jnp.arange(starts.shape[0], dtype=jnp.int32)[None, :]
    piece_begin = lax.optimization_barrier(jnp.sum(jnp.where(picked_slot, starts[None, :], 0), axis=1))
    inside = (positions >= piece_begin) & (positions < piece_begin + piece_len)
    return jnp.where(inside, slot_index, -1)

def allowed(query_pos, key_pos, query_doc, key_doc, query_pic, key_pic):
    same_doc = query_doc[:, None] == key_doc[None, :]
    earlier = key_pos[None, :] <= query_pos[:, None]
    same_pic = (query_pic[:, None] == key_pic[None, :]) & (query_pic[:, None] >= 0)
    return same_doc & (earlier | same_pic)

def device_slots(block_routes):
    hit_count = lax.optimization_barrier(jnp.sum((block_routes[:, :, None] == jnp.arange(EXPERTS, dtype=jnp.int32)[None, None, :]).astype(jnp.int32), 1))
    before = jnp.cumsum(hit_count, 0) - hit_count
    return jnp.take_along_axis(before, block_routes, 1)

def reference(tokens_in, output_cotangent, routes, doc_ids, picture_starts, qkv_weight, out_weight, router_weight, attn_gain, moe_gain, gate_up_weight, down_weight):
    devices = N_EXPERT * N_SHARD
    groups = HEADS // KV_HEADS
    q_width = HEADS * HEAD_DIM
    kv_width = KV_HEADS * HEAD_DIM
    score_scale = HEAD_DIM ** (-0.5)
    positions = jnp.arange(TOKENS, dtype=jnp.int32) % SEQ
    slot_index = jax.vmap(device_slots)(routes.reshape(devices, TOK_DEV, TOP)).reshape(TOKENS, TOP)
    kept_pair = slot_index < CAP
    block_of = (jnp.arange(TOKENS, dtype=jnp.int32) // TOK_DEV)[:, None]
    global_slot = (routes * (devices * CAP) + block_of * CAP + slot_index).astype(jnp.int32)
    table_size = EXPERTS * devices * CAP
    target = jnp.where(kept_pair, global_slot, table_size).astype(jnp.int32)
    token_ids = jnp.broadcast_to(jnp.arange(TOKENS, dtype=jnp.int32)[:, None], (TOKENS, TOP))
    owner_row = jnp.full((table_size + 1,), -1, jnp.int32).at[target.reshape(-1)].set(token_ids.reshape(-1))[:table_size]
    owner_row = owner_row.reshape(EXPERTS, devices * CAP)
    slot_valid = (owner_row >= 0).astype(jnp.float32)
    owner_safe = jnp.maximum(owner_row, 0).astype(jnp.int32)
    safe_slot = jnp.where(kept_pair, global_slot, 0).astype(jnp.int32)

    def attend_sequence(inputs):
        seq_queries, seq_keys, seq_values, seq_docs, seq_starts = inputs
        seq_pos = jnp.arange(SEQ, dtype=jnp.int32)
        seq_pics = picture_ids(seq_pos, seq_starts, SLOT, PIECE)
        visible = allowed(seq_pos, seq_pos, seq_docs, seq_docs, seq_pics, seq_pics)

        def one_head(head_inputs):
            head_queries, head_keys, head_values = head_inputs
            raw_scores = low_back(jnp.einsum('qrd,kd->rqk', head_queries, head_keys, precision=full_precision) * score_scale)
            masked = jnp.where(visible[None], raw_scores, masked_score)
            log_total = jax.nn.logsumexp(masked, axis=-1, keepdims=True)
            prob_full = jnp.exp(masked - log_total)
            return jnp.einsum('rqk,kd->qrd', low(prob_full), head_values, precision=full_precision)
        per_head = lax.map(jax.checkpoint(one_head), (seq_queries.transpose(1, 0, 2, 3), seq_keys.transpose(1, 0, 2), seq_values.transpose(1, 0, 2)))
        return per_head.transpose(1, 0, 2, 3)

    def forward(tokens, qkv_w, out_w, router_w, gain_one, gain_two, gate_up_w, down_w):
        normed_in = low(rms_norm(tokens, gain_one))
        qkv_rows = low_back(jnp.dot(normed_in, qkv_w, precision=full_precision))
        cosine, sine_table = rope_tables(positions, HEAD_DIM)
        queries = low(rotate(qkv_rows[:, :q_width].reshape(TOKENS, HEADS, HEAD_DIM), cosine, sine_table))
        key_rows = low(rotate(qkv_rows[:, q_width:q_width + kv_width].reshape(TOKENS, KV_HEADS, HEAD_DIM), cosine, sine_table))
        value_rows = low(qkv_rows[:, q_width + kv_width:].reshape(TOKENS, KV_HEADS, HEAD_DIM))
        attended = lax.map(jax.checkpoint(attend_sequence), (queries.reshape(SEQS, SEQ, KV_HEADS, groups, HEAD_DIM), key_rows.reshape(SEQS, SEQ, KV_HEADS, HEAD_DIM), value_rows.reshape(SEQS, SEQ, KV_HEADS, HEAD_DIM), doc_ids, picture_starts))
        attended = low(low_back(attended.reshape(TOKENS, q_width)))
        branch = low_back(lax.dot_general(attended, out_w, (((1,), (1,)), ((), ())), precision=full_precision))
        middle = tokens + branch
        normed_mid = low(rms_norm(middle, gain_two))
        logits = low_back(jnp.dot(normed_mid, router_w, precision=full_precision))
        gates = jax.nn.softmax(jnp.take_along_axis(logits, routes, 1), axis=-1)
        gate_up_all = gate_up_w.reshape(D, EXPERTS, 2 * H).transpose(1, 0, 2)
        down_all = down_w.reshape(D, EXPERTS, H).transpose(1, 0, 2)

        def one_expert(inputs):
            gate_up_e, down_e, rows_at, rows_live = inputs
            rows_in = low_back(normed_mid[rows_at] * rows_live[:, None])
            projected = low_back(jnp.dot(rows_in, gate_up_e, precision=full_precision))
            hidden = low(jax.nn.silu(projected[:, :H]) * projected[:, H:])
            return low(low_back(jnp.dot(hidden, down_e.T, precision=full_precision)))
        expert_out = lax.map(jax.checkpoint(one_expert), (gate_up_all, down_all, owner_safe, slot_valid)).reshape(table_size, D)
        pair_weight = jnp.where(kept_pair, gates, 0.0)
        moe_sum = jnp.zeros_like(middle)
        for pair_index in range(TOP):
            moe_sum = moe_sum + pair_weight[:, pair_index:pair_index + 1] * expert_out[safe_slot[:, pair_index]]
        return middle + moe_sum
    primal = tuple((array.astype(jnp.float32) for array in (tokens_in, qkv_weight, out_weight, router_weight, attn_gain, moe_gain, gate_up_weight, down_weight)))
    result, pullback = jax.vjp(forward, *primal)
    gradients = pullback(output_cotangent.astype(jnp.float32))
    return (result.astype(jnp.bfloat16), gradients[0].astype(jnp.bfloat16), gradients[1], gradients[2], gradients[3], gradients[4], gradients[5], gradients[6], gradients[7])
```

```python
import jax
import jax.numpy as jnp
from jax import lax
from jax.sharding import PartitionSpec as P

D = 1536
HEADS = 24
KV_HEADS = 8
HEAD_DIM = 64
H = 512
EXPERTS = 40
TOP = 8
PIECE = 256
SLOT = 512
CAP = 32


norm_eps = 1e-06
rope_base = 10000.0
masked_score = -1e30


def rope_tables(positions, head_dim):
    half_dim = head_dim // 2
    frequency = rope_base ** (-2.0 * jnp.arange(half_dim, dtype=jnp.float32) / head_dim)
    angles = positions.astype(jnp.float32)[:, None] * frequency[None, :]
    return (jnp.cos(angles)[:, None, :], jnp.sin(angles)[:, None, :])


def rotate(values, cosine, sine_table):
    half_dim = values.shape[-1] // 2
    first_half = values[..., :half_dim]
    second = values[..., half_dim:]
    return jnp.concatenate(
        [first_half * cosine - second * sine_table, second * cosine + first_half * sine_table], -1
    )


def rotate_back(grad_rows, cosine, sine_table):
    half_dim = grad_rows.shape[-1] // 2
    first_half = grad_rows[..., :half_dim]
    second = grad_rows[..., half_dim:]
    return jnp.concatenate(
        [first_half * cosine + second * sine_table, second * cosine - first_half * sine_table], -1
    )


def rms_norm(values, gain):
    inverse = lax.rsqrt(jnp.mean(values * values, -1, keepdims=True) + norm_eps)
    normal = values * inverse
    return (normal * gain, normal, inverse)


def rms_back(grad_rows, gain, normal, inverse):
    scaled = grad_rows * gain
    grad_in = inverse * (scaled - normal * jnp.mean(scaled * normal, -1, keepdims=True))
    return (grad_in, jnp.sum(grad_rows * normal, 0))


def picture_ids(positions, starts, slot_len, piece_len):
    slot_index = positions // slot_len
    picked_slot = slot_index[:, None] == jnp.arange(starts.shape[0], dtype=jnp.int32)[None, :]
    piece_begin = jnp.sum(jnp.where(picked_slot, starts[None, :], 0), axis=1)
    inside = (positions >= piece_begin) & (positions < piece_begin + piece_len)
    return jnp.where(inside, slot_index, -1)


def allowed(query_pos, key_pos, query_doc, key_doc, query_pic, key_pic):
    same_doc = query_doc[:, None] == key_doc[None, :]
    earlier = key_pos[None, :] <= query_pos[:, None]
    same_pic = (query_pic[:, None] == key_pic[None, :]) & (query_pic[:, None] >= 0)
    return same_doc & (earlier | same_pic)


def local(
    tokens_in,
    output_cotangent,
    routes,
    doc_ids,
    picture_starts,
    qkv_weight,
    out_weight,
    router_weight,
    attn_gain,
    moe_gain,
    gate_up_weight,
    down_weight,
):
    qkv_full, out_full, router_full, gain_first, gain_second = (
        lax.all_gather(qkv_weight, "shard", axis=0, tiled=True),
        lax.all_gather(out_weight, "shard", axis=0, tiled=True),
        lax.all_gather(router_weight, "shard", axis=0, tiled=True),
        lax.all_gather(attn_gain, "shard", axis=0, tiled=True),
        lax.all_gather(moe_gain, "shard", axis=0, tiled=True),
    )
    gain_one = gain_first.astype(jnp.float32)
    gain_two = gain_second.astype(jnp.float32)
    tok_rows = tokens_in.shape[0]
    seq_len = doc_ids.shape[1]
    groups = HEADS // KV_HEADS
    q_width = HEADS * HEAD_DIM
    kv_width = KV_HEADS * HEAD_DIM
    score_scale = HEAD_DIM ** (-0.5)
    shard_at = lax.axis_index("shard")
    query_pos = shard_at * tok_rows + jnp.arange(tok_rows, dtype=jnp.int32)
    key_pos = jnp.arange(seq_len, dtype=jnp.int32)
    key_doc = doc_ids[0]
    key_pic = picture_ids(key_pos, picture_starts[0], SLOT, PIECE)
    query_doc = lax.dynamic_slice_in_dim(key_doc, shard_at * tok_rows, tok_rows)
    query_pic = lax.dynamic_slice_in_dim(key_pic, shard_at * tok_rows, tok_rows)
    tokens_f = tokens_in.astype(jnp.float32)
    normed_one, normal_one, inverse_one = rms_norm(tokens_f, gain_one)
    normed_in = normed_one.astype(jnp.bfloat16)
    qkv_rows = jnp.dot(normed_in, qkv_full, preferred_element_type=jnp.float32)
    cosine, sine_table = rope_tables(query_pos, HEAD_DIM)
    queries = (
        rotate(qkv_rows[:, :q_width].reshape(tok_rows, HEADS, HEAD_DIM), cosine, sine_table)
        .astype(jnp.bfloat16)
        .reshape(tok_rows, KV_HEADS, groups, HEAD_DIM)
    )
    key_local = (
        rotate(
            qkv_rows[:, q_width : q_width + kv_width].reshape(tok_rows, KV_HEADS, HEAD_DIM),
            cosine,
            sine_table,
        )
        .astype(jnp.bfloat16)
        .reshape(tok_rows, kv_width)
    )
    value_local = qkv_rows[:, q_width + kv_width :].astype(jnp.bfloat16)
    all_keys, all_values = (
        lax.all_gather(key_local, "shard", axis=0, tiled=True),
        lax.all_gather(value_local, "shard", axis=0, tiled=True),
    )
    span_len = min(512, seq_len)
    span_count = seq_len // span_len

    def block_scores(first_row, key_rows):
        key_block = lax.dynamic_slice_in_dim(key_rows, first_row, span_len, 0).reshape(
            span_len, KV_HEADS, HEAD_DIM
        )
        raw_scores = (
            jnp.einsum("tgrd,kgd->tgrk", queries, key_block, preferred_element_type=jnp.float32)
            * score_scale
        )
        block_pos = lax.dynamic_slice_in_dim(key_pos, first_row, span_len)
        block_doc = lax.dynamic_slice_in_dim(key_doc, first_row, span_len)
        block_pic = lax.dynamic_slice_in_dim(key_pic, first_row, span_len)
        visible = allowed(query_pos, block_pos, query_doc, block_doc, query_pic, block_pic)[
            :, None, None, :
        ]
        return (raw_scores, visible, key_block)

    def value_block_at(first_row, value_rows):
        return lax.dynamic_slice_in_dim(value_rows, first_row, span_len, 0).reshape(
            span_len, KV_HEADS, HEAD_DIM
        )

    def max_step(step_index, carry):
        run_max, run_sum = carry
        raw_scores, visible, key_block = block_scores(step_index * span_len, all_keys)
        masked = jnp.where(visible, raw_scores, masked_score)
        new_max = jnp.maximum(run_max, jnp.max(masked, -1))
        shifted = jnp.where(visible, jnp.exp(masked - new_max[..., None]), 0.0)
        return (new_max, run_sum * jnp.exp(run_max - new_max) + jnp.sum(shifted, -1))

    stat_shape = (tok_rows, KV_HEADS, groups)
    run_max, run_sum = lax.fori_loop(
        0,
        span_count,
        max_step,
        (jnp.full(stat_shape, masked_score, jnp.float32), jnp.zeros(stat_shape, jnp.float32)),
    )
    log_total = run_max + jnp.log(run_sum)

    def probs_of(raw_scores, visible):
        return jnp.exp(jnp.where(visible, raw_scores - log_total[..., None], masked_score))

    def value_step(step_index, summed):
        first_row = step_index * span_len
        raw_scores, visible, key_block = block_scores(first_row, all_keys)
        probs = probs_of(raw_scores, visible).astype(jnp.bfloat16)
        return summed + jnp.einsum(
            "tgrk,kgd->tgrd",
            probs,
            value_block_at(first_row, all_values),
            preferred_element_type=jnp.float32,
        )

    summed = lax.fori_loop(
        0, span_count, value_step, jnp.zeros((tok_rows, KV_HEADS, groups, HEAD_DIM), jnp.float32)
    )
    attended = summed.reshape(tok_rows, q_width).astype(jnp.bfloat16)
    branch = lax.dot_general(
        attended, out_full, (((1,), (1,)), ((), ())), preferred_element_type=jnp.float32
    )
    middle = tokens_f + branch
    normed_two, normal_two, inverse_two = rms_norm(middle, gain_two)
    normed_mid = normed_two.astype(jnp.bfloat16)
    logits = jnp.dot(normed_mid, router_full, preferred_element_type=jnp.float32)
    gates = jax.nn.softmax(jnp.take_along_axis(logits, routes, 1), axis=-1)
    route_hits = routes[:, :, None] == jnp.arange(EXPERTS, dtype=jnp.int32)[None, None, :]
    hit_count = jnp.sum(route_hits.astype(jnp.int32), 1)
    before = jnp.cumsum(hit_count, 0) - hit_count
    slot_index = jnp.take_along_axis(before, routes, 1)
    kept_pair = slot_index < CAP
    flat_slot = routes * CAP + slot_index
    capacity_rows = EXPERTS * CAP
    target = jnp.where(kept_pair, flat_slot, capacity_rows)
    token_ids = jnp.broadcast_to(jnp.arange(tok_rows, dtype=jnp.int32)[:, None], (tok_rows, TOP))
    owner_row = (
        jnp.full((capacity_rows + 1,), -1, jnp.int32)
        .at[target.reshape(-1)]
        .set(token_ids.reshape(-1))[:capacity_rows]
    )
    filled = owner_row >= 0
    source_row = jnp.maximum(owner_row, 0)
    expert_groups = lax.axis_size("expert")
    local_experts = EXPERTS // expert_groups
    send_rows = jnp.where(
        filled[:, None], normed_mid[source_row], jnp.zeros((), jnp.bfloat16)
    ).reshape(expert_groups, local_experts, CAP, D)
    received = lax.all_to_all(send_rows, "expert", split_axis=0, concat_axis=0, tiled=True)
    gate_up_full, down_full = (
        lax.all_gather(gate_up_weight, "shard", axis=0, tiled=True),
        lax.all_gather(down_weight, "shard", axis=0, tiled=True),
    )
    gate_up3 = gate_up_full.reshape(D, local_experts, 2 * H)
    down3 = down_full.reshape(D, local_experts, H)
    projected = jnp.einsum("secd,dej->secj", received, gate_up3, preferred_element_type=jnp.float32)
    gate_part = projected[..., :H]
    up_part = projected[..., H:]
    sigma = jax.nn.sigmoid(gate_part)
    silu_value = gate_part * sigma
    hidden = (silu_value * up_part).astype(jnp.bfloat16)
    expert_out = jnp.einsum(
        "secj,dej->secd", hidden, down3, preferred_element_type=jnp.float32
    ).astype(jnp.bfloat16)
    returned = lax.all_to_all(
        expert_out, "expert", split_axis=0, concat_axis=0, tiled=True
    ).reshape(capacity_rows, D)
    safe_flat = jnp.where(kept_pair, flat_slot, 0)
    picked = returned[safe_flat].astype(jnp.float32)
    pair_weight = jnp.where(kept_pair, gates, 0.0)
    moe_sum = jnp.einsum("tk,tkd->td", pair_weight, picked)
    output = (middle + moe_sum).astype(jnp.bfloat16)
    grad_out = output_cotangent.astype(jnp.float32)
    gate_grad = jnp.where(kept_pair, jnp.einsum("td,tkd->tk", grad_out, picked), 0.0)
    slot_gate = (
        jnp.zeros((capacity_rows + 1,), jnp.float32)
        .at[target.reshape(-1)]
        .set(gates.reshape(-1))[:capacity_rows]
    )
    grad_send = (
        jnp.where(filled[:, None], slot_gate[:, None] * grad_out[source_row], 0.0)
        .astype(jnp.bfloat16)
        .reshape(expert_groups, local_experts, CAP, D)
    )
    grad_received = lax.all_to_all(grad_send, "expert", split_axis=0, concat_axis=0, tiled=True)
    keys_back, values_back = (
        lax.all_gather(key_local, "shard", axis=0, tiled=True),
        lax.all_gather(value_local, "shard", axis=0, tiled=True),
    )
    again_up, again_down = (
        lax.all_gather(gate_up_weight, "shard", axis=0, tiled=True),
        lax.all_gather(down_weight, "shard", axis=0, tiled=True),
    )
    gate_up_back = again_up.reshape(D, local_experts, 2 * H)
    down_back = again_down.reshape(D, local_experts, H)
    hidden_grad = jnp.einsum(
        "secd,dej->secj", grad_received, down_back, preferred_element_type=jnp.float32
    )
    silu_slope = sigma * (1.0 + gate_part * (1.0 - sigma))
    proj_grad = jnp.concatenate(
        [hidden_grad * up_part * silu_slope, hidden_grad * silu_value], -1
    ).astype(jnp.bfloat16)
    row_grad = jnp.einsum(
        "secj,dej->secd", proj_grad, gate_up_back, preferred_element_type=jnp.float32
    ).astype(jnp.bfloat16)
    grad_back = lax.all_to_all(row_grad, "expert", split_axis=0, concat_axis=0, tiled=True).reshape(
        capacity_rows, D
    )
    row_count = gate_up_weight.shape[0] * lax.axis_size("shard")
    up_terms = jnp.einsum(
        "secd,secj->dej", received, proj_grad, preferred_element_type=jnp.float32
    ).reshape(row_count, local_experts * 2 * H)
    down_terms = jnp.einsum(
        "secd,secj->dej", grad_received, hidden, preferred_element_type=jnp.float32
    ).reshape(row_count, local_experts * H)
    expert_sums = lax.psum_scatter(
        jnp.concatenate([up_terms, down_terms], 1).astype(jnp.bfloat16),
        "shard",
        scatter_dimension=0,
        tiled=True,
    ).astype(jnp.float32)
    gate_up_grad = expert_sums[:, : local_experts * 2 * H]
    down_grad = expert_sums[:, local_experts * 2 * H :]
    mid_norm_grad = jnp.einsum(
        "tk,tkd->td", kept_pair.astype(jnp.float32), grad_back[safe_flat].astype(jnp.float32)
    )
    chosen_grad = gates * (gate_grad - jnp.sum(gates * gate_grad, -1, keepdims=True))
    logit_grad = jnp.sum(jnp.where(route_hits, chosen_grad[:, :, None], 0.0), 1).astype(
        jnp.bfloat16
    )
    mid_norm_grad = mid_norm_grad + lax.dot_general(
        logit_grad, router_full, (((1,), (1,)), ((), ())), preferred_element_type=jnp.float32
    )
    router_grad = lax.dot_general(
        normed_mid, logit_grad, (((0,), (0,)), ((), ())), preferred_element_type=jnp.float32
    )
    mid_part, moe_gain_grad = rms_back(mid_norm_grad, gain_two, normal_two, inverse_two)
    mid_grad = grad_out + mid_part
    branch_grad = mid_grad.astype(jnp.bfloat16)
    out_weight_grad = lax.dot_general(
        branch_grad, attended, (((0,), (0,)), ((), ())), preferred_element_type=jnp.float32
    )
    attended_grad = (
        jnp.dot(branch_grad, out_full, preferred_element_type=jnp.float32)
        .astype(jnp.bfloat16)
        .reshape(tok_rows, KV_HEADS, groups, HEAD_DIM)
    )

    def dot_step(step_index, row_dot):
        first_row = step_index * span_len
        raw_scores, visible, key_block = block_scores(first_row, keys_back)
        prob_full = probs_of(raw_scores, visible)
        prob_grad = jnp.einsum(
            "tgrd,kgd->tgrk",
            attended_grad,
            value_block_at(first_row, values_back),
            preferred_element_type=jnp.float32,
        )
        return row_dot + jnp.sum(prob_full * prob_grad, -1)

    row_dot = lax.fori_loop(0, span_count, dot_step, jnp.zeros(stat_shape, jnp.float32))

    def grad_step(step_index, carry):
        query_grad, key_terms, value_terms = carry
        first_row = step_index * span_len
        raw_scores, visible, key_block = block_scores(first_row, keys_back)
        prob_full = probs_of(raw_scores, visible)
        prob_grad = jnp.einsum(
            "tgrd,kgd->tgrk",
            attended_grad,
            value_block_at(first_row, values_back),
            preferred_element_type=jnp.float32,
        )
        score_grad = (prob_full * (prob_grad - row_dot[..., None])).astype(jnp.bfloat16)
        query_grad = query_grad + jnp.einsum(
            "tgrk,kgd->tgrd", score_grad, key_block, preferred_element_type=jnp.float32
        )
        key_part = (
            jnp.einsum(
                "tgrk,tgrd->kgd", score_grad, queries, preferred_element_type=jnp.float32
            ).reshape(span_len, kv_width)
            * score_scale
        )
        value_part = jnp.einsum(
            "tgrk,tgrd->kgd",
            prob_full.astype(jnp.bfloat16),
            attended_grad,
            preferred_element_type=jnp.float32,
        ).reshape(span_len, kv_width)
        key_terms = lax.dynamic_update_slice_in_dim(key_terms, key_part, first_row, 0)
        value_terms = lax.dynamic_update_slice_in_dim(value_terms, value_part, first_row, 0)
        return (query_grad, key_terms, value_terms)

    query_grad, key_terms, value_terms = lax.fori_loop(
        0,
        span_count,
        grad_step,
        (
            jnp.zeros((tok_rows, KV_HEADS, groups, HEAD_DIM), jnp.float32),
            jnp.zeros((seq_len, kv_width), jnp.float32),
            jnp.zeros((seq_len, kv_width), jnp.float32),
        ),
    )
    key_grad, value_grad = (
        lax.psum_scatter(
            key_terms.astype(jnp.bfloat16), "shard", scatter_dimension=0, tiled=True
        ).astype(jnp.float32),
        lax.psum_scatter(
            value_terms.astype(jnp.bfloat16), "shard", scatter_dimension=0, tiled=True
        ).astype(jnp.float32),
    )
    query_back = rotate_back(
        (query_grad * score_scale).reshape(tok_rows, HEADS, HEAD_DIM), cosine, sine_table
    ).reshape(tok_rows, q_width)
    key_back = rotate_back(
        key_grad.reshape(tok_rows, KV_HEADS, HEAD_DIM), cosine, sine_table
    ).reshape(tok_rows, kv_width)
    qkv_grad_rows = jnp.concatenate([query_back, key_back, value_grad], 1).astype(jnp.bfloat16)
    qkv_weight_grad = lax.dot_general(
        normed_in, qkv_grad_rows, (((0,), (0,)), ((), ())), preferred_element_type=jnp.float32
    )
    in_norm_grad = lax.dot_general(
        qkv_grad_rows, qkv_full, (((1,), (1,)), ((), ())), preferred_element_type=jnp.float32
    )
    in_part, attn_gain_grad = rms_back(in_norm_grad, gain_one, normal_one, inverse_one)
    input_grad = (mid_grad + in_part).astype(jnp.bfloat16)
    dense_sums = (
        lax.psum_scatter(
            qkv_weight_grad.astype(jnp.bfloat16), "shard", scatter_dimension=0, tiled=True
        ).astype(jnp.float32),
        lax.psum_scatter(
            out_weight_grad.astype(jnp.bfloat16), "shard", scatter_dimension=0, tiled=True
        ).astype(jnp.float32),
        lax.psum_scatter(
            router_grad.astype(jnp.bfloat16), "shard", scatter_dimension=0, tiled=True
        ).astype(jnp.float32),
        lax.psum_scatter(
            attn_gain_grad.astype(jnp.bfloat16), "shard", scatter_dimension=0, tiled=True
        ).astype(jnp.float32),
        lax.psum_scatter(
            moe_gain_grad.astype(jnp.bfloat16), "shard", scatter_dimension=0, tiled=True
        ).astype(jnp.float32),
    )
    dense_totals = (
        lax.psum(dense_sums[0].astype(jnp.bfloat16), "expert").astype(jnp.float32),
        lax.psum(dense_sums[1].astype(jnp.bfloat16), "expert").astype(jnp.float32),
        lax.psum(dense_sums[2].astype(jnp.bfloat16), "expert").astype(jnp.float32),
        lax.psum(dense_sums[3].astype(jnp.bfloat16), "expert").astype(jnp.float32),
        lax.psum(dense_sums[4].astype(jnp.bfloat16), "expert").astype(jnp.float32),
    )
    return (
        output,
        input_grad,
        dense_totals[0],
        dense_totals[1],
        dense_totals[2],
        dense_totals[3],
        dense_totals[4],
        gate_up_grad,
        down_grad,
    )


def hop(values, pairs):
    return lax.ppermute(values, ("expert", "shard"), pairs)


def hop_pairs(step):
    return [
        (e * SHARDS + s, step(e, s)[0] * SHARDS + step(e, s)[1])
        for e in range(GROUPS)
        for s in range(SHARDS)
    ]


GROUPS = 4
SHARDS = 8
to_core = hop_pairs(lambda e, s: (e, s ^ 1))
to_line = [hop_pairs(lambda e, s, k=k: (e, s ^ (2 * k))) for k in range(4)]
to_first = hop_pairs(lambda e, s: (e ^ (1 + s % 2), s))
to_second = hop_pairs(lambda e, s: (e ^ (2 - s % 2), s))


def add_low(one, two):
    return (one.astype(jnp.float32) + two.astype(jnp.float32)).astype(jnp.bfloat16)


def spread(own):
    line = [own] + [hop(own, to_line[k]) for k in (1, 2, 3)]
    parts = []
    for piece in line:
        first = hop(piece, to_first)
        second = hop(jnp.stack([piece, first]), to_second)
        half = jnp.concatenate([piece[None], first[None], second])
        parts += [half, hop(half, to_core)]
    return jnp.concatenate(parts)


def collect(blocks):
    rows = blocks.shape[1:]
    blocks = blocks.reshape((4, 2, 4) + rows)
    line = []
    for k in (3, 2, 1, 0):
        half = add_low(blocks[k, 0], hop(blocks[k, 1], to_core))
        pair = add_low(half[:2], hop(half[2:], to_second))
        one = add_low(pair[0], hop(pair[1], to_first))
        line.append(hop(one, to_line[k]) if k else one)
    return sum(piece.astype(jnp.float32) for piece in line)


def gather_line(own):
    line = jnp.stack([own] + [hop(own, to_line[k]) for k in (1, 2, 3)])
    return jnp.stack([line, hop(line, to_core)], 1)


def sum_line(blocks):
    half = add_low(blocks[:, 0], hop(blocks[:, 1], to_core))
    return half[0].astype(jnp.float32) + sum(
        hop(half[k], to_line[k]).astype(jnp.float32) for k in (1, 2, 3)
    )


def dot(one, two, dims):
    return lax.dot_general(one, two, (dims, ((), ())), preferred_element_type=jnp.float32)


def local_hops(
    tokens_in,
    output_cotangent,
    routes,
    doc_ids,
    picture_starts,
    qkv_weight,
    out_weight,
    router_weight,
    attn_gain,
    moe_gain,
    gate_up_weight,
    down_weight,
):
    low = jnp.bfloat16
    full = jnp.float32
    rows = tokens_in.shape[0]
    seq_len = doc_ids.shape[1]
    groups = HEADS // KV_HEADS
    q_width = HEADS * HEAD_DIM
    kv_width = KV_HEADS * HEAD_DIM
    qkv_width = q_width + 2 * kv_width
    score_scale = HEAD_DIM ** (-0.5)
    group_at = lax.axis_index("expert")
    shard_at = lax.axis_index("shard")
    own_experts = EXPERTS // GROUPS
    whole = own_experts // SHARDS * SHARDS
    split = own_experts - whole
    share = SHARDS // split
    part = H // share
    depth = gate_up_weight.shape[0]
    pad = 128 - EXPERTS
    gain_one = attn_gain.astype(full)[:, None]
    gain_two = moe_gain.astype(full)[:, None]

    expert_ids = jnp.arange(EXPERTS, dtype=jnp.int32)
    hits = jnp.any(routes[:, :, None] == expert_ids[None, None, :], 1)
    earlier = jnp.arange(rows)[:, None] > jnp.arange(rows)[None, :]
    before = dot(earlier.astype(low), hits.astype(low), ((1,), (0,)))
    slots = jnp.where(hits & (before < CAP), before, -1.0)
    kept = slots >= 0
    grad_pay = jnp.concatenate(
        [output_cotangent, jnp.pad(slots.astype(low), ((0, 0), (0, pad)))], 1
    )

    dense_own = jnp.concatenate(
        [
            (qkv_weight.astype(full) * gain_one).astype(low),
            jnp.pad((router_weight.astype(full) * gain_two).astype(low), ((0, 0), (0, pad))),
        ],
        1,
    )
    dense_full = lax.all_gather(dense_own, "shard", axis=0, tiled=True)
    qkv_full = dense_full[:, :qkv_width]
    router_full = dense_full[:, qkv_width:]
    out_full = lax.all_gather(out_weight, "shard", axis=0, tiled=True)

    up3 = (gate_up_weight.astype(full) * gain_two).astype(low).reshape(depth, own_experts, 2 * H)
    down3 = down_weight.reshape(depth, own_experts, H)
    halves = up3[:, whole:].reshape(depth, split, 2, share, part)
    pack = jnp.concatenate(
        [
            up3[:, :whole].transpose(1, 0, 2),
            down3[:, :whole].transpose(1, 0, 2),
            halves.transpose(1, 3, 0, 2, 4).reshape(SHARDS, depth, 2 * part),
            down3[:, whole:]
            .reshape(depth, split, share, part)
            .transpose(1, 2, 0, 3)
            .reshape(SHARDS, depth, part),
        ],
        2,
    )
    owned = lax.all_to_all(pack, "shard", split_axis=0, concat_axis=0, tiled=True)
    owned = owned.reshape(SHARDS * depth, 3 * H + 3 * part)
    up_one = owned[:, : 2 * H]
    down_one = owned[:, 2 * H : 3 * H]
    up_two = owned[:, 3 * H : 3 * H + 2 * part]
    down_two = owned[:, 3 * H + 2 * part :]

    tokens_f = tokens_in.astype(full)
    inverse_one = lax.rsqrt(jnp.mean(tokens_f * tokens_f, -1, keepdims=True) + norm_eps)
    normal_one = tokens_f * inverse_one
    normed_in = normal_one.astype(low)
    qkv_rows = dot(normed_in, qkv_full, ((1,), (0,)))
    query_pos = shard_at * rows + jnp.arange(rows, dtype=jnp.int32)
    cosine, sine_table = rope_tables(query_pos, HEAD_DIM)
    queries = (
        rotate(qkv_rows[:, :q_width].reshape(rows, HEADS, HEAD_DIM), cosine, sine_table)
        .astype(low)
        .reshape(rows, KV_HEADS, groups, HEAD_DIM)
    )
    key_local = rotate(
        qkv_rows[:, q_width : q_width + kv_width].reshape(rows, KV_HEADS, HEAD_DIM),
        cosine,
        sine_table,
    ).reshape(rows, kv_width)
    key_value = jnp.concatenate([key_local, qkv_rows[:, q_width + kv_width :]], 1).astype(low)
    all_kv = gather_line(key_value).reshape(seq_len, 2 * KV_HEADS, HEAD_DIM)
    keys = all_kv[:, :KV_HEADS]
    values = all_kv[:, KV_HEADS:]
    block_order = shard_at ^ jnp.arange(SHARDS, dtype=jnp.int32)
    key_pos = (
        block_order[:, None] * rows + jnp.arange(rows, dtype=jnp.int32)[None, :]
    ).reshape(seq_len)
    doc_blocks = doc_ids[0].reshape(SHARDS, rows)
    key_doc = jnp.concatenate(
        [
            lax.dynamic_index_in_dim(doc_blocks, shard_at ^ k, 0, keepdims=False)
            for k in range(SHARDS)
        ]
    )
    query_doc = key_doc[:rows]
    key_pic = picture_ids(key_pos, picture_starts[0], SLOT, PIECE)
    query_pic = key_pic[:rows]
    visible = allowed(query_pos, key_pos, query_doc, key_doc, query_pic, key_pic)
    visible = visible[None, None]
    raw_scores = (
        jnp.einsum("tgrd,kgd->grtk", queries, keys, preferred_element_type=full) * score_scale
    )
    masked = jnp.where(visible, raw_scores, masked_score)
    top = jnp.max(masked, -1, keepdims=True)
    raised = jnp.exp(masked - top)
    total = jnp.sum(raised, -1, keepdims=True)
    prob_full = raised / total
    probs = prob_full.astype(low)
    attended = (
        jnp.einsum("grtk,kgd->tgrd", probs, values, preferred_element_type=full)
        .astype(low)
        .reshape(rows, q_width)
    )
    branch = dot(attended, out_full, ((1,), (1,)))
    middle = tokens_f + branch
    inverse_two = lax.rsqrt(jnp.mean(middle * middle, -1, keepdims=True) + norm_eps)
    normal_two = middle * inverse_two
    normed_mid = normal_two.astype(low)
    logits = dot(normed_mid, router_full, ((1,), (0,)))[:, :EXPERTS]
    logits = jnp.where(hits, logits, masked_score)
    gates = jnp.exp(logits - jnp.max(logits, -1, keepdims=True))
    gates = jnp.where(hits, gates, 0.0)
    gates = gates / jnp.sum(gates, -1, keepdims=True)
    gate_low = gates.astype(low)
    gate_rest = (gates - gate_low.astype(full)).astype(low)
    row_pay = jnp.concatenate(
        [normed_mid, gate_low, gate_rest, jnp.zeros((rows, 128 - 2 * EXPERTS), low)], 1
    )

    grad_all = spread(grad_pay)
    row_all = spread(row_pay)

    def column(extra, index):
        return lax.dynamic_slice_in_dim(extra, index, 1, 2)

    slot_cols = grad_all[:, :, D:].astype(full)
    gate_cols = row_all[:, :, D:].astype(full)
    expert_one = group_at * own_experts + shard_at
    expert_two = group_at * own_experts + whole + shard_at // share
    slot_ids = jnp.arange(CAP, dtype=full)[None, None, :]

    def pick_of(index):
        pick = column(slot_cols, index) == slot_ids
        gate = column(gate_cols, index) + column(gate_cols, index + EXPERTS)
        slot_gate = jnp.sum(jnp.where(pick, gate, 0.0), 1).reshape(-1, 1)
        return pick.astype(low), slot_gate

    def dispatch(pick, blocks):
        return jnp.einsum(
            "btc,btd->bcd", pick, blocks[:, :, :D], preferred_element_type=full
        ).astype(low).reshape(-1, D)

    def expert(index, up_weight, down_cols):
        width = down_cols.shape[1]
        pick, slot_gate = pick_of(index)
        rows_in = dispatch(pick, row_all)
        grads_in = dispatch(pick, grad_all)
        projected = dot(rows_in, up_weight, ((1,), (0,)))
        plain = dot(grads_in, down_cols, ((1,), (0,)))
        gate_part = projected[:, :width]
        up_part = projected[:, width:]
        sigma = jax.nn.sigmoid(gate_part)
        silu_value = gate_part * sigma
        hidden = silu_value * up_part
        gate_grad = jnp.sum(hidden * plain, -1, keepdims=True)
        hidden_gated = (hidden * slot_gate).astype(low)
        hidden_grad = plain * slot_gate
        silu_slope = sigma * (1.0 + gate_part * (1.0 - sigma))
        proj_grad = jnp.concatenate(
            [hidden_grad * up_part * silu_slope, hidden_grad * silu_value], -1
        ).astype(low)
        out_rows = dot(hidden_gated, down_cols, ((1,), (1,))).astype(low)
        row_grad = dot(proj_grad, up_weight, ((1,), (1,))).astype(low)
        up_terms = dot(rows_in, proj_grad, ((0,), (0,))).astype(low)
        down_terms = dot(grads_in, hidden_gated, ((0,), (0,))).astype(low)
        token_gate = jnp.einsum(
            "btc,bc->bt", pick.astype(full), gate_grad.reshape(-1, CAP)
        )[:, :, None]
        return (
            pick,
            out_rows.reshape(-1, CAP, D),
            row_grad.reshape(-1, CAP, D),
            token_gate,
            up_terms,
            down_terms,
        )

    one = expert(expert_one, up_one, down_one)
    two = expert(expert_two, up_two, down_two)
    picks = jnp.concatenate([one[0], two[0]], 2)

    def combine(slot_one, slot_two):
        return jnp.einsum(
            "btc,bcd->btd",
            picks,
            jnp.concatenate([slot_one, slot_two], 1),
            preferred_element_type=full,
        ).astype(low)

    lane = jnp.arange(128, dtype=jnp.int32)[None, None, :]
    gate_lanes = (
        jnp.where(lane == expert_one, one[3], 0.0) + jnp.where(lane == expert_two, two[3], 0.0)
    ).astype(low)
    grad_back = jnp.concatenate([combine(one[2], two[2]), gate_lanes], 2)
    grad_sum = collect(grad_back)
    moe_sum = collect(combine(one[1], two[1]))
    output = (middle + moe_sum).astype(low)

    terms = jnp.concatenate([one[4], one[5], two[4], two[5]], 1)
    terms = lax.all_to_all(
        terms.reshape(SHARDS, depth, -1), "shard", split_axis=0, concat_axis=0, tiled=True
    ).astype(full)
    up_whole = terms[:, :, : 2 * H].transpose(1, 0, 2).reshape(depth, whole * 2 * H)
    up_parts = (
        terms[:, :, 3 * H : 3 * H + 2 * part]
        .reshape(split, share, depth, 2, part)
        .transpose(2, 0, 3, 1, 4)
        .reshape(depth, split * 2 * H)
    )
    gate_up_grad = jnp.concatenate([up_whole, up_parts], 1) * gain_two
    down_whole = terms[:, :, 2 * H : 3 * H].transpose(1, 0, 2).reshape(depth, whole * H)
    down_parts = (
        terms[:, :, 3 * H + 2 * part :]
        .reshape(split, share, depth, part)
        .transpose(2, 0, 1, 3)
        .reshape(depth, split * H)
    )
    down_grad = jnp.concatenate([down_whole, down_parts], 1)

    gate_grad = jnp.where(kept, grad_sum[:, D : D + EXPERTS], 0.0)
    logit_grad = gates * (gate_grad - jnp.sum(gates * gate_grad, -1, keepdims=True))
    logit_grad = jnp.pad(logit_grad.astype(low), ((0, 0), (0, pad)))
    scaled_two = grad_sum[:, :D] + dot(logit_grad, router_full, ((1,), (1,)))
    grad_out = output_cotangent.astype(full)
    mean_two = jnp.mean(scaled_two * normal_two, -1, keepdims=True)
    mid_grad = grad_out + inverse_two * (scaled_two - normal_two * mean_two)
    moe_gain_part = jnp.sum(scaled_two * normal_two, 0)
    router_part = dot(normed_mid, logit_grad, ((0,), (0,)))
    branch_grad = mid_grad.astype(low)
    out_part = dot(branch_grad, attended, ((0,), (0,)))
    attended_grad = (
        dot(branch_grad, out_full, ((1,), (0,)))
        .astype(low)
        .reshape(rows, KV_HEADS, groups, HEAD_DIM)
    )

    prob_grad = jnp.einsum("tgrd,kgd->grtk", attended_grad, values, preferred_element_type=full)
    row_dot = jnp.sum(prob_full * prob_grad, -1, keepdims=True)
    score_grad = (prob_full * (prob_grad - row_dot)).astype(low)
    query_grad = jnp.einsum("grtk,kgd->tgrd", score_grad, keys, preferred_element_type=full)
    key_part = (
        jnp.einsum("grtk,tgrd->kgd", score_grad, queries, preferred_element_type=full)
        * score_scale
    ).reshape(seq_len, kv_width)
    value_part = jnp.einsum(
        "grtk,tgrd->kgd", probs, attended_grad, preferred_element_type=full
    ).reshape(seq_len, kv_width)
    kv_part = jnp.concatenate([key_part, value_part], 1).astype(low)
    kv_grad = sum_line(kv_part.reshape(4, 2, rows, 2 * kv_width))
    query_back = rotate_back(
        (query_grad * score_scale).reshape(rows, HEADS, HEAD_DIM), cosine, sine_table
    ).reshape(rows, q_width)
    key_back = rotate_back(
        kv_grad[:, :kv_width].reshape(rows, KV_HEADS, HEAD_DIM), cosine, sine_table
    ).reshape(rows, kv_width)
    qkv_grad_rows = jnp.concatenate([query_back, key_back, kv_grad[:, kv_width:]], 1).astype(low)
    qkv_part = dot(normed_in, qkv_grad_rows, ((0,), (0,)))
    scaled_one = dot(qkv_grad_rows, qkv_full, ((1,), (1,)))
    mean_one = jnp.mean(scaled_one * normal_one, -1, keepdims=True)
    input_grad = mid_grad + inverse_one * (scaled_one - normal_one * mean_one)
    attn_gain_part = jnp.sum(scaled_one * normal_one, 0)

    def dense_sum(parts):
        joined = lax.psum_scatter(
            parts.astype(low), "shard", scatter_dimension=0, tiled=True
        )
        return lax.psum(joined, "expert").astype(full)

    out_sum = dense_sum(out_part)
    small = jnp.concatenate(
        [
            router_part[:, :EXPERTS],
            moe_gain_part[:, None],
            attn_gain_part[:, None],
            jnp.zeros((router_part.shape[0], pad - 2), full),
        ],
        1,
    )
    late_sum = dense_sum(jnp.concatenate([qkv_part, small], 1))
    return (
        output,
        input_grad.astype(low),
        late_sum[:, :qkv_width] * gain_one,
        out_sum,
        late_sum[:, qkv_width : qkv_width + EXPERTS] * gain_two,
        late_sum[:, qkv_width + EXPERTS + 1] / gain_one[:, 0],
        late_sum[:, qkv_width + EXPERTS] / gain_two[:, 0],
        gate_up_grad,
        down_grad,
    )


def solution(mesh):
    body = local
    if mesh.shape["expert"] == GROUPS and mesh.shape["shard"] == SHARDS:
        body = local_hops
    return jax.shard_map(
        body,
        mesh=mesh,
        in_specs=(
            P(("expert", "shard"), None),
            P(("expert", "shard"), None),
            P(("expert", "shard"), None),
            P("expert", None),
            P("expert", None),
            P("shard", None),
            P("shard", None),
            P("shard", None),
            P("shard"),
            P("shard"),
            P("shard", "expert"),
            P("shard", "expert"),
        ),
        out_specs=(
            P(("expert", "shard"), None),
            P(("expert", "shard"), None),
            P("shard", None),
            P("shard", None),
            P("shard", None),
            P("shard"),
            P("shard"),
            P("shard", "expert"),
            P("shard", "expert"),
        ),
        check_vma=False,
    )
```

```python
import jax
import jax.numpy as jnp
from jax import lax
from jax.experimental import pallas as pl
from jax.experimental.pallas import tpu as pltpu
from jax.sharding import PartitionSpec as P

D = 1536
HEADS = 24
KV_HEADS = 8
HEAD_DIM = 64
H = 512
EXPERTS = 40
TOP = 8
PIECE = 256
SLOT = 512
CAP = 32


norm_eps = 1e-06
rope_base = 10000.0
masked_score = -1e30


def rope_tables(positions, head_dim):
    half_dim = head_dim // 2
    frequency = rope_base ** (-2.0 * jnp.arange(half_dim, dtype=jnp.float32) / head_dim)
    angles = positions.astype(jnp.float32)[:, None] * frequency[None, :]
    return (jnp.cos(angles)[:, None, :], jnp.sin(angles)[:, None, :])


def rotate(values, cosine, sine_table):
    half_dim = values.shape[-1] // 2
    first_half = values[..., :half_dim]
    second = values[..., half_dim:]
    return jnp.concatenate(
        [first_half * cosine - second * sine_table, second * cosine + first_half * sine_table], -1
    )


def rotate_back(grad_rows, cosine, sine_table):
    half_dim = grad_rows.shape[-1] // 2
    first_half = grad_rows[..., :half_dim]
    second = grad_rows[..., half_dim:]
    return jnp.concatenate(
        [first_half * cosine + second * sine_table, second * cosine - first_half * sine_table], -1
    )


def rms_norm(values, gain):
    inverse = lax.rsqrt(jnp.mean(values * values, -1, keepdims=True) + norm_eps)
    normal = values * inverse
    return (normal * gain, normal, inverse)


def rms_back(grad_rows, gain, normal, inverse):
    scaled = grad_rows * gain
    grad_in = inverse * (scaled - normal * jnp.mean(scaled * normal, -1, keepdims=True))
    return (grad_in, jnp.sum(grad_rows * normal, 0))


def picture_ids(positions, starts, slot_len, piece_len):
    slot_index = positions // slot_len
    picked_slot = slot_index[:, None] == jnp.arange(starts.shape[0], dtype=jnp.int32)[None, :]
    piece_begin = jnp.sum(jnp.where(picked_slot, starts[None, :], 0), axis=1)
    inside = (positions >= piece_begin) & (positions < piece_begin + piece_len)
    return jnp.where(inside, slot_index, -1)


def allowed(query_pos, key_pos, query_doc, key_doc, query_pic, key_pic):
    same_doc = query_doc[:, None] == key_doc[None, :]
    earlier = key_pos[None, :] <= query_pos[:, None]
    same_pic = (query_pic[:, None] == key_pic[None, :]) & (query_pic[:, None] >= 0)
    return same_doc & (earlier | same_pic)


def local(
    tokens_in,
    output_cotangent,
    routes,
    doc_ids,
    picture_starts,
    qkv_weight,
    out_weight,
    router_weight,
    attn_gain,
    moe_gain,
    gate_up_weight,
    down_weight,
):
    qkv_full, out_full, router_full, gain_first, gain_second = (
        lax.all_gather(qkv_weight, "shard", axis=0, tiled=True),
        lax.all_gather(out_weight, "shard", axis=0, tiled=True),
        lax.all_gather(router_weight, "shard", axis=0, tiled=True),
        lax.all_gather(attn_gain, "shard", axis=0, tiled=True),
        lax.all_gather(moe_gain, "shard", axis=0, tiled=True),
    )
    gain_one = gain_first.astype(jnp.float32)
    gain_two = gain_second.astype(jnp.float32)
    tok_rows = tokens_in.shape[0]
    seq_len = doc_ids.shape[1]
    groups = HEADS // KV_HEADS
    q_width = HEADS * HEAD_DIM
    kv_width = KV_HEADS * HEAD_DIM
    score_scale = HEAD_DIM ** (-0.5)
    shard_at = lax.axis_index("shard")
    query_pos = shard_at * tok_rows + jnp.arange(tok_rows, dtype=jnp.int32)
    key_pos = jnp.arange(seq_len, dtype=jnp.int32)
    key_doc = doc_ids[0]
    key_pic = picture_ids(key_pos, picture_starts[0], SLOT, PIECE)
    query_doc = lax.dynamic_slice_in_dim(key_doc, shard_at * tok_rows, tok_rows)
    query_pic = lax.dynamic_slice_in_dim(key_pic, shard_at * tok_rows, tok_rows)
    tokens_f = tokens_in.astype(jnp.float32)
    normed_one, normal_one, inverse_one = rms_norm(tokens_f, gain_one)
    normed_in = normed_one.astype(jnp.bfloat16)
    qkv_rows = jnp.dot(normed_in, qkv_full, preferred_element_type=jnp.float32)
    cosine, sine_table = rope_tables(query_pos, HEAD_DIM)
    queries = (
        rotate(qkv_rows[:, :q_width].reshape(tok_rows, HEADS, HEAD_DIM), cosine, sine_table)
        .astype(jnp.bfloat16)
        .reshape(tok_rows, KV_HEADS, groups, HEAD_DIM)
    )
    key_local = (
        rotate(
            qkv_rows[:, q_width : q_width + kv_width].reshape(tok_rows, KV_HEADS, HEAD_DIM),
            cosine,
            sine_table,
        )
        .astype(jnp.bfloat16)
        .reshape(tok_rows, kv_width)
    )
    value_local = qkv_rows[:, q_width + kv_width :].astype(jnp.bfloat16)
    all_keys, all_values = (
        lax.all_gather(key_local, "shard", axis=0, tiled=True),
        lax.all_gather(value_local, "shard", axis=0, tiled=True),
    )
    span_len = min(512, seq_len)
    span_count = seq_len // span_len

    def block_scores(first_row, key_rows):
        key_block = lax.dynamic_slice_in_dim(key_rows, first_row, span_len, 0).reshape(
            span_len, KV_HEADS, HEAD_DIM
        )
        raw_scores = (
            jnp.einsum("tgrd,kgd->tgrk", queries, key_block, preferred_element_type=jnp.float32)
            * score_scale
        )
        block_pos = lax.dynamic_slice_in_dim(key_pos, first_row, span_len)
        block_doc = lax.dynamic_slice_in_dim(key_doc, first_row, span_len)
        block_pic = lax.dynamic_slice_in_dim(key_pic, first_row, span_len)
        visible = allowed(query_pos, block_pos, query_doc, block_doc, query_pic, block_pic)[
            :, None, None, :
        ]
        return (raw_scores, visible, key_block)

    def value_block_at(first_row, value_rows):
        return lax.dynamic_slice_in_dim(value_rows, first_row, span_len, 0).reshape(
            span_len, KV_HEADS, HEAD_DIM
        )

    def max_step(step_index, carry):
        run_max, run_sum = carry
        raw_scores, visible, key_block = block_scores(step_index * span_len, all_keys)
        masked = jnp.where(visible, raw_scores, masked_score)
        new_max = jnp.maximum(run_max, jnp.max(masked, -1))
        shifted = jnp.where(visible, jnp.exp(masked - new_max[..., None]), 0.0)
        return (new_max, run_sum * jnp.exp(run_max - new_max) + jnp.sum(shifted, -1))

    stat_shape = (tok_rows, KV_HEADS, groups)
    run_max, run_sum = lax.fori_loop(
        0,
        span_count,
        max_step,
        (jnp.full(stat_shape, masked_score, jnp.float32), jnp.zeros(stat_shape, jnp.float32)),
    )
    log_total = run_max + jnp.log(run_sum)

    def probs_of(raw_scores, visible):
        return jnp.exp(jnp.where(visible, raw_scores - log_total[..., None], masked_score))

    def value_step(step_index, summed):
        first_row = step_index * span_len
        raw_scores, visible, key_block = block_scores(first_row, all_keys)
        probs = probs_of(raw_scores, visible).astype(jnp.bfloat16)
        return summed + jnp.einsum(
            "tgrk,kgd->tgrd",
            probs,
            value_block_at(first_row, all_values),
            preferred_element_type=jnp.float32,
        )

    summed = lax.fori_loop(
        0, span_count, value_step, jnp.zeros((tok_rows, KV_HEADS, groups, HEAD_DIM), jnp.float32)
    )
    attended = summed.reshape(tok_rows, q_width).astype(jnp.bfloat16)
    branch = lax.dot_general(
        attended, out_full, (((1,), (1,)), ((), ())), preferred_element_type=jnp.float32
    )
    middle = tokens_f + branch
    normed_two, normal_two, inverse_two = rms_norm(middle, gain_two)
    normed_mid = normed_two.astype(jnp.bfloat16)
    logits = jnp.dot(normed_mid, router_full, preferred_element_type=jnp.float32)
    gates = jax.nn.softmax(jnp.take_along_axis(logits, routes, 1), axis=-1)
    route_hits = routes[:, :, None] == jnp.arange(EXPERTS, dtype=jnp.int32)[None, None, :]
    hit_count = jnp.sum(route_hits.astype(jnp.int32), 1)
    before = jnp.cumsum(hit_count, 0) - hit_count
    slot_index = jnp.take_along_axis(before, routes, 1)
    kept_pair = slot_index < CAP
    flat_slot = routes * CAP + slot_index
    capacity_rows = EXPERTS * CAP
    target = jnp.where(kept_pair, flat_slot, capacity_rows)
    token_ids = jnp.broadcast_to(jnp.arange(tok_rows, dtype=jnp.int32)[:, None], (tok_rows, TOP))
    owner_row = (
        jnp.full((capacity_rows + 1,), -1, jnp.int32)
        .at[target.reshape(-1)]
        .set(token_ids.reshape(-1))[:capacity_rows]
    )
    filled = owner_row >= 0
    source_row = jnp.maximum(owner_row, 0)
    expert_groups = lax.axis_size("expert")
    local_experts = EXPERTS // expert_groups
    send_rows = jnp.where(
        filled[:, None], normed_mid[source_row], jnp.zeros((), jnp.bfloat16)
    ).reshape(expert_groups, local_experts, CAP, D)
    received = lax.all_to_all(send_rows, "expert", split_axis=0, concat_axis=0, tiled=True)
    gate_up_full, down_full = (
        lax.all_gather(gate_up_weight, "shard", axis=0, tiled=True),
        lax.all_gather(down_weight, "shard", axis=0, tiled=True),
    )
    gate_up3 = gate_up_full.reshape(D, local_experts, 2 * H)
    down3 = down_full.reshape(D, local_experts, H)
    projected = jnp.einsum("secd,dej->secj", received, gate_up3, preferred_element_type=jnp.float32)
    gate_part = projected[..., :H]
    up_part = projected[..., H:]
    sigma = jax.nn.sigmoid(gate_part)
    silu_value = gate_part * sigma
    hidden = (silu_value * up_part).astype(jnp.bfloat16)
    expert_out = jnp.einsum(
        "secj,dej->secd", hidden, down3, preferred_element_type=jnp.float32
    ).astype(jnp.bfloat16)
    returned = lax.all_to_all(
        expert_out, "expert", split_axis=0, concat_axis=0, tiled=True
    ).reshape(capacity_rows, D)
    safe_flat = jnp.where(kept_pair, flat_slot, 0)
    picked = returned[safe_flat].astype(jnp.float32)
    pair_weight = jnp.where(kept_pair, gates, 0.0)
    moe_sum = jnp.einsum("tk,tkd->td", pair_weight, picked)
    output = (middle + moe_sum).astype(jnp.bfloat16)
    grad_out = output_cotangent.astype(jnp.float32)
    gate_grad = jnp.where(kept_pair, jnp.einsum("td,tkd->tk", grad_out, picked), 0.0)
    slot_gate = (
        jnp.zeros((capacity_rows + 1,), jnp.float32)
        .at[target.reshape(-1)]
        .set(gates.reshape(-1))[:capacity_rows]
    )
    grad_send = (
        jnp.where(filled[:, None], slot_gate[:, None] * grad_out[source_row], 0.0)
        .astype(jnp.bfloat16)
        .reshape(expert_groups, local_experts, CAP, D)
    )
    grad_received = lax.all_to_all(grad_send, "expert", split_axis=0, concat_axis=0, tiled=True)
    keys_back, values_back = (
        lax.all_gather(key_local, "shard", axis=0, tiled=True),
        lax.all_gather(value_local, "shard", axis=0, tiled=True),
    )
    again_up, again_down = (
        lax.all_gather(gate_up_weight, "shard", axis=0, tiled=True),
        lax.all_gather(down_weight, "shard", axis=0, tiled=True),
    )
    gate_up_back = again_up.reshape(D, local_experts, 2 * H)
    down_back = again_down.reshape(D, local_experts, H)
    hidden_grad = jnp.einsum(
        "secd,dej->secj", grad_received, down_back, preferred_element_type=jnp.float32
    )
    silu_slope = sigma * (1.0 + gate_part * (1.0 - sigma))
    proj_grad = jnp.concatenate(
        [hidden_grad * up_part * silu_slope, hidden_grad * silu_value], -1
    ).astype(jnp.bfloat16)
    row_grad = jnp.einsum(
        "secj,dej->secd", proj_grad, gate_up_back, preferred_element_type=jnp.float32
    ).astype(jnp.bfloat16)
    grad_back = lax.all_to_all(row_grad, "expert", split_axis=0, concat_axis=0, tiled=True).reshape(
        capacity_rows, D
    )
    row_count = gate_up_weight.shape[0] * lax.axis_size("shard")
    up_terms = jnp.einsum(
        "secd,secj->dej", received, proj_grad, preferred_element_type=jnp.float32
    ).reshape(row_count, local_experts * 2 * H)
    down_terms = jnp.einsum(
        "secd,secj->dej", grad_received, hidden, preferred_element_type=jnp.float32
    ).reshape(row_count, local_experts * H)
    expert_sums = lax.psum_scatter(
        jnp.concatenate([up_terms, down_terms], 1).astype(jnp.bfloat16),
        "shard",
        scatter_dimension=0,
        tiled=True,
    ).astype(jnp.float32)
    gate_up_grad = expert_sums[:, : local_experts * 2 * H]
    down_grad = expert_sums[:, local_experts * 2 * H :]
    mid_norm_grad = jnp.einsum(
        "tk,tkd->td", kept_pair.astype(jnp.float32), grad_back[safe_flat].astype(jnp.float32)
    )
    chosen_grad = gates * (gate_grad - jnp.sum(gates * gate_grad, -1, keepdims=True))
    logit_grad = jnp.sum(jnp.where(route_hits, chosen_grad[:, :, None], 0.0), 1).astype(
        jnp.bfloat16
    )
    mid_norm_grad = mid_norm_grad + lax.dot_general(
        logit_grad, router_full, (((1,), (1,)), ((), ())), preferred_element_type=jnp.float32
    )
    router_grad = lax.dot_general(
        normed_mid, logit_grad, (((0,), (0,)), ((), ())), preferred_element_type=jnp.float32
    )
    mid_part, moe_gain_grad = rms_back(mid_norm_grad, gain_two, normal_two, inverse_two)
    mid_grad = grad_out + mid_part
    branch_grad = mid_grad.astype(jnp.bfloat16)
    out_weight_grad = lax.dot_general(
        branch_grad, attended, (((0,), (0,)), ((), ())), preferred_element_type=jnp.float32
    )
    attended_grad = (
        jnp.dot(branch_grad, out_full, preferred_element_type=jnp.float32)
        .astype(jnp.bfloat16)
        .reshape(tok_rows, KV_HEADS, groups, HEAD_DIM)
    )

    def dot_step(step_index, row_dot):
        first_row = step_index * span_len
        raw_scores, visible, key_block = block_scores(first_row, keys_back)
        prob_full = probs_of(raw_scores, visible)
        prob_grad = jnp.einsum(
            "tgrd,kgd->tgrk",
            attended_grad,
            value_block_at(first_row, values_back),
            preferred_element_type=jnp.float32,
        )
        return row_dot + jnp.sum(prob_full * prob_grad, -1)

    row_dot = lax.fori_loop(0, span_count, dot_step, jnp.zeros(stat_shape, jnp.float32))

    def grad_step(step_index, carry):
        query_grad, key_terms, value_terms = carry
        first_row = step_index * span_len
        raw_scores, visible, key_block = block_scores(first_row, keys_back)
        prob_full = probs_of(raw_scores, visible)
        prob_grad = jnp.einsum(
            "tgrd,kgd->tgrk",
            attended_grad,
            value_block_at(first_row, values_back),
            preferred_element_type=jnp.float32,
        )
        score_grad = (prob_full * (prob_grad - row_dot[..., None])).astype(jnp.bfloat16)
        query_grad = query_grad + jnp.einsum(
            "tgrk,kgd->tgrd", score_grad, key_block, preferred_element_type=jnp.float32
        )
        key_part = (
            jnp.einsum(
                "tgrk,tgrd->kgd", score_grad, queries, preferred_element_type=jnp.float32
            ).reshape(span_len, kv_width)
            * score_scale
        )
        value_part = jnp.einsum(
            "tgrk,tgrd->kgd",
            prob_full.astype(jnp.bfloat16),
            attended_grad,
            preferred_element_type=jnp.float32,
        ).reshape(span_len, kv_width)
        key_terms = lax.dynamic_update_slice_in_dim(key_terms, key_part, first_row, 0)
        value_terms = lax.dynamic_update_slice_in_dim(value_terms, value_part, first_row, 0)
        return (query_grad, key_terms, value_terms)

    query_grad, key_terms, value_terms = lax.fori_loop(
        0,
        span_count,
        grad_step,
        (
            jnp.zeros((tok_rows, KV_HEADS, groups, HEAD_DIM), jnp.float32),
            jnp.zeros((seq_len, kv_width), jnp.float32),
            jnp.zeros((seq_len, kv_width), jnp.float32),
        ),
    )
    key_grad, value_grad = (
        lax.psum_scatter(
            key_terms.astype(jnp.bfloat16), "shard", scatter_dimension=0, tiled=True
        ).astype(jnp.float32),
        lax.psum_scatter(
            value_terms.astype(jnp.bfloat16), "shard", scatter_dimension=0, tiled=True
        ).astype(jnp.float32),
    )
    query_back = rotate_back(
        (query_grad * score_scale).reshape(tok_rows, HEADS, HEAD_DIM), cosine, sine_table
    ).reshape(tok_rows, q_width)
    key_back = rotate_back(
        key_grad.reshape(tok_rows, KV_HEADS, HEAD_DIM), cosine, sine_table
    ).reshape(tok_rows, kv_width)
    qkv_grad_rows = jnp.concatenate([query_back, key_back, value_grad], 1).astype(jnp.bfloat16)
    qkv_weight_grad = lax.dot_general(
        normed_in, qkv_grad_rows, (((0,), (0,)), ((), ())), preferred_element_type=jnp.float32
    )
    in_norm_grad = lax.dot_general(
        qkv_grad_rows, qkv_full, (((1,), (1,)), ((), ())), preferred_element_type=jnp.float32
    )
    in_part, attn_gain_grad = rms_back(in_norm_grad, gain_one, normal_one, inverse_one)
    input_grad = (mid_grad + in_part).astype(jnp.bfloat16)
    dense_sums = (
        lax.psum_scatter(
            qkv_weight_grad.astype(jnp.bfloat16), "shard", scatter_dimension=0, tiled=True
        ).astype(jnp.float32),
        lax.psum_scatter(
            out_weight_grad.astype(jnp.bfloat16), "shard", scatter_dimension=0, tiled=True
        ).astype(jnp.float32),
        lax.psum_scatter(
            router_grad.astype(jnp.bfloat16), "shard", scatter_dimension=0, tiled=True
        ).astype(jnp.float32),
        lax.psum_scatter(
            attn_gain_grad.astype(jnp.bfloat16), "shard", scatter_dimension=0, tiled=True
        ).astype(jnp.float32),
        lax.psum_scatter(
            moe_gain_grad.astype(jnp.bfloat16), "shard", scatter_dimension=0, tiled=True
        ).astype(jnp.float32),
    )
    dense_totals = (
        lax.psum(dense_sums[0].astype(jnp.bfloat16), "expert").astype(jnp.float32),
        lax.psum(dense_sums[1].astype(jnp.bfloat16), "expert").astype(jnp.float32),
        lax.psum(dense_sums[2].astype(jnp.bfloat16), "expert").astype(jnp.float32),
        lax.psum(dense_sums[3].astype(jnp.bfloat16), "expert").astype(jnp.float32),
        lax.psum(dense_sums[4].astype(jnp.bfloat16), "expert").astype(jnp.float32),
    )
    return (
        output,
        input_grad,
        dense_totals[0],
        dense_totals[1],
        dense_totals[2],
        dense_totals[3],
        dense_totals[4],
        gate_up_grad,
        down_grad,
    )


GROUPS = 4
SHARDS = 8
rows_by_cols = ((1,), (0,))
rows_by_rows = ((1,), (1,))
cols_by_cols = ((0,), (0,))


def dot(one, two, dims):
    return lax.dot_general(one, two, (dims, ((), ())), preferred_element_type=jnp.float32)


def whole_spec(shape):
    return pl.BlockSpec(shape, lambda i, ids: (0,) * len(shape), pipeline_mode=pl.Buffered(1))


def block_spec(shape, index):
    return pl.BlockSpec(shape, lambda i, ids: index, pipeline_mode=pl.Buffered(1))


def out_spec(shape, index):
    return pl.BlockSpec(shape, lambda i, ids: index)


in_place = pl.BlockSpec(memory_space=pl.ANY)


def shaped(shape, dtype=jnp.bfloat16):
    return jax.ShapeDtypeStruct(shape, dtype)


def call(kernel, name, out_shape, in_specs, out_specs, args, scratch=(), aliases=None, flops=0, steps=1):
    moved = sum(a.size * a.dtype.itemsize for a in args[1:])
    return pl.pallas_call(
        kernel,
        name=name,
        out_shape=out_shape,
        grid_spec=pltpu.PrefetchScalarGridSpec(
            num_scalar_prefetch=1,
            grid=(steps,),
            in_specs=in_specs,
            out_specs=out_specs,
            scratch_shapes=list(scratch),
        ),
        input_output_aliases=aliases or {},
        compiler_params=pltpu.CompilerParams(
            vmem_limit_bytes=58 * 1024 * 1024, dimension_semantics=("arbitrary",)
        ),
        cost_estimate=pl.CostEstimate(flops=flops, transcendentals=0, bytes_accessed=moved),
    )(*args)


def place_rows(offsets, parts, height):
    count, fine, width = parts[0].shape

    def kernel(at, *refs):
        sources, target, done = refs[: len(parts)], refs[len(parts)], refs[-1]
        copies = []
        for n, source in enumerate(sources):
            for i in range(count):
                row = pl.multiple_of(at[n * count + i], 16)
                copies.append(
                    pltpu.make_async_copy(
                        source.at[i], target.at[pl.ds(row, fine)], done.at[n * count + i]
                    )
                )
        for copy in copies:
            copy.start()
        for copy in copies:
            copy.wait()

    return call(
        kernel,
        "place_rows",
        shaped((height, width), parts[0].dtype),
        [in_place] * len(parts),
        out_spec((height, width), (0, 0)),
        (offsets,) + tuple(parts),
        scratch=[pltpu.SemaphoreType.DMA((len(parts) * count,))],
    )


def take_rows(offsets, array, parts, count, fine):
    width = array.shape[1]

    def kernel(at, source, *refs):
        targets, done = refs[:parts], refs[-1]
        copies = []
        for n, target in enumerate(targets):
            for i in range(count):
                row = pl.multiple_of(at[n * count + i], 16)
                copies.append(
                    pltpu.make_async_copy(
                        source.at[pl.ds(row, fine)], target.at[i], done.at[n * count + i]
                    )
                )
        for copy in copies:
            copy.start()
        for copy in copies:
            copy.wait()

    return call(
        kernel,
        "take_rows",
        [shaped((count, fine, width), array.dtype)] * parts,
        [in_place],
        [out_spec((count, fine, width), (0, 0, 0))] * parts,
        (offsets, array),
        scratch=[pltpu.SemaphoreType.DMA((parts * count,))],
    )


def pack_kernel(ids, up, gate_part, up_part, down, down_part, gain, ups, downs):
    width = up.shape[1]
    part = gate_part.shape[1]
    scale = gain[...]

    def scaled(ref):
        return (ref[...].astype(jnp.float32) * scale).astype(jnp.bfloat16)

    ups[0, :, :width] = scaled(up)
    ups[0, :, width : width + part] = scaled(gate_part)
    ups[0, :, width + part :] = scaled(up_part)
    downs[0, :, : down.shape[1]] = down[...]
    downs[0, :, down.shape[1] :] = down_part[...]


def unpack_kernel(ids, up, up_parts, down, down_parts, gain, up_grad, down_grad):
    part = down_parts.shape[2]
    scale = gain[...]
    expert = pl.program_id(0)
    whole = pl.num_programs(0) - 2

    @pl.when(expert < whole)
    def _():
        up_grad[...] = up[0].astype(jnp.float32) * scale
        down_grad[...] = down[0].astype(jnp.float32)

    @pl.when(expert >= whole)
    def _():
        for i in range(up_parts.shape[0]):
            at = i * part
            up_grad[:, at : at + part] = up_parts[i, :, :part].astype(jnp.float32) * scale
            up_grad[:, H + at : H + at + part] = up_parts[i, :, part:].astype(jnp.float32) * scale
            down_grad[:, at : at + part] = down_parts[i].astype(jnp.float32)


def turn(rows, cosine, sine):
    width = rows.shape[1]
    lanes = lax.broadcasted_iota(jnp.int32, (rows.shape[0], 128), 1)
    first = lanes % HEAD_DIM < HEAD_DIM // 2
    turned = []
    for at in range(0, width, 128):
        piece = rows[:, at : at + 128]
        swapped = jnp.where(
            first,
            pltpu.roll(piece, 128 - HEAD_DIM // 2, 1),
            pltpu.roll(piece, HEAD_DIM // 2, 1),
        )
        turned.append(piece * cosine + swapped * sine)
    return jnp.concatenate(turned, 1)


def qkv_kernel(ids, normed, weight, cosine, sine, queries, key_value):
    step = pl.program_id(0)
    found = dot(normed[...], weight[...], rows_by_cols)

    @pl.when(step < 3)
    def _():
        queries[...] = turn(found, cosine[...], sine[...]).astype(jnp.bfloat16)

    @pl.when(step == 3)
    def _():
        key_value[...] = turn(found, cosine[...], sine[...]).astype(jnp.bfloat16)

    @pl.when(step == 4)
    def _():
        key_value[...] = found.astype(jnp.bfloat16)


def attend_kernel(ids, queries, key_line, key_other, value_line, value_other, bias, attended, logs):
    scale = HEAD_DIM ** (-0.5)
    groups = HEADS // KV_HEADS
    hidden = bias[...]
    keys = jnp.concatenate([key_line[...], key_other[...]], 0)
    values = jnp.concatenate([value_line[...], value_other[...]], 0)
    lanes = lax.broadcasted_iota(jnp.int32, (queries.shape[0], 128), 1)
    totals = jnp.zeros((queries.shape[0], 128), jnp.float32)
    found = []
    for n in range(2 * groups):
        at = n // groups * HEAD_DIM
        scores = dot(
            queries[:, n * HEAD_DIM : (n + 1) * HEAD_DIM], keys[:, at : at + HEAD_DIM], rows_by_rows
        )
        scores = scores * scale + hidden
        top = jnp.max(scores, 1, keepdims=True)
        raised = jnp.exp(scores - top)
        total = jnp.sum(raised, 1, keepdims=True)
        probs = (raised / total).astype(jnp.bfloat16)
        found.append(dot(probs, values[:, at : at + HEAD_DIM], rows_by_cols))
        totals = jnp.where(lanes == n, top + jnp.log(total), totals)
    attended[...] = jnp.concatenate(found, 1).astype(jnp.bfloat16)
    logs[0] = totals


def attend_back_kernel(
    ids, queries, grads, key_line, key_other, value_line, value_other, bias, logs, cosine, sine,
    query_grad, key_mine, key_theirs, value_mine, value_theirs,
):
    scale = HEAD_DIM ** (-0.5)
    groups = HEADS // KV_HEADS
    hidden = bias[...]
    keys = jnp.concatenate([key_line[...], key_other[...]], 0)
    values = jnp.concatenate([value_line[...], value_other[...]], 0)
    half = key_line.shape[0]
    found = []
    key_found, value_found = [], []
    for n in range(2 * groups):
        own = n // groups
        at = own * HEAD_DIM
        head = slice(n * HEAD_DIM, (n + 1) * HEAD_DIM)
        query = queries[:, head]
        grad = grads[:, head]
        scores = dot(query, keys[:, at : at + HEAD_DIM], rows_by_rows) * scale + hidden
        probs = jnp.exp(scores - lane_value(logs[0], n))
        prob_grad = dot(grad, values[:, at : at + HEAD_DIM], rows_by_rows)
        row_dot = jnp.sum(probs * prob_grad, 1, keepdims=True)
        score_grad = (probs * (prob_grad - row_dot)).astype(jnp.bfloat16)
        found.append(dot(score_grad, keys[:, at : at + HEAD_DIM], rows_by_cols))
        key_part = dot(score_grad, query, cols_by_cols)
        value_part = dot(probs.astype(jnp.bfloat16), grad, cols_by_cols)
        if n % groups:
            key_found[own] = key_found[own] + key_part
            value_found[own] = value_found[own] + value_part
        else:
            key_found.append(key_part)
            value_found.append(value_part)
    found = jnp.concatenate(found, 1) * scale
    query_grad[...] = turn(found, cosine[...], -sine[...]).astype(jnp.bfloat16)
    key_found = (jnp.concatenate(key_found, 1) * scale).astype(jnp.bfloat16)
    value_found = jnp.concatenate(value_found, 1).astype(jnp.bfloat16)
    key_mine[...] = key_found[:half]
    key_theirs[...] = key_found[half:]
    value_mine[...] = value_found[:half]
    value_theirs[...] = value_found[half:]


def lane_value(rows, index):
    lanes = lax.broadcasted_iota(jnp.int32, rows.shape, 1)
    return jnp.sum(jnp.where(lanes == index, rows, 0.0), 1, keepdims=True)


def picks_of(extra, one, two):
    extra = extra.astype(jnp.float32)
    lanes = lax.broadcasted_iota(jnp.int32, (extra.shape[0], 2 * CAP), 1)
    wanted = jnp.where(lanes < CAP, lane_value(extra, one), lane_value(extra, two))
    place = jnp.where(lanes < CAP, lanes, lanes - CAP).astype(jnp.float32)
    return jnp.where(wanted == place, 1.0, 0.0).astype(jnp.bfloat16)


def grad_side_kernel(ids, half, other, down_one, down_two, kept_gs, gs, plain):
    count = half.shape[0]
    for i in range(2 * count):
        source = half if i < count else other
        pick = picks_of(source[i % count, :, D:], ids[0], ids[1])
        found = dot(pick, source[i % count, :, :D], cols_by_cols).astype(jnp.bfloat16)
        gs[0, i * CAP : (i + 1) * CAP] = found[:CAP]
        gs[1, i * CAP : (i + 1) * CAP] = found[CAP:]
    width = down_one.shape[1]
    plain[:, :width] = dot(gs[0], down_one[...], rows_by_cols)
    plain[:, width:] = dot(gs[1], down_two[...], rows_by_cols)


def combine_rows(ids, rows, slots_half, slots_other, back_half, back_other):
    count = slots_half.shape[0]
    for i in range(2 * count):
        target = back_half if i < count else back_other
        slots = slots_half if i < count else slots_other
        pick = picks_of(slots[i % count], ids[0], ids[1])
        at = slice(i * CAP, (i + 1) * CAP)
        both = jnp.concatenate([rows[0, at], rows[1, at]], 0)
        target[i % count] = dot(pick, both, rows_by_cols).astype(jnp.bfloat16)


def row_side_kernel(
    ids, half, other, slots_half, slots_other, plain, up_one, up_two, kept_xs, kept_hid, kept_pg,
    back_half, back_other, xs, hid, pg, gates, tokens, back_rows,
):
    total = xs.shape[1]
    count = half.shape[0]
    for i in range(2 * count):
        source = half if i < count else other
        slots = slots_half if i < count else slots_other
        pick = picks_of(slots[i % count], ids[0], ids[1])
        found = dot(pick, source[i % count], cols_by_cols)
        extra = found[:, D:]
        found = found.astype(jnp.bfloat16)
        at = slice(i * CAP, (i + 1) * CAP)
        for n in range(2):
            xs[n, at] = found[n * CAP : (n + 1) * CAP, :D]
            own = extra[n * CAP : (n + 1) * CAP]
            gates[n, at] = lane_value(own, ids[n]) + lane_value(own, ids[n] + EXPERTS)
    first = 0
    for n, up in ((0, up_one), (1, up_two)):
        width = up.shape[1] // 2
        projected = dot(xs[n], up[...], rows_by_cols)
        gate_part = projected[:, :width]
        up_part = projected[:, width:]
        own_plain = plain[:, first : first + width]
        sigma = 1.0 / (1.0 + jnp.exp(-gate_part))
        silu_value = gate_part * sigma
        hidden = silu_value * up_part
        tokens[n] = jnp.sum(hidden * own_plain, 1, keepdims=True)
        hid[:, first : first + width] = (hidden * gates[n]).astype(jnp.bfloat16)
        hidden_grad = own_plain * gates[n]
        slope = sigma * (1.0 + gate_part * (1.0 - sigma))
        pg[:, 2 * first : 2 * first + width] = (hidden_grad * up_part * slope).astype(jnp.bfloat16)
        pg[:, 2 * first + width : 2 * first + 2 * width] = (hidden_grad * silu_value).astype(
            jnp.bfloat16
        )
        own_pg = pg[:, 2 * first : 2 * first + 2 * width]
        back_rows[n, :, :D] = dot(own_pg, up[...], rows_by_rows).astype(jnp.bfloat16)
        lanes = lax.broadcasted_iota(jnp.int32, (total, 128), 1)
        back_rows[n, :, D:] = jnp.where(lanes == ids[n], tokens[n], 0.0).astype(jnp.bfloat16)
        first += width
    combine_rows(ids, back_rows, slots_half, slots_other, back_half, back_other)


def out_side_kernel(
    ids, hid, slots_half, slots_other, down_one, down_two, back_half, back_other, out_rows
):
    width = down_one.shape[1]
    out_rows[0] = dot(hid[:, :width], down_one[...], rows_by_rows).astype(jnp.bfloat16)
    out_rows[1] = dot(hid[:, width:], down_two[...], rows_by_rows).astype(jnp.bfloat16)
    combine_rows(ids, out_rows, slots_half, slots_other, back_half, back_other)


def terms_kernel(ids, xs, gs, pg, hid, terms_up, terms_down):
    depth = terms_up.shape[1]
    width = terms_down.shape[2]
    pieces = (
        (terms_up, xs, pg, 0, 0, 2 * H),
        (terms_up, xs, pg, 1, 2 * H, 2 * width),
        (terms_down, gs, hid, 0, 0, H),
        (terms_down, gs, hid, 1, H, width),
    )
    for target, one, two, n, left, right in pieces:
        found = dot(one[n], two[:, left:right], cols_by_cols).astype(jnp.bfloat16)
        for i in range(2):
            target[i, :, left:right] = found[i * depth : (i + 1) * depth]


def hop(values, pairs):
    return lax.ppermute(values, ("expert", "shard"), pairs)


def hop_pairs(step):
    return [
        (e * SHARDS + s, step(e, s)[0] * SHARDS + step(e, s)[1])
        for e in range(GROUPS)
        for s in range(SHARDS)
    ]


to_core = hop_pairs(lambda e, s: (e, s ^ 1))
to_line = [hop_pairs(lambda e, s, k=k: (e, s ^ (2 * k))) for k in range(4)]
to_first = hop_pairs(lambda e, s: (e ^ (1 + s % 2), s))
to_second = hop_pairs(lambda e, s: (e ^ (2 - s % 2), s))


def add_low(one, two):
    return (one.astype(jnp.float32) + two.astype(jnp.float32)).astype(jnp.bfloat16)


def total_of(line):
    return sum(piece.astype(jnp.float32) for piece in line)


class Flow:
    def __init__(self, steps):
        self.steps = steps
        self.result = None
        self.feed(None)

    def feed(self, values):
        try:
            self.want = self.steps.send(values)
        except StopIteration as stop:
            self.want = None
            self.result = stop.value


class Order:
    def __init__(self, mark):
        self.mark = mark

    def tie(self, values):
        values, self.mark = lax.optimization_barrier((values, self.mark))
        return values

    def round(self, flows, work=None):
        values, self.mark = lax.optimization_barrier(([f.want[0] for f in flows], self.mark))
        found = [hop(v, f.want[1]) for v, f in zip(values, flows)]
        found, work, self.mark = lax.optimization_barrier((found, work, self.mark))
        for flow, values in zip(flows, found):
            flow.feed(values)
        return work


def one_hop(values, pairs):
    found = yield values, pairs
    return found


def line_flows(own):
    return [Flow(one_hop(own, to_line[k])) for k in (1, 2, 3)]


def spread_pair(pieces):
    two = jnp.stack(pieces)
    first = yield two, to_first
    four = jnp.concatenate([two, first])
    second = yield four, to_second
    eight = jnp.concatenate([four, second])
    other = yield eight, to_core
    return eight, other


def collect_pair(mine, theirs):
    found = yield theirs, to_core
    keep, give = add_low(mine[:4], found[:4]), add_low(mine[4:], found[4:])
    found = yield give, to_second
    keep, give = add_low(keep[:2], found[:2]), add_low(keep[2:], found[2:])
    found = yield give, to_first
    return [add_low(keep[i], found[i]) for i in range(2)]


def collect_all(mine, theirs):
    found = yield theirs, to_core
    keep, give = add_low(mine[:8], found[:8]), add_low(mine[8:], found[8:])
    found = yield give, to_second
    keep, give = add_low(keep[:4], found[:4]), add_low(keep[4:], found[4:])
    found = yield give, to_first
    return [add_low(keep[i], found[i]) for i in range(4)]


def share_flow(own, places):
    first = yield own, to_first
    pair = jnp.stack([own, first])
    second = yield pair, to_second
    quarters = jnp.concatenate([pair, second])
    return jnp.concatenate(
        [lax.dynamic_index_in_dim(quarters, place, 0, keepdims=False) for place in places]
    )


def local_hops(
    tokens_in,
    output_cotangent,
    routes,
    doc_ids,
    picture_starts,
    qkv_weight,
    out_weight,
    router_weight,
    attn_gain,
    moe_gain,
    gate_up_weight,
    down_weight,
):
    low = jnp.bfloat16
    full = jnp.float32
    rows = tokens_in.shape[0]
    seq_len = doc_ids.shape[1]
    q_width = HEADS * HEAD_DIM
    kv_width = KV_HEADS * HEAD_DIM
    qkv_width = q_width + 2 * kv_width
    group_at = lax.axis_index("expert")
    shard_at = lax.axis_index("shard")
    own_experts = EXPERTS // GROUPS
    whole = own_experts // SHARDS * SHARDS
    split = own_experts - whole
    share = SHARDS // split
    part = H // share
    hid_width = H + part
    depth = gate_up_weight.shape[0]
    height = SHARDS * depth
    fine = depth // GROUPS
    pad = 128 - EXPERTS
    gain_one = attn_gain.astype(full)[:, None]
    gain_two = moe_gain.astype(full)[:, None]
    expert_one = group_at * own_experts + shard_at
    expert_two = group_at * own_experts + whole + shard_at // share
    ids = jnp.stack([expert_one, expert_two])
    order = Order(jnp.zeros((8, 128), full))

    spot = jnp.arange(GROUPS * SHARDS, dtype=jnp.int32)
    spot_core = spot // 8 % 2
    spot_mate = 1 + (shard_at % 2 ^ spot_core)
    spot_q = spot % 8 // 2
    spot_group = jnp.where(spot_q == 1, spot_mate, jnp.where(spot_q == 2, 3 - spot_mate, spot_q))
    spot_line = spot // 16 * 2 + spot % 2
    fine_at = (shard_at ^ (2 * spot_line + spot_core)) * depth + (group_at ^ spot_group) * fine

    expert_ids = jnp.arange(EXPERTS, dtype=jnp.int32)
    hits = jnp.any(routes[:, :, None] == expert_ids[None, None, :], 1)
    earlier = jnp.arange(rows)[:, None] > jnp.arange(rows)[None, :]
    before = dot(earlier.astype(low), hits.astype(low), rows_by_cols)
    slots = jnp.where(hits & (before < CAP), before, -1.0)
    kept = slots >= 0
    grad_pay = jnp.concatenate(
        [output_cotangent, jnp.pad(slots.astype(low), ((0, 0), (0, pad)))], 1
    )

    def fine_rows(array):
        return lax.dynamic_slice_in_dim(array, group_at * fine, fine, 0)

    qkv_own = fine_rows(qkv_weight).astype(full) * fine_rows(gain_one)
    router_own = fine_rows(router_weight).astype(full) * fine_rows(gain_two)
    dense_own = jnp.concatenate([qkv_own, jnp.pad(router_own, ((0, 0), (0, pad)))], 1).astype(low)
    out_own = fine_rows(out_weight)

    def column_spec(width, index):
        return pl.BlockSpec((depth, width), lambda d, ids: (0, index(d)))

    to_parts = H // part
    pack_up, pack_down = call(
        pack_kernel,
        "pack",
        (shaped((SHARDS, depth, 2 * hid_width)), shaped((SHARDS, depth, hid_width))),
        [
            column_spec(2 * H, lambda d: d),
            column_spec(part, lambda d: (whole + d // share) * 2 * to_parts + d % share),
            column_spec(part, lambda d: (whole + d // share) * 2 * to_parts + to_parts + d % share),
            column_spec(H, lambda d: d),
            column_spec(part, lambda d: (whole + d // share) * to_parts + d % share),
            pl.BlockSpec((depth, 1), lambda d, ids: (0, 0)),
        ],
        [
            pl.BlockSpec((1, depth, 2 * hid_width), lambda d, ids: (d, 0, 0)),
            pl.BlockSpec((1, depth, hid_width), lambda d, ids: (d, 0, 0)),
        ],
        (ids, gate_up_weight, gate_up_weight, gate_up_weight, down_weight, down_weight, gain_two),
        steps=SHARDS,
    )

    def exchange(packed):
        return lax.all_to_all(packed, "shard", split_axis=0, concat_axis=0, tiled=True)

    w = line_flows(dense_own)
    order.round(w[:2])
    w_near = Flow(spread_pair([dense_own, w[0].result]))
    order.round([w[2], w_near])
    w_far = Flow(spread_pair([w[1].result, w[2].result]))
    owned_down = exchange(order.tie(pack_down)).reshape(height, hid_width)
    order.round([w_near, w_far])
    order.round([w_near, w_far])
    o = line_flows(out_own)
    order.round([w_far] + o)
    dense_full = place_rows(fine_at, w_near.result + w_far.result, height)
    router_full = dense_full[:, qkv_width:]
    owned_up = exchange(order.tie(pack_up)).reshape(height, 2 * hid_width)

    tokens_f = tokens_in.astype(full)
    inverse_one = lax.rsqrt(jnp.mean(tokens_f * tokens_f, -1, keepdims=True) + norm_eps)
    normal_one = tokens_f * inverse_one
    normed_in = normal_one.astype(low)
    query_pos = shard_at * rows + jnp.arange(rows, dtype=jnp.int32)
    cosine, sine = rope_tables(query_pos, HEAD_DIM)
    cosine = jnp.tile(cosine[:, 0], (1, 4))
    sine = jnp.tile(jnp.concatenate([-sine[:, 0], sine[:, 0]], 1), (1, 2))
    tile = 512
    queries, key_value = call(
        qkv_kernel,
        "qkv",
        (shaped((rows, q_width)), shaped((rows, 2 * kv_width))),
        [
            whole_spec((rows, D)),
            pl.BlockSpec((D, tile), lambda j, ids: (0, j)),
            whole_spec((rows, 128)),
            whole_spec((rows, 128)),
        ],
        [
            pl.BlockSpec((rows, tile), lambda j, ids: (0, jnp.minimum(j, 2))),
            pl.BlockSpec((rows, tile), lambda j, ids: (0, jnp.maximum(j - 3, 0))),
        ],
        (ids, normed_in, dense_full, cosine, sine),
        flops=2 * rows * D * qkv_width,
        steps=qkv_width // tile,
    )
    o_pairs = [
        Flow(spread_pair([out_own, o[0].result])),
        Flow(spread_pair([o[1].result, o[2].result])),
    ]
    queries, key_value = order.round(o_pairs, (queries, key_value))
    kv = line_flows(key_value)
    order.round(kv + o_pairs)
    kv_line = jnp.concatenate([key_value] + [flow.result for flow in kv])
    kv_core = Flow(one_hop(kv_line, to_core))
    owned_down = order.round([kv_core] + o_pairs, owned_down)
    kv_other = kv_core.result
    out_full = place_rows(fine_at, o_pairs[0].result + o_pairs[1].result, height)
    block_order = jnp.arange(SHARDS, dtype=jnp.int32)
    block_order = shard_at ^ (block_order % 4 * 2 + block_order // 4)
    key_pos = (
        block_order[:, None] * rows + jnp.arange(rows, dtype=jnp.int32)[None, :]
    ).reshape(seq_len)
    doc_blocks = doc_ids[0].reshape(SHARDS, rows)
    block_hits = block_order[:, None] == jnp.arange(SHARDS)[None, :]
    key_doc = jnp.sum(
        jnp.where(block_hits[:, :, None], doc_blocks[None], 0), 1
    ).reshape(seq_len)
    query_doc = key_doc[:rows]
    key_pic = picture_ids(key_pos, picture_starts[0], SLOT, PIECE)
    query_pic = key_pic[:rows]
    visible = allowed(query_pos, key_pos, query_doc, key_doc, query_pic, key_pic)
    bias = jnp.where(visible, 0.0, masked_score)
    pairs = KV_HEADS // 2
    q_tile = q_width // pairs
    kv_tile = kv_width // pairs
    half_len = seq_len // 2

    def kv_specs(first):
        return [pl.BlockSpec((half_len, kv_tile), lambda j, ids: (0, first + j))] * 2

    q_spec = pl.BlockSpec((rows, q_tile), lambda j, ids: (0, j))
    log_spec = pl.BlockSpec((1, rows, 128), lambda j, ids: (j, 0, 0))
    attended, logs = call(
        attend_kernel,
        "attend",
        (shaped((rows, q_width)), shaped((pairs, rows, 128), full)),
        [q_spec] + kv_specs(0) + kv_specs(pairs) + [whole_spec((rows, seq_len))],
        [q_spec, log_spec],
        (ids, queries, kv_line, kv_other, kv_line, kv_other, bias),
        flops=4 * rows * seq_len * q_width,
        steps=pairs,
    )
    branch = dot(attended, out_full, rows_by_rows)
    middle = tokens_f + branch
    inverse_two = lax.rsqrt(jnp.mean(middle * middle, -1, keepdims=True) + norm_eps)
    normal_two = middle * inverse_two
    normed_mid = normal_two.astype(low)
    logits = dot(normed_mid, router_full, rows_by_cols)[:, :EXPERTS]
    logits = jnp.where(hits, logits, masked_score)
    gates = jnp.exp(logits - jnp.max(logits, -1, keepdims=True))
    gates = jnp.where(hits, gates, 0.0)
    gates = gates / jnp.sum(gates, -1, keepdims=True)
    gate_low = gates.astype(low)
    gate_rest = (gates - gate_low.astype(full)).astype(low)
    row_pay = jnp.concatenate(
        [normed_mid, gate_low, gate_rest, jnp.zeros((rows, 128 - 2 * EXPERTS), low)], 1
    )

    g = line_flows(grad_pay)
    row_pay = order.round(g[:2], row_pay)
    g_near = Flow(spread_pair([grad_pay, g[0].result]))
    x = line_flows(row_pay)
    order.round([x[0], g[2], g_near])
    g_far = Flow(spread_pair([g[1].result, g[2].result]))
    x_near = Flow(spread_pair([row_pay, x[0].result]))
    order.round([x[1], x_near, g_near])
    order.round([x[2], x_near, g_near, g_far])
    x_far = Flow(spread_pair([x[1].result, x[2].result]))
    owned_up = order.round([x_near, x_far, g_far], owned_up)
    order.round([x_far, g_far])
    grad_parts = [g_near.result, g_far.result]
    row_parts = [x_near, x_far]

    slot_rows = GROUPS * SHARDS * CAP
    step_rows = slot_rows // 2
    blocks = 2 * GROUPS
    pay_spec = whole_spec((blocks, rows, D + 128))
    pay_out = out_spec((blocks, rows, D + 128), (0, 0, 0))
    slot_spec = block_spec((blocks, rows, 128), (0, 0, D // 128))
    up_specs = [
        block_spec((height, 2 * H), (0, 0)),
        block_spec((height, 2 * part), (0, H // part)),
    ]
    down_specs = [
        block_spec((height, H), (0, 0)),
        block_spec((height, part), (0, H // part)),
    ]
    back_shape = shaped((blocks, rows, D + 128))
    gs = jnp.zeros((2, slot_rows, D), low)
    xs = jnp.zeros((2, slot_rows, D), low)
    hid = jnp.zeros((slot_rows, hid_width), low)
    pg = jnp.zeros((slot_rows, 2 * hid_width), low)

    def like(array):
        return shaped(array.shape, array.dtype)

    plain = []
    for k in range(2):
        gs, found = call(
            grad_side_kernel,
            "grad_side",
            (like(gs), shaped((step_rows, hid_width), full)),
            [pay_spec, pay_spec] + down_specs + [in_place],
            [
                out_spec((2, step_rows, D), (0, k, 0)),
                out_spec((step_rows, hid_width), (0, 0)),
            ],
            (ids,) + grad_parts[k] + (owned_down, owned_down, gs),
            aliases={5: 0},
            flops=2 * step_rows * D * (hid_width + 2 * rows),
        )
        plain.append(found)

    def row_side(k):
        nonlocal xs, hid, pg
        half_back, other_back, xs, hid, pg = call(
            row_side_kernel,
            "row_side",
            (back_shape, back_shape, like(xs), like(hid), like(pg)),
            [pay_spec, pay_spec, slot_spec, slot_spec, whole_spec((step_rows, hid_width))]
            + up_specs
            + [in_place] * 3,
            [
                pay_out,
                pay_out,
                out_spec((2, step_rows, D), (0, k, 0)),
                out_spec((step_rows, hid_width), (k, 0)),
                out_spec((step_rows, 2 * hid_width), (k, 0)),
            ],
            (ids,) + row_parts[k].result + grad_parts[k] + (plain[k], owned_up, owned_up, xs, hid, pg),
            scratch=[
                pltpu.VMEM((2, step_rows, 1), full),
                pltpu.VMEM((2, step_rows, 1), full),
                pltpu.VMEM((2, step_rows, D + 128), low),
            ],
            aliases={8: 2, 9: 3, 10: 4},
            flops=8 * step_rows * D * (hid_width + rows),
        )
        return half_back, other_back

    back_near = order.round([x_far], row_side(0))
    b_near = Flow(collect_pair(*back_near))
    back_far = order.round([b_near], row_side(1))
    b_far = Flow(collect_pair(*back_far))

    def lane_block(i, ids):
        return (0, 0, i)

    terms = call(
        terms_kernel,
        "terms",
        (shaped((SHARDS, depth, 2 * hid_width)), shaped((SHARDS, depth, hid_width))),
        [
            pl.BlockSpec((2, slot_rows, 2 * depth), lane_block),
            pl.BlockSpec((2, slot_rows, 2 * depth), lane_block),
            whole_spec((slot_rows, 2 * hid_width)),
            whole_spec((slot_rows, hid_width)),
        ],
        [
            pl.BlockSpec((2, depth, 2 * hid_width), lambda i, ids: (i, 0, 0)),
            pl.BlockSpec((2, depth, hid_width), lambda i, ids: (i, 0, 0)),
        ],
        (ids, xs, gs, pg, hid),
        flops=2 * slot_rows * D * 3 * hid_width,
        steps=4,
    )
    terms = order.round([b_near, b_far], terms)
    order.round([b_near, b_far])
    b_line = [Flow(one_hop(b_near.result[1], to_line[1]))]
    terms_down = exchange(order.tie(terms[1]))
    order.round([b_far] + b_line)

    def out_side(k):
        return call(
            out_side_kernel,
            "out_side",
            (shaped((blocks, rows, D)),) * 2,
            [block_spec((step_rows, hid_width), (k, 0)), slot_spec, slot_spec] + down_specs,
            [out_spec((blocks, rows, D), (0, 0, 0))] * 2,
            (ids, hid) + grad_parts[k] + (owned_down, owned_down),
            scratch=[pltpu.VMEM((2, step_rows, D), low)],
            flops=2 * step_rows * D * (hid_width + 2 * rows),
        )

    b_line += [Flow(one_hop(b_far.result[i], to_line[2 + i])) for i in range(2)]
    out_near, out_far = order.round(b_line[1:], (out_side(0), out_side(1)))
    m_near, m_far = Flow(collect_pair(*out_near)), Flow(collect_pair(*out_far))
    grad_sum = total_of([b_near.result[0]] + [flow.result for flow in b_line])
    terms_up = exchange(order.tie(terms[0]))

    gate_grad = jnp.where(kept, grad_sum[:, D : D + EXPERTS], 0.0)
    logit_grad = gates * (gate_grad - jnp.sum(gates * gate_grad, -1, keepdims=True))
    logit_grad = jnp.pad(logit_grad.astype(low), ((0, 0), (0, pad)))
    scaled_two = grad_sum[:, :D] + dot(logit_grad, router_full, rows_by_rows)
    grad_out = output_cotangent.astype(full)
    mean_two = jnp.mean(scaled_two * normal_two, -1, keepdims=True)
    mid_grad = grad_out + inverse_two * (scaled_two - normal_two * mean_two)
    moe_gain_part = jnp.sum(scaled_two * normal_two, 0)
    router_part = dot(normed_mid, logit_grad, cols_by_cols)
    branch_grad = mid_grad.astype(low)
    attended_grad = dot(branch_grad, out_full, rows_by_cols).astype(low)

    kv_out = pl.BlockSpec((half_len, kv_tile), lambda j, ids: (0, j))
    query_back, key_mine, key_theirs, value_mine, value_theirs = call(
        attend_back_kernel,
        "attend_back",
        (shaped((rows, q_width)),) + (shaped((half_len, kv_width)),) * 4,
        [q_spec, q_spec]
        + kv_specs(0)
        + kv_specs(pairs)
        + [whole_spec((rows, seq_len)), log_spec, whole_spec((rows, 128)), whole_spec((rows, 128))],
        [q_spec] + [kv_out] * 4,
        (ids, queries, attended_grad, kv_line, kv_other, kv_line, kv_other, bias, logs, cosine, sine),
        flops=10 * rows * seq_len * q_width,
        steps=pairs,
    )
    kv_theirs = jnp.concatenate([key_theirs, value_theirs], 1)
    kv_mine = jnp.concatenate([key_mine, value_mine], 1)
    kv_theirs, kv_mine = order.round([m_near, m_far], (kv_theirs, kv_mine))
    kv_core = Flow(one_hop(kv_theirs, to_core))
    order.round([kv_core, m_near])
    kv_half = add_low(kv_mine, kv_core.result).reshape(4, rows, 2 * kv_width)
    kv = [Flow(one_hop(kv_half[k], to_line[k])) for k in (1, 2, 3)]
    early_part = jnp.concatenate(
        [
            dot(branch_grad, attended, cols_by_cols).astype(low),
            dot(normed_in, query_back, cols_by_cols).astype(low),
        ],
        1,
    )
    early_part, terms_down = order.round(kv + [m_far, m_near], (early_part, terms_down))
    kv_grad = total_of([kv_half[0]] + [flow.result for flow in kv])

    def dense_flow(parts):
        found = take_rows(fine_at, parts, 4, 8, fine)
        mine, theirs = ([found[core], found[2 + core]] for core in range(2))
        return [Flow(collect_pair(mine[i], theirs[i])) for i in range(2)]

    def line_of(near, far):
        return [Flow(one_hop(near[1], to_line[1]))] + [
            Flow(one_hop(far[i], to_line[2 + i])) for i in range(2)
        ]

    early = dense_flow(early_part)

    def swapped(values):
        lanes = jnp.arange(values.shape[1]) % HEAD_DIM < HEAD_DIM // 2
        return jnp.where(
            lanes[None], jnp.roll(values, -HEAD_DIM // 2, 1), jnp.roll(values, HEAD_DIM // 2, 1)
        )

    key_grad = kv_grad[:, :kv_width]
    key_back = key_grad * jnp.tile(cosine, (1, pairs)) - swapped(key_grad) * jnp.tile(sine, (1, pairs))
    kv_rows = jnp.concatenate([key_back, kv_grad[:, kv_width:]], 1).astype(low)
    scaled_one = dot(query_back, dense_full[:, :q_width], rows_by_rows) + dot(
        kv_rows, dense_full[:, q_width:qkv_width], rows_by_rows
    )
    mean_one = jnp.mean(scaled_one * normal_one, -1, keepdims=True)
    input_grad = mid_grad + inverse_one * (scaled_one - normal_one * mean_one)
    attn_gain_part = jnp.sum(scaled_one * normal_one, 0)
    small = jnp.concatenate(
        [
            router_part[:, :EXPERTS],
            moe_gain_part[:, None],
            attn_gain_part[:, None],
            jnp.zeros((height, pad - 2), full),
        ],
        1,
    )
    late_part = jnp.concatenate(
        [dot(normed_in, kv_rows, cols_by_cols).astype(low), small.astype(low)], 1
    )
    late_part, input_grad = order.round(early + [m_far], (late_part, input_grad.astype(low)))
    late = dense_flow(late_part)
    order.round(late + early)
    order.round(late + early)
    early_line = line_of(early[0].result, early[1].result)
    order.round(late + early_line)
    late_line = line_of(late[0].result, late[1].result)
    spots = jnp.arange(GROUPS, dtype=jnp.int32) ^ group_at
    mate = 1 + shard_at % 2
    spots = jnp.where(spots == mate, 1, jnp.where(spots == 3 - mate, 2, spots))
    places = [spots[i] for i in range(GROUPS)]

    def shared(first, line):
        own = total_of([first] + [flow.result for flow in line]).astype(low)
        return Flow(share_flow(own, places))

    early_share = shared(early[0].result[0], early_line)
    terms_up = order.round(late_line + [early_share], terms_up)
    late_share = shared(late[0].result[0], late_line)
    order.round([late_share, early_share])
    m_line = line_of(m_near.result, m_far.result)
    order.round([late_share] + m_line)
    output = (middle + total_of([m_near.result[0]] + [flow.result for flow in m_line])).astype(low)
    early_sum = early_share.result.astype(full)
    late_sum = late_share.result.astype(full)

    gate_up_grad, down_grad = call(
        unpack_kernel,
        "unpack",
        (shaped(gate_up_weight.shape, full), shaped(down_weight.shape, full)),
        [
            pl.BlockSpec((1, depth, 2 * H), lambda j, ids: (jnp.minimum(j, whole - 1), 0, 0)),
            pl.BlockSpec(
                (share, depth, 2 * part), lambda j, ids: (jnp.maximum(j - whole, 0), 0, to_parts)
            ),
            pl.BlockSpec((1, depth, H), lambda j, ids: (jnp.minimum(j, whole - 1), 0, 0)),
            pl.BlockSpec(
                (share, depth, part), lambda j, ids: (jnp.maximum(j - whole, 0), 0, to_parts)
            ),
            whole_spec((depth, 1)),
        ],
        [
            pl.BlockSpec((depth, 2 * H), lambda j, ids: (0, j)),
            pl.BlockSpec((depth, H), lambda j, ids: (0, j)),
        ],
        (ids, terms_up, terms_up, terms_down, terms_down, gain_two),
        steps=own_experts,
    )
    return (
        output,
        input_grad,
        jnp.concatenate([early_sum[:, q_width:], late_sum[:, : 2 * kv_width]], 1) * gain_one,
        early_sum[:, :q_width],
        late_sum[:, 2 * kv_width : 2 * kv_width + EXPERTS] * gain_two,
        late_sum[:, 2 * kv_width + EXPERTS + 1] / gain_one[:, 0],
        late_sum[:, 2 * kv_width + EXPERTS] / gain_two[:, 0],
        gate_up_grad,
        down_grad,
    )


def solution(mesh):
    body = local
    if mesh.shape["expert"] == GROUPS and mesh.shape["shard"] == SHARDS:
        body = local_hops
    return jax.shard_map(
        body,
        mesh=mesh,
        in_specs=(
            P(("expert", "shard"), None),
            P(("expert", "shard"), None),
            P(("expert", "shard"), None),
            P("expert", None),
            P("expert", None),
            P("shard", None),
            P("shard", None),
            P("shard", None),
            P("shard"),
            P("shard"),
            P("shard", "expert"),
            P("shard", "expert"),
        ),
        out_specs=(
            P(("expert", "shard"), None),
            P(("expert", "shard"), None),
            P("shard", None),
            P("shard", None),
            P("shard", None),
            P("shard"),
            P("shard"),
            P("shard", "expert"),
            P("shard", "expert"),
        ),
        check_vma=False,
    )
```

```python
import jax
import jax.numpy as jnp
from jax import lax
from jax.experimental import pallas as pl
from jax.experimental.pallas import tpu as pltpu
from jax.sharding import PartitionSpec as P

D = 1536
HEADS = 24
KV_HEADS = 8
HEAD_DIM = 64
H = 512
EXPERTS = 40
TOP = 8
PIECE = 256
SLOT = 512
CAP = 32


norm_eps = 1e-06
rope_base = 10000.0
masked_score = -1e30


def rope_tables(positions, head_dim):
    half_dim = head_dim // 2
    frequency = rope_base ** (-2.0 * jnp.arange(half_dim, dtype=jnp.float32) / head_dim)
    angles = positions.astype(jnp.float32)[:, None] * frequency[None, :]
    return (jnp.cos(angles)[:, None, :], jnp.sin(angles)[:, None, :])


def rotate(values, cosine, sine_table):
    half_dim = values.shape[-1] // 2
    first_half = values[..., :half_dim]
    second = values[..., half_dim:]
    return jnp.concatenate(
        [first_half * cosine - second * sine_table, second * cosine + first_half * sine_table], -1
    )


def rotate_back(grad_rows, cosine, sine_table):
    half_dim = grad_rows.shape[-1] // 2
    first_half = grad_rows[..., :half_dim]
    second = grad_rows[..., half_dim:]
    return jnp.concatenate(
        [first_half * cosine + second * sine_table, second * cosine - first_half * sine_table], -1
    )


def rms_norm(values, gain):
    inverse = lax.rsqrt(jnp.mean(values * values, -1, keepdims=True) + norm_eps)
    normal = values * inverse
    return (normal * gain, normal, inverse)


def rms_back(grad_rows, gain, normal, inverse):
    scaled = grad_rows * gain
    grad_in = inverse * (scaled - normal * jnp.mean(scaled * normal, -1, keepdims=True))
    return (grad_in, jnp.sum(grad_rows * normal, 0))


def picture_ids(positions, starts, slot_len, piece_len):
    slot_index = positions // slot_len
    picked_slot = slot_index[:, None] == jnp.arange(starts.shape[0], dtype=jnp.int32)[None, :]
    piece_begin = jnp.sum(jnp.where(picked_slot, starts[None, :], 0), axis=1)
    inside = (positions >= piece_begin) & (positions < piece_begin + piece_len)
    return jnp.where(inside, slot_index, -1)


def allowed(query_pos, key_pos, query_doc, key_doc, query_pic, key_pic):
    same_doc = query_doc[:, None] == key_doc[None, :]
    earlier = key_pos[None, :] <= query_pos[:, None]
    same_pic = (query_pic[:, None] == key_pic[None, :]) & (query_pic[:, None] >= 0)
    return same_doc & (earlier | same_pic)


def local(
    tokens_in,
    output_cotangent,
    routes,
    doc_ids,
    picture_starts,
    qkv_weight,
    out_weight,
    router_weight,
    attn_gain,
    moe_gain,
    gate_up_weight,
    down_weight,
):
    qkv_full, out_full, router_full, gain_first, gain_second = (
        lax.all_gather(qkv_weight, "shard", axis=0, tiled=True),
        lax.all_gather(out_weight, "shard", axis=0, tiled=True),
        lax.all_gather(router_weight, "shard", axis=0, tiled=True),
        lax.all_gather(attn_gain, "shard", axis=0, tiled=True),
        lax.all_gather(moe_gain, "shard", axis=0, tiled=True),
    )
    gain_one = gain_first.astype(jnp.float32)
    gain_two = gain_second.astype(jnp.float32)
    tok_rows = tokens_in.shape[0]
    seq_len = doc_ids.shape[1]
    groups = HEADS // KV_HEADS
    q_width = HEADS * HEAD_DIM
    kv_width = KV_HEADS * HEAD_DIM
    score_scale = HEAD_DIM ** (-0.5)
    shard_at = lax.axis_index("shard")
    query_pos = shard_at * tok_rows + jnp.arange(tok_rows, dtype=jnp.int32)
    key_pos = jnp.arange(seq_len, dtype=jnp.int32)
    key_doc = doc_ids[0]
    key_pic = picture_ids(key_pos, picture_starts[0], SLOT, PIECE)
    query_doc = lax.dynamic_slice_in_dim(key_doc, shard_at * tok_rows, tok_rows)
    query_pic = lax.dynamic_slice_in_dim(key_pic, shard_at * tok_rows, tok_rows)
    tokens_f = tokens_in.astype(jnp.float32)
    normed_one, normal_one, inverse_one = rms_norm(tokens_f, gain_one)
    normed_in = normed_one.astype(jnp.bfloat16)
    qkv_rows = jnp.dot(normed_in, qkv_full, preferred_element_type=jnp.float32)
    cosine, sine_table = rope_tables(query_pos, HEAD_DIM)
    queries = (
        rotate(qkv_rows[:, :q_width].reshape(tok_rows, HEADS, HEAD_DIM), cosine, sine_table)
        .astype(jnp.bfloat16)
        .reshape(tok_rows, KV_HEADS, groups, HEAD_DIM)
    )
    key_local = (
        rotate(
            qkv_rows[:, q_width : q_width + kv_width].reshape(tok_rows, KV_HEADS, HEAD_DIM),
            cosine,
            sine_table,
        )
        .astype(jnp.bfloat16)
        .reshape(tok_rows, kv_width)
    )
    value_local = qkv_rows[:, q_width + kv_width :].astype(jnp.bfloat16)
    all_keys, all_values = (
        lax.all_gather(key_local, "shard", axis=0, tiled=True),
        lax.all_gather(value_local, "shard", axis=0, tiled=True),
    )
    span_len = min(512, seq_len)
    span_count = seq_len // span_len

    def block_scores(first_row, key_rows):
        key_block = lax.dynamic_slice_in_dim(key_rows, first_row, span_len, 0).reshape(
            span_len, KV_HEADS, HEAD_DIM
        )
        raw_scores = (
            jnp.einsum("tgrd,kgd->tgrk", queries, key_block, preferred_element_type=jnp.float32)
            * score_scale
        )
        block_pos = lax.dynamic_slice_in_dim(key_pos, first_row, span_len)
        block_doc = lax.dynamic_slice_in_dim(key_doc, first_row, span_len)
        block_pic = lax.dynamic_slice_in_dim(key_pic, first_row, span_len)
        visible = allowed(query_pos, block_pos, query_doc, block_doc, query_pic, block_pic)[
            :, None, None, :
        ]
        return (raw_scores, visible, key_block)

    def value_block_at(first_row, value_rows):
        return lax.dynamic_slice_in_dim(value_rows, first_row, span_len, 0).reshape(
            span_len, KV_HEADS, HEAD_DIM
        )

    def max_step(step_index, carry):
        run_max, run_sum = carry
        raw_scores, visible, key_block = block_scores(step_index * span_len, all_keys)
        masked = jnp.where(visible, raw_scores, masked_score)
        new_max = jnp.maximum(run_max, jnp.max(masked, -1))
        shifted = jnp.where(visible, jnp.exp(masked - new_max[..., None]), 0.0)
        return (new_max, run_sum * jnp.exp(run_max - new_max) + jnp.sum(shifted, -1))

    stat_shape = (tok_rows, KV_HEADS, groups)
    run_max, run_sum = lax.fori_loop(
        0,
        span_count,
        max_step,
        (jnp.full(stat_shape, masked_score, jnp.float32), jnp.zeros(stat_shape, jnp.float32)),
    )
    log_total = run_max + jnp.log(run_sum)

    def probs_of(raw_scores, visible):
        return jnp.exp(jnp.where(visible, raw_scores - log_total[..., None], masked_score))

    def value_step(step_index, summed):
        first_row = step_index * span_len
        raw_scores, visible, key_block = block_scores(first_row, all_keys)
        probs = probs_of(raw_scores, visible).astype(jnp.bfloat16)
        return summed + jnp.einsum(
            "tgrk,kgd->tgrd",
            probs,
            value_block_at(first_row, all_values),
            preferred_element_type=jnp.float32,
        )

    summed = lax.fori_loop(
        0, span_count, value_step, jnp.zeros((tok_rows, KV_HEADS, groups, HEAD_DIM), jnp.float32)
    )
    attended = summed.reshape(tok_rows, q_width).astype(jnp.bfloat16)
    branch = lax.dot_general(
        attended, out_full, (((1,), (1,)), ((), ())), preferred_element_type=jnp.float32
    )
    middle = tokens_f + branch
    normed_two, normal_two, inverse_two = rms_norm(middle, gain_two)
    normed_mid = normed_two.astype(jnp.bfloat16)
    logits = jnp.dot(normed_mid, router_full, preferred_element_type=jnp.float32)
    gates = jax.nn.softmax(jnp.take_along_axis(logits, routes, 1), axis=-1)
    route_hits = routes[:, :, None] == jnp.arange(EXPERTS, dtype=jnp.int32)[None, None, :]
    hit_count = jnp.sum(route_hits.astype(jnp.int32), 1)
    before = jnp.cumsum(hit_count, 0) - hit_count
    slot_index = jnp.take_along_axis(before, routes, 1)
    kept_pair = slot_index < CAP
    flat_slot = routes * CAP + slot_index
    capacity_rows = EXPERTS * CAP
    target = jnp.where(kept_pair, flat_slot, capacity_rows)
    token_ids = jnp.broadcast_to(jnp.arange(tok_rows, dtype=jnp.int32)[:, None], (tok_rows, TOP))
    owner_row = (
        jnp.full((capacity_rows + 1,), -1, jnp.int32)
        .at[target.reshape(-1)]
        .set(token_ids.reshape(-1))[:capacity_rows]
    )
    filled = owner_row >= 0
    source_row = jnp.maximum(owner_row, 0)
    expert_groups = lax.axis_size("expert")
    local_experts = EXPERTS // expert_groups
    send_rows = jnp.where(
        filled[:, None], normed_mid[source_row], jnp.zeros((), jnp.bfloat16)
    ).reshape(expert_groups, local_experts, CAP, D)
    received = lax.all_to_all(send_rows, "expert", split_axis=0, concat_axis=0, tiled=True)
    gate_up_full, down_full = (
        lax.all_gather(gate_up_weight, "shard", axis=0, tiled=True),
        lax.all_gather(down_weight, "shard", axis=0, tiled=True),
    )
    gate_up3 = gate_up_full.reshape(D, local_experts, 2 * H)
    down3 = down_full.reshape(D, local_experts, H)
    projected = jnp.einsum("secd,dej->secj", received, gate_up3, preferred_element_type=jnp.float32)
    gate_part = projected[..., :H]
    up_part = projected[..., H:]
    sigma = jax.nn.sigmoid(gate_part)
    silu_value = gate_part * sigma
    hidden = (silu_value * up_part).astype(jnp.bfloat16)
    expert_out = jnp.einsum(
        "secj,dej->secd", hidden, down3, preferred_element_type=jnp.float32
    ).astype(jnp.bfloat16)
    returned = lax.all_to_all(
        expert_out, "expert", split_axis=0, concat_axis=0, tiled=True
    ).reshape(capacity_rows, D)
    safe_flat = jnp.where(kept_pair, flat_slot, 0)
    picked = returned[safe_flat].astype(jnp.float32)
    pair_weight = jnp.where(kept_pair, gates, 0.0)
    moe_sum = jnp.einsum("tk,tkd->td", pair_weight, picked)
    output = (middle + moe_sum).astype(jnp.bfloat16)
    grad_out = output_cotangent.astype(jnp.float32)
    gate_grad = jnp.where(kept_pair, jnp.einsum("td,tkd->tk", grad_out, picked), 0.0)
    slot_gate = (
        jnp.zeros((capacity_rows + 1,), jnp.float32)
        .at[target.reshape(-1)]
        .set(gates.reshape(-1))[:capacity_rows]
    )
    grad_send = (
        jnp.where(filled[:, None], slot_gate[:, None] * grad_out[source_row], 0.0)
        .astype(jnp.bfloat16)
        .reshape(expert_groups, local_experts, CAP, D)
    )
    grad_received = lax.all_to_all(grad_send, "expert", split_axis=0, concat_axis=0, tiled=True)
    keys_back, values_back = (
        lax.all_gather(key_local, "shard", axis=0, tiled=True),
        lax.all_gather(value_local, "shard", axis=0, tiled=True),
    )
    again_up, again_down = (
        lax.all_gather(gate_up_weight, "shard", axis=0, tiled=True),
        lax.all_gather(down_weight, "shard", axis=0, tiled=True),
    )
    gate_up_back = again_up.reshape(D, local_experts, 2 * H)
    down_back = again_down.reshape(D, local_experts, H)
    hidden_grad = jnp.einsum(
        "secd,dej->secj", grad_received, down_back, preferred_element_type=jnp.float32
    )
    silu_slope = sigma * (1.0 + gate_part * (1.0 - sigma))
    proj_grad = jnp.concatenate(
        [hidden_grad * up_part * silu_slope, hidden_grad * silu_value], -1
    ).astype(jnp.bfloat16)
    row_grad = jnp.einsum(
        "secj,dej->secd", proj_grad, gate_up_back, preferred_element_type=jnp.float32
    ).astype(jnp.bfloat16)
    grad_back = lax.all_to_all(row_grad, "expert", split_axis=0, concat_axis=0, tiled=True).reshape(
        capacity_rows, D
    )
    row_count = gate_up_weight.shape[0] * lax.axis_size("shard")
    up_terms = jnp.einsum(
        "secd,secj->dej", received, proj_grad, preferred_element_type=jnp.float32
    ).reshape(row_count, local_experts * 2 * H)
    down_terms = jnp.einsum(
        "secd,secj->dej", grad_received, hidden, preferred_element_type=jnp.float32
    ).reshape(row_count, local_experts * H)
    expert_sums = lax.psum_scatter(
        jnp.concatenate([up_terms, down_terms], 1).astype(jnp.bfloat16),
        "shard",
        scatter_dimension=0,
        tiled=True,
    ).astype(jnp.float32)
    gate_up_grad = expert_sums[:, : local_experts * 2 * H]
    down_grad = expert_sums[:, local_experts * 2 * H :]
    mid_norm_grad = jnp.einsum(
        "tk,tkd->td", kept_pair.astype(jnp.float32), grad_back[safe_flat].astype(jnp.float32)
    )
    chosen_grad = gates * (gate_grad - jnp.sum(gates * gate_grad, -1, keepdims=True))
    logit_grad = jnp.sum(jnp.where(route_hits, chosen_grad[:, :, None], 0.0), 1).astype(
        jnp.bfloat16
    )
    mid_norm_grad = mid_norm_grad + lax.dot_general(
        logit_grad, router_full, (((1,), (1,)), ((), ())), preferred_element_type=jnp.float32
    )
    router_grad = lax.dot_general(
        normed_mid, logit_grad, (((0,), (0,)), ((), ())), preferred_element_type=jnp.float32
    )
    mid_part, moe_gain_grad = rms_back(mid_norm_grad, gain_two, normal_two, inverse_two)
    mid_grad = grad_out + mid_part
    branch_grad = mid_grad.astype(jnp.bfloat16)
    out_weight_grad = lax.dot_general(
        branch_grad, attended, (((0,), (0,)), ((), ())), preferred_element_type=jnp.float32
    )
    attended_grad = (
        jnp.dot(branch_grad, out_full, preferred_element_type=jnp.float32)
        .astype(jnp.bfloat16)
        .reshape(tok_rows, KV_HEADS, groups, HEAD_DIM)
    )

    def dot_step(step_index, row_dot):
        first_row = step_index * span_len
        raw_scores, visible, key_block = block_scores(first_row, keys_back)
        prob_full = probs_of(raw_scores, visible)
        prob_grad = jnp.einsum(
            "tgrd,kgd->tgrk",
            attended_grad,
            value_block_at(first_row, values_back),
            preferred_element_type=jnp.float32,
        )
        return row_dot + jnp.sum(prob_full * prob_grad, -1)

    row_dot = lax.fori_loop(0, span_count, dot_step, jnp.zeros(stat_shape, jnp.float32))

    def grad_step(step_index, carry):
        query_grad, key_terms, value_terms = carry
        first_row = step_index * span_len
        raw_scores, visible, key_block = block_scores(first_row, keys_back)
        prob_full = probs_of(raw_scores, visible)
        prob_grad = jnp.einsum(
            "tgrd,kgd->tgrk",
            attended_grad,
            value_block_at(first_row, values_back),
            preferred_element_type=jnp.float32,
        )
        score_grad = (prob_full * (prob_grad - row_dot[..., None])).astype(jnp.bfloat16)
        query_grad = query_grad + jnp.einsum(
            "tgrk,kgd->tgrd", score_grad, key_block, preferred_element_type=jnp.float32
        )
        key_part = (
            jnp.einsum(
                "tgrk,tgrd->kgd", score_grad, queries, preferred_element_type=jnp.float32
            ).reshape(span_len, kv_width)
            * score_scale
        )
        value_part = jnp.einsum(
            "tgrk,tgrd->kgd",
            prob_full.astype(jnp.bfloat16),
            attended_grad,
            preferred_element_type=jnp.float32,
        ).reshape(span_len, kv_width)
        key_terms = lax.dynamic_update_slice_in_dim(key_terms, key_part, first_row, 0)
        value_terms = lax.dynamic_update_slice_in_dim(value_terms, value_part, first_row, 0)
        return (query_grad, key_terms, value_terms)

    query_grad, key_terms, value_terms = lax.fori_loop(
        0,
        span_count,
        grad_step,
        (
            jnp.zeros((tok_rows, KV_HEADS, groups, HEAD_DIM), jnp.float32),
            jnp.zeros((seq_len, kv_width), jnp.float32),
            jnp.zeros((seq_len, kv_width), jnp.float32),
        ),
    )
    key_grad, value_grad = (
        lax.psum_scatter(
            key_terms.astype(jnp.bfloat16), "shard", scatter_dimension=0, tiled=True
        ).astype(jnp.float32),
        lax.psum_scatter(
            value_terms.astype(jnp.bfloat16), "shard", scatter_dimension=0, tiled=True
        ).astype(jnp.float32),
    )
    query_back = rotate_back(
        (query_grad * score_scale).reshape(tok_rows, HEADS, HEAD_DIM), cosine, sine_table
    ).reshape(tok_rows, q_width)
    key_back = rotate_back(
        key_grad.reshape(tok_rows, KV_HEADS, HEAD_DIM), cosine, sine_table
    ).reshape(tok_rows, kv_width)
    qkv_grad_rows = jnp.concatenate([query_back, key_back, value_grad], 1).astype(jnp.bfloat16)
    qkv_weight_grad = lax.dot_general(
        normed_in, qkv_grad_rows, (((0,), (0,)), ((), ())), preferred_element_type=jnp.float32
    )
    in_norm_grad = lax.dot_general(
        qkv_grad_rows, qkv_full, (((1,), (1,)), ((), ())), preferred_element_type=jnp.float32
    )
    in_part, attn_gain_grad = rms_back(in_norm_grad, gain_one, normal_one, inverse_one)
    input_grad = (mid_grad + in_part).astype(jnp.bfloat16)
    dense_sums = (
        lax.psum_scatter(
            qkv_weight_grad.astype(jnp.bfloat16), "shard", scatter_dimension=0, tiled=True
        ).astype(jnp.float32),
        lax.psum_scatter(
            out_weight_grad.astype(jnp.bfloat16), "shard", scatter_dimension=0, tiled=True
        ).astype(jnp.float32),
        lax.psum_scatter(
            router_grad.astype(jnp.bfloat16), "shard", scatter_dimension=0, tiled=True
        ).astype(jnp.float32),
        lax.psum_scatter(
            attn_gain_grad.astype(jnp.bfloat16), "shard", scatter_dimension=0, tiled=True
        ).astype(jnp.float32),
        lax.psum_scatter(
            moe_gain_grad.astype(jnp.bfloat16), "shard", scatter_dimension=0, tiled=True
        ).astype(jnp.float32),
    )
    dense_totals = (
        lax.psum(dense_sums[0].astype(jnp.bfloat16), "expert").astype(jnp.float32),
        lax.psum(dense_sums[1].astype(jnp.bfloat16), "expert").astype(jnp.float32),
        lax.psum(dense_sums[2].astype(jnp.bfloat16), "expert").astype(jnp.float32),
        lax.psum(dense_sums[3].astype(jnp.bfloat16), "expert").astype(jnp.float32),
        lax.psum(dense_sums[4].astype(jnp.bfloat16), "expert").astype(jnp.float32),
    )
    return (
        output,
        input_grad,
        dense_totals[0],
        dense_totals[1],
        dense_totals[2],
        dense_totals[3],
        dense_totals[4],
        gate_up_grad,
        down_grad,
    )


GROUPS = 4
SHARDS = 8
rows_by_cols = ((1,), (0,))
rows_by_rows = ((1,), (1,))
cols_by_cols = ((0,), (0,))


def dot(one, two, dims):
    return lax.dot_general(one, two, (dims, ((), ())), preferred_element_type=jnp.float32)


def whole_spec(shape):
    return pl.BlockSpec(shape, lambda i, ids: (0,) * len(shape), pipeline_mode=pl.Buffered(1))


def block_spec(shape, index):
    return pl.BlockSpec(shape, lambda i, ids: index, pipeline_mode=pl.Buffered(1))


def out_spec(shape, index):
    return pl.BlockSpec(shape, lambda i, ids: index)


in_place = pl.BlockSpec(memory_space=pl.ANY)


def shaped(shape, dtype=jnp.bfloat16):
    return jax.ShapeDtypeStruct(shape, dtype)


def call(kernel, name, out_shape, in_specs, out_specs, args, scratch=(), aliases=None, flops=0, steps=1):
    moved = sum(a.size * a.dtype.itemsize for a in args[1:])
    return pl.pallas_call(
        kernel,
        name=name,
        out_shape=out_shape,
        grid_spec=pltpu.PrefetchScalarGridSpec(
            num_scalar_prefetch=1,
            grid=(steps,),
            in_specs=in_specs,
            out_specs=out_specs,
            scratch_shapes=list(scratch),
        ),
        input_output_aliases=aliases or {},
        compiler_params=pltpu.CompilerParams(
            vmem_limit_bytes=58 * 1024 * 1024, dimension_semantics=("arbitrary",)
        ),
        cost_estimate=pl.CostEstimate(flops=flops, transcendentals=0, bytes_accessed=moved),
    )(*args)


def place_rows(offsets, parts, height):
    count, fine, width = parts[0].shape

    def kernel(at, *refs):
        sources, target, done = refs[: len(parts)], refs[len(parts)], refs[-1]
        copies = []
        for n, source in enumerate(sources):
            for i in range(count):
                row = pl.multiple_of(at[n * count + i], 16)
                copies.append(
                    pltpu.make_async_copy(
                        source.at[i], target.at[pl.ds(row, fine)], done.at[n * count + i]
                    )
                )
        for copy in copies:
            copy.start()
        for copy in copies:
            copy.wait()

    return call(
        kernel,
        "place_rows",
        shaped((height, width), parts[0].dtype),
        [in_place] * len(parts),
        out_spec((height, width), (0, 0)),
        (offsets,) + tuple(parts),
        scratch=[pltpu.SemaphoreType.DMA((len(parts) * count,))],
    )


def dense_terms(offsets, products, parts, count, fine):
    height = products[0][0].shape[1]
    width = max(first + two.shape[1] for _, two, first in products)
    firsts = [first for _, _, first in products]

    def kernel(at, *refs):
        sources, targets, held = refs[: 2 * len(firsts)], refs[2 * len(firsts) : -1], refs[-1]
        total = {}
        for n, first in enumerate(firsts):
            found = dot(sources[2 * n][...], sources[2 * n + 1][...], cols_by_cols)
            total[first] = total[first] + found if first in total else found
        for first, found in total.items():
            held[:, first : first + found.shape[1]] = found.astype(jnp.bfloat16)
        for n, target in enumerate(targets):
            for i in range(count):
                row = pl.multiple_of(at[n * count + i], 16)
                target[i] = held[pl.ds(row, fine)]

    operands = [array for one, two, _ in products for array in (one, two)]
    return call(
        kernel,
        "dense_terms",
        [shaped((count, fine, width))] * parts,
        [whole_spec(array.shape) for array in operands],
        [out_spec((count, fine, width), (0, 0, 0))] * parts,
        (offsets,) + tuple(operands),
        scratch=[pltpu.VMEM((height, width), jnp.bfloat16)],
        flops=2 * height * width * products[0][0].shape[0],
    )


def pack_kernel(ids, up, gate_part, up_part, down, down_part, gain, ups, downs):
    width = up.shape[1]
    part = gate_part.shape[1]
    scale = gain[...]

    def scaled(ref):
        return (ref[...].astype(jnp.float32) * scale).astype(jnp.bfloat16)

    ups[0, :, :width] = scaled(up)
    ups[0, :, width : width + part] = scaled(gate_part)
    ups[0, :, width + part :] = scaled(up_part)
    downs[0, :, : down.shape[1]] = down[...]
    downs[0, :, down.shape[1] :] = down_part[...]


def unpack_kernel(ids, up, up_parts, down, down_parts, gain, up_grad, down_grad):
    part = down_parts.shape[2]
    scale = gain[...]
    expert = pl.program_id(0)
    whole = pl.num_programs(0) - 2

    @pl.when(expert < whole)
    def _():
        up_grad[...] = up[0].astype(jnp.float32) * scale
        down_grad[...] = down[0].astype(jnp.float32)

    @pl.when(expert >= whole)
    def _():
        for i in range(up_parts.shape[0]):
            at = i * part
            up_grad[:, at : at + part] = up_parts[i, :, :part].astype(jnp.float32) * scale
            up_grad[:, H + at : H + at + part] = up_parts[i, :, part:].astype(jnp.float32) * scale
            down_grad[:, at : at + part] = down_parts[i].astype(jnp.float32)


def turn(rows, cosine, sine):
    width = rows.shape[1]
    lanes = lax.broadcasted_iota(jnp.int32, (rows.shape[0], 128), 1)
    first = lanes % HEAD_DIM < HEAD_DIM // 2
    turned = []
    for at in range(0, width, 128):
        piece = rows[:, at : at + 128]
        swapped = jnp.where(
            first,
            pltpu.roll(piece, 128 - HEAD_DIM // 2, 1),
            pltpu.roll(piece, HEAD_DIM // 2, 1),
        )
        turned.append(piece * cosine + swapped * sine)
    return jnp.concatenate(turned, 1)


def qkv_kernel(ids, normed, weight, cosine, sine, queries, key_value):
    step = pl.program_id(0)
    found = dot(normed[...], weight[...], rows_by_cols)

    @pl.when(step < 3)
    def _():
        queries[...] = turn(found, cosine[...], sine[...]).astype(jnp.bfloat16)

    @pl.when(step == 3)
    def _():
        key_value[...] = turn(found, cosine[...], sine[...]).astype(jnp.bfloat16)

    @pl.when(step == 4)
    def _():
        key_value[...] = found.astype(jnp.bfloat16)


def attend_kernel(ids, queries, key_line, key_other, value_line, value_other, bias, attended, logs):
    scale = HEAD_DIM ** (-0.5)
    groups = HEADS // KV_HEADS
    hidden = bias[...]
    keys = jnp.concatenate([key_line[...], key_other[...]], 0)
    values = jnp.concatenate([value_line[...], value_other[...]], 0)
    lanes = lax.broadcasted_iota(jnp.int32, (queries.shape[0], 128), 1)
    totals = jnp.zeros((queries.shape[0], 128), jnp.float32)
    found = []
    for n in range(2 * groups):
        at = n // groups * HEAD_DIM
        scores = dot(
            queries[:, n * HEAD_DIM : (n + 1) * HEAD_DIM], keys[:, at : at + HEAD_DIM], rows_by_rows
        )
        scores = scores * scale + hidden
        top = jnp.max(scores, 1, keepdims=True)
        raised = jnp.exp(scores - top)
        total = jnp.sum(raised, 1, keepdims=True)
        probs = (raised / total).astype(jnp.bfloat16)
        found.append(dot(probs, values[:, at : at + HEAD_DIM], rows_by_cols))
        totals = jnp.where(lanes == n, top + jnp.log(total), totals)
    attended[...] = jnp.concatenate(found, 1).astype(jnp.bfloat16)
    logs[0] = totals


def attend_back_kernel(
    ids, queries, grads, key_line, key_other, value_line, value_other, bias, logs, cosine, sine,
    query_grad, key_mine, key_theirs, value_mine, value_theirs,
):
    scale = HEAD_DIM ** (-0.5)
    groups = HEADS // KV_HEADS
    hidden = bias[...]
    keys = jnp.concatenate([key_line[...], key_other[...]], 0)
    values = jnp.concatenate([value_line[...], value_other[...]], 0)
    half = key_line.shape[0]
    found = []
    key_found, value_found = [], []
    for n in range(2 * groups):
        own = n // groups
        at = own * HEAD_DIM
        head = slice(n * HEAD_DIM, (n + 1) * HEAD_DIM)
        query = queries[:, head]
        grad = grads[:, head]
        scores = dot(query, keys[:, at : at + HEAD_DIM], rows_by_rows) * scale + hidden
        probs = jnp.exp(scores - lane_value(logs[0], n))
        prob_grad = dot(grad, values[:, at : at + HEAD_DIM], rows_by_rows)
        row_dot = jnp.sum(probs * prob_grad, 1, keepdims=True)
        score_grad = (probs * (prob_grad - row_dot)).astype(jnp.bfloat16)
        found.append(dot(score_grad, keys[:, at : at + HEAD_DIM], rows_by_cols))
        key_part = dot(score_grad, query, cols_by_cols)
        value_part = dot(probs.astype(jnp.bfloat16), grad, cols_by_cols)
        if n % groups:
            key_found[own] = key_found[own] + key_part
            value_found[own] = value_found[own] + value_part
        else:
            key_found.append(key_part)
            value_found.append(value_part)
    found = jnp.concatenate(found, 1) * scale
    query_grad[...] = turn(found, cosine[...], -sine[...]).astype(jnp.bfloat16)
    key_found = (jnp.concatenate(key_found, 1) * scale).astype(jnp.bfloat16)
    value_found = jnp.concatenate(value_found, 1).astype(jnp.bfloat16)
    key_mine[...] = key_found[:half]
    key_theirs[...] = key_found[half:]
    value_mine[...] = value_found[:half]
    value_theirs[...] = value_found[half:]


def lane_value(rows, index):
    lanes = lax.broadcasted_iota(jnp.int32, rows.shape, 1)
    return jnp.sum(jnp.where(lanes == index, rows, 0.0), 1, keepdims=True)


def picks_of(extra, one, two):
    extra = extra.astype(jnp.float32)
    lanes = lax.broadcasted_iota(jnp.int32, (extra.shape[0], 2 * CAP), 1)
    wanted = jnp.where(lanes < CAP, lane_value(extra, one), lane_value(extra, two))
    place = jnp.where(lanes < CAP, lanes, lanes - CAP).astype(jnp.float32)
    return jnp.where(wanted == place, 1.0, 0.0).astype(jnp.bfloat16)


def grad_side_kernel(ids, half, other, down_one, down_two, kept_gs, gs, plain):
    count = half.shape[0]
    for i in range(2 * count):
        source = half if i < count else other
        pick = picks_of(source[i % count, :, D:], ids[0], ids[1])
        found = dot(pick, source[i % count, :, :D], cols_by_cols).astype(jnp.bfloat16)
        gs[0, i * CAP : (i + 1) * CAP] = found[:CAP]
        gs[1, i * CAP : (i + 1) * CAP] = found[CAP:]
    width = down_one.shape[1]
    plain[:, :width] = dot(gs[0], down_one[...], rows_by_cols)
    plain[:, width:] = dot(gs[1], down_two[...], rows_by_cols)


def combine_rows(ids, rows, slots_half, slots_other, back_half, back_other):
    count = slots_half.shape[0]
    for i in range(2 * count):
        target = back_half if i < count else back_other
        slots = slots_half if i < count else slots_other
        pick = picks_of(slots[i % count], ids[0], ids[1])
        at = slice(i * CAP, (i + 1) * CAP)
        both = jnp.concatenate([rows[0, at], rows[1, at]], 0)
        target[i % count] = dot(pick, both, rows_by_cols).astype(jnp.bfloat16)


def row_side_kernel(
    ids, half, other, slots_half, slots_other, plain, up_one, up_two, kept_xs, kept_hid, kept_pg,
    back_half, back_other, xs, hid, pg, gates, tokens, back_rows,
):
    total = xs.shape[1]
    count = half.shape[0]
    for i in range(2 * count):
        source = half if i < count else other
        slots = slots_half if i < count else slots_other
        pick = picks_of(slots[i % count], ids[0], ids[1])
        found = dot(pick, source[i % count], cols_by_cols)
        extra = found[:, D:]
        found = found.astype(jnp.bfloat16)
        at = slice(i * CAP, (i + 1) * CAP)
        for n in range(2):
            xs[n, at] = found[n * CAP : (n + 1) * CAP, :D]
            own = extra[n * CAP : (n + 1) * CAP]
            gates[n, at] = lane_value(own, ids[n]) + lane_value(own, ids[n] + EXPERTS)
    first = 0
    for n, up in ((0, up_one), (1, up_two)):
        width = up.shape[1] // 2
        projected = dot(xs[n], up[...], rows_by_cols)
        gate_part = projected[:, :width]
        up_part = projected[:, width:]
        own_plain = plain[:, first : first + width]
        sigma = 1.0 / (1.0 + jnp.exp(-gate_part))
        silu_value = gate_part * sigma
        hidden = silu_value * up_part
        tokens[n] = jnp.sum(hidden * own_plain, 1, keepdims=True)
        hid[:, first : first + width] = (hidden * gates[n]).astype(jnp.bfloat16)
        hidden_grad = own_plain * gates[n]
        slope = sigma * (1.0 + gate_part * (1.0 - sigma))
        pg[:, 2 * first : 2 * first + width] = (hidden_grad * up_part * slope).astype(jnp.bfloat16)
        pg[:, 2 * first + width : 2 * first + 2 * width] = (hidden_grad * silu_value).astype(
            jnp.bfloat16
        )
        own_pg = pg[:, 2 * first : 2 * first + 2 * width]
        back_rows[n, :, :D] = dot(own_pg, up[...], rows_by_rows).astype(jnp.bfloat16)
        lanes = lax.broadcasted_iota(jnp.int32, (total, 128), 1)
        back_rows[n, :, D:] = jnp.where(lanes == ids[n], tokens[n], 0.0).astype(jnp.bfloat16)
        first += width
    combine_rows(ids, back_rows, slots_half, slots_other, back_half, back_other)


def out_side_kernel(
    ids, hid, slots_half, slots_other, down_one, down_two, back_half, back_other, out_rows
):
    width = down_one.shape[1]
    out_rows[0] = dot(hid[:, :width], down_one[...], rows_by_rows).astype(jnp.bfloat16)
    out_rows[1] = dot(hid[:, width:], down_two[...], rows_by_rows).astype(jnp.bfloat16)
    combine_rows(ids, out_rows, slots_half, slots_other, back_half, back_other)


def terms_kernel(ids, xs, gs, pg, hid, terms_up, terms_down):
    depth = terms_up.shape[1]
    width = terms_down.shape[2]
    pieces = (
        (terms_up, xs, pg, 0, 0, 2 * H),
        (terms_up, xs, pg, 1, 2 * H, 2 * width),
        (terms_down, gs, hid, 0, 0, H),
        (terms_down, gs, hid, 1, H, width),
    )
    for target, one, two, n, left, right in pieces:
        found = dot(one[n], two[:, left:right], cols_by_cols).astype(jnp.bfloat16)
        for i in range(2):
            target[i, :, left:right] = found[i * depth : (i + 1) * depth]


def hop(values, pairs):
    return lax.ppermute(values, ("expert", "shard"), pairs)


def hop_pairs(step):
    return [
        (e * SHARDS + s, step(e, s)[0] * SHARDS + step(e, s)[1])
        for e in range(GROUPS)
        for s in range(SHARDS)
    ]


to_core = hop_pairs(lambda e, s: (e, s ^ 1))
to_line = [hop_pairs(lambda e, s, k=k: (e, s ^ (2 * k))) for k in range(4)]
over_middle = [
    (e * SHARDS + s, e * SHARDS + (s ^ 6)) for e in range(GROUPS) for s in range(2, 6)
]
from_middle = [
    (e * SHARDS + s, e * SHARDS + (s ^ 2)) for e in range(GROUPS) for s in range(2, 6)
]
to_middle = [(there, here) for here, there in from_middle]
to_first = hop_pairs(lambda e, s: (e ^ (1 + s % 2), s))
to_second = hop_pairs(lambda e, s: (e ^ (2 - s % 2), s))


def add_low(one, two):
    return (one.astype(jnp.float32) + two.astype(jnp.float32)).astype(jnp.bfloat16)


def total_of(line):
    return sum(piece.astype(jnp.float32) for piece in line)


class Flow:
    def __init__(self, steps):
        self.steps = steps
        self.result = None
        self.feed(None)

    def feed(self, values):
        try:
            self.want = self.steps.send(values)
        except StopIteration as stop:
            self.want = None
            self.result = stop.value


class Order:
    def __init__(self, mark):
        self.mark = mark

    def tie(self, values):
        values, self.mark = lax.optimization_barrier((values, self.mark))
        return values

    def round(self, flows, work=None):
        values, self.mark = lax.optimization_barrier(([f.want[0] for f in flows], self.mark))
        found = [hop(v, f.want[1]) for v, f in zip(values, flows)]
        found, work, self.mark = lax.optimization_barrier((found, work, self.mark))
        for flow, values in zip(flows, found):
            flow.feed(values)
        return work


def one_hop(values, pairs):
    found = yield values, pairs
    return found


def line_flows(own):
    return [Flow(one_hop(own, to_line[k])) for k in (1, 2, 3)]


def line_spread(own, marks):
    near = yield own, to_line[1]
    marks.append(near)
    two = jnp.stack([own, near])
    crossed = yield two, over_middle
    passed = yield crossed, from_middle
    at = lax.axis_index("shard") // 2
    return jnp.where((at == 1) | (at == 2), crossed, passed)


def line_collect(near, far):
    passed = yield jnp.stack(far), to_middle
    far = add_low(jnp.stack(far), passed)
    crossed = yield far, over_middle
    at = lax.axis_index("shard") // 2
    middle = (at == 1) | (at == 2)
    both = jnp.stack(near).astype(jnp.float32) + jnp.where(middle, crossed, 0).astype(jnp.float32)
    back = yield both[1].astype(jnp.bfloat16), to_line[1]
    return both[0] + back.astype(jnp.float32)


def by_distance(far):
    at = lax.axis_index("shard") // 2
    middle = (at == 1) | (at == 2)
    return [jnp.where(middle, far[1 - i], far[i]) for i in range(2)]


def spread_pair(pieces):
    two = jnp.stack(pieces) if isinstance(pieces, list) else pieces
    first = yield two, to_first
    four = jnp.concatenate([two, first])
    second = yield four, to_second
    eight = jnp.concatenate([four, second])
    other = yield eight, to_core
    return eight, other


def collect_pair(mine, theirs):
    found = yield theirs, to_core
    keep, give = add_low(mine[:4], found[:4]), add_low(mine[4:], found[4:])
    found = yield give, to_second
    keep, give = add_low(keep[:2], found[:2]), add_low(keep[2:], found[2:])
    found = yield give, to_first
    return [add_low(keep[i], found[i]) for i in range(2)]


def collect_all(mine, theirs):
    found = yield theirs, to_core
    keep, give = add_low(mine[:8], found[:8]), add_low(mine[8:], found[8:])
    found = yield give, to_second
    keep, give = add_low(keep[:4], found[:4]), add_low(keep[4:], found[4:])
    found = yield give, to_first
    return [add_low(keep[i], found[i]) for i in range(4)]


def share_flow(own, places):
    first = yield own, to_first
    pair = jnp.stack([own, first])
    second = yield pair, to_second
    quarters = jnp.concatenate([pair, second])
    return jnp.concatenate(
        [lax.dynamic_index_in_dim(quarters, place, 0, keepdims=False) for place in places]
    )


def local_hops(
    tokens_in,
    output_cotangent,
    routes,
    doc_ids,
    picture_starts,
    qkv_weight,
    out_weight,
    router_weight,
    attn_gain,
    moe_gain,
    gate_up_weight,
    down_weight,
):
    low = jnp.bfloat16
    full = jnp.float32
    rows = tokens_in.shape[0]
    seq_len = doc_ids.shape[1]
    q_width = HEADS * HEAD_DIM
    kv_width = KV_HEADS * HEAD_DIM
    qkv_width = q_width + 2 * kv_width
    group_at = lax.axis_index("expert")
    shard_at = lax.axis_index("shard")
    own_experts = EXPERTS // GROUPS
    whole = own_experts // SHARDS * SHARDS
    split = own_experts - whole
    share = SHARDS // split
    part = H // share
    hid_width = H + part
    depth = gate_up_weight.shape[0]
    height = SHARDS * depth
    fine = depth // GROUPS
    pad = 128 - EXPERTS
    gain_one = attn_gain.astype(full)[:, None]
    gain_two = moe_gain.astype(full)[:, None]
    expert_one = group_at * own_experts + shard_at
    expert_two = group_at * own_experts + whole + shard_at // share
    ids = jnp.stack([expert_one, expert_two])
    order = Order(jnp.zeros((8, 128), full))

    spot = jnp.arange(GROUPS * SHARDS, dtype=jnp.int32)
    spot_core = spot // 8 % 2
    spot_mate = 1 + (shard_at % 2 ^ spot_core)
    spot_q = spot % 8 // 2
    spot_group = jnp.where(spot_q == 1, spot_mate, jnp.where(spot_q == 2, 3 - spot_mate, spot_q))
    spot_line = spot // 16 * 2 + spot % 2
    fine_at = (shard_at ^ (2 * spot_line + spot_core)) * depth + (group_at ^ spot_group) * fine

    expert_ids = jnp.arange(EXPERTS, dtype=jnp.int32)
    hits = jnp.any(routes[:, :, None] == expert_ids[None, None, :], 1)
    earlier = jnp.arange(rows)[:, None] > jnp.arange(rows)[None, :]
    before = dot(earlier.astype(low), hits.astype(low), rows_by_cols)
    slots = jnp.where(hits & (before < CAP), before, -1.0)
    kept = slots >= 0
    grad_pay = jnp.concatenate(
        [output_cotangent, jnp.pad(slots.astype(low), ((0, 0), (0, pad)))], 1
    )

    def fine_rows(array):
        return lax.dynamic_slice_in_dim(array, group_at * fine, fine, 0)

    qkv_own = fine_rows(qkv_weight).astype(full) * fine_rows(gain_one)
    router_own = fine_rows(router_weight).astype(full) * fine_rows(gain_two)
    dense_own = jnp.concatenate([qkv_own, jnp.pad(router_own, ((0, 0), (0, pad)))], 1).astype(low)
    out_own = fine_rows(out_weight)

    def column_spec(width, index):
        return pl.BlockSpec((depth, width), lambda d, ids: (0, index(d)))

    to_parts = H // part
    pack_up, pack_down = call(
        pack_kernel,
        "pack",
        (shaped((SHARDS, depth, 2 * hid_width)), shaped((SHARDS, depth, hid_width))),
        [
            column_spec(2 * H, lambda d: d),
            column_spec(part, lambda d: (whole + d // share) * 2 * to_parts + d % share),
            column_spec(part, lambda d: (whole + d // share) * 2 * to_parts + to_parts + d % share),
            column_spec(H, lambda d: d),
            column_spec(part, lambda d: (whole + d // share) * to_parts + d % share),
            pl.BlockSpec((depth, 1), lambda d, ids: (0, 0)),
        ],
        [
            pl.BlockSpec((1, depth, 2 * hid_width), lambda d, ids: (d, 0, 0)),
            pl.BlockSpec((1, depth, hid_width), lambda d, ids: (d, 0, 0)),
        ],
        (ids, gate_up_weight, gate_up_weight, gate_up_weight, down_weight, down_weight, gain_two),
        steps=SHARDS,
    )

    def exchange(packed):
        return lax.all_to_all(packed, "shard", split_axis=0, concat_axis=0, tiled=True)

    w = line_flows(dense_own)
    g_marks, x_marks = [], []
    g_line = Flow(line_spread(grad_pay, g_marks))
    order.round(w[:2])
    w_near = Flow(spread_pair([dense_own, w[0].result]))
    order.round([w[2], w_near, g_line])
    w_far = Flow(spread_pair([w[1].result, w[2].result]))
    g_near = Flow(spread_pair([grad_pay, g_marks[0]]))
    owned_down = exchange(order.tie(pack_down)).reshape(height, hid_width)
    order.round([w_near, w_far])
    order.round([w_near, w_far, g_line])
    o = line_flows(out_own)
    order.round([w_far] + o)
    dense_full = place_rows(fine_at, w_near.result + w_far.result, height)
    router_full = dense_full[:, qkv_width:]
    owned_up = exchange(order.tie(pack_up)).reshape(height, 2 * hid_width)

    tokens_f = tokens_in.astype(full)
    inverse_one = lax.rsqrt(jnp.mean(tokens_f * tokens_f, -1, keepdims=True) + norm_eps)
    normal_one = tokens_f * inverse_one
    normed_in = normal_one.astype(low)
    query_pos = shard_at * rows + jnp.arange(rows, dtype=jnp.int32)
    cosine, sine = rope_tables(query_pos, HEAD_DIM)
    cosine = jnp.tile(cosine[:, 0], (1, 4))
    sine = jnp.tile(jnp.concatenate([-sine[:, 0], sine[:, 0]], 1), (1, 2))
    tile = 512
    queries, key_value = call(
        qkv_kernel,
        "qkv",
        (shaped((rows, q_width)), shaped((rows, 2 * kv_width))),
        [
            whole_spec((rows, D)),
            pl.BlockSpec((D, tile), lambda j, ids: (0, j)),
            whole_spec((rows, 128)),
            whole_spec((rows, 128)),
        ],
        [
            pl.BlockSpec((rows, tile), lambda j, ids: (0, jnp.minimum(j, 2))),
            pl.BlockSpec((rows, tile), lambda j, ids: (0, jnp.maximum(j - 3, 0))),
        ],
        (ids, normed_in, dense_full, cosine, sine),
        flops=2 * rows * D * qkv_width,
        steps=qkv_width // tile,
    )
    o_pairs = [
        Flow(spread_pair([out_own, o[0].result])),
        Flow(spread_pair([o[1].result, o[2].result])),
    ]
    queries, key_value = order.round(o_pairs + [g_line, g_near], (queries, key_value))
    g_far = Flow(spread_pair(g_line.result))
    kv = line_flows(key_value)
    order.round(kv + o_pairs + [g_near])
    kv_line = jnp.concatenate([key_value] + [flow.result for flow in kv])
    kv_core = Flow(one_hop(kv_line, to_core))
    owned_down = order.round([kv_core] + o_pairs + [g_near, g_far], owned_down)
    kv_other = kv_core.result
    out_full = place_rows(fine_at, o_pairs[0].result + o_pairs[1].result, height)
    block_order = jnp.arange(SHARDS, dtype=jnp.int32)
    block_order = shard_at ^ (block_order % 4 * 2 + block_order // 4)
    key_pos = (
        block_order[:, None] * rows + jnp.arange(rows, dtype=jnp.int32)[None, :]
    ).reshape(seq_len)
    doc_blocks = doc_ids[0].reshape(SHARDS, rows)
    block_hits = block_order[:, None] == jnp.arange(SHARDS)[None, :]
    key_doc = jnp.sum(
        jnp.where(block_hits[:, :, None], doc_blocks[None], 0), 1
    ).reshape(seq_len)
    query_doc = key_doc[:rows]
    key_pic = picture_ids(key_pos, picture_starts[0], SLOT, PIECE)
    query_pic = key_pic[:rows]
    visible = allowed(query_pos, key_pos, query_doc, key_doc, query_pic, key_pic)
    bias = jnp.where(visible, 0.0, masked_score)
    pairs = KV_HEADS // 2
    q_tile = q_width // pairs
    kv_tile = kv_width // pairs
    half_len = seq_len // 2

    def kv_specs(first):
        return [pl.BlockSpec((half_len, kv_tile), lambda j, ids: (0, first + j))] * 2

    q_spec = pl.BlockSpec((rows, q_tile), lambda j, ids: (0, j))
    log_spec = pl.BlockSpec((1, rows, 128), lambda j, ids: (j, 0, 0))
    attended, logs = call(
        attend_kernel,
        "attend",
        (shaped((rows, q_width)), shaped((pairs, rows, 128), full)),
        [q_spec] + kv_specs(0) + kv_specs(pairs) + [whole_spec((rows, seq_len))],
        [q_spec, log_spec],
        (ids, queries, kv_line, kv_other, kv_line, kv_other, bias),
        flops=4 * rows * seq_len * q_width,
        steps=pairs,
    )
    branch = dot(attended, out_full, rows_by_rows)
    middle = tokens_f + branch
    inverse_two = lax.rsqrt(jnp.mean(middle * middle, -1, keepdims=True) + norm_eps)
    normal_two = middle * inverse_two
    normed_mid = normal_two.astype(low)
    logits = dot(normed_mid, router_full, rows_by_cols)[:, :EXPERTS]
    logits = jnp.where(hits, logits, masked_score)
    gates = jnp.exp(logits - jnp.max(logits, -1, keepdims=True))
    gates = jnp.where(hits, gates, 0.0)
    gates = gates / jnp.sum(gates, -1, keepdims=True)
    gate_low = gates.astype(low)
    gate_rest = (gates - gate_low.astype(full)).astype(low)
    row_pay = jnp.concatenate(
        [normed_mid, gate_low, gate_rest, jnp.zeros((rows, 128 - 2 * EXPERTS), low)], 1
    )

    row_pay = order.round([g_far], row_pay)
    x_line = Flow(line_spread(row_pay, x_marks))
    order.round([x_line, g_far])
    x_near = Flow(spread_pair([row_pay, x_marks[0]]))
    grad_parts = [g_near.result, g_far.result]
    row_parts = [x_near, None]

    slot_rows = GROUPS * SHARDS * CAP
    step_rows = slot_rows // 2
    blocks = 2 * GROUPS
    pay_spec = whole_spec((blocks, rows, D + 128))
    pay_out = out_spec((blocks, rows, D + 128), (0, 0, 0))
    slot_spec = block_spec((blocks, rows, 128), (0, 0, D // 128))
    up_specs = [
        block_spec((height, 2 * H), (0, 0)),
        block_spec((height, 2 * part), (0, H // part)),
    ]
    down_specs = [
        block_spec((height, H), (0, 0)),
        block_spec((height, part), (0, H // part)),
    ]
    back_shape = shaped((blocks, rows, D + 128))
    gs = jnp.zeros((2, slot_rows, D), low)
    xs = jnp.zeros((2, slot_rows, D), low)
    hid = jnp.zeros((slot_rows, hid_width), low)
    pg = jnp.zeros((slot_rows, 2 * hid_width), low)

    def like(array):
        return shaped(array.shape, array.dtype)

    plain = []
    for k in range(2):
        gs, found = call(
            grad_side_kernel,
            "grad_side",
            (like(gs), shaped((step_rows, hid_width), full)),
            [pay_spec, pay_spec] + down_specs + [in_place],
            [
                out_spec((2, step_rows, D), (0, k, 0)),
                out_spec((step_rows, hid_width), (0, 0)),
            ],
            (ids,) + grad_parts[k] + (owned_down, owned_down, gs),
            aliases={5: 0},
            flops=2 * step_rows * D * (hid_width + 2 * rows),
        )
        plain.append(found)
    order.round([x_line, x_near])
    plain = order.round([x_line, x_near], plain)
    x_far = Flow(spread_pair(x_line.result))
    row_parts[1] = x_far
    owned_up = order.round([x_near, x_far], owned_up)

    def row_side(k):
        nonlocal xs, hid, pg
        half_back, other_back, xs, hid, pg = call(
            row_side_kernel,
            "row_side",
            (back_shape, back_shape, like(xs), like(hid), like(pg)),
            [pay_spec, pay_spec, slot_spec, slot_spec, whole_spec((step_rows, hid_width))]
            + up_specs
            + [in_place] * 3,
            [
                pay_out,
                pay_out,
                out_spec((2, step_rows, D), (0, k, 0)),
                out_spec((step_rows, hid_width), (k, 0)),
                out_spec((step_rows, 2 * hid_width), (k, 0)),
            ],
            (ids,) + row_parts[k].result + grad_parts[k] + (plain[k], owned_up, owned_up, xs, hid, pg),
            scratch=[
                pltpu.VMEM((2, step_rows, 1), full),
                pltpu.VMEM((2, step_rows, 1), full),
                pltpu.VMEM((2, step_rows, D + 128), low),
            ],
            aliases={8: 2, 9: 3, 10: 4},
            flops=8 * step_rows * D * (hid_width + rows),
        )
        return half_back, other_back

    back_near = order.round([x_far], row_side(0))
    b_near = Flow(collect_pair(*back_near))
    order.round([x_far, b_near])
    back_far = order.round([b_near], row_side(1))
    b_far = Flow(collect_pair(*back_far))

    def lane_block(i, ids):
        return (0, 0, i)

    terms = call(
        terms_kernel,
        "terms",
        (shaped((SHARDS, depth, 2 * hid_width)), shaped((SHARDS, depth, hid_width))),
        [
            pl.BlockSpec((2, slot_rows, 2 * depth), lane_block),
            pl.BlockSpec((2, slot_rows, 2 * depth), lane_block),
            whole_spec((slot_rows, 2 * hid_width)),
            whole_spec((slot_rows, hid_width)),
        ],
        [
            pl.BlockSpec((2, depth, 2 * hid_width), lambda i, ids: (i, 0, 0)),
            pl.BlockSpec((2, depth, hid_width), lambda i, ids: (i, 0, 0)),
        ],
        (ids, xs, gs, pg, hid),
        flops=2 * slot_rows * D * 3 * hid_width,
        steps=4,
    )
    terms = order.round([b_near, b_far], terms)
    terms_down = exchange(order.tie(terms[1]))
    b_line = [Flow(one_hop(b_near.result[1], to_line[1]))]
    order.round([b_far] + b_line)

    def out_side(k):
        return call(
            out_side_kernel,
            "out_side",
            (shaped((blocks, rows, D)),) * 2,
            [block_spec((step_rows, hid_width), (k, 0)), slot_spec, slot_spec] + down_specs,
            [out_spec((blocks, rows, D), (0, 0, 0))] * 2,
            (ids, hid) + grad_parts[k] + (owned_down, owned_down),
            scratch=[pltpu.VMEM((2, step_rows, D), low)],
            flops=2 * step_rows * D * (hid_width + 2 * rows),
        )

    out_near = order.round([b_far], out_side(0))
    m_near = Flow(collect_pair(*out_near))
    b_line += [Flow(one_hop(piece, to_line[2 + i])) for i, piece in enumerate(by_distance(b_far.result))]
    out_far, terms_down = order.round(b_line[1:] + [m_near], (out_side(1), terms_down))
    m_far = Flow(collect_pair(*out_far))
    grad_sum = total_of([b_near.result[0]] + [flow.result for flow in b_line])
    terms_up = exchange(order.tie(terms[0]))

    gate_grad = jnp.where(kept, grad_sum[:, D : D + EXPERTS], 0.0)
    logit_grad = gates * (gate_grad - jnp.sum(gates * gate_grad, -1, keepdims=True))
    logit_grad = jnp.pad(logit_grad.astype(low), ((0, 0), (0, pad)))
    scaled_two = grad_sum[:, :D] + dot(logit_grad, router_full, rows_by_rows)
    grad_out = output_cotangent.astype(full)
    mean_two = jnp.mean(scaled_two * normal_two, -1, keepdims=True)
    mid_grad = grad_out + inverse_two * (scaled_two - normal_two * mean_two)
    branch_grad = mid_grad.astype(low)
    attended_grad = dot(branch_grad, out_full, rows_by_cols).astype(low)

    kv_out = pl.BlockSpec((half_len, kv_tile), lambda j, ids: (0, j))
    query_back, key_mine, key_theirs, value_mine, value_theirs = call(
        attend_back_kernel,
        "attend_back",
        (shaped((rows, q_width)),) + (shaped((half_len, kv_width)),) * 4,
        [q_spec, q_spec]
        + kv_specs(0)
        + kv_specs(pairs)
        + [whole_spec((rows, seq_len)), log_spec, whole_spec((rows, 128)), whole_spec((rows, 128))],
        [q_spec] + [kv_out] * 4,
        (ids, queries, attended_grad, kv_line, kv_other, kv_line, kv_other, bias, logs, cosine, sine),
        flops=10 * rows * seq_len * q_width,
        steps=pairs,
    )
    kv_theirs = jnp.concatenate([key_theirs, value_theirs], 1)
    kv_mine = jnp.concatenate([key_mine, value_mine], 1)
    def dense_flow(products):
        found = dense_terms(fine_at, products, 4, 8, fine)
        return found, [[found[core], found[2 + core]] for core in range(2)]

    out_found, out_blocks = dense_flow([(branch_grad, attended, 0)])
    kv_theirs, kv_mine, out_blocks = order.round([m_near, m_far], (kv_theirs, kv_mine, out_blocks))
    early = [Flow(collect_pair(out_blocks[0][i], out_blocks[1][i])) for i in range(2)]
    kv_core = Flow(one_hop(kv_theirs, to_core))
    order.round([kv_core] + early)
    kv_half = add_low(kv_mine, kv_core.result).reshape(4, rows, 2 * kv_width)
    kv = [Flow(one_hop(kv_half[k], to_line[k])) for k in (1, 2, 3)]
    query_blocks = dense_flow([(normed_in, query_back, 0)])[1]
    query_blocks = order.round(kv + [m_far] + early, query_blocks)
    middle_flows = [Flow(collect_pair(query_blocks[0][i], query_blocks[1][i])) for i in range(2)]
    kv_grad = total_of([kv_half[0]] + [flow.result for flow in kv])

    def line_of(near, far):
        return [Flow(one_hop(near[1], to_line[1]))] + [
            Flow(one_hop(far[i], to_line[2 + i])) for i in range(2)
        ]


    def swapped(values):
        lanes = jnp.arange(values.shape[1]) % HEAD_DIM < HEAD_DIM // 2
        return jnp.where(
            lanes[None], jnp.roll(values, -HEAD_DIM // 2, 1), jnp.roll(values, HEAD_DIM // 2, 1)
        )

    key_grad = kv_grad[:, :kv_width]
    key_back = key_grad * jnp.tile(cosine, (1, pairs)) - swapped(key_grad) * jnp.tile(sine, (1, pairs))
    kv_rows = jnp.concatenate([key_back, kv_grad[:, kv_width:]], 1).astype(low)
    scaled_one = dot(query_back, dense_full[:, :q_width], rows_by_rows) + dot(
        kv_rows, dense_full[:, q_width:qkv_width], rows_by_rows
    )
    mean_one = jnp.mean(scaled_one * normal_one, -1, keepdims=True)
    input_grad = mid_grad + inverse_one * (scaled_one - normal_one * mean_one)
    pad_lanes = jnp.arange(128)[None, :]

    def marker(lane):
        return jnp.broadcast_to(jnp.where(pad_lanes == lane, 1.0, 0.0), (rows, 128)).astype(low)

    late_blocks = dense_flow(
        [
            (normed_in, kv_rows, 0),
            (normed_mid, logit_grad, 2 * kv_width),
            ((scaled_two * normal_two).astype(low), marker(EXPERTS), 2 * kv_width),
            ((scaled_one * normal_one).astype(low), marker(EXPERTS + 1), 2 * kv_width),
        ]
    )[1]
    late_blocks, input_grad = order.round(
        early + middle_flows, (late_blocks, input_grad.astype(low))
    )
    late = [Flow(collect_pair(late_blocks[0][i], late_blocks[1][i])) for i in range(2)]
    early_line = line_of(early[0].result, early[1].result)
    order.round(late + middle_flows)
    order.round(late + middle_flows + [m_near])
    middle_line = line_of(middle_flows[0].result, middle_flows[1].result)
    order.round(late + early_line)
    late_line = line_of(late[0].result, late[1].result)
    spots = jnp.arange(GROUPS, dtype=jnp.int32) ^ group_at
    mate = 1 + shard_at % 2
    spots = jnp.where(spots == mate, 1, jnp.where(spots == 3 - mate, 2, spots))
    places = [spots[i] for i in range(GROUPS)]

    def shared(first, line):
        own = total_of([first] + [flow.result for flow in line]).astype(low)
        return Flow(share_flow(own, places))

    early_share = shared(early[0].result[0], early_line)
    order.round(late_line + [early_share, m_far])
    late_share = shared(late[0].result[0], late_line)
    terms_up = order.round([late_share, early_share] + middle_line, terms_up)
    middle_share = shared(middle_flows[0].result[0], middle_line)
    order.round([late_share, middle_share])
    m_line = line_of(m_near.result, by_distance(m_far.result))
    order.round([middle_share] + m_line)
    output = (middle + total_of([m_near.result[0]] + [flow.result for flow in m_line])).astype(low)
    out_sum = early_share.result.astype(full)
    query_sum = middle_share.result.astype(full)
    late_sum = late_share.result.astype(full)

    gate_up_grad, down_grad = call(
        unpack_kernel,
        "unpack",
        (shaped(gate_up_weight.shape, full), shaped(down_weight.shape, full)),
        [
            pl.BlockSpec((1, depth, 2 * H), lambda j, ids: (jnp.minimum(j, whole - 1), 0, 0)),
            pl.BlockSpec(
                (share, depth, 2 * part), lambda j, ids: (jnp.maximum(j - whole, 0), 0, to_parts)
            ),
            pl.BlockSpec((1, depth, H), lambda j, ids: (jnp.minimum(j, whole - 1), 0, 0)),
            pl.BlockSpec(
                (share, depth, part), lambda j, ids: (jnp.maximum(j - whole, 0), 0, to_parts)
            ),
            whole_spec((depth, 1)),
        ],
        [
            pl.BlockSpec((depth, 2 * H), lambda j, ids: (0, j)),
            pl.BlockSpec((depth, H), lambda j, ids: (0, j)),
        ],
        (ids, terms_up, terms_up, terms_down, terms_down, gain_two),
        steps=own_experts,
    )
    return (
        output,
        input_grad,
        jnp.concatenate([query_sum, late_sum[:, : 2 * kv_width]], 1) * gain_one,
        out_sum,
        late_sum[:, 2 * kv_width : 2 * kv_width + EXPERTS] * gain_two,
        late_sum[:, 2 * kv_width + EXPERTS + 1] / gain_one[:, 0],
        late_sum[:, 2 * kv_width + EXPERTS] / gain_two[:, 0],
        gate_up_grad,
        down_grad,
    )


def solution(mesh):
    body = local
    if mesh.shape["expert"] == GROUPS and mesh.shape["shard"] == SHARDS:
        body = local_hops
    return jax.shard_map(
        body,
        mesh=mesh,
        in_specs=(
            P(("expert", "shard"), None),
            P(("expert", "shard"), None),
            P(("expert", "shard"), None),
            P("expert", None),
            P("expert", None),
            P("shard", None),
            P("shard", None),
            P("shard", None),
            P("shard"),
            P("shard"),
            P("shard", "expert"),
            P("shard", "expert"),
        ),
        out_specs=(
            P(("expert", "shard"), None),
            P(("expert", "shard"), None),
            P("shard", None),
            P("shard", None),
            P("shard", None),
            P("shard"),
            P("shard"),
            P("shard", "expert"),
            P("shard", "expert"),
        ),
        check_vma=False,
    )
```

```python
import jax
import jax.numpy as jnp
from jax import lax
from jax.experimental import pallas as pl
from jax.experimental.pallas import tpu as pltpu
from jax.sharding import PartitionSpec as P

D = 1536
HEADS = 24
KV_HEADS = 8
HEAD_DIM = 64
H = 512
EXPERTS = 40
TOP = 8
PIECE = 256
SLOT = 512
CAP = 32


norm_eps = 1e-06
rope_base = 10000.0
masked_score = -1e30


def rope_tables(positions, head_dim):
    half_dim = head_dim // 2
    frequency = rope_base ** (-2.0 * jnp.arange(half_dim, dtype=jnp.float32) / head_dim)
    angles = positions.astype(jnp.float32)[:, None] * frequency[None, :]
    return (jnp.cos(angles)[:, None, :], jnp.sin(angles)[:, None, :])


def rotate(values, cosine, sine_table):
    half_dim = values.shape[-1] // 2
    first_half = values[..., :half_dim]
    second = values[..., half_dim:]
    return jnp.concatenate(
        [first_half * cosine - second * sine_table, second * cosine + first_half * sine_table], -1
    )


def rotate_back(grad_rows, cosine, sine_table):
    half_dim = grad_rows.shape[-1] // 2
    first_half = grad_rows[..., :half_dim]
    second = grad_rows[..., half_dim:]
    return jnp.concatenate(
        [first_half * cosine + second * sine_table, second * cosine - first_half * sine_table], -1
    )


def rms_norm(values, gain):
    inverse = lax.rsqrt(jnp.mean(values * values, -1, keepdims=True) + norm_eps)
    normal = values * inverse
    return (normal * gain, normal, inverse)


def rms_back(grad_rows, gain, normal, inverse):
    scaled = grad_rows * gain
    grad_in = inverse * (scaled - normal * jnp.mean(scaled * normal, -1, keepdims=True))
    return (grad_in, jnp.sum(grad_rows * normal, 0))


def picture_ids(positions, starts, slot_len, piece_len):
    slot_index = positions // slot_len
    picked_slot = slot_index[:, None] == jnp.arange(starts.shape[0], dtype=jnp.int32)[None, :]
    piece_begin = jnp.sum(jnp.where(picked_slot, starts[None, :], 0), axis=1)
    inside = (positions >= piece_begin) & (positions < piece_begin + piece_len)
    return jnp.where(inside, slot_index, -1)


def allowed(query_pos, key_pos, query_doc, key_doc, query_pic, key_pic):
    same_doc = query_doc[:, None] == key_doc[None, :]
    earlier = key_pos[None, :] <= query_pos[:, None]
    same_pic = (query_pic[:, None] == key_pic[None, :]) & (query_pic[:, None] >= 0)
    return same_doc & (earlier | same_pic)


def local(
    tokens_in,
    output_cotangent,
    routes,
    doc_ids,
    picture_starts,
    qkv_weight,
    out_weight,
    router_weight,
    attn_gain,
    moe_gain,
    gate_up_weight,
    down_weight,
):
    qkv_full, out_full, router_full, gain_first, gain_second = (
        lax.all_gather(qkv_weight, "shard", axis=0, tiled=True),
        lax.all_gather(out_weight, "shard", axis=0, tiled=True),
        lax.all_gather(router_weight, "shard", axis=0, tiled=True),
        lax.all_gather(attn_gain, "shard", axis=0, tiled=True),
        lax.all_gather(moe_gain, "shard", axis=0, tiled=True),
    )
    gain_one = gain_first.astype(jnp.float32)
    gain_two = gain_second.astype(jnp.float32)
    tok_rows = tokens_in.shape[0]
    seq_len = doc_ids.shape[1]
    groups = HEADS // KV_HEADS
    q_width = HEADS * HEAD_DIM
    kv_width = KV_HEADS * HEAD_DIM
    score_scale = HEAD_DIM ** (-0.5)
    shard_at = lax.axis_index("shard")
    query_pos = shard_at * tok_rows + jnp.arange(tok_rows, dtype=jnp.int32)
    key_pos = jnp.arange(seq_len, dtype=jnp.int32)
    key_doc = doc_ids[0]
    key_pic = picture_ids(key_pos, picture_starts[0], SLOT, PIECE)
    query_doc = lax.dynamic_slice_in_dim(key_doc, shard_at * tok_rows, tok_rows)
    query_pic = lax.dynamic_slice_in_dim(key_pic, shard_at * tok_rows, tok_rows)
    tokens_f = tokens_in.astype(jnp.float32)
    normed_one, normal_one, inverse_one = rms_norm(tokens_f, gain_one)
    normed_in = normed_one.astype(jnp.bfloat16)
    qkv_rows = jnp.dot(normed_in, qkv_full, preferred_element_type=jnp.float32)
    cosine, sine_table = rope_tables(query_pos, HEAD_DIM)
    queries = (
        rotate(qkv_rows[:, :q_width].reshape(tok_rows, HEADS, HEAD_DIM), cosine, sine_table)
        .astype(jnp.bfloat16)
        .reshape(tok_rows, KV_HEADS, groups, HEAD_DIM)
    )
    key_local = (
        rotate(
            qkv_rows[:, q_width : q_width + kv_width].reshape(tok_rows, KV_HEADS, HEAD_DIM),
            cosine,
            sine_table,
        )
        .astype(jnp.bfloat16)
        .reshape(tok_rows, kv_width)
    )
    value_local = qkv_rows[:, q_width + kv_width :].astype(jnp.bfloat16)
    all_keys, all_values = (
        lax.all_gather(key_local, "shard", axis=0, tiled=True),
        lax.all_gather(value_local, "shard", axis=0, tiled=True),
    )
    span_len = min(512, seq_len)
    span_count = seq_len // span_len

    def block_scores(first_row, key_rows):
        key_block = lax.dynamic_slice_in_dim(key_rows, first_row, span_len, 0).reshape(
            span_len, KV_HEADS, HEAD_DIM
        )
        raw_scores = (
            jnp.einsum("tgrd,kgd->tgrk", queries, key_block, preferred_element_type=jnp.float32)
            * score_scale
        )
        block_pos = lax.dynamic_slice_in_dim(key_pos, first_row, span_len)
        block_doc = lax.dynamic_slice_in_dim(key_doc, first_row, span_len)
        block_pic = lax.dynamic_slice_in_dim(key_pic, first_row, span_len)
        visible = allowed(query_pos, block_pos, query_doc, block_doc, query_pic, block_pic)[
            :, None, None, :
        ]
        return (raw_scores, visible, key_block)

    def value_block_at(first_row, value_rows):
        return lax.dynamic_slice_in_dim(value_rows, first_row, span_len, 0).reshape(
            span_len, KV_HEADS, HEAD_DIM
        )

    def max_step(step_index, carry):
        run_max, run_sum = carry
        raw_scores, visible, key_block = block_scores(step_index * span_len, all_keys)
        masked = jnp.where(visible, raw_scores, masked_score)
        new_max = jnp.maximum(run_max, jnp.max(masked, -1))
        shifted = jnp.where(visible, jnp.exp(masked - new_max[..., None]), 0.0)
        return (new_max, run_sum * jnp.exp(run_max - new_max) + jnp.sum(shifted, -1))

    stat_shape = (tok_rows, KV_HEADS, groups)
    run_max, run_sum = lax.fori_loop(
        0,
        span_count,
        max_step,
        (jnp.full(stat_shape, masked_score, jnp.float32), jnp.zeros(stat_shape, jnp.float32)),
    )
    log_total = run_max + jnp.log(run_sum)

    def probs_of(raw_scores, visible):
        return jnp.exp(jnp.where(visible, raw_scores - log_total[..., None], masked_score))

    def value_step(step_index, summed):
        first_row = step_index * span_len
        raw_scores, visible, key_block = block_scores(first_row, all_keys)
        probs = probs_of(raw_scores, visible).astype(jnp.bfloat16)
        return summed + jnp.einsum(
            "tgrk,kgd->tgrd",
            probs,
            value_block_at(first_row, all_values),
            preferred_element_type=jnp.float32,
        )

    summed = lax.fori_loop(
        0, span_count, value_step, jnp.zeros((tok_rows, KV_HEADS, groups, HEAD_DIM), jnp.float32)
    )
    attended = summed.reshape(tok_rows, q_width).astype(jnp.bfloat16)
    branch = lax.dot_general(
        attended, out_full, (((1,), (1,)), ((), ())), preferred_element_type=jnp.float32
    )
    middle = tokens_f + branch
    normed_two, normal_two, inverse_two = rms_norm(middle, gain_two)
    normed_mid = normed_two.astype(jnp.bfloat16)
    logits = jnp.dot(normed_mid, router_full, preferred_element_type=jnp.float32)
    gates = jax.nn.softmax(jnp.take_along_axis(logits, routes, 1), axis=-1)
    route_hits = routes[:, :, None] == jnp.arange(EXPERTS, dtype=jnp.int32)[None, None, :]
    hit_count = jnp.sum(route_hits.astype(jnp.int32), 1)
    before = jnp.cumsum(hit_count, 0) - hit_count
    slot_index = jnp.take_along_axis(before, routes, 1)
    kept_pair = slot_index < CAP
    flat_slot = routes * CAP + slot_index
    capacity_rows = EXPERTS * CAP
    target = jnp.where(kept_pair, flat_slot, capacity_rows)
    token_ids = jnp.broadcast_to(jnp.arange(tok_rows, dtype=jnp.int32)[:, None], (tok_rows, TOP))
    owner_row = (
        jnp.full((capacity_rows + 1,), -1, jnp.int32)
        .at[target.reshape(-1)]
        .set(token_ids.reshape(-1))[:capacity_rows]
    )
    filled = owner_row >= 0
    source_row = jnp.maximum(owner_row, 0)
    expert_groups = lax.axis_size("expert")
    local_experts = EXPERTS // expert_groups
    send_rows = jnp.where(
        filled[:, None], normed_mid[source_row], jnp.zeros((), jnp.bfloat16)
    ).reshape(expert_groups, local_experts, CAP, D)
    received = lax.all_to_all(send_rows, "expert", split_axis=0, concat_axis=0, tiled=True)
    gate_up_full, down_full = (
        lax.all_gather(gate_up_weight, "shard", axis=0, tiled=True),
        lax.all_gather(down_weight, "shard", axis=0, tiled=True),
    )
    gate_up3 = gate_up_full.reshape(D, local_experts, 2 * H)
    down3 = down_full.reshape(D, local_experts, H)
    projected = jnp.einsum("secd,dej->secj", received, gate_up3, preferred_element_type=jnp.float32)
    gate_part = projected[..., :H]
    up_part = projected[..., H:]
    sigma = jax.nn.sigmoid(gate_part)
    silu_value = gate_part * sigma
    hidden = (silu_value * up_part).astype(jnp.bfloat16)
    expert_out = jnp.einsum(
        "secj,dej->secd", hidden, down3, preferred_element_type=jnp.float32
    ).astype(jnp.bfloat16)
    returned = lax.all_to_all(
        expert_out, "expert", split_axis=0, concat_axis=0, tiled=True
    ).reshape(capacity_rows, D)
    safe_flat = jnp.where(kept_pair, flat_slot, 0)
    picked = returned[safe_flat].astype(jnp.float32)
    pair_weight = jnp.where(kept_pair, gates, 0.0)
    moe_sum = jnp.einsum("tk,tkd->td", pair_weight, picked)
    output = (middle + moe_sum).astype(jnp.bfloat16)
    grad_out = output_cotangent.astype(jnp.float32)
    gate_grad = jnp.where(kept_pair, jnp.einsum("td,tkd->tk", grad_out, picked), 0.0)
    slot_gate = (
        jnp.zeros((capacity_rows + 1,), jnp.float32)
        .at[target.reshape(-1)]
        .set(gates.reshape(-1))[:capacity_rows]
    )
    grad_send = (
        jnp.where(filled[:, None], slot_gate[:, None] * grad_out[source_row], 0.0)
        .astype(jnp.bfloat16)
        .reshape(expert_groups, local_experts, CAP, D)
    )
    grad_received = lax.all_to_all(grad_send, "expert", split_axis=0, concat_axis=0, tiled=True)
    keys_back, values_back = (
        lax.all_gather(key_local, "shard", axis=0, tiled=True),
        lax.all_gather(value_local, "shard", axis=0, tiled=True),
    )
    again_up, again_down = (
        lax.all_gather(gate_up_weight, "shard", axis=0, tiled=True),
        lax.all_gather(down_weight, "shard", axis=0, tiled=True),
    )
    gate_up_back = again_up.reshape(D, local_experts, 2 * H)
    down_back = again_down.reshape(D, local_experts, H)
    hidden_grad = jnp.einsum(
        "secd,dej->secj", grad_received, down_back, preferred_element_type=jnp.float32
    )
    silu_slope = sigma * (1.0 + gate_part * (1.0 - sigma))
    proj_grad = jnp.concatenate(
        [hidden_grad * up_part * silu_slope, hidden_grad * silu_value], -1
    ).astype(jnp.bfloat16)
    row_grad = jnp.einsum(
        "secj,dej->secd", proj_grad, gate_up_back, preferred_element_type=jnp.float32
    ).astype(jnp.bfloat16)
    grad_back = lax.all_to_all(row_grad, "expert", split_axis=0, concat_axis=0, tiled=True).reshape(
        capacity_rows, D
    )
    row_count = gate_up_weight.shape[0] * lax.axis_size("shard")
    up_terms = jnp.einsum(
        "secd,secj->dej", received, proj_grad, preferred_element_type=jnp.float32
    ).reshape(row_count, local_experts * 2 * H)
    down_terms = jnp.einsum(
        "secd,secj->dej", grad_received, hidden, preferred_element_type=jnp.float32
    ).reshape(row_count, local_experts * H)
    expert_sums = lax.psum_scatter(
        jnp.concatenate([up_terms, down_terms], 1).astype(jnp.bfloat16),
        "shard",
        scatter_dimension=0,
        tiled=True,
    ).astype(jnp.float32)
    gate_up_grad = expert_sums[:, : local_experts * 2 * H]
    down_grad = expert_sums[:, local_experts * 2 * H :]
    mid_norm_grad = jnp.einsum(
        "tk,tkd->td", kept_pair.astype(jnp.float32), grad_back[safe_flat].astype(jnp.float32)
    )
    chosen_grad = gates * (gate_grad - jnp.sum(gates * gate_grad, -1, keepdims=True))
    logit_grad = jnp.sum(jnp.where(route_hits, chosen_grad[:, :, None], 0.0), 1).astype(
        jnp.bfloat16
    )
    mid_norm_grad = mid_norm_grad + lax.dot_general(
        logit_grad, router_full, (((1,), (1,)), ((), ())), preferred_element_type=jnp.float32
    )
    router_grad = lax.dot_general(
        normed_mid, logit_grad, (((0,), (0,)), ((), ())), preferred_element_type=jnp.float32
    )
    mid_part, moe_gain_grad = rms_back(mid_norm_grad, gain_two, normal_two, inverse_two)
    mid_grad = grad_out + mid_part
    branch_grad = mid_grad.astype(jnp.bfloat16)
    out_weight_grad = lax.dot_general(
        branch_grad, attended, (((0,), (0,)), ((), ())), preferred_element_type=jnp.float32
    )
    attended_grad = (
        jnp.dot(branch_grad, out_full, preferred_element_type=jnp.float32)
        .astype(jnp.bfloat16)
        .reshape(tok_rows, KV_HEADS, groups, HEAD_DIM)
    )

    def dot_step(step_index, row_dot):
        first_row = step_index * span_len
        raw_scores, visible, key_block = block_scores(first_row, keys_back)
        prob_full = probs_of(raw_scores, visible)
        prob_grad = jnp.einsum(
            "tgrd,kgd->tgrk",
            attended_grad,
            value_block_at(first_row, values_back),
            preferred_element_type=jnp.float32,
        )
        return row_dot + jnp.sum(prob_full * prob_grad, -1)

    row_dot = lax.fori_loop(0, span_count, dot_step, jnp.zeros(stat_shape, jnp.float32))

    def grad_step(step_index, carry):
        query_grad, key_terms, value_terms = carry
        first_row = step_index * span_len
        raw_scores, visible, key_block = block_scores(first_row, keys_back)
        prob_full = probs_of(raw_scores, visible)
        prob_grad = jnp.einsum(
            "tgrd,kgd->tgrk",
            attended_grad,
            value_block_at(first_row, values_back),
            preferred_element_type=jnp.float32,
        )
        score_grad = (prob_full * (prob_grad - row_dot[..., None])).astype(jnp.bfloat16)
        query_grad = query_grad + jnp.einsum(
            "tgrk,kgd->tgrd", score_grad, key_block, preferred_element_type=jnp.float32
        )
        key_part = (
            jnp.einsum(
                "tgrk,tgrd->kgd", score_grad, queries, preferred_element_type=jnp.float32
            ).reshape(span_len, kv_width)
            * score_scale
        )
        value_part = jnp.einsum(
            "tgrk,tgrd->kgd",
            prob_full.astype(jnp.bfloat16),
            attended_grad,
            preferred_element_type=jnp.float32,
        ).reshape(span_len, kv_width)
        key_terms = lax.dynamic_update_slice_in_dim(key_terms, key_part, first_row, 0)
        value_terms = lax.dynamic_update_slice_in_dim(value_terms, value_part, first_row, 0)
        return (query_grad, key_terms, value_terms)

    query_grad, key_terms, value_terms = lax.fori_loop(
        0,
        span_count,
        grad_step,
        (
            jnp.zeros((tok_rows, KV_HEADS, groups, HEAD_DIM), jnp.float32),
            jnp.zeros((seq_len, kv_width), jnp.float32),
            jnp.zeros((seq_len, kv_width), jnp.float32),
        ),
    )
    key_grad, value_grad = (
        lax.psum_scatter(
            key_terms.astype(jnp.bfloat16), "shard", scatter_dimension=0, tiled=True
        ).astype(jnp.float32),
        lax.psum_scatter(
            value_terms.astype(jnp.bfloat16), "shard", scatter_dimension=0, tiled=True
        ).astype(jnp.float32),
    )
    query_back = rotate_back(
        (query_grad * score_scale).reshape(tok_rows, HEADS, HEAD_DIM), cosine, sine_table
    ).reshape(tok_rows, q_width)
    key_back = rotate_back(
        key_grad.reshape(tok_rows, KV_HEADS, HEAD_DIM), cosine, sine_table
    ).reshape(tok_rows, kv_width)
    qkv_grad_rows = jnp.concatenate([query_back, key_back, value_grad], 1).astype(jnp.bfloat16)
    qkv_weight_grad = lax.dot_general(
        normed_in, qkv_grad_rows, (((0,), (0,)), ((), ())), preferred_element_type=jnp.float32
    )
    in_norm_grad = lax.dot_general(
        qkv_grad_rows, qkv_full, (((1,), (1,)), ((), ())), preferred_element_type=jnp.float32
    )
    in_part, attn_gain_grad = rms_back(in_norm_grad, gain_one, normal_one, inverse_one)
    input_grad = (mid_grad + in_part).astype(jnp.bfloat16)
    dense_sums = (
        lax.psum_scatter(
            qkv_weight_grad.astype(jnp.bfloat16), "shard", scatter_dimension=0, tiled=True
        ).astype(jnp.float32),
        lax.psum_scatter(
            out_weight_grad.astype(jnp.bfloat16), "shard", scatter_dimension=0, tiled=True
        ).astype(jnp.float32),
        lax.psum_scatter(
            router_grad.astype(jnp.bfloat16), "shard", scatter_dimension=0, tiled=True
        ).astype(jnp.float32),
        lax.psum_scatter(
            attn_gain_grad.astype(jnp.bfloat16), "shard", scatter_dimension=0, tiled=True
        ).astype(jnp.float32),
        lax.psum_scatter(
            moe_gain_grad.astype(jnp.bfloat16), "shard", scatter_dimension=0, tiled=True
        ).astype(jnp.float32),
    )
    dense_totals = (
        lax.psum(dense_sums[0].astype(jnp.bfloat16), "expert").astype(jnp.float32),
        lax.psum(dense_sums[1].astype(jnp.bfloat16), "expert").astype(jnp.float32),
        lax.psum(dense_sums[2].astype(jnp.bfloat16), "expert").astype(jnp.float32),
        lax.psum(dense_sums[3].astype(jnp.bfloat16), "expert").astype(jnp.float32),
        lax.psum(dense_sums[4].astype(jnp.bfloat16), "expert").astype(jnp.float32),
    )
    return (
        output,
        input_grad,
        dense_totals[0],
        dense_totals[1],
        dense_totals[2],
        dense_totals[3],
        dense_totals[4],
        gate_up_grad,
        down_grad,
    )


GROUPS = 4
SHARDS = 8
rows_by_cols = ((1,), (0,))
rows_by_rows = ((1,), (1,))
cols_by_cols = ((0,), (0,))


def dot(one, two, dims):
    return lax.dot_general(one, two, (dims, ((), ())), preferred_element_type=jnp.float32)


def whole_spec(shape):
    return pl.BlockSpec(shape, lambda i, ids: (0,) * len(shape), pipeline_mode=pl.Buffered(1))


def block_spec(shape, index):
    return pl.BlockSpec(shape, lambda i, ids: index, pipeline_mode=pl.Buffered(1))


def out_spec(shape, index):
    return pl.BlockSpec(shape, lambda i, ids: index)


in_place = pl.BlockSpec(memory_space=pl.ANY)


def shaped(shape, dtype=jnp.bfloat16):
    return jax.ShapeDtypeStruct(shape, dtype)


def call(kernel, name, out_shape, in_specs, out_specs, args, scratch=(), aliases=None, flops=0, steps=1):
    moved = sum(a.size * a.dtype.itemsize for a in args[1:])
    return pl.pallas_call(
        kernel,
        name=name,
        out_shape=out_shape,
        grid_spec=pltpu.PrefetchScalarGridSpec(
            num_scalar_prefetch=1,
            grid=(steps,),
            in_specs=in_specs,
            out_specs=out_specs,
            scratch_shapes=list(scratch),
        ),
        input_output_aliases=aliases or {},
        compiler_params=pltpu.CompilerParams(
            vmem_limit_bytes=58 * 1024 * 1024, dimension_semantics=("arbitrary",)
        ),
        cost_estimate=pl.CostEstimate(flops=flops, transcendentals=0, bytes_accessed=moved),
    )(*args)


def place_rows(offsets, parts, height):
    count, fine, width = parts[0].shape

    def kernel(at, *refs):
        sources, target, done = refs[: len(parts)], refs[len(parts)], refs[-1]
        copies = []
        for n, source in enumerate(sources):
            for i in range(count):
                row = pl.multiple_of(at[n * count + i], 16)
                copies.append(
                    pltpu.make_async_copy(
                        source.at[i], target.at[pl.ds(row, fine)], done.at[n * count + i]
                    )
                )
        for copy in copies:
            copy.start()
        for copy in copies:
            copy.wait()

    return call(
        kernel,
        "place_rows",
        shaped((height, width), parts[0].dtype),
        [in_place] * len(parts),
        out_spec((height, width), (0, 0)),
        (offsets,) + tuple(parts),
        scratch=[pltpu.SemaphoreType.DMA((len(parts) * count,))],
    )


def dense_terms(offsets, products, parts, count, fine):
    height = products[0][0].shape[1]
    width = max(first + two.shape[1] for _, two, first in products)
    firsts = [first for _, _, first in products]

    def kernel(at, *refs):
        sources, targets, held = refs[: 2 * len(firsts)], refs[2 * len(firsts) : -1], refs[-1]
        total = {}
        for n, first in enumerate(firsts):
            found = dot(sources[2 * n][...], sources[2 * n + 1][...], cols_by_cols)
            total[first] = total[first] + found if first in total else found
        for first, found in total.items():
            held[:, first : first + found.shape[1]] = found.astype(jnp.bfloat16)
        for n, target in enumerate(targets):
            for i in range(count):
                row = pl.multiple_of(at[n * count + i], 16)
                target[i] = held[pl.ds(row, fine)]

    operands = [array for one, two, _ in products for array in (one, two)]
    return call(
        kernel,
        "dense_terms",
        [shaped((count, fine, width))] * parts,
        [whole_spec(array.shape) for array in operands],
        [out_spec((count, fine, width), (0, 0, 0))] * parts,
        (offsets,) + tuple(operands),
        scratch=[pltpu.VMEM((height, width), jnp.bfloat16)],
        flops=2 * height * width * products[0][0].shape[0],
    )


def pack_kernel(ids, up, gate_part, up_part, down, down_part, gain, *packs):
    width = down.shape[1]
    scale = gain[...]
    step = pl.program_id(0)

    def scaled(rows):
        return (rows.astype(jnp.float32) * scale).astype(jnp.bfloat16)

    for k in range(SHARDS):

        @pl.when(step == k)
        def _(k=k):
            downs, ups = packs[2 * k : 2 * k + 2]
            downs[0, :, :width] = down[...]
            downs[0, :, width:] = down_part[...]
            ups[0, :, : 2 * width] = scaled(up[...])
            part = down_part.shape[1]
            ups[0, :, 2 * width : 2 * width + part] = scaled(gate_part[...])
            ups[0, :, 2 * width + part :] = scaled(up_part[...])


def unpack_kernel(ids, *refs):
    pieces, gain, up_grad, down_grad = refs[: 2 * SHARDS], refs[-3], refs[-2], refs[-1]
    scale = gain[...]
    step = pl.program_id(0)
    share = SHARDS // (pl.num_programs(0) - SHARDS)
    part = (pieces[1].shape[2] - H) // 3
    for k in range(SHARDS):
        one, two = pieces[2 * k : 2 * k + 2]
        source = ids[2] ^ k

        @pl.when(step == k)
        def _(one=one, two=two):
            down_grad[...] = one[0, :, :H].astype(jnp.float32)
            up_grad[:, :H] = one[0, :, H:].astype(jnp.float32) * scale
            up_grad[:, H:] = two[0, :, :H].astype(jnp.float32) * scale

        @pl.when(step == SHARDS + source // share)
        def _(two=two, source=source):
            at = pl.multiple_of(source % share * part, part)
            at_up = pl.multiple_of(H + source % share * part, part)
            down_grad[:, pl.ds(at, part)] = two[0, :, H : H + part].astype(jnp.float32)
            gate = two[0, :, H + part : H + 2 * part].astype(jnp.float32)
            up_grad[:, pl.ds(at, part)] = gate * scale
            up = two[0, :, H + 2 * part :].astype(jnp.float32)
            up_grad[:, pl.ds(at_up, part)] = up * scale


def turn(rows, cosine, sine):
    width = rows.shape[1]
    lanes = lax.broadcasted_iota(jnp.int32, (rows.shape[0], 128), 1)
    first = lanes % HEAD_DIM < HEAD_DIM // 2
    turned = []
    for at in range(0, width, 128):
        piece = rows[:, at : at + 128]
        swapped = jnp.where(
            first,
            pltpu.roll(piece, 128 - HEAD_DIM // 2, 1),
            pltpu.roll(piece, HEAD_DIM // 2, 1),
        )
        turned.append(piece * cosine + swapped * sine)
    return jnp.concatenate(turned, 1)


def qkv_kernel(ids, normed, weight, cosine, sine, queries, key_value):
    step = pl.program_id(0)
    found = dot(normed[...], weight[...], rows_by_cols)

    @pl.when(step < 3)
    def _():
        queries[...] = turn(found, cosine[...], sine[...]).astype(jnp.bfloat16)

    @pl.when(step == 3)
    def _():
        key_value[...] = turn(found, cosine[...], sine[...]).astype(jnp.bfloat16)

    @pl.when(step == 4)
    def _():
        key_value[...] = found.astype(jnp.bfloat16)


def attend_kernel(ids, queries, key_line, key_other, value_line, value_other, bias, attended, logs):
    scale = HEAD_DIM ** (-0.5)
    groups = HEADS // KV_HEADS
    hidden = bias[...]
    keys = jnp.concatenate([key_line[...], key_other[...]], 0)
    values = jnp.concatenate([value_line[...], value_other[...]], 0)
    lanes = lax.broadcasted_iota(jnp.int32, (queries.shape[0], 128), 1)
    totals = jnp.zeros((queries.shape[0], 128), jnp.float32)
    found = []
    for n in range(2 * groups):
        at = n // groups * HEAD_DIM
        scores = dot(
            queries[:, n * HEAD_DIM : (n + 1) * HEAD_DIM], keys[:, at : at + HEAD_DIM], rows_by_rows
        )
        scores = scores * scale + hidden
        top = jnp.max(scores, 1, keepdims=True)
        raised = jnp.exp(scores - top)
        total = jnp.sum(raised, 1, keepdims=True)
        probs = (raised / total).astype(jnp.bfloat16)
        found.append(dot(probs, values[:, at : at + HEAD_DIM], rows_by_cols))
        totals = jnp.where(lanes == n, top + jnp.log(total), totals)
    attended[...] = jnp.concatenate(found, 1).astype(jnp.bfloat16)
    logs[0] = totals


def attend_back_kernel(
    ids, queries, grads, key_line, key_other, value_line, value_other, bias, logs, cosine, sine,
    query_grad, key_mine, key_theirs, value_mine, value_theirs,
):
    scale = HEAD_DIM ** (-0.5)
    groups = HEADS // KV_HEADS
    hidden = bias[...]
    keys = jnp.concatenate([key_line[...], key_other[...]], 0)
    values = jnp.concatenate([value_line[...], value_other[...]], 0)
    half = key_line.shape[0]
    found = []
    key_found, value_found = [], []
    for n in range(2 * groups):
        own = n // groups
        at = own * HEAD_DIM
        head = slice(n * HEAD_DIM, (n + 1) * HEAD_DIM)
        query = queries[:, head]
        grad = grads[:, head]
        scores = dot(query, keys[:, at : at + HEAD_DIM], rows_by_rows) * scale + hidden
        probs = jnp.exp(scores - lane_value(logs[0], n))
        prob_grad = dot(grad, values[:, at : at + HEAD_DIM], rows_by_rows)
        row_dot = jnp.sum(probs * prob_grad, 1, keepdims=True)
        score_grad = (probs * (prob_grad - row_dot)).astype(jnp.bfloat16)
        found.append(dot(score_grad, keys[:, at : at + HEAD_DIM], rows_by_cols))
        key_part = dot(score_grad, query, cols_by_cols)
        value_part = dot(probs.astype(jnp.bfloat16), grad, cols_by_cols)
        if n % groups:
            key_found[own] = key_found[own] + key_part
            value_found[own] = value_found[own] + value_part
        else:
            key_found.append(key_part)
            value_found.append(value_part)
    found = jnp.concatenate(found, 1) * scale
    query_grad[...] = turn(found, cosine[...], -sine[...]).astype(jnp.bfloat16)
    key_found = (jnp.concatenate(key_found, 1) * scale).astype(jnp.bfloat16)
    value_found = jnp.concatenate(value_found, 1).astype(jnp.bfloat16)
    key_mine[...] = key_found[:half]
    key_theirs[...] = key_found[half:]
    value_mine[...] = value_found[:half]
    value_theirs[...] = value_found[half:]


def lane_value(rows, index):
    lanes = lax.broadcasted_iota(jnp.int32, rows.shape, 1)
    return jnp.sum(jnp.where(lanes == index, rows, 0.0), 1, keepdims=True)


def picks_of(extra, one, two):
    extra = extra.astype(jnp.float32)
    lanes = lax.broadcasted_iota(jnp.int32, (extra.shape[0], 2 * CAP), 1)
    wanted = jnp.where(lanes < CAP, lane_value(extra, one), lane_value(extra, two))
    place = jnp.where(lanes < CAP, lanes, lanes - CAP).astype(jnp.float32)
    return jnp.where(wanted == place, 1.0, 0.0).astype(jnp.bfloat16)


def grad_side_kernel(ids, half, other, down_one, down_two, *refs):
    gs, plain = refs[-2:]
    count = half.shape[0]
    for i in range(2 * count):
        source = half if i < count else other
        pick = picks_of(source[i % count, :, D:], ids[0], ids[1])
        found = dot(pick, source[i % count, :, :D], cols_by_cols).astype(jnp.bfloat16)
        gs[0, i * CAP : (i + 1) * CAP] = found[:CAP]
        gs[1, i * CAP : (i + 1) * CAP] = found[CAP:]
    width = down_one.shape[1]
    plain[:, :width] = dot(gs[0], down_one[...], rows_by_cols)
    plain[:, width:] = dot(gs[1], down_two[...], rows_by_cols)


def combine_rows(ids, rows, slots_half, slots_other, back_half, back_other):
    count = slots_half.shape[0]
    for i in range(2 * count):
        target = back_half if i < count else back_other
        slots = slots_half if i < count else slots_other
        pick = picks_of(slots[i % count], ids[0], ids[1])
        at = slice(i * CAP, (i + 1) * CAP)
        both = jnp.concatenate([rows[0, at], rows[1, at]], 0)
        target[i % count] = dot(pick, both, rows_by_cols).astype(jnp.bfloat16)


def row_side_kernel(
    ids, half, other, slots_half, slots_other, plain, gate_one, gate_two, up_one, up_two, *refs
):
    back_half, back_other, xs, hid, pg, gates, tokens, back_rows = refs[-8:]
    total = xs.shape[1]
    count = half.shape[0]
    for i in range(2 * count):
        source = half if i < count else other
        slots = slots_half if i < count else slots_other
        pick = picks_of(slots[i % count], ids[0], ids[1])
        found = dot(pick, source[i % count], cols_by_cols)
        extra = found[:, D:]
        found = found.astype(jnp.bfloat16)
        at = slice(i * CAP, (i + 1) * CAP)
        for n in range(2):
            xs[n, at] = found[n * CAP : (n + 1) * CAP, :D]
            own = extra[n * CAP : (n + 1) * CAP]
            gates[n, at] = lane_value(own, ids[n]) + lane_value(own, ids[n] + EXPERTS)
    first = 0
    second = hid.shape[1]
    for n, gate_weight, up_weight in ((0, gate_one, up_one), (1, gate_two, up_two)):
        width = up_weight.shape[1]
        gate_part = dot(xs[n], gate_weight[...], rows_by_cols)
        up_part = dot(xs[n], up_weight[...], rows_by_cols)
        at = slice(first, first + width)
        at_up = slice(second + first, second + first + width)
        own_plain = plain[:, at]
        sigma = 1.0 / (1.0 + jnp.exp(-gate_part))
        silu_value = gate_part * sigma
        hidden = silu_value * up_part
        tokens[n] = jnp.sum(hidden * own_plain, 1, keepdims=True)
        hid[:, at] = (hidden * gates[n]).astype(jnp.bfloat16)
        hidden_grad = own_plain * gates[n]
        slope = sigma * (1.0 + gate_part * (1.0 - sigma))
        pg[:, at] = (hidden_grad * up_part * slope).astype(jnp.bfloat16)
        pg[:, at_up] = (hidden_grad * silu_value).astype(jnp.bfloat16)
        row_grad = dot(pg[:, at], gate_weight[...], rows_by_rows)
        row_grad = row_grad + dot(pg[:, at_up], up_weight[...], rows_by_rows)
        back_rows[n, :, :D] = row_grad.astype(jnp.bfloat16)
        lanes = lax.broadcasted_iota(jnp.int32, (total, 128), 1)
        back_rows[n, :, D:] = jnp.where(lanes == ids[n], tokens[n], 0.0).astype(jnp.bfloat16)
        first += width
    combine_rows(ids, back_rows, slots_half, slots_other, back_half, back_other)


def out_side_kernel(
    ids, hid, slots_half, slots_other, down_one, down_two, back_half, back_other, out_rows
):
    width = down_one.shape[1]
    out_rows[0] = dot(hid[:, :width], down_one[...], rows_by_rows).astype(jnp.bfloat16)
    out_rows[1] = dot(hid[:, width:], down_two[...], rows_by_rows).astype(jnp.bfloat16)
    combine_rows(ids, out_rows, slots_half, slots_other, back_half, back_other)


def terms_kernel(ids, xs, gs, pg, hid, terms):
    depth = terms.shape[1]
    width = hid.shape[1]
    for one, two, n, shift, first, count in (
        (gs, hid, 0, 0, 0, H),
        (xs, pg, 0, 0, H, H),
        (xs, pg, 0, width, 2 * H, H),
        (gs, hid, 1, H, 3 * H, width - H),
        (xs, pg, 1, H, 2 * H + width, width - H),
        (xs, pg, 1, width + H, H + 2 * width, width - H),
    ):
        found = dot(one[n], two[:, shift : shift + count], cols_by_cols).astype(jnp.bfloat16)
        for i in range(2):
            at = i ^ ids[2] % 2
            terms[pl.ds(at, 1), :, first : first + count] = found[i * depth : (i + 1) * depth][None]


def hop(values, pairs):
    return lax.ppermute(values, ("expert", "shard"), pairs)


def hop_pairs(step):
    return [
        (e * SHARDS + s, step(e, s)[0] * SHARDS + step(e, s)[1])
        for e in range(GROUPS)
        for s in range(SHARDS)
    ]


to_core = hop_pairs(lambda e, s: (e, s ^ 1))
to_line = [hop_pairs(lambda e, s, k=k: (e, s ^ (2 * k))) for k in range(4)]
over_middle = [
    (e * SHARDS + s, e * SHARDS + (s ^ 6)) for e in range(GROUPS) for s in range(2, 6)
]
from_middle = [
    (e * SHARDS + s, e * SHARDS + (s ^ 2)) for e in range(GROUPS) for s in range(2, 6)
]
to_middle = [(there, here) for here, there in from_middle]
to_first = hop_pairs(lambda e, s: (e ^ (1 + s % 2), s))
to_second = hop_pairs(lambda e, s: (e ^ (2 - s % 2), s))


def add_low(one, two):
    return (one.astype(jnp.float32) + two.astype(jnp.float32)).astype(jnp.bfloat16)


def total_of(line):
    return sum(piece.astype(jnp.float32) for piece in line)


class Flow:
    def __init__(self, steps):
        self.steps = steps
        self.result = None
        self.feed(None)

    def feed(self, values):
        try:
            self.want = self.steps.send(values)
        except StopIteration as stop:
            self.want = None
            self.result = stop.value


class Order:
    def __init__(self, mark):
        self.mark = mark

    def tie(self, values):
        values, self.mark = lax.optimization_barrier((values, self.mark))
        return values

    def round(self, flows, work=None):
        values, self.mark = lax.optimization_barrier(([f.want[0] for f in flows], self.mark))
        found = [hop(v, f.want[1]) for v, f in zip(values, flows)]
        found, work, self.mark = lax.optimization_barrier((found, work, self.mark))
        for flow, values in zip(flows, found):
            flow.feed(values)
        return work


def one_hop(values, pairs):
    found = yield values, pairs
    return found


def line_flows(own):
    return [Flow(one_hop(own, to_line[k])) for k in (1, 2, 3)]


def line_spread(own, marks):
    near = yield own, to_line[1]
    marks.append(near)
    two = jnp.stack([own, near])
    crossed = yield two, over_middle
    passed = yield crossed, from_middle
    at = lax.axis_index("shard") // 2
    return jnp.where((at == 1) | (at == 2), crossed, passed)


def line_collect(near, far):
    passed = yield jnp.stack(far), to_middle
    far = add_low(jnp.stack(far), passed)
    crossed = yield far, over_middle
    at = lax.axis_index("shard") // 2
    middle = (at == 1) | (at == 2)
    both = jnp.stack(near).astype(jnp.float32) + jnp.where(middle, crossed, 0).astype(jnp.float32)
    back = yield both[1].astype(jnp.bfloat16), to_line[1]
    return both[0] + back.astype(jnp.float32)


def by_distance(far):
    at = lax.axis_index("shard") // 2
    middle = (at == 1) | (at == 2)
    return [jnp.where(middle, far[1 - i], far[i]) for i in range(2)]


def spread_pair(pieces):
    two = jnp.stack(pieces) if isinstance(pieces, list) else pieces
    first = yield two, to_first
    four = jnp.concatenate([two, first])
    second = yield four, to_second
    eight = jnp.concatenate([four, second])
    other = yield eight, to_core
    return eight, other


def spread_all(line):
    four = jnp.stack(line)
    first = yield four, to_first
    eight = jnp.concatenate([four, first])
    second = yield eight, to_second
    half = jnp.concatenate([eight, second])
    other = yield half, to_core
    return half, other


def collect_pair(mine, theirs):
    found = yield theirs, to_core
    keep, give = add_low(mine[:4], found[:4]), add_low(mine[4:], found[4:])
    found = yield give, to_second
    keep, give = add_low(keep[:2], found[:2]), add_low(keep[2:], found[2:])
    found = yield give, to_first
    return [add_low(keep[i], found[i]) for i in range(2)]


def collect_all(mine, theirs):
    found = yield theirs, to_core
    keep, give = add_low(mine[:8], found[:8]), add_low(mine[8:], found[8:])
    found = yield give, to_second
    keep, give = add_low(keep[:4], found[:4]), add_low(keep[4:], found[4:])
    found = yield give, to_first
    return [add_low(keep[i], found[i]) for i in range(4)]


def share_flow(own, places):
    first = yield own, to_first
    pair = jnp.stack([own, first])
    second = yield pair, to_second
    quarters = jnp.concatenate([pair, second])
    return jnp.concatenate(
        [lax.dynamic_index_in_dim(quarters, place, 0, keepdims=False) for place in places]
    )


def local_hops(
    tokens_in,
    output_cotangent,
    routes,
    doc_ids,
    picture_starts,
    qkv_weight,
    out_weight,
    router_weight,
    attn_gain,
    moe_gain,
    gate_up_weight,
    down_weight,
):
    low = jnp.bfloat16
    full = jnp.float32
    rows = tokens_in.shape[0]
    seq_len = doc_ids.shape[1]
    q_width = HEADS * HEAD_DIM
    kv_width = KV_HEADS * HEAD_DIM
    qkv_width = q_width + 2 * kv_width
    group_at = lax.axis_index("expert")
    shard_at = lax.axis_index("shard")
    own_experts = EXPERTS // GROUPS
    whole = own_experts // SHARDS * SHARDS
    split = own_experts - whole
    share = SHARDS // split
    part = H // share
    hid_width = H + part
    depth = gate_up_weight.shape[0]
    height = SHARDS * depth
    fine = depth // GROUPS
    pad = 128 - EXPERTS
    gain_one = attn_gain.astype(full)[:, None]
    gain_two = moe_gain.astype(full)[:, None]
    expert_one = group_at * own_experts + shard_at
    expert_two = group_at * own_experts + whole + shard_at // share
    ids = jnp.stack([expert_one, expert_two, shard_at])
    order = Order(jnp.zeros((8, 128), full))

    spot = jnp.arange(GROUPS * SHARDS, dtype=jnp.int32)
    spot_core = spot // 8 % 2
    spot_mate = 1 + (shard_at % 2 ^ spot_core)
    spot_q = spot % 8 // 2
    spot_group = jnp.where(spot_q == 1, spot_mate, jnp.where(spot_q == 2, 3 - spot_mate, spot_q))
    spot_line = spot // 16 * 2 + spot % 2
    fine_at = (shard_at ^ (2 * spot_line + spot_core)) * depth + (group_at ^ spot_group) * fine
    half_core = spot // 16
    half_mate = 1 + (shard_at % 2 ^ half_core)
    half_q = spot % 16 // 4
    half_group = jnp.where(half_q == 1, half_mate, jnp.where(half_q == 2, 3 - half_mate, half_q))
    half_at = (shard_at ^ (2 * (spot % 4) + half_core)) * depth + (group_at ^ half_group) * fine

    expert_ids = jnp.arange(EXPERTS, dtype=jnp.int32)
    hits = jnp.any(routes[:, :, None] == expert_ids[None, None, :], 1)
    earlier = jnp.arange(rows)[:, None] > jnp.arange(rows)[None, :]
    before = dot(earlier.astype(low), hits.astype(low), rows_by_cols)
    slots = jnp.where(hits & (before < CAP), before, -1.0)
    kept = slots >= 0
    grad_pay = jnp.concatenate(
        [output_cotangent, jnp.pad(slots.astype(low), ((0, 0), (0, pad)))], 1
    )

    def fine_rows(array):
        return lax.dynamic_slice_in_dim(array, group_at * fine, fine, 0)

    qkv_own = fine_rows(qkv_weight).astype(full) * fine_rows(gain_one)
    router_own = fine_rows(router_weight).astype(full) * fine_rows(gain_two)
    dense_own = jnp.concatenate([qkv_own, jnp.pad(router_own, ((0, 0), (0, pad)))], 1).astype(low)
    out_own = fine_rows(out_weight)

    def column_spec(width, index):
        return pl.BlockSpec((depth, width), lambda k, ids: (0, index(ids[2] ^ k)))

    to_parts = H // part
    packs = call(
        pack_kernel,
        "pack",
        [shaped((1, depth, hid_width)), shaped((1, depth, 2 * hid_width))] * SHARDS,
        [
            column_spec(2 * H, lambda d: d),
            column_spec(part, lambda d: (whole + d // share) * 2 * to_parts + d % share),
            column_spec(part, lambda d: (whole + d // share) * 2 * to_parts + to_parts + d % share),
            column_spec(H, lambda d: d),
            column_spec(part, lambda d: (whole + d // share) * to_parts + d % share),
            pl.BlockSpec((depth, 1), lambda d, ids: (0, 0)),
        ],
        [
            out_spec((1, depth, hid_width), (0, 0, 0)),
            out_spec((1, depth, 2 * hid_width), (0, 0, 0)),
        ]
        * SHARDS,
        (ids, gate_up_weight, gate_up_weight, gate_up_weight, down_weight, down_weight, gain_two),
        steps=SHARDS,
    )

    to_shard = [hop_pairs(lambda e, s, k=k: (e, s ^ k)) for k in range(SHARDS)]
    shard_rows = (shard_at ^ jnp.arange(SHARDS, dtype=jnp.int32)) * depth

    def exchange(pieces):
        flows = [[Flow(one_hop(piece, to_shard[k])) for piece in pieces[k]] for k in range(1, SHARDS)]
        near = [flows[k - 1][n] for n in range(len(pieces[0])) for k in (2, 3)]
        far = [flows[k - 1][n] for n in range(len(pieces[0])) for k in (4, 5, 6, 7)]
        return flows, flows[0], near, far

    def exchanged(pieces, flows, n):
        parts = [pieces[0][n]] + [flow[n].result for flow in flows]
        return place_rows(shard_rows, parts, height)

    s_pieces = [packs[2 * k : 2 * k + 2] for k in range(SHARDS)]
    s_flows, core, near, far = exchange(s_pieces)

    def some(flows, count):
        taken = flows[:count]
        del flows[:count]
        return taken

    w = line_flows(dense_own)
    o = line_flows(out_own)
    g_marks, x_marks = [], []
    g_line = Flow(line_spread(grad_pay, g_marks))
    order.round(w[:2])
    w_near = Flow(spread_pair([dense_own, w[0].result]))
    order.round([w[2], w_near, g_line])
    w_far = Flow(spread_pair([w[1].result, w[2].result]))
    g_near = Flow(spread_pair([grad_pay, g_marks[0]]))
    order.round([w_near, w_far] + some(far, 1) + some(near, 1) + core)
    order.round([w_near, w_far] + o)
    o_all = Flow(spread_all([out_own] + [flow.result for flow in o]))
    order.round([w_far, o_all])
    dense_full = place_rows(fine_at, w_near.result + w_far.result, height)
    router_full = dense_full[:, qkv_width:]

    tokens_f = tokens_in.astype(full)
    inverse_one = lax.rsqrt(jnp.mean(tokens_f * tokens_f, -1, keepdims=True) + norm_eps)
    normal_one = tokens_f * inverse_one
    normed_in = normal_one.astype(low)
    query_pos = shard_at * rows + jnp.arange(rows, dtype=jnp.int32)
    cosine, sine = rope_tables(query_pos, HEAD_DIM)
    cosine = jnp.tile(cosine[:, 0], (1, 4))
    sine = jnp.tile(jnp.concatenate([-sine[:, 0], sine[:, 0]], 1), (1, 2))
    tile = 512
    queries, key_value = call(
        qkv_kernel,
        "qkv",
        (shaped((rows, q_width)), shaped((rows, 2 * kv_width))),
        [
            whole_spec((rows, D)),
            pl.BlockSpec((D, tile), lambda j, ids: (0, j)),
            whole_spec((rows, 128)),
            whole_spec((rows, 128)),
        ],
        [
            pl.BlockSpec((rows, tile), lambda j, ids: (0, jnp.minimum(j, 2))),
            pl.BlockSpec((rows, tile), lambda j, ids: (0, jnp.maximum(j - 3, 0))),
        ],
        (ids, normed_in, dense_full, cosine, sine),
        flops=2 * rows * D * qkv_width,
        steps=qkv_width // tile,
    )
    queries, key_value = order.round(
        [o_all, g_near, g_line] + some(near, 1), (queries, key_value)
    )
    kv = line_flows(key_value)
    order.round(kv + [o_all, g_near])
    kv_line = jnp.concatenate([key_value] + [flow.result for flow in kv])
    kv_core = Flow(one_hop(kv_line, to_core))
    out_full = place_rows(half_at, o_all.result, height)
    out_full = order.round([kv_core], out_full)
    kv_other = kv_core.result
    block_order = jnp.arange(SHARDS, dtype=jnp.int32)
    block_order = shard_at ^ (block_order % 4 * 2 + block_order // 4)
    key_pos = (
        block_order[:, None] * rows + jnp.arange(rows, dtype=jnp.int32)[None, :]
    ).reshape(seq_len)
    doc_blocks = doc_ids[0].reshape(SHARDS, rows)
    block_hits = block_order[:, None] == jnp.arange(SHARDS)[None, :]
    key_doc = jnp.sum(
        jnp.where(block_hits[:, :, None], doc_blocks[None], 0), 1
    ).reshape(seq_len)
    query_doc = key_doc[:rows]
    key_pic = picture_ids(key_pos, picture_starts[0], SLOT, PIECE)
    query_pic = key_pic[:rows]
    visible = allowed(query_pos, key_pos, query_doc, key_doc, query_pic, key_pic)
    bias = jnp.where(visible, 0.0, masked_score)
    pairs = KV_HEADS // 2
    q_tile = q_width // pairs
    kv_tile = kv_width // pairs
    half_len = seq_len // 2

    def kv_specs(first):
        return [pl.BlockSpec((half_len, kv_tile), lambda j, ids: (0, first + j))] * 2

    q_spec = pl.BlockSpec((rows, q_tile), lambda j, ids: (0, j))
    log_spec = pl.BlockSpec((1, rows, 128), lambda j, ids: (j, 0, 0))
    attended, logs = call(
        attend_kernel,
        "attend",
        (shaped((rows, q_width)), shaped((pairs, rows, 128), full)),
        [q_spec] + kv_specs(0) + kv_specs(pairs) + [whole_spec((rows, seq_len))],
        [q_spec, log_spec],
        (ids, queries, kv_line, kv_other, kv_line, kv_other, bias),
        flops=4 * rows * seq_len * q_width,
        steps=pairs,
    )
    branch = dot(attended, out_full, rows_by_rows)
    middle = tokens_f + branch
    inverse_two = lax.rsqrt(jnp.mean(middle * middle, -1, keepdims=True) + norm_eps)
    normal_two = middle * inverse_two
    normed_mid = normal_two.astype(low)
    logits = dot(normed_mid, router_full, rows_by_cols)[:, :EXPERTS]
    logits = jnp.where(hits, logits, masked_score)
    gates = jnp.exp(logits - jnp.max(logits, -1, keepdims=True))
    gates = jnp.where(hits, gates, 0.0)
    gates = gates / jnp.sum(gates, -1, keepdims=True)
    gate_low = gates.astype(low)
    gate_rest = (gates - gate_low.astype(full)).astype(low)
    row_pay = jnp.concatenate(
        [normed_mid, gate_low, gate_rest, jnp.zeros((rows, 128 - 2 * EXPERTS), low)], 1
    )

    slot_rows = GROUPS * SHARDS * CAP
    step_rows = slot_rows // 2
    blocks = 2 * GROUPS
    pay_spec = whole_spec((blocks, rows, D + 128))
    pay_out = out_spec((blocks, rows, D + 128), (0, 0, 0))
    slot_spec = block_spec((blocks, rows, 128), (0, 0, D // 128))
    up_specs = [
        block_spec((height, H), (0, 0)),
        block_spec((height, part), (0, 2 * to_parts)),
        block_spec((height, H), (0, 1)),
        block_spec((height, part), (0, 2 * to_parts + 1)),
    ]
    down_specs = [
        block_spec((height, H), (0, 0)),
        block_spec((height, part), (0, H // part)),
    ]
    back_shape = shaped((blocks, rows, D + 128))
    gs_shape = shaped((2, slot_rows, D))
    kept_shapes = (gs_shape, shaped((slot_rows, hid_width)), shaped((slot_rows, 2 * hid_width)))
    kept_rows = ()

    gs, plain = (), []

    def grad_side(k):
        nonlocal gs
        gs_next, found = call(
            grad_side_kernel,
            "grad_side",
            (gs_shape, shaped((step_rows, hid_width), full)),
            [pay_spec, pay_spec] + down_specs + [in_place] * len(gs),
            [
                out_spec((2, step_rows, D), (0, k, 0)),
                out_spec((step_rows, hid_width), (0, 0)),
            ],
            (ids,) + (g_near, g_far)[k].result + (owned_down, owned_down) + gs,
            aliases={5: 0} if gs else None,
            flops=2 * step_rows * D * (hid_width + 2 * rows),
        )
        gs = (gs_next,)
        return found

    def row_side(k):
        nonlocal kept_rows
        half_back, other_back, *kept_next = call(
            row_side_kernel,
            "row_side",
            (back_shape, back_shape) + kept_shapes,
            [pay_spec, pay_spec, slot_spec, slot_spec, whole_spec((step_rows, hid_width))]
            + up_specs
            + [in_place] * len(kept_rows),
            [
                pay_out,
                pay_out,
                out_spec((2, step_rows, D), (0, k, 0)),
                out_spec((step_rows, hid_width), (k, 0)),
                out_spec((step_rows, 2 * hid_width), (k, 0)),
            ],
            (ids,)
            + (x_near, x_far)[k].result
            + (g_near, g_far)[k].result
            + (plain[k],)
            + (owned_up,) * 4
            + kept_rows,
            scratch=[
                pltpu.VMEM((2, step_rows, 1), full),
                pltpu.VMEM((2, step_rows, 1), full),
                pltpu.VMEM((2, step_rows, D + 128), low),
            ],
            aliases={10: 2, 11: 3, 12: 4} if kept_rows else None,
            flops=8 * step_rows * D * (hid_width + rows),
        )
        kept_rows = tuple(kept_next)
        return half_back, other_back

    row_pay = order.round([g_near, g_line] + some(far, 3), row_pay)
    x_line = Flow(line_spread(row_pay, x_marks))
    g_far = Flow(spread_pair(g_line.result))
    order.round([x_line] + some(far, 1))
    x_near = Flow(spread_pair([row_pay, x_marks[0]]))
    owned_down = exchanged(s_pieces, s_flows, 0)
    owned_down = order.round([x_line, x_near, g_far] + some(near, 1), owned_down)
    plain = [order.round([x_line, x_near, g_far] + some(far, 1), grad_side(0))]
    x_far = Flow(spread_pair(x_line.result))
    order.round([x_near, x_far, g_far] + some(far, 1) + near)
    plain.append(order.round([x_far] + far, grad_side(1)))
    owned_up = exchanged(s_pieces, s_flows, 1)
    back_near = order.round([x_far], row_side(0))
    b_near = Flow(collect_pair(*back_near))
    back_far = order.round([b_near], row_side(1))
    b_far = Flow(collect_pair(*back_far))

    xs, hid, pg = kept_rows

    def lane_block(i, ids):
        return (0, 0, i ^ ids[2] // 2)

    terms = call(
        terms_kernel,
        "terms",
        shaped((SHARDS, depth, 3 * hid_width)),
        [
            pl.BlockSpec((2, slot_rows, 2 * depth), lane_block),
            pl.BlockSpec((2, slot_rows, 2 * depth), lane_block),
            whole_spec((slot_rows, 2 * hid_width)),
            whole_spec((slot_rows, hid_width)),
        ],
        pl.BlockSpec((2, depth, 3 * hid_width), lambda i, ids: (i, 0, 0)),
        (ids, xs, gs[0], pg, hid),
        flops=2 * slot_rows * D * 3 * hid_width,
        steps=4,
    )
    terms = order.round([b_near, b_far], terms)
    t_edge = 2 * H
    t_pieces = [[terms[k, :, :t_edge][None], terms[k, :, t_edge:][None]] for k in range(SHARDS)]
    t_flows, core, near, far = exchange(t_pieces)

    def out_side(k):
        return call(
            out_side_kernel,
            "out_side",
            (shaped((blocks, rows, D)),) * 2,
            [block_spec((step_rows, hid_width), (k, 0)), slot_spec, slot_spec] + down_specs,
            [out_spec((blocks, rows, D), (0, 0, 0))] * 2,
            (ids, hid) + (g_near, g_far)[k].result + (owned_down, owned_down),
            scratch=[pltpu.VMEM((2, step_rows, D), low)],
            flops=2 * step_rows * D * (hid_width + 2 * rows),
        )

    out_near = order.round([b_near, b_far] + some(near, 1) + some(far, 1), out_side(0))
    b_line = [Flow(one_hop(b_near.result[1], to_line[1]))]
    out_far = order.round([b_far] + b_line + core, out_side(1))
    b_line += [
        Flow(one_hop(piece, to_line[2 + i])) for i, piece in enumerate(by_distance(b_far.result))
    ]
    m_near, m_far = Flow(collect_pair(*out_near)), Flow(collect_pair(*out_far))
    order.round(b_line[1:] + [m_near, m_far])
    grad_sum = total_of([b_near.result[0]] + [flow.result for flow in b_line])

    gate_grad = jnp.where(kept, grad_sum[:, D : D + EXPERTS], 0.0)
    logit_grad = gates * (gate_grad - jnp.sum(gates * gate_grad, -1, keepdims=True))
    logit_grad = jnp.pad(logit_grad.astype(low), ((0, 0), (0, pad)))
    scaled_two = grad_sum[:, :D] + dot(logit_grad, router_full, rows_by_rows)
    grad_out = output_cotangent.astype(full)
    mean_two = jnp.mean(scaled_two * normal_two, -1, keepdims=True)
    mid_grad = grad_out + inverse_two * (scaled_two - normal_two * mean_two)
    branch_grad = mid_grad.astype(low)
    attended_grad = dot(branch_grad, out_full, rows_by_cols).astype(low)

    kv_out = pl.BlockSpec((half_len, kv_tile), lambda j, ids: (0, j))
    query_back, key_mine, key_theirs, value_mine, value_theirs = call(
        attend_back_kernel,
        "attend_back",
        (shaped((rows, q_width)),) + (shaped((half_len, kv_width)),) * 4,
        [q_spec, q_spec]
        + kv_specs(0)
        + kv_specs(pairs)
        + [whole_spec((rows, seq_len)), log_spec, whole_spec((rows, 128)), whole_spec((rows, 128))],
        [q_spec] + [kv_out] * 4,
        (ids, queries, attended_grad, kv_line, kv_other, kv_line, kv_other, bias, logs, cosine, sine),
        flops=10 * rows * seq_len * q_width,
        steps=pairs,
    )
    kv_theirs = jnp.concatenate([key_theirs, value_theirs], 1)
    kv_mine = jnp.concatenate([key_mine, value_mine], 1)
    def dense_flow(products):
        return dense_terms(half_at, products, 2, 4 * GROUPS, fine)

    kv_theirs, kv_mine = order.round(
        [m_near, m_far] + some(far, 3) + some(near, 2), (kv_theirs, kv_mine)
    )
    kv_core = Flow(one_hop(kv_theirs, to_core))
    order.round([kv_core, m_near, m_far])
    m_line = Flow(line_collect(m_near.result, m_far.result))
    kv_half = add_low(kv_mine, kv_core.result).reshape(4, rows, 2 * kv_width)
    kv = [Flow(one_hop(kv_half[k], to_line[k])) for k in (1, 2, 3)]
    early_blocks = dense_flow([(branch_grad, attended, 0), (normed_in, query_back, q_width)])
    early_blocks = order.round(kv, early_blocks)
    early = Flow(collect_all(*early_blocks))
    kv_grad = total_of([kv_half[0]] + [flow.result for flow in kv])

    def line_of(blocks):
        return [Flow(one_hop(blocks[k], to_line[k])) for k in (1, 2, 3)]

    def swapped(values):
        lanes = jnp.arange(values.shape[1]) % HEAD_DIM < HEAD_DIM // 2
        return jnp.where(
            lanes[None], jnp.roll(values, -HEAD_DIM // 2, 1), jnp.roll(values, HEAD_DIM // 2, 1)
        )

    key_grad = kv_grad[:, :kv_width]
    key_back = key_grad * jnp.tile(cosine, (1, pairs)) - swapped(key_grad) * jnp.tile(sine, (1, pairs))
    kv_rows = jnp.concatenate([key_back, kv_grad[:, kv_width:]], 1).astype(low)
    scaled_one = dot(query_back, dense_full[:, :q_width], rows_by_rows) + dot(
        kv_rows, dense_full[:, q_width:qkv_width], rows_by_rows
    )
    mean_one = jnp.mean(scaled_one * normal_one, -1, keepdims=True)
    input_grad = mid_grad + inverse_one * (scaled_one - normal_one * mean_one)
    pad_lanes = jnp.arange(128)[None, :]

    def marker(lane):
        return jnp.broadcast_to(jnp.where(pad_lanes == lane, 1.0, 0.0), (rows, 128)).astype(low)

    late_blocks = dense_flow(
        [
            (normed_in, kv_rows, 0),
            (normed_mid, logit_grad, 2 * kv_width),
            ((scaled_two * normal_two).astype(low), marker(EXPERTS), 2 * kv_width),
        ]
    )
    late_blocks = order.round([early] + some(far, 1) + some(near, 1), late_blocks)
    late = Flow(collect_all(*late_blocks))
    input_grad = order.round(
        [late, early, m_line] + some(far, 1), input_grad.astype(low)
    )
    order.round([late, early] + some(far, 1))
    early_line = line_of(early.result)
    order.round([late, m_line] + early_line[:1] + some(far, 1))
    late_line = line_of(late.result)
    spots = jnp.arange(GROUPS, dtype=jnp.int32) ^ group_at
    mate = 1 + shard_at % 2
    spots = jnp.where(spots == mate, 1, jnp.where(spots == 3 - mate, 2, spots))
    places = [spots[i] for i in range(GROUPS)]

    def shared(first, line):
        own = total_of([first] + [flow.result for flow in line]).astype(low)
        return Flow(share_flow(own, places))

    order.round(late_line + early_line[1:] + [m_line])
    late_share = shared(late.result[0], late_line)
    early_share = shared(early.result[0], early_line)
    order.round([late_share, early_share] + far)
    order.round([late_share, early_share])
    output = (middle + m_line.result).astype(low)
    early_sum = early_share.result.astype(full)
    out_sum, query_sum = early_sum[:, :q_width], early_sum[:, q_width:]
    late_sum = late_share.result.astype(full)

    t_parts = t_pieces[0] + [flow.result for flows in t_flows for flow in flows]

    def to_expert(k, ids):
        return (0, jnp.where(k < SHARDS, ids[2] ^ k, k))

    gate_up_grad, down_grad = call(
        unpack_kernel,
        "unpack",
        (shaped(gate_up_weight.shape, full), shaped(down_weight.shape, full)),
        [whole_spec((1, depth, t_edge)), whole_spec((1, depth, 3 * hid_width - t_edge))] * SHARDS
        + [whole_spec((depth, 1))],
        [pl.BlockSpec((depth, 2 * H), to_expert), pl.BlockSpec((depth, H), to_expert)],
        (ids,) + tuple(t_parts) + (gain_two,),
        steps=own_experts,
    )
    qkv_sum = jnp.concatenate([query_sum, late_sum[:, : 2 * kv_width]], 1)
    return (
        output,
        input_grad,
        qkv_sum * gain_one,
        out_sum,
        late_sum[:, 2 * kv_width : 2 * kv_width + EXPERTS] * gain_two,
        jnp.sum(qkv_sum * qkv_weight.astype(full), 1),
        late_sum[:, 2 * kv_width + EXPERTS] / gain_two[:, 0],
        gate_up_grad,
        down_grad,
    )


def solution(mesh):
    body = local
    if mesh.shape["expert"] == GROUPS and mesh.shape["shard"] == SHARDS:
        body = local_hops
    return jax.shard_map(
        body,
        mesh=mesh,
        in_specs=(
            P(("expert", "shard"), None),
            P(("expert", "shard"), None),
            P(("expert", "shard"), None),
            P("expert", None),
            P("expert", None),
            P("shard", None),
            P("shard", None),
            P("shard", None),
            P("shard"),
            P("shard"),
            P("shard", "expert"),
            P("shard", "expert"),
        ),
        out_specs=(
            P(("expert", "shard"), None),
            P(("expert", "shard"), None),
            P("shard", None),
            P("shard", None),
            P("shard", None),
            P("shard"),
            P("shard"),
            P("shard", "expert"),
            P("shard", "expert"),
        ),
        check_vma=False,
    )
```

```python
import jax
import jax.numpy as jnp
from jax import lax
from jax.experimental import pallas as pl
from jax.experimental.pallas import tpu as pltpu
from jax.sharding import PartitionSpec as P

D = 1536
HEADS = 24
KV_HEADS = 8
HEAD_DIM = 64
H = 512
EXPERTS = 40
TOP = 8
PIECE = 256
SLOT = 512
CAP = 32


norm_eps = 1e-06
rope_base = 10000.0
masked_score = -1e30


def rope_tables(positions, head_dim):
    half_dim = head_dim // 2
    frequency = rope_base ** (-2.0 * jnp.arange(half_dim, dtype=jnp.float32) / head_dim)
    angles = positions.astype(jnp.float32)[:, None] * frequency[None, :]
    return (jnp.cos(angles)[:, None, :], jnp.sin(angles)[:, None, :])


def rotate(values, cosine, sine_table):
    half_dim = values.shape[-1] // 2
    first_half = values[..., :half_dim]
    second = values[..., half_dim:]
    return jnp.concatenate(
        [first_half * cosine - second * sine_table, second * cosine + first_half * sine_table], -1
    )


def rotate_back(grad_rows, cosine, sine_table):
    half_dim = grad_rows.shape[-1] // 2
    first_half = grad_rows[..., :half_dim]
    second = grad_rows[..., half_dim:]
    return jnp.concatenate(
        [first_half * cosine + second * sine_table, second * cosine - first_half * sine_table], -1
    )


def rms_norm(values, gain):
    inverse = lax.rsqrt(jnp.mean(values * values, -1, keepdims=True) + norm_eps)
    normal = values * inverse
    return (normal * gain, normal, inverse)


def rms_back(grad_rows, gain, normal, inverse):
    scaled = grad_rows * gain
    grad_in = inverse * (scaled - normal * jnp.mean(scaled * normal, -1, keepdims=True))
    return (grad_in, jnp.sum(grad_rows * normal, 0))


def picture_ids(positions, starts, slot_len, piece_len):
    slot_index = positions // slot_len
    picked_slot = slot_index[:, None] == jnp.arange(starts.shape[0], dtype=jnp.int32)[None, :]
    piece_begin = jnp.sum(jnp.where(picked_slot, starts[None, :], 0), axis=1)
    inside = (positions >= piece_begin) & (positions < piece_begin + piece_len)
    return jnp.where(inside, slot_index, -1)


def allowed(query_pos, key_pos, query_doc, key_doc, query_pic, key_pic):
    same_doc = query_doc[:, None] == key_doc[None, :]
    earlier = key_pos[None, :] <= query_pos[:, None]
    same_pic = (query_pic[:, None] == key_pic[None, :]) & (query_pic[:, None] >= 0)
    return same_doc & (earlier | same_pic)


def local(
    tokens_in,
    output_cotangent,
    routes,
    doc_ids,
    picture_starts,
    qkv_weight,
    out_weight,
    router_weight,
    attn_gain,
    moe_gain,
    gate_up_weight,
    down_weight,
):
    qkv_full, out_full, router_full, gain_first, gain_second = (
        lax.all_gather(qkv_weight, "shard", axis=0, tiled=True),
        lax.all_gather(out_weight, "shard", axis=0, tiled=True),
        lax.all_gather(router_weight, "shard", axis=0, tiled=True),
        lax.all_gather(attn_gain, "shard", axis=0, tiled=True),
        lax.all_gather(moe_gain, "shard", axis=0, tiled=True),
    )
    gain_one = gain_first.astype(jnp.float32)
    gain_two = gain_second.astype(jnp.float32)
    tok_rows = tokens_in.shape[0]
    seq_len = doc_ids.shape[1]
    groups = HEADS // KV_HEADS
    q_width = HEADS * HEAD_DIM
    kv_width = KV_HEADS * HEAD_DIM
    score_scale = HEAD_DIM ** (-0.5)
    shard_at = lax.axis_index("shard")
    query_pos = shard_at * tok_rows + jnp.arange(tok_rows, dtype=jnp.int32)
    key_pos = jnp.arange(seq_len, dtype=jnp.int32)
    key_doc = doc_ids[0]
    key_pic = picture_ids(key_pos, picture_starts[0], SLOT, PIECE)
    query_doc = lax.dynamic_slice_in_dim(key_doc, shard_at * tok_rows, tok_rows)
    query_pic = lax.dynamic_slice_in_dim(key_pic, shard_at * tok_rows, tok_rows)
    tokens_f = tokens_in.astype(jnp.float32)
    normed_one, normal_one, inverse_one = rms_norm(tokens_f, gain_one)
    normed_in = normed_one.astype(jnp.bfloat16)
    qkv_rows = jnp.dot(normed_in, qkv_full, preferred_element_type=jnp.float32)
    cosine, sine_table = rope_tables(query_pos, HEAD_DIM)
    queries = (
        rotate(qkv_rows[:, :q_width].reshape(tok_rows, HEADS, HEAD_DIM), cosine, sine_table)
        .astype(jnp.bfloat16)
        .reshape(tok_rows, KV_HEADS, groups, HEAD_DIM)
    )
    key_local = (
        rotate(
            qkv_rows[:, q_width : q_width + kv_width].reshape(tok_rows, KV_HEADS, HEAD_DIM),
            cosine,
            sine_table,
        )
        .astype(jnp.bfloat16)
        .reshape(tok_rows, kv_width)
    )
    value_local = qkv_rows[:, q_width + kv_width :].astype(jnp.bfloat16)
    all_keys, all_values = (
        lax.all_gather(key_local, "shard", axis=0, tiled=True),
        lax.all_gather(value_local, "shard", axis=0, tiled=True),
    )
    span_len = min(512, seq_len)
    span_count = seq_len // span_len

    def block_scores(first_row, key_rows):
        key_block = lax.dynamic_slice_in_dim(key_rows, first_row, span_len, 0).reshape(
            span_len, KV_HEADS, HEAD_DIM
        )
        raw_scores = (
            jnp.einsum("tgrd,kgd->tgrk", queries, key_block, preferred_element_type=jnp.float32)
            * score_scale
        )
        block_pos = lax.dynamic_slice_in_dim(key_pos, first_row, span_len)
        block_doc = lax.dynamic_slice_in_dim(key_doc, first_row, span_len)
        block_pic = lax.dynamic_slice_in_dim(key_pic, first_row, span_len)
        visible = allowed(query_pos, block_pos, query_doc, block_doc, query_pic, block_pic)[
            :, None, None, :
        ]
        return (raw_scores, visible, key_block)

    def value_block_at(first_row, value_rows):
        return lax.dynamic_slice_in_dim(value_rows, first_row, span_len, 0).reshape(
            span_len, KV_HEADS, HEAD_DIM
        )

    def max_step(step_index, carry):
        run_max, run_sum = carry
        raw_scores, visible, key_block = block_scores(step_index * span_len, all_keys)
        masked = jnp.where(visible, raw_scores, masked_score)
        new_max = jnp.maximum(run_max, jnp.max(masked, -1))
        shifted = jnp.where(visible, jnp.exp(masked - new_max[..., None]), 0.0)
        return (new_max, run_sum * jnp.exp(run_max - new_max) + jnp.sum(shifted, -1))

    stat_shape = (tok_rows, KV_HEADS, groups)
    run_max, run_sum = lax.fori_loop(
        0,
        span_count,
        max_step,
        (jnp.full(stat_shape, masked_score, jnp.float32), jnp.zeros(stat_shape, jnp.float32)),
    )
    log_total = run_max + jnp.log(run_sum)

    def probs_of(raw_scores, visible):
        return jnp.exp(jnp.where(visible, raw_scores - log_total[..., None], masked_score))

    def value_step(step_index, summed):
        first_row = step_index * span_len
        raw_scores, visible, key_block = block_scores(first_row, all_keys)
        probs = probs_of(raw_scores, visible).astype(jnp.bfloat16)
        return summed + jnp.einsum(
            "tgrk,kgd->tgrd",
            probs,
            value_block_at(first_row, all_values),
            preferred_element_type=jnp.float32,
        )

    summed = lax.fori_loop(
        0, span_count, value_step, jnp.zeros((tok_rows, KV_HEADS, groups, HEAD_DIM), jnp.float32)
    )
    attended = summed.reshape(tok_rows, q_width).astype(jnp.bfloat16)
    branch = lax.dot_general(
        attended, out_full, (((1,), (1,)), ((), ())), preferred_element_type=jnp.float32
    )
    middle = tokens_f + branch
    normed_two, normal_two, inverse_two = rms_norm(middle, gain_two)
    normed_mid = normed_two.astype(jnp.bfloat16)
    logits = jnp.dot(normed_mid, router_full, preferred_element_type=jnp.float32)
    gates = jax.nn.softmax(jnp.take_along_axis(logits, routes, 1), axis=-1)
    route_hits = routes[:, :, None] == jnp.arange(EXPERTS, dtype=jnp.int32)[None, None, :]
    hit_count = jnp.sum(route_hits.astype(jnp.int32), 1)
    before = jnp.cumsum(hit_count, 0) - hit_count
    slot_index = jnp.take_along_axis(before, routes, 1)
    kept_pair = slot_index < CAP
    flat_slot = routes * CAP + slot_index
    capacity_rows = EXPERTS * CAP
    target = jnp.where(kept_pair, flat_slot, capacity_rows)
    token_ids = jnp.broadcast_to(jnp.arange(tok_rows, dtype=jnp.int32)[:, None], (tok_rows, TOP))
    owner_row = (
        jnp.full((capacity_rows + 1,), -1, jnp.int32)
        .at[target.reshape(-1)]
        .set(token_ids.reshape(-1))[:capacity_rows]
    )
    filled = owner_row >= 0
    source_row = jnp.maximum(owner_row, 0)
    expert_groups = lax.axis_size("expert")
    local_experts = EXPERTS // expert_groups
    send_rows = jnp.where(
        filled[:, None], normed_mid[source_row], jnp.zeros((), jnp.bfloat16)
    ).reshape(expert_groups, local_experts, CAP, D)
    received = lax.all_to_all(send_rows, "expert", split_axis=0, concat_axis=0, tiled=True)
    gate_up_full, down_full = (
        lax.all_gather(gate_up_weight, "shard", axis=0, tiled=True),
        lax.all_gather(down_weight, "shard", axis=0, tiled=True),
    )
    gate_up3 = gate_up_full.reshape(D, local_experts, 2 * H)
    down3 = down_full.reshape(D, local_experts, H)
    projected = jnp.einsum("secd,dej->secj", received, gate_up3, preferred_element_type=jnp.float32)
    gate_part = projected[..., :H]
    up_part = projected[..., H:]
    sigma = jax.nn.sigmoid(gate_part)
    silu_value = gate_part * sigma
    hidden = (silu_value * up_part).astype(jnp.bfloat16)
    expert_out = jnp.einsum(
        "secj,dej->secd", hidden, down3, preferred_element_type=jnp.float32
    ).astype(jnp.bfloat16)
    returned = lax.all_to_all(
        expert_out, "expert", split_axis=0, concat_axis=0, tiled=True
    ).reshape(capacity_rows, D)
    safe_flat = jnp.where(kept_pair, flat_slot, 0)
    picked = returned[safe_flat].astype(jnp.float32)
    pair_weight = jnp.where(kept_pair, gates, 0.0)
    moe_sum = jnp.einsum("tk,tkd->td", pair_weight, picked)
    output = (middle + moe_sum).astype(jnp.bfloat16)
    grad_out = output_cotangent.astype(jnp.float32)
    gate_grad = jnp.where(kept_pair, jnp.einsum("td,tkd->tk", grad_out, picked), 0.0)
    slot_gate = (
        jnp.zeros((capacity_rows + 1,), jnp.float32)
        .at[target.reshape(-1)]
        .set(gates.reshape(-1))[:capacity_rows]
    )
    grad_send = (
        jnp.where(filled[:, None], slot_gate[:, None] * grad_out[source_row], 0.0)
        .astype(jnp.bfloat16)
        .reshape(expert_groups, local_experts, CAP, D)
    )
    grad_received = lax.all_to_all(grad_send, "expert", split_axis=0, concat_axis=0, tiled=True)
    keys_back, values_back = (
        lax.all_gather(key_local, "shard", axis=0, tiled=True),
        lax.all_gather(value_local, "shard", axis=0, tiled=True),
    )
    again_up, again_down = (
        lax.all_gather(gate_up_weight, "shard", axis=0, tiled=True),
        lax.all_gather(down_weight, "shard", axis=0, tiled=True),
    )
    gate_up_back = again_up.reshape(D, local_experts, 2 * H)
    down_back = again_down.reshape(D, local_experts, H)
    hidden_grad = jnp.einsum(
        "secd,dej->secj", grad_received, down_back, preferred_element_type=jnp.float32
    )
    silu_slope = sigma * (1.0 + gate_part * (1.0 - sigma))
    proj_grad = jnp.concatenate(
        [hidden_grad * up_part * silu_slope, hidden_grad * silu_value], -1
    ).astype(jnp.bfloat16)
    row_grad = jnp.einsum(
        "secj,dej->secd", proj_grad, gate_up_back, preferred_element_type=jnp.float32
    ).astype(jnp.bfloat16)
    grad_back = lax.all_to_all(row_grad, "expert", split_axis=0, concat_axis=0, tiled=True).reshape(
        capacity_rows, D
    )
    row_count = gate_up_weight.shape[0] * lax.axis_size("shard")
    up_terms = jnp.einsum(
        "secd,secj->dej", received, proj_grad, preferred_element_type=jnp.float32
    ).reshape(row_count, local_experts * 2 * H)
    down_terms = jnp.einsum(
        "secd,secj->dej", grad_received, hidden, preferred_element_type=jnp.float32
    ).reshape(row_count, local_experts * H)
    expert_sums = lax.psum_scatter(
        jnp.concatenate([up_terms, down_terms], 1).astype(jnp.bfloat16),
        "shard",
        scatter_dimension=0,
        tiled=True,
    ).astype(jnp.float32)
    gate_up_grad = expert_sums[:, : local_experts * 2 * H]
    down_grad = expert_sums[:, local_experts * 2 * H :]
    mid_norm_grad = jnp.einsum(
        "tk,tkd->td", kept_pair.astype(jnp.float32), grad_back[safe_flat].astype(jnp.float32)
    )
    chosen_grad = gates * (gate_grad - jnp.sum(gates * gate_grad, -1, keepdims=True))
    logit_grad = jnp.sum(jnp.where(route_hits, chosen_grad[:, :, None], 0.0), 1).astype(
        jnp.bfloat16
    )
    mid_norm_grad = mid_norm_grad + lax.dot_general(
        logit_grad, router_full, (((1,), (1,)), ((), ())), preferred_element_type=jnp.float32
    )
    router_grad = lax.dot_general(
        normed_mid, logit_grad, (((0,), (0,)), ((), ())), preferred_element_type=jnp.float32
    )
    mid_part, moe_gain_grad = rms_back(mid_norm_grad, gain_two, normal_two, inverse_two)
    mid_grad = grad_out + mid_part
    branch_grad = mid_grad.astype(jnp.bfloat16)
    out_weight_grad = lax.dot_general(
        branch_grad, attended, (((0,), (0,)), ((), ())), preferred_element_type=jnp.float32
    )
    attended_grad = (
        jnp.dot(branch_grad, out_full, preferred_element_type=jnp.float32)
        .astype(jnp.bfloat16)
        .reshape(tok_rows, KV_HEADS, groups, HEAD_DIM)
    )

    def dot_step(step_index, row_dot):
        first_row = step_index * span_len
        raw_scores, visible, key_block = block_scores(first_row, keys_back)
        prob_full = probs_of(raw_scores, visible)
        prob_grad = jnp.einsum(
            "tgrd,kgd->tgrk",
            attended_grad,
            value_block_at(first_row, values_back),
            preferred_element_type=jnp.float32,
        )
        return row_dot + jnp.sum(prob_full * prob_grad, -1)

    row_dot = lax.fori_loop(0, span_count, dot_step, jnp.zeros(stat_shape, jnp.float32))

    def grad_step(step_index, carry):
        query_grad, key_terms, value_terms = carry
        first_row = step_index * span_len
        raw_scores, visible, key_block = block_scores(first_row, keys_back)
        prob_full = probs_of(raw_scores, visible)
        prob_grad = jnp.einsum(
            "tgrd,kgd->tgrk",
            attended_grad,
            value_block_at(first_row, values_back),
            preferred_element_type=jnp.float32,
        )
        score_grad = (prob_full * (prob_grad - row_dot[..., None])).astype(jnp.bfloat16)
        query_grad = query_grad + jnp.einsum(
            "tgrk,kgd->tgrd", score_grad, key_block, preferred_element_type=jnp.float32
        )
        key_part = (
            jnp.einsum(
                "tgrk,tgrd->kgd", score_grad, queries, preferred_element_type=jnp.float32
            ).reshape(span_len, kv_width)
            * score_scale
        )
        value_part = jnp.einsum(
            "tgrk,tgrd->kgd",
            prob_full.astype(jnp.bfloat16),
            attended_grad,
            preferred_element_type=jnp.float32,
        ).reshape(span_len, kv_width)
        key_terms = lax.dynamic_update_slice_in_dim(key_terms, key_part, first_row, 0)
        value_terms = lax.dynamic_update_slice_in_dim(value_terms, value_part, first_row, 0)
        return (query_grad, key_terms, value_terms)

    query_grad, key_terms, value_terms = lax.fori_loop(
        0,
        span_count,
        grad_step,
        (
            jnp.zeros((tok_rows, KV_HEADS, groups, HEAD_DIM), jnp.float32),
            jnp.zeros((seq_len, kv_width), jnp.float32),
            jnp.zeros((seq_len, kv_width), jnp.float32),
        ),
    )
    key_grad, value_grad = (
        lax.psum_scatter(
            key_terms.astype(jnp.bfloat16), "shard", scatter_dimension=0, tiled=True
        ).astype(jnp.float32),
        lax.psum_scatter(
            value_terms.astype(jnp.bfloat16), "shard", scatter_dimension=0, tiled=True
        ).astype(jnp.float32),
    )
    query_back = rotate_back(
        (query_grad * score_scale).reshape(tok_rows, HEADS, HEAD_DIM), cosine, sine_table
    ).reshape(tok_rows, q_width)
    key_back = rotate_back(
        key_grad.reshape(tok_rows, KV_HEADS, HEAD_DIM), cosine, sine_table
    ).reshape(tok_rows, kv_width)
    qkv_grad_rows = jnp.concatenate([query_back, key_back, value_grad], 1).astype(jnp.bfloat16)
    qkv_weight_grad = lax.dot_general(
        normed_in, qkv_grad_rows, (((0,), (0,)), ((), ())), preferred_element_type=jnp.float32
    )
    in_norm_grad = lax.dot_general(
        qkv_grad_rows, qkv_full, (((1,), (1,)), ((), ())), preferred_element_type=jnp.float32
    )
    in_part, attn_gain_grad = rms_back(in_norm_grad, gain_one, normal_one, inverse_one)
    input_grad = (mid_grad + in_part).astype(jnp.bfloat16)
    dense_sums = (
        lax.psum_scatter(
            qkv_weight_grad.astype(jnp.bfloat16), "shard", scatter_dimension=0, tiled=True
        ).astype(jnp.float32),
        lax.psum_scatter(
            out_weight_grad.astype(jnp.bfloat16), "shard", scatter_dimension=0, tiled=True
        ).astype(jnp.float32),
        lax.psum_scatter(
            router_grad.astype(jnp.bfloat16), "shard", scatter_dimension=0, tiled=True
        ).astype(jnp.float32),
        lax.psum_scatter(
            attn_gain_grad.astype(jnp.bfloat16), "shard", scatter_dimension=0, tiled=True
        ).astype(jnp.float32),
        lax.psum_scatter(
            moe_gain_grad.astype(jnp.bfloat16), "shard", scatter_dimension=0, tiled=True
        ).astype(jnp.float32),
    )
    dense_totals = (
        lax.psum(dense_sums[0].astype(jnp.bfloat16), "expert").astype(jnp.float32),
        lax.psum(dense_sums[1].astype(jnp.bfloat16), "expert").astype(jnp.float32),
        lax.psum(dense_sums[2].astype(jnp.bfloat16), "expert").astype(jnp.float32),
        lax.psum(dense_sums[3].astype(jnp.bfloat16), "expert").astype(jnp.float32),
        lax.psum(dense_sums[4].astype(jnp.bfloat16), "expert").astype(jnp.float32),
    )
    return (
        output,
        input_grad,
        dense_totals[0],
        dense_totals[1],
        dense_totals[2],
        dense_totals[3],
        dense_totals[4],
        gate_up_grad,
        down_grad,
    )


GROUPS = 4
SHARDS = 8
rows_by_cols = ((1,), (0,))
rows_by_rows = ((1,), (1,))
cols_by_cols = ((0,), (0,))


def dot(one, two, dims):
    return lax.dot_general(one, two, (dims, ((), ())), preferred_element_type=jnp.float32)


def whole_spec(shape):
    return pl.BlockSpec(shape, lambda i, ids: (0,) * len(shape), pipeline_mode=pl.Buffered(1))


def block_spec(shape, index):
    return pl.BlockSpec(shape, lambda i, ids: index, pipeline_mode=pl.Buffered(1))


def out_spec(shape, index):
    return pl.BlockSpec(shape, lambda i, ids: index)


in_place = pl.BlockSpec(memory_space=pl.ANY)


def shaped(shape, dtype=jnp.bfloat16):
    return jax.ShapeDtypeStruct(shape, dtype)


def call(kernel, name, out_shape, in_specs, out_specs, args, scratch=(), aliases=None, flops=0, steps=1):
    moved = sum(a.size * a.dtype.itemsize for a in args[1:])
    return pl.pallas_call(
        kernel,
        name=name,
        out_shape=out_shape,
        grid_spec=pltpu.PrefetchScalarGridSpec(
            num_scalar_prefetch=1,
            grid=(steps,),
            in_specs=in_specs,
            out_specs=out_specs,
            scratch_shapes=list(scratch),
        ),
        input_output_aliases=aliases or {},
        compiler_params=pltpu.CompilerParams(
            vmem_limit_bytes=58 * 1024 * 1024, dimension_semantics=("arbitrary",)
        ),
        cost_estimate=pl.CostEstimate(flops=flops, transcendentals=0, bytes_accessed=moved),
    )(*args)


def place_rows(offsets, parts, height):
    count, fine, width = parts[0].shape

    def kernel(at, *refs):
        sources, target, done = refs[: len(parts)], refs[len(parts)], refs[-1]
        copies = []
        for n, source in enumerate(sources):
            for i in range(count):
                row = pl.multiple_of(at[n * count + i], 16)
                copies.append(
                    pltpu.make_async_copy(
                        source.at[i], target.at[pl.ds(row, fine)], done.at[n * count + i]
                    )
                )
        for copy in copies:
            copy.start()
        for copy in copies:
            copy.wait()

    return call(
        kernel,
        "place_rows",
        shaped((height, width), parts[0].dtype),
        [in_place] * len(parts),
        out_spec((height, width), (0, 0)),
        (offsets,) + tuple(parts),
        scratch=[pltpu.SemaphoreType.DMA((len(parts) * count,))],
    )


def dense_terms(offsets, products, parts, count, fine):
    height = products[0][0].shape[1]
    width = max(first + two.shape[1] for _, two, first in products)
    firsts = [first for _, _, first in products]

    def kernel(at, *refs):
        sources, targets, held = refs[: 2 * len(firsts)], refs[2 * len(firsts) : -1], refs[-1]
        total = {}
        for n, first in enumerate(firsts):
            found = dot(sources[2 * n][...], sources[2 * n + 1][...], cols_by_cols)
            total[first] = total[first] + found if first in total else found
        for first, found in total.items():
            held[:, first : first + found.shape[1]] = found.astype(jnp.bfloat16)
        for n, target in enumerate(targets):
            for i in range(count):
                row = pl.multiple_of(at[n * count + i], 16)
                target[i] = held[pl.ds(row, fine)]

    operands = [array for one, two, _ in products for array in (one, two)]
    return call(
        kernel,
        "dense_terms",
        [shaped((count, fine, width))] * parts,
        [whole_spec(array.shape) for array in operands],
        [out_spec((count, fine, width), (0, 0, 0))] * parts,
        (offsets,) + tuple(operands),
        scratch=[pltpu.VMEM((height, width), jnp.bfloat16)],
        flops=2 * height * width * products[0][0].shape[0],
    )


def pack_kernel(ids, up, gate_part, up_part, down, down_part, gain, *packs):
    width = down.shape[1]
    scale = gain[...]
    step = pl.program_id(0)

    def scaled(rows):
        return (rows.astype(jnp.float32) * scale).astype(jnp.bfloat16)

    for k in range(SHARDS):

        @pl.when(step == k)
        def _(k=k):
            downs, ups = packs[2 * k : 2 * k + 2]
            downs[0, :, :width] = down[...]
            downs[0, :, width:] = down_part[...]
            ups[0, :, : 2 * width] = scaled(up[...])
            part = down_part.shape[1]
            ups[0, :, 2 * width : 2 * width + part] = scaled(gate_part[...])
            ups[0, :, 2 * width + part :] = scaled(up_part[...])


def unpack_kernel(ids, *refs):
    pieces, gain, up_grad, down_grad = refs[: SHARDS + 2], refs[-3], refs[-2], refs[-1]
    scale = gain[...]
    step = pl.program_id(0)
    share = SHARDS // (pl.num_programs(0) - SHARDS)
    part = pieces[0].shape[2] // 3 - H
    edge = pieces[6].shape[2]

    def columns(k, first, count):
        if k < 6:
            found = pieces[k][0, :, first : first + count]
        elif first < edge:
            found = pieces[2 * k - 6][0, :, first : first + count]
        else:
            found = pieces[2 * k - 5][0, :, first - edge : first - edge + count]
        return found.astype(jnp.float32)

    for k in range(SHARDS):
        source = ids[2] ^ k

        @pl.when(step == k)
        def _(k=k):
            down_grad[...] = columns(k, 0, H)
            up_grad[:, :H] = columns(k, H, H) * scale
            up_grad[:, H:] = columns(k, 2 * H, H) * scale

        @pl.when(step == SHARDS + source // share)
        def _(k=k, source=source):
            at = pl.multiple_of(source % share * part, part)
            at_up = pl.multiple_of(H + source % share * part, part)
            down_grad[:, pl.ds(at, part)] = columns(k, 3 * H, part)
            up_grad[:, pl.ds(at, part)] = columns(k, 3 * H + part, part) * scale
            up_grad[:, pl.ds(at_up, part)] = columns(k, 3 * H + 2 * part, part) * scale


def turn(rows, cosine, sine):
    width = rows.shape[1]
    lanes = lax.broadcasted_iota(jnp.int32, (rows.shape[0], 128), 1)
    first = lanes % HEAD_DIM < HEAD_DIM // 2
    turned = []
    for at in range(0, width, 128):
        piece = rows[:, at : at + 128]
        swapped = jnp.where(
            first,
            pltpu.roll(piece, 128 - HEAD_DIM // 2, 1),
            pltpu.roll(piece, HEAD_DIM // 2, 1),
        )
        turned.append(piece * cosine + swapped * sine)
    return jnp.concatenate(turned, 1)


def qkv_kernel(ids, normed, weight, cosine, sine, queries, key_value):
    step = pl.program_id(0)
    found = dot(normed[...], weight[...], rows_by_cols)

    @pl.when(step < 3)
    def _():
        queries[...] = turn(found, cosine[...], sine[...]).astype(jnp.bfloat16)

    @pl.when(step == 3)
    def _():
        key_value[...] = turn(found, cosine[...], sine[...]).astype(jnp.bfloat16)

    @pl.when(step == 4)
    def _():
        key_value[...] = found.astype(jnp.bfloat16)


def attend_kernel(ids, queries, key_line, key_other, value_line, value_other, bias, attended, logs):
    scale = HEAD_DIM ** (-0.5)
    groups = HEADS // KV_HEADS
    hidden = bias[...]
    keys = jnp.concatenate([key_line[...], key_other[...]], 0)
    values = jnp.concatenate([value_line[...], value_other[...]], 0)
    lanes = lax.broadcasted_iota(jnp.int32, (queries.shape[0], 128), 1)
    totals = jnp.zeros((queries.shape[0], 128), jnp.float32)
    found = []
    for n in range(2 * groups):
        at = n // groups * HEAD_DIM
        scores = dot(
            queries[:, n * HEAD_DIM : (n + 1) * HEAD_DIM], keys[:, at : at + HEAD_DIM], rows_by_rows
        )
        scores = scores * scale + hidden
        top = jnp.max(scores, 1, keepdims=True)
        raised = jnp.exp(scores - top)
        total = jnp.sum(raised, 1, keepdims=True)
        probs = (raised / total).astype(jnp.bfloat16)
        found.append(dot(probs, values[:, at : at + HEAD_DIM], rows_by_cols))
        totals = jnp.where(lanes == n, top + jnp.log(total), totals)
    attended[...] = jnp.concatenate(found, 1).astype(jnp.bfloat16)
    logs[0] = totals


def attend_back_kernel(
    ids, queries, grads, key_line, key_other, value_line, value_other, bias, logs, cosine, sine,
    query_grad, key_mine, key_theirs, value_mine, value_theirs,
):
    scale = HEAD_DIM ** (-0.5)
    groups = HEADS // KV_HEADS
    hidden = bias[...]
    keys = jnp.concatenate([key_line[...], key_other[...]], 0)
    values = jnp.concatenate([value_line[...], value_other[...]], 0)
    half = key_line.shape[0]
    found = []
    key_found, value_found = [], []
    for n in range(2 * groups):
        own = n // groups
        at = own * HEAD_DIM
        head = slice(n * HEAD_DIM, (n + 1) * HEAD_DIM)
        query = queries[:, head]
        grad = grads[:, head]
        scores = dot(query, keys[:, at : at + HEAD_DIM], rows_by_rows) * scale + hidden
        probs = jnp.exp(scores - lane_value(logs[0], n))
        prob_grad = dot(grad, values[:, at : at + HEAD_DIM], rows_by_rows)
        row_dot = jnp.sum(probs * prob_grad, 1, keepdims=True)
        score_grad = (probs * (prob_grad - row_dot)).astype(jnp.bfloat16)
        found.append(dot(score_grad, keys[:, at : at + HEAD_DIM], rows_by_cols))
        key_part = dot(score_grad, query, cols_by_cols)
        value_part = dot(probs.astype(jnp.bfloat16), grad, cols_by_cols)
        if n % groups:
            key_found[own] = key_found[own] + key_part
            value_found[own] = value_found[own] + value_part
        else:
            key_found.append(key_part)
            value_found.append(value_part)
    found = jnp.concatenate(found, 1) * scale
    query_grad[...] = turn(found, cosine[...], -sine[...]).astype(jnp.bfloat16)
    key_found = (jnp.concatenate(key_found, 1) * scale).astype(jnp.bfloat16)
    value_found = jnp.concatenate(value_found, 1).astype(jnp.bfloat16)
    key_mine[...] = key_found[:half]
    key_theirs[...] = key_found[half:]
    value_mine[...] = value_found[:half]
    value_theirs[...] = value_found[half:]


def lane_value(rows, index):
    lanes = lax.broadcasted_iota(jnp.int32, rows.shape, 1)
    return jnp.sum(jnp.where(lanes == index, rows, 0.0), 1, keepdims=True)


def picks_of(extra, one, two):
    extra = extra.astype(jnp.float32)
    lanes = lax.broadcasted_iota(jnp.int32, (extra.shape[0], 2 * CAP), 1)
    wanted = jnp.where(lanes < CAP, lane_value(extra, one), lane_value(extra, two))
    place = jnp.where(lanes < CAP, lanes, lanes - CAP).astype(jnp.float32)
    return jnp.where(wanted == place, 1.0, 0.0).astype(jnp.bfloat16)


def grad_side_kernel(ids, half, other, down_one, down_two, *refs):
    gs, plain = refs[-2:]
    count = half.shape[0]
    for i in range(2 * count):
        source = half if i < count else other
        pick = picks_of(source[i % count, :, D:], ids[0], ids[1])
        found = dot(pick, source[i % count, :, :D], cols_by_cols).astype(jnp.bfloat16)
        gs[0, i * CAP : (i + 1) * CAP] = found[:CAP]
        gs[1, i * CAP : (i + 1) * CAP] = found[CAP:]
    width = down_one.shape[1]
    plain[:, :width] = dot(gs[0], down_one[...], rows_by_cols)
    plain[:, width:] = dot(gs[1], down_two[...], rows_by_cols)


def combine_rows(ids, rows, slots_half, slots_other, back_half, back_other):
    count = slots_half.shape[0]
    for i in range(2 * count):
        target = back_half if i < count else back_other
        slots = slots_half if i < count else slots_other
        pick = picks_of(slots[i % count], ids[0], ids[1])
        at = slice(i * CAP, (i + 1) * CAP)
        both = jnp.concatenate([rows[0, at], rows[1, at]], 0)
        target[i % count] = dot(pick, both, rows_by_cols).astype(jnp.bfloat16)


def row_side_kernel(
    ids, half, other, slots_half, slots_other, plain, gate_one, gate_two, up_one, up_two, *refs
):
    back_half, back_other, xs, hid, pg, gates, tokens, back_rows = refs[-8:]
    total = xs.shape[1]
    count = half.shape[0]
    for i in range(2 * count):
        source = half if i < count else other
        slots = slots_half if i < count else slots_other
        pick = picks_of(slots[i % count], ids[0], ids[1])
        found = dot(pick, source[i % count], cols_by_cols)
        extra = found[:, D:]
        found = found.astype(jnp.bfloat16)
        at = slice(i * CAP, (i + 1) * CAP)
        for n in range(2):
            xs[n, at] = found[n * CAP : (n + 1) * CAP, :D]
            own = extra[n * CAP : (n + 1) * CAP]
            gates[n, at] = lane_value(own, ids[n]) + lane_value(own, ids[n] + EXPERTS)
    first = 0
    second = hid.shape[1]
    for n, gate_weight, up_weight in ((0, gate_one, up_one), (1, gate_two, up_two)):
        width = up_weight.shape[1]
        gate_part = dot(xs[n], gate_weight[...], rows_by_cols)
        up_part = dot(xs[n], up_weight[...], rows_by_cols)
        at = slice(first, first + width)
        at_up = slice(second + first, second + first + width)
        own_plain = plain[:, at]
        sigma = 1.0 / (1.0 + jnp.exp(-gate_part))
        silu_value = gate_part * sigma
        hidden = silu_value * up_part
        tokens[n] = jnp.sum(hidden * own_plain, 1, keepdims=True)
        hid[:, at] = (hidden * gates[n]).astype(jnp.bfloat16)
        hidden_grad = own_plain * gates[n]
        slope = sigma * (1.0 + gate_part * (1.0 - sigma))
        pg[:, at] = (hidden_grad * up_part * slope).astype(jnp.bfloat16)
        pg[:, at_up] = (hidden_grad * silu_value).astype(jnp.bfloat16)
        row_grad = dot(pg[:, at], gate_weight[...], rows_by_rows)
        row_grad = row_grad + dot(pg[:, at_up], up_weight[...], rows_by_rows)
        back_rows[n, :, :D] = row_grad.astype(jnp.bfloat16)
        lanes = lax.broadcasted_iota(jnp.int32, (total, 128), 1)
        back_rows[n, :, D:] = jnp.where(lanes == ids[n], tokens[n], 0.0).astype(jnp.bfloat16)
        first += width
    combine_rows(ids, back_rows, slots_half, slots_other, back_half, back_other)


def out_side_kernel(ids, hid, *refs):
    slots, (down_one, down_two), (mine, theirs, out_rows) = refs[:4], refs[4:6], refs[6:]
    width = down_one.shape[1]
    count = slots[0].shape[0]
    out_rows[0] = dot(hid[:, :width], down_one[...], rows_by_rows).astype(jnp.bfloat16)
    out_rows[1] = dot(hid[:, width:], down_two[...], rows_by_rows).astype(jnp.bfloat16)
    for n, own in enumerate(slots):
        target = theirs if n % 2 else mine
        for i in range(count):
            pick = picks_of(own[i], ids[0], ids[1])
            at = slice((n * count + i) * CAP, (n * count + i + 1) * CAP)
            both = jnp.concatenate([out_rows[0, at], out_rows[1, at]], 0)
            place = i // 2 * 4 + n // 2 * 2 + i % 2
            target[place] = dot(pick, both, rows_by_cols).astype(jnp.bfloat16)


def terms_kernel(ids, xs, gs, pg, hid, terms):
    depth = terms.shape[1]
    width = hid.shape[1]
    for one, two, n, shift, first, count in (
        (gs, hid, 0, 0, 0, H),
        (xs, pg, 0, 0, H, H),
        (xs, pg, 0, width, 2 * H, H),
        (gs, hid, 1, H, 3 * H, width - H),
        (xs, pg, 1, H, 2 * H + width, width - H),
        (xs, pg, 1, width + H, H + 2 * width, width - H),
    ):
        found = dot(one[n], two[:, shift : shift + count], cols_by_cols).astype(jnp.bfloat16)
        for i in range(2):
            at = i ^ ids[2] % 2
            terms[pl.ds(at, 1), :, first : first + count] = found[i * depth : (i + 1) * depth][None]


def hop(values, pairs):
    return lax.ppermute(values, ("expert", "shard"), pairs)


def hop_pairs(step):
    return [
        (e * SHARDS + s, step(e, s)[0] * SHARDS + step(e, s)[1])
        for e in range(GROUPS)
        for s in range(SHARDS)
    ]


to_core = hop_pairs(lambda e, s: (e, s ^ 1))
to_line = [hop_pairs(lambda e, s, k=k: (e, s ^ (2 * k))) for k in range(4)]
over_middle = [
    (e * SHARDS + s, e * SHARDS + (s ^ 6)) for e in range(GROUPS) for s in range(2, 6)
]
from_middle = [
    (e * SHARDS + s, e * SHARDS + (s ^ 2)) for e in range(GROUPS) for s in range(2, 6)
]
to_middle = [(there, here) for here, there in from_middle]
to_first = hop_pairs(lambda e, s: (e ^ (1 + s % 2), s))
to_second = hop_pairs(lambda e, s: (e ^ (2 - s % 2), s))


def add_low(one, two):
    return (one.astype(jnp.float32) + two.astype(jnp.float32)).astype(jnp.bfloat16)


def total_of(line):
    return sum(piece.astype(jnp.float32) for piece in line)


class Flow:
    def __init__(self, steps):
        self.steps = steps
        self.result = None
        self.feed(None)

    def feed(self, values):
        try:
            self.want = self.steps.send(values)
        except StopIteration as stop:
            self.want = None
            self.result = stop.value


class Order:
    def __init__(self, mark):
        self.mark = mark

    def tie(self, values):
        values, self.mark = lax.optimization_barrier((values, self.mark))
        return values

    def round(self, flows, work=None):
        values, self.mark = lax.optimization_barrier(([f.want[0] for f in flows], self.mark))
        found = [hop(v, f.want[1]) for v, f in zip(values, flows)]
        found, work, self.mark = lax.optimization_barrier((found, work, self.mark))
        for flow, values in zip(flows, found):
            flow.feed(values)
        return work


def one_hop(values, pairs):
    found = yield values, pairs
    return found


def line_flows(own):
    return [Flow(one_hop(own, to_line[k])) for k in (1, 2, 3)]


def line_spread(own, marks):
    near = yield own, to_line[1]
    marks.append(near)
    two = jnp.stack([own, near])
    crossed = yield two, over_middle
    passed = yield crossed, from_middle
    at = lax.axis_index("shard") // 2
    return jnp.where((at == 1) | (at == 2), crossed, passed)


def line_collect(near, far):
    passed = yield jnp.stack(far), to_middle
    far = add_low(jnp.stack(far), passed)
    crossed = yield far, over_middle
    at = lax.axis_index("shard") // 2
    middle = (at == 1) | (at == 2)
    both = jnp.stack(near).astype(jnp.float32) + jnp.where(middle, crossed, 0).astype(jnp.float32)
    back = yield both[1].astype(jnp.bfloat16), to_line[1]
    return both[0] + back.astype(jnp.float32)


def by_distance(far):
    at = lax.axis_index("shard") // 2
    middle = (at == 1) | (at == 2)
    return [jnp.where(middle, far[1 - i], far[i]) for i in range(2)]


def spread_pair(pieces):
    two = jnp.stack(pieces) if isinstance(pieces, list) else pieces
    first = yield two, to_first
    four = jnp.concatenate([two, first])
    second = yield four, to_second
    eight = jnp.concatenate([four, second])
    other = yield eight, to_core
    return eight, other


def spread_all(line):
    four = jnp.stack(line)
    first = yield four, to_first
    eight = jnp.concatenate([four, first])
    second = yield eight, to_second
    half = jnp.concatenate([eight, second])
    other = yield half, to_core
    return half, other


def collect_pair(mine, theirs):
    found = yield theirs, to_core
    keep, give = add_low(mine[:4], found[:4]), add_low(mine[4:], found[4:])
    found = yield give, to_second
    keep, give = add_low(keep[:2], found[:2]), add_low(keep[2:], found[2:])
    found = yield give, to_first
    return [add_low(keep[i], found[i]) for i in range(2)]


def collect_all(mine, theirs):
    found = yield theirs, to_core
    keep, give = add_low(mine[:8], found[:8]), add_low(mine[8:], found[8:])
    found = yield give, to_second
    keep, give = add_low(keep[:4], found[:4]), add_low(keep[4:], found[4:])
    found = yield give, to_first
    return [add_low(keep[i], found[i]) for i in range(4)]


def share_flow(own, places):
    first = yield own, to_first
    pair = jnp.stack([own, first])
    second = yield pair, to_second
    quarters = jnp.concatenate([pair, second])
    return jnp.concatenate(
        [lax.dynamic_index_in_dim(quarters, place, 0, keepdims=False) for place in places]
    )


def local_hops(
    tokens_in,
    output_cotangent,
    routes,
    doc_ids,
    picture_starts,
    qkv_weight,
    out_weight,
    router_weight,
    attn_gain,
    moe_gain,
    gate_up_weight,
    down_weight,
):
    low = jnp.bfloat16
    full = jnp.float32
    rows = tokens_in.shape[0]
    seq_len = doc_ids.shape[1]
    q_width = HEADS * HEAD_DIM
    kv_width = KV_HEADS * HEAD_DIM
    qkv_width = q_width + 2 * kv_width
    group_at = lax.axis_index("expert")
    shard_at = lax.axis_index("shard")
    own_experts = EXPERTS // GROUPS
    whole = own_experts // SHARDS * SHARDS
    split = own_experts - whole
    share = SHARDS // split
    part = H // share
    hid_width = H + part
    depth = gate_up_weight.shape[0]
    height = SHARDS * depth
    fine = depth // GROUPS
    pad = 128 - EXPERTS
    gain_one = attn_gain.astype(full)[:, None]
    gain_two = moe_gain.astype(full)[:, None]
    expert_one = group_at * own_experts + shard_at
    expert_two = group_at * own_experts + whole + shard_at // share
    ids = jnp.stack([expert_one, expert_two, shard_at])
    order = Order(jnp.zeros((8, 128), full))

    spot = jnp.arange(GROUPS * SHARDS, dtype=jnp.int32)
    spot_core = spot // 8 % 2
    spot_mate = 1 + (shard_at % 2 ^ spot_core)
    spot_q = spot % 8 // 2
    spot_group = jnp.where(spot_q == 1, spot_mate, jnp.where(spot_q == 2, 3 - spot_mate, spot_q))
    spot_line = spot // 16 * 2 + spot % 2
    fine_at = (shard_at ^ (2 * spot_line + spot_core)) * depth + (group_at ^ spot_group) * fine
    half_core = spot // 16
    half_mate = 1 + (shard_at % 2 ^ half_core)
    half_q = spot % 16 // 4
    half_group = jnp.where(half_q == 1, half_mate, jnp.where(half_q == 2, 3 - half_mate, half_q))
    half_at = (shard_at ^ (2 * (spot % 4) + half_core)) * depth + (group_at ^ half_group) * fine

    expert_ids = jnp.arange(EXPERTS, dtype=jnp.int32)
    hits = jnp.any(routes[:, :, None] == expert_ids[None, None, :], 1)
    earlier = jnp.arange(rows)[:, None] > jnp.arange(rows)[None, :]
    before = dot(earlier.astype(low), hits.astype(low), rows_by_cols)
    slots = jnp.where(hits & (before < CAP), before, -1.0)
    kept = slots >= 0
    grad_pay = jnp.concatenate(
        [output_cotangent, jnp.pad(slots.astype(low), ((0, 0), (0, pad)))], 1
    )

    def fine_rows(array):
        return lax.dynamic_slice_in_dim(array, group_at * fine, fine, 0)

    qkv_own = fine_rows(qkv_weight).astype(full) * fine_rows(gain_one)
    router_own = fine_rows(router_weight).astype(full) * fine_rows(gain_two)
    dense_own = jnp.concatenate([qkv_own, jnp.pad(router_own, ((0, 0), (0, pad)))], 1).astype(low)
    out_own = fine_rows(out_weight)

    def column_spec(width, index):
        return pl.BlockSpec((depth, width), lambda k, ids: (0, index(ids[2] ^ k)))

    to_parts = H // part
    packs = call(
        pack_kernel,
        "pack",
        [shaped((1, depth, hid_width)), shaped((1, depth, 2 * hid_width))] * SHARDS,
        [
            column_spec(2 * H, lambda d: d),
            column_spec(part, lambda d: (whole + d // share) * 2 * to_parts + d % share),
            column_spec(part, lambda d: (whole + d // share) * 2 * to_parts + to_parts + d % share),
            column_spec(H, lambda d: d),
            column_spec(part, lambda d: (whole + d // share) * to_parts + d % share),
            pl.BlockSpec((depth, 1), lambda d, ids: (0, 0)),
        ],
        [
            out_spec((1, depth, hid_width), (0, 0, 0)),
            out_spec((1, depth, 2 * hid_width), (0, 0, 0)),
        ]
        * SHARDS,
        (ids, gate_up_weight, gate_up_weight, gate_up_weight, down_weight, down_weight, gain_two),
        steps=SHARDS,
    )

    to_shard = [hop_pairs(lambda e, s, k=k: (e, s ^ k)) for k in range(SHARDS)]
    shard_rows = (shard_at ^ jnp.arange(SHARDS, dtype=jnp.int32)) * depth

    def exchange(pieces):
        flows = [[Flow(one_hop(piece, to_shard[k])) for piece in pieces[k]] for k in range(1, SHARDS)]
        near = [flows[k - 1][n] for n in range(len(pieces[0])) for k in (2, 3)]
        far = [flows[k - 1][n] for n in range(len(pieces[0])) for k in (4, 5, 6, 7)]
        return flows, flows[0], near, far

    def exchanged(pieces, flows, n):
        parts = [pieces[0][n]] + [flow[n].result for flow in flows]
        return place_rows(shard_rows, parts, height)

    s_pieces = [packs[2 * k : 2 * k + 2] for k in range(SHARDS)]
    s_flows, core, near, far = exchange(s_pieces)

    def some(flows, count):
        taken = flows[:count]
        del flows[:count]
        return taken

    w = line_flows(dense_own)
    o = line_flows(out_own)
    g_marks, x_marks = [], []
    g_line = Flow(line_spread(grad_pay, g_marks))
    order.round(w[:2])
    w_near = Flow(spread_pair([dense_own, w[0].result]))
    order.round([w[2], w_near, g_line])
    w_far = Flow(spread_pair([w[1].result, w[2].result]))
    g_near = Flow(spread_pair([grad_pay, g_marks[0]]))
    order.round([w_near, w_far] + some(far, 1) + some(near, 1) + core)
    order.round([w_near, w_far] + o)
    o_all = Flow(spread_all([out_own] + [flow.result for flow in o]))
    order.round([w_far, o_all])
    dense_full = place_rows(fine_at, w_near.result + w_far.result, height)
    router_full = dense_full[:, qkv_width:]

    tokens_f = tokens_in.astype(full)
    inverse_one = lax.rsqrt(jnp.mean(tokens_f * tokens_f, -1, keepdims=True) + norm_eps)
    normal_one = tokens_f * inverse_one
    normed_in = normal_one.astype(low)
    query_pos = shard_at * rows + jnp.arange(rows, dtype=jnp.int32)
    cosine, sine = rope_tables(query_pos, HEAD_DIM)
    cosine = jnp.tile(cosine[:, 0], (1, 4))
    sine = jnp.tile(jnp.concatenate([-sine[:, 0], sine[:, 0]], 1), (1, 2))
    tile = 512
    queries, key_value = call(
        qkv_kernel,
        "qkv",
        (shaped((rows, q_width)), shaped((rows, 2 * kv_width))),
        [
            whole_spec((rows, D)),
            pl.BlockSpec((D, tile), lambda j, ids: (0, j)),
            whole_spec((rows, 128)),
            whole_spec((rows, 128)),
        ],
        [
            pl.BlockSpec((rows, tile), lambda j, ids: (0, jnp.minimum(j, 2))),
            pl.BlockSpec((rows, tile), lambda j, ids: (0, jnp.maximum(j - 3, 0))),
        ],
        (ids, normed_in, dense_full, cosine, sine),
        flops=2 * rows * D * qkv_width,
        steps=qkv_width // tile,
    )
    queries, key_value = order.round(
        [o_all, g_near, g_line] + some(near, 1), (queries, key_value)
    )
    kv = line_flows(key_value)
    order.round(kv + [o_all, g_near])
    kv_line = jnp.concatenate([key_value] + [flow.result for flow in kv])
    kv_core = Flow(one_hop(kv_line, to_core))
    out_full = place_rows(half_at, o_all.result, height)
    out_full = order.round([kv_core], out_full)
    kv_other = kv_core.result
    block_order = jnp.arange(SHARDS, dtype=jnp.int32)
    block_order = shard_at ^ (block_order % 4 * 2 + block_order // 4)
    key_pos = (
        block_order[:, None] * rows + jnp.arange(rows, dtype=jnp.int32)[None, :]
    ).reshape(seq_len)
    doc_blocks = doc_ids[0].reshape(SHARDS, rows)
    block_hits = block_order[:, None] == jnp.arange(SHARDS)[None, :]
    key_doc = jnp.sum(
        jnp.where(block_hits[:, :, None], doc_blocks[None], 0), 1
    ).reshape(seq_len)
    query_doc = key_doc[:rows]
    key_pic = picture_ids(key_pos, picture_starts[0], SLOT, PIECE)
    query_pic = key_pic[:rows]
    visible = allowed(query_pos, key_pos, query_doc, key_doc, query_pic, key_pic)
    bias = jnp.where(visible, 0.0, masked_score)
    pairs = KV_HEADS // 2
    q_tile = q_width // pairs
    kv_tile = kv_width // pairs
    half_len = seq_len // 2

    def kv_specs(first):
        return [pl.BlockSpec((half_len, kv_tile), lambda j, ids: (0, first + j))] * 2

    q_spec = pl.BlockSpec((rows, q_tile), lambda j, ids: (0, j))
    log_spec = pl.BlockSpec((1, rows, 128), lambda j, ids: (j, 0, 0))
    attended, logs = call(
        attend_kernel,
        "attend",
        (shaped((rows, q_width)), shaped((pairs, rows, 128), full)),
        [q_spec] + kv_specs(0) + kv_specs(pairs) + [whole_spec((rows, seq_len))],
        [q_spec, log_spec],
        (ids, queries, kv_line, kv_other, kv_line, kv_other, bias),
        flops=4 * rows * seq_len * q_width,
        steps=pairs,
    )
    branch = dot(attended, out_full, rows_by_rows)
    middle = tokens_f + branch
    inverse_two = lax.rsqrt(jnp.mean(middle * middle, -1, keepdims=True) + norm_eps)
    normal_two = middle * inverse_two
    normed_mid = normal_two.astype(low)
    logits = dot(normed_mid, router_full, rows_by_cols)[:, :EXPERTS]
    logits = jnp.where(hits, logits, masked_score)
    gates = jnp.exp(logits - jnp.max(logits, -1, keepdims=True))
    gates = jnp.where(hits, gates, 0.0)
    gates = gates / jnp.sum(gates, -1, keepdims=True)
    gate_low = gates.astype(low)
    gate_rest = (gates - gate_low.astype(full)).astype(low)
    row_pay = jnp.concatenate(
        [normed_mid, gate_low, gate_rest, jnp.zeros((rows, 128 - 2 * EXPERTS), low)], 1
    )

    slot_rows = GROUPS * SHARDS * CAP
    step_rows = slot_rows // 2
    blocks = 2 * GROUPS
    pay_spec = whole_spec((blocks, rows, D + 128))
    pay_out = out_spec((blocks, rows, D + 128), (0, 0, 0))
    slot_spec = block_spec((blocks, rows, 128), (0, 0, D // 128))
    up_specs = [
        block_spec((height, H), (0, 0)),
        block_spec((height, part), (0, 2 * to_parts)),
        block_spec((height, H), (0, 1)),
        block_spec((height, part), (0, 2 * to_parts + 1)),
    ]
    down_specs = [
        block_spec((height, H), (0, 0)),
        block_spec((height, part), (0, H // part)),
    ]
    back_shape = shaped((blocks, rows, D + 128))
    gs_shape = shaped((2, slot_rows, D))
    kept_shapes = (gs_shape, shaped((slot_rows, hid_width)), shaped((slot_rows, 2 * hid_width)))
    kept_rows = ()

    gs, plain = (), []

    def grad_side(k):
        nonlocal gs
        gs_next, found = call(
            grad_side_kernel,
            "grad_side",
            (gs_shape, shaped((step_rows, hid_width), full)),
            [pay_spec, pay_spec] + down_specs + [in_place] * len(gs),
            [
                out_spec((2, step_rows, D), (0, k, 0)),
                out_spec((step_rows, hid_width), (0, 0)),
            ],
            (ids,) + (g_near, g_far)[k].result + (owned_down, owned_down) + gs,
            aliases={5: 0} if gs else None,
            flops=2 * step_rows * D * (hid_width + 2 * rows),
        )
        gs = (gs_next,)
        return found

    def row_side(k):
        nonlocal kept_rows
        half_back, other_back, *kept_next = call(
            row_side_kernel,
            "row_side",
            (back_shape, back_shape) + kept_shapes,
            [pay_spec, pay_spec, slot_spec, slot_spec, whole_spec((step_rows, hid_width))]
            + up_specs
            + [in_place] * len(kept_rows),
            [
                pay_out,
                pay_out,
                out_spec((2, step_rows, D), (0, k, 0)),
                out_spec((step_rows, hid_width), (k, 0)),
                out_spec((step_rows, 2 * hid_width), (k, 0)),
            ],
            (ids,)
            + (x_near, x_far)[k].result
            + (g_near, g_far)[k].result
            + (plain[k],)
            + (owned_up,) * 4
            + kept_rows,
            scratch=[
                pltpu.VMEM((2, step_rows, 1), full),
                pltpu.VMEM((2, step_rows, 1), full),
                pltpu.VMEM((2, step_rows, D + 128), low),
            ],
            aliases={10: 2, 11: 3, 12: 4} if kept_rows else None,
            flops=8 * step_rows * D * (hid_width + rows),
        )
        kept_rows = tuple(kept_next)
        return half_back, other_back

    row_pay = order.round([g_near, g_line] + some(far, 3), row_pay)
    x_line = Flow(line_spread(row_pay, x_marks))
    g_far = Flow(spread_pair(g_line.result))
    order.round([x_line, g_far] + some(far, 1))
    x_near = Flow(spread_pair([row_pay, x_marks[0]]))
    owned_down = exchanged(s_pieces, s_flows, 0)
    owned_down = order.round([x_line, x_near, g_far] + some(near, 1), owned_down)
    plain = [order.round([x_line, x_near, g_far] + some(far, 1), grad_side(0))]
    x_far = Flow(spread_pair(x_line.result))
    plain.append(order.round([x_near, x_far] + some(far, 1) + near, grad_side(1)))
    order.round([x_far] + far)
    owned_up = exchanged(s_pieces, s_flows, 1)
    back_near = order.round([x_far], row_side(0))
    b_near = Flow(collect_pair(*back_near))
    back_far = order.round([b_near], row_side(1))
    b_far = Flow(collect_pair(*back_far))

    xs, hid, pg = kept_rows

    def lane_block(i, ids):
        return (0, 0, i ^ ids[2] // 2)

    terms = call(
        terms_kernel,
        "terms",
        shaped((SHARDS, depth, 3 * hid_width)),
        [
            pl.BlockSpec((2, slot_rows, 2 * depth), lane_block),
            pl.BlockSpec((2, slot_rows, 2 * depth), lane_block),
            whole_spec((slot_rows, 2 * hid_width)),
            whole_spec((slot_rows, hid_width)),
        ],
        pl.BlockSpec((2, depth, 3 * hid_width), lambda i, ids: (i, 0, 0)),
        (ids, xs, gs[0], pg, hid),
        flops=2 * slot_rows * D * 3 * hid_width,
        steps=4,
    )
    terms = order.round([b_near, b_far], terms)
    t_edge = 2 * H
    t_pieces = [[terms[k][None]] for k in range(6)]
    t_pieces += [[terms[k, :, :t_edge][None], terms[k, :, t_edge:][None]] for k in (6, 7)]
    t_flows = [[Flow(one_hop(piece, to_shard[k])) for piece in t_pieces[k]] for k in range(1, SHARDS)]
    core, near = t_flows[0], t_flows[1] + t_flows[2]
    far = t_flows[5][:1] + t_flows[3] + t_flows[4] + t_flows[5][1:] + t_flows[6]

    order.round([b_near, b_far] + some(far, 1))
    b_line = [Flow(one_hop(b_near.result[1], to_line[1]))]
    moe_blocks = call(
        out_side_kernel,
        "out_side",
        (shaped((2 * blocks, rows, D)),) * 2,
        [whole_spec((slot_rows, hid_width))] + [slot_spec] * 4 + down_specs,
        [out_spec((2 * blocks, rows, D), (0, 0, 0))] * 2,
        (ids, hid) + g_near.result + g_far.result + (owned_down, owned_down),
        scratch=[pltpu.VMEM((2, slot_rows, D), low)],
        flops=2 * slot_rows * D * (hid_width + 2 * rows),
    )
    moe_blocks = order.round([b_far] + b_line + core, moe_blocks)
    b_line += [
        Flow(one_hop(piece, to_line[2 + i])) for i, piece in enumerate(by_distance(b_far.result))
    ]
    moe = Flow(collect_all(*moe_blocks))
    order.round(b_line[1:] + [moe] + some(near, 1))
    grad_sum = total_of([b_near.result[0]] + [flow.result for flow in b_line])

    gate_grad = jnp.where(kept, grad_sum[:, D : D + EXPERTS], 0.0)
    logit_grad = gates * (gate_grad - jnp.sum(gates * gate_grad, -1, keepdims=True))
    logit_grad = jnp.pad(logit_grad.astype(low), ((0, 0), (0, pad)))
    scaled_two = grad_sum[:, :D] + dot(logit_grad, router_full, rows_by_rows)
    grad_out = output_cotangent.astype(full)
    mean_two = jnp.mean(scaled_two * normal_two, -1, keepdims=True)
    mid_grad = grad_out + inverse_two * (scaled_two - normal_two * mean_two)
    branch_grad = mid_grad.astype(low)
    attended_grad = dot(branch_grad, out_full, rows_by_cols).astype(low)

    kv_out = pl.BlockSpec((half_len, kv_tile), lambda j, ids: (0, j))
    query_back, key_mine, key_theirs, value_mine, value_theirs = call(
        attend_back_kernel,
        "attend_back",
        (shaped((rows, q_width)),) + (shaped((half_len, kv_width)),) * 4,
        [q_spec, q_spec]
        + kv_specs(0)
        + kv_specs(pairs)
        + [whole_spec((rows, seq_len)), log_spec, whole_spec((rows, 128)), whole_spec((rows, 128))],
        [q_spec] + [kv_out] * 4,
        (ids, queries, attended_grad, kv_line, kv_other, kv_line, kv_other, bias, logs, cosine, sine),
        flops=10 * rows * seq_len * q_width,
        steps=pairs,
    )
    kv_theirs = jnp.concatenate([key_theirs, value_theirs], 1)
    kv_mine = jnp.concatenate([key_mine, value_mine], 1)
    def dense_flow(products):
        return dense_terms(half_at, products, 2, 4 * GROUPS, fine)

    kv_theirs, kv_mine = order.round(
        [moe] + some(far, 2) + near, (kv_theirs, kv_mine)
    )
    kv_core = Flow(one_hop(kv_theirs, to_core))
    order.round([kv_core])
    kv_half = add_low(kv_mine, kv_core.result).reshape(4, rows, 2 * kv_width)
    kv = [Flow(one_hop(kv_half[k], to_line[k])) for k in (1, 2, 3)]
    early_blocks = dense_flow([(branch_grad, attended, 0), (normed_in, query_back, q_width)])
    early_blocks = order.round(kv + [moe], early_blocks)
    m_line = Flow(line_collect(moe.result[:2], moe.result[2:]))
    early = Flow(collect_all(*early_blocks))
    kv_grad = total_of([kv_half[0]] + [flow.result for flow in kv])

    def line_of(blocks):
        return [Flow(one_hop(blocks[k], to_line[k])) for k in (1, 2, 3)]

    def swapped(values):
        lanes = jnp.arange(values.shape[1]) % HEAD_DIM < HEAD_DIM // 2
        return jnp.where(
            lanes[None], jnp.roll(values, -HEAD_DIM // 2, 1), jnp.roll(values, HEAD_DIM // 2, 1)
        )

    key_grad = kv_grad[:, :kv_width]
    key_back = key_grad * jnp.tile(cosine, (1, pairs)) - swapped(key_grad) * jnp.tile(sine, (1, pairs))
    kv_rows = jnp.concatenate([key_back, kv_grad[:, kv_width:]], 1).astype(low)
    scaled_one = dot(query_back, dense_full[:, :q_width], rows_by_rows) + dot(
        kv_rows, dense_full[:, q_width:qkv_width], rows_by_rows
    )
    mean_one = jnp.mean(scaled_one * normal_one, -1, keepdims=True)
    input_grad = mid_grad + inverse_one * (scaled_one - normal_one * mean_one)
    pad_lanes = jnp.arange(128)[None, :]

    def marker(lane):
        return jnp.broadcast_to(jnp.where(pad_lanes == lane, 1.0, 0.0), (rows, 128)).astype(low)

    late_blocks = dense_flow(
        [
            (normed_in, kv_rows, 0),
            (normed_mid, logit_grad, 2 * kv_width),
            ((scaled_two * normal_two).astype(low), marker(EXPERTS), 2 * kv_width),
        ]
    )
    late_blocks = order.round([early, m_line] + some(far, 1), late_blocks)
    late = Flow(collect_all(*late_blocks))
    input_grad = order.round(
        [late, early, m_line], input_grad.astype(low)
    )
    order.round([late, early, m_line] + some(far, 1))
    order.round([late] + far)
    dense_line = line_of(
        [jnp.concatenate(pair, 1) for pair in zip(early.result, late.result)]
    )
    spots = jnp.arange(GROUPS, dtype=jnp.int32) ^ group_at
    mate = 1 + shard_at % 2
    spots = jnp.where(spots == mate, 1, jnp.where(spots == 3 - mate, 2, spots))
    places = [spots[i] for i in range(GROUPS)]

    t_parts = t_pieces[0] + [flow.result for flows in t_flows for flow in flows]

    def to_expert(k, ids):
        return (0, jnp.where(k < SHARDS, ids[2] ^ k, k))

    gate_up_grad, down_grad = call(
        unpack_kernel,
        "unpack",
        (shaped(gate_up_weight.shape, full), shaped(down_weight.shape, full)),
        [whole_spec(piece.shape) for piece in t_parts] + [whole_spec((depth, 1))],
        [pl.BlockSpec((depth, 2 * H), to_expert), pl.BlockSpec((depth, H), to_expert)],
        (ids,) + tuple(t_parts) + (gain_two,),
        steps=own_experts,
    )
    gate_up_grad, down_grad = order.round(dense_line, (gate_up_grad, down_grad))
    own_sum = jnp.concatenate([early.result[0], late.result[0]], 1)
    own_sum = total_of([own_sum] + [flow.result for flow in dense_line]).astype(low)
    share_all = Flow(share_flow(own_sum, places))
    order.round([share_all])
    order.round([share_all])
    output = (middle + m_line.result).astype(low)
    dense_sums = share_all.result.astype(full)
    early_sum, late_sum = dense_sums[:, : 2 * q_width], dense_sums[:, 2 * q_width :]
    out_sum, query_sum = early_sum[:, :q_width], early_sum[:, q_width:]

    qkv_sum = jnp.concatenate([query_sum, late_sum[:, : 2 * kv_width]], 1)
    return (
        output,
        input_grad,
        qkv_sum * gain_one,
        out_sum,
        late_sum[:, 2 * kv_width : 2 * kv_width + EXPERTS] * gain_two,
        jnp.sum(qkv_sum * qkv_weight.astype(full), 1),
        late_sum[:, 2 * kv_width + EXPERTS] / gain_two[:, 0],
        gate_up_grad,
        down_grad,
    )


def solution(mesh):
    body = local
    if mesh.shape["expert"] == GROUPS and mesh.shape["shard"] == SHARDS:
        body = local_hops
    return jax.shard_map(
        body,
        mesh=mesh,
        in_specs=(
            P(("expert", "shard"), None),
            P(("expert", "shard"), None),
            P(("expert", "shard"), None),
            P("expert", None),
            P("expert", None),
            P("shard", None),
            P("shard", None),
            P("shard", None),
            P("shard"),
            P("shard"),
            P("shard", "expert"),
            P("shard", "expert"),
        ),
        out_specs=(
            P(("expert", "shard"), None),
            P(("expert", "shard"), None),
            P("shard", None),
            P("shard", None),
            P("shard", None),
            P("shard"),
            P("shard"),
            P("shard", "expert"),
            P("shard", "expert"),
        ),
        check_vma=False,
    )
```

```python
import jax
import jax.numpy as jnp
from jax import lax
from jax.experimental import pallas as pl
from jax.experimental.pallas import tpu as pltpu
from jax.sharding import PartitionSpec as P

D = 1536
HEADS = 24
KV_HEADS = 8
HEAD_DIM = 64
H = 512
EXPERTS = 40
TOP = 8
PIECE = 256
SLOT = 512
CAP = 32


norm_eps = 1e-06
rope_base = 10000.0
masked_score = -1e30


def rope_tables(positions, head_dim):
    half_dim = head_dim // 2
    frequency = rope_base ** (-2.0 * jnp.arange(half_dim, dtype=jnp.float32) / head_dim)
    angles = positions.astype(jnp.float32)[:, None] * frequency[None, :]
    return (jnp.cos(angles)[:, None, :], jnp.sin(angles)[:, None, :])


def rotate(values, cosine, sine_table):
    half_dim = values.shape[-1] // 2
    first_half = values[..., :half_dim]
    second = values[..., half_dim:]
    return jnp.concatenate(
        [first_half * cosine - second * sine_table, second * cosine + first_half * sine_table], -1
    )


def rotate_back(grad_rows, cosine, sine_table):
    half_dim = grad_rows.shape[-1] // 2
    first_half = grad_rows[..., :half_dim]
    second = grad_rows[..., half_dim:]
    return jnp.concatenate(
        [first_half * cosine + second * sine_table, second * cosine - first_half * sine_table], -1
    )


def rms_norm(values, gain):
    inverse = lax.rsqrt(jnp.mean(values * values, -1, keepdims=True) + norm_eps)
    normal = values * inverse
    return (normal * gain, normal, inverse)


def rms_back(grad_rows, gain, normal, inverse):
    scaled = grad_rows * gain
    grad_in = inverse * (scaled - normal * jnp.mean(scaled * normal, -1, keepdims=True))
    return (grad_in, jnp.sum(grad_rows * normal, 0))


def picture_ids(positions, starts, slot_len, piece_len):
    slot_index = positions // slot_len
    picked_slot = slot_index[:, None] == jnp.arange(starts.shape[0], dtype=jnp.int32)[None, :]
    piece_begin = jnp.sum(jnp.where(picked_slot, starts[None, :], 0), axis=1)
    inside = (positions >= piece_begin) & (positions < piece_begin + piece_len)
    return jnp.where(inside, slot_index, -1)


def allowed(query_pos, key_pos, query_doc, key_doc, query_pic, key_pic):
    same_doc = query_doc[:, None] == key_doc[None, :]
    earlier = key_pos[None, :] <= query_pos[:, None]
    same_pic = (query_pic[:, None] == key_pic[None, :]) & (query_pic[:, None] >= 0)
    return same_doc & (earlier | same_pic)


def local(
    tokens_in,
    output_cotangent,
    routes,
    doc_ids,
    picture_starts,
    qkv_weight,
    out_weight,
    router_weight,
    attn_gain,
    moe_gain,
    gate_up_weight,
    down_weight,
):
    qkv_full, out_full, router_full, gain_first, gain_second = (
        lax.all_gather(qkv_weight, "shard", axis=0, tiled=True),
        lax.all_gather(out_weight, "shard", axis=0, tiled=True),
        lax.all_gather(router_weight, "shard", axis=0, tiled=True),
        lax.all_gather(attn_gain, "shard", axis=0, tiled=True),
        lax.all_gather(moe_gain, "shard", axis=0, tiled=True),
    )
    gain_one = gain_first.astype(jnp.float32)
    gain_two = gain_second.astype(jnp.float32)
    tok_rows = tokens_in.shape[0]
    seq_len = doc_ids.shape[1]
    groups = HEADS // KV_HEADS
    q_width = HEADS * HEAD_DIM
    kv_width = KV_HEADS * HEAD_DIM
    score_scale = HEAD_DIM ** (-0.5)
    shard_at = lax.axis_index("shard")
    query_pos = shard_at * tok_rows + jnp.arange(tok_rows, dtype=jnp.int32)
    key_pos = jnp.arange(seq_len, dtype=jnp.int32)
    key_doc = doc_ids[0]
    key_pic = picture_ids(key_pos, picture_starts[0], SLOT, PIECE)
    query_doc = lax.dynamic_slice_in_dim(key_doc, shard_at * tok_rows, tok_rows)
    query_pic = lax.dynamic_slice_in_dim(key_pic, shard_at * tok_rows, tok_rows)
    tokens_f = tokens_in.astype(jnp.float32)
    normed_one, normal_one, inverse_one = rms_norm(tokens_f, gain_one)
    normed_in = normed_one.astype(jnp.bfloat16)
    qkv_rows = jnp.dot(normed_in, qkv_full, preferred_element_type=jnp.float32)
    cosine, sine_table = rope_tables(query_pos, HEAD_DIM)
    queries = (
        rotate(qkv_rows[:, :q_width].reshape(tok_rows, HEADS, HEAD_DIM), cosine, sine_table)
        .astype(jnp.bfloat16)
        .reshape(tok_rows, KV_HEADS, groups, HEAD_DIM)
    )
    key_local = (
        rotate(
            qkv_rows[:, q_width : q_width + kv_width].reshape(tok_rows, KV_HEADS, HEAD_DIM),
            cosine,
            sine_table,
        )
        .astype(jnp.bfloat16)
        .reshape(tok_rows, kv_width)
    )
    value_local = qkv_rows[:, q_width + kv_width :].astype(jnp.bfloat16)
    all_keys, all_values = (
        lax.all_gather(key_local, "shard", axis=0, tiled=True),
        lax.all_gather(value_local, "shard", axis=0, tiled=True),
    )
    span_len = min(512, seq_len)
    span_count = seq_len // span_len

    def block_scores(first_row, key_rows):
        key_block = lax.dynamic_slice_in_dim(key_rows, first_row, span_len, 0).reshape(
            span_len, KV_HEADS, HEAD_DIM
        )
        raw_scores = (
            jnp.einsum("tgrd,kgd->tgrk", queries, key_block, preferred_element_type=jnp.float32)
            * score_scale
        )
        block_pos = lax.dynamic_slice_in_dim(key_pos, first_row, span_len)
        block_doc = lax.dynamic_slice_in_dim(key_doc, first_row, span_len)
        block_pic = lax.dynamic_slice_in_dim(key_pic, first_row, span_len)
        visible = allowed(query_pos, block_pos, query_doc, block_doc, query_pic, block_pic)[
            :, None, None, :
        ]
        return (raw_scores, visible, key_block)

    def value_block_at(first_row, value_rows):
        return lax.dynamic_slice_in_dim(value_rows, first_row, span_len, 0).reshape(
            span_len, KV_HEADS, HEAD_DIM
        )

    def max_step(step_index, carry):
        run_max, run_sum = carry
        raw_scores, visible, key_block = block_scores(step_index * span_len, all_keys)
        masked = jnp.where(visible, raw_scores, masked_score)
        new_max = jnp.maximum(run_max, jnp.max(masked, -1))
        shifted = jnp.where(visible, jnp.exp(masked - new_max[..., None]), 0.0)
        return (new_max, run_sum * jnp.exp(run_max - new_max) + jnp.sum(shifted, -1))

    stat_shape = (tok_rows, KV_HEADS, groups)
    run_max, run_sum = lax.fori_loop(
        0,
        span_count,
        max_step,
        (jnp.full(stat_shape, masked_score, jnp.float32), jnp.zeros(stat_shape, jnp.float32)),
    )
    log_total = run_max + jnp.log(run_sum)

    def probs_of(raw_scores, visible):
        return jnp.exp(jnp.where(visible, raw_scores - log_total[..., None], masked_score))

    def value_step(step_index, summed):
        first_row = step_index * span_len
        raw_scores, visible, key_block = block_scores(first_row, all_keys)
        probs = probs_of(raw_scores, visible).astype(jnp.bfloat16)
        return summed + jnp.einsum(
            "tgrk,kgd->tgrd",
            probs,
            value_block_at(first_row, all_values),
            preferred_element_type=jnp.float32,
        )

    summed = lax.fori_loop(
        0, span_count, value_step, jnp.zeros((tok_rows, KV_HEADS, groups, HEAD_DIM), jnp.float32)
    )
    attended = summed.reshape(tok_rows, q_width).astype(jnp.bfloat16)
    branch = lax.dot_general(
        attended, out_full, (((1,), (1,)), ((), ())), preferred_element_type=jnp.float32
    )
    middle = tokens_f + branch
    normed_two, normal_two, inverse_two = rms_norm(middle, gain_two)
    normed_mid = normed_two.astype(jnp.bfloat16)
    logits = jnp.dot(normed_mid, router_full, preferred_element_type=jnp.float32)
    gates = jax.nn.softmax(jnp.take_along_axis(logits, routes, 1), axis=-1)
    route_hits = routes[:, :, None] == jnp.arange(EXPERTS, dtype=jnp.int32)[None, None, :]
    hit_count = jnp.sum(route_hits.astype(jnp.int32), 1)
    before = jnp.cumsum(hit_count, 0) - hit_count
    slot_index = jnp.take_along_axis(before, routes, 1)
    kept_pair = slot_index < CAP
    flat_slot = routes * CAP + slot_index
    capacity_rows = EXPERTS * CAP
    target = jnp.where(kept_pair, flat_slot, capacity_rows)
    token_ids = jnp.broadcast_to(jnp.arange(tok_rows, dtype=jnp.int32)[:, None], (tok_rows, TOP))
    owner_row = (
        jnp.full((capacity_rows + 1,), -1, jnp.int32)
        .at[target.reshape(-1)]
        .set(token_ids.reshape(-1))[:capacity_rows]
    )
    filled = owner_row >= 0
    source_row = jnp.maximum(owner_row, 0)
    expert_groups = lax.axis_size("expert")
    local_experts = EXPERTS // expert_groups
    send_rows = jnp.where(
        filled[:, None], normed_mid[source_row], jnp.zeros((), jnp.bfloat16)
    ).reshape(expert_groups, local_experts, CAP, D)
    received = lax.all_to_all(send_rows, "expert", split_axis=0, concat_axis=0, tiled=True)
    gate_up_full, down_full = (
        lax.all_gather(gate_up_weight, "shard", axis=0, tiled=True),
        lax.all_gather(down_weight, "shard", axis=0, tiled=True),
    )
    gate_up3 = gate_up_full.reshape(D, local_experts, 2 * H)
    down3 = down_full.reshape(D, local_experts, H)
    projected = jnp.einsum("secd,dej->secj", received, gate_up3, preferred_element_type=jnp.float32)
    gate_part = projected[..., :H]
    up_part = projected[..., H:]
    sigma = jax.nn.sigmoid(gate_part)
    silu_value = gate_part * sigma
    hidden = (silu_value * up_part).astype(jnp.bfloat16)
    expert_out = jnp.einsum(
        "secj,dej->secd", hidden, down3, preferred_element_type=jnp.float32
    ).astype(jnp.bfloat16)
    returned = lax.all_to_all(
        expert_out, "expert", split_axis=0, concat_axis=0, tiled=True
    ).reshape(capacity_rows, D)
    safe_flat = jnp.where(kept_pair, flat_slot, 0)
    picked = returned[safe_flat].astype(jnp.float32)
    pair_weight = jnp.where(kept_pair, gates, 0.0)
    moe_sum = jnp.einsum("tk,tkd->td", pair_weight, picked)
    output = (middle + moe_sum).astype(jnp.bfloat16)
    grad_out = output_cotangent.astype(jnp.float32)
    gate_grad = jnp.where(kept_pair, jnp.einsum("td,tkd->tk", grad_out, picked), 0.0)
    slot_gate = (
        jnp.zeros((capacity_rows + 1,), jnp.float32)
        .at[target.reshape(-1)]
        .set(gates.reshape(-1))[:capacity_rows]
    )
    grad_send = (
        jnp.where(filled[:, None], slot_gate[:, None] * grad_out[source_row], 0.0)
        .astype(jnp.bfloat16)
        .reshape(expert_groups, local_experts, CAP, D)
    )
    grad_received = lax.all_to_all(grad_send, "expert", split_axis=0, concat_axis=0, tiled=True)
    keys_back, values_back = (
        lax.all_gather(key_local, "shard", axis=0, tiled=True),
        lax.all_gather(value_local, "shard", axis=0, tiled=True),
    )
    again_up, again_down = (
        lax.all_gather(gate_up_weight, "shard", axis=0, tiled=True),
        lax.all_gather(down_weight, "shard", axis=0, tiled=True),
    )
    gate_up_back = again_up.reshape(D, local_experts, 2 * H)
    down_back = again_down.reshape(D, local_experts, H)
    hidden_grad = jnp.einsum(
        "secd,dej->secj", grad_received, down_back, preferred_element_type=jnp.float32
    )
    silu_slope = sigma * (1.0 + gate_part * (1.0 - sigma))
    proj_grad = jnp.concatenate(
        [hidden_grad * up_part * silu_slope, hidden_grad * silu_value], -1
    ).astype(jnp.bfloat16)
    row_grad = jnp.einsum(
        "secj,dej->secd", proj_grad, gate_up_back, preferred_element_type=jnp.float32
    ).astype(jnp.bfloat16)
    grad_back = lax.all_to_all(row_grad, "expert", split_axis=0, concat_axis=0, tiled=True).reshape(
        capacity_rows, D
    )
    row_count = gate_up_weight.shape[0] * lax.axis_size("shard")
    up_terms = jnp.einsum(
        "secd,secj->dej", received, proj_grad, preferred_element_type=jnp.float32
    ).reshape(row_count, local_experts * 2 * H)
    down_terms = jnp.einsum(
        "secd,secj->dej", grad_received, hidden, preferred_element_type=jnp.float32
    ).reshape(row_count, local_experts * H)
    expert_sums = lax.psum_scatter(
        jnp.concatenate([up_terms, down_terms], 1).astype(jnp.bfloat16),
        "shard",
        scatter_dimension=0,
        tiled=True,
    ).astype(jnp.float32)
    gate_up_grad = expert_sums[:, : local_experts * 2 * H]
    down_grad = expert_sums[:, local_experts * 2 * H :]
    mid_norm_grad = jnp.einsum(
        "tk,tkd->td", kept_pair.astype(jnp.float32), grad_back[safe_flat].astype(jnp.float32)
    )
    chosen_grad = gates * (gate_grad - jnp.sum(gates * gate_grad, -1, keepdims=True))
    logit_grad = jnp.sum(jnp.where(route_hits, chosen_grad[:, :, None], 0.0), 1).astype(
        jnp.bfloat16
    )
    mid_norm_grad = mid_norm_grad + lax.dot_general(
        logit_grad, router_full, (((1,), (1,)), ((), ())), preferred_element_type=jnp.float32
    )
    router_grad = lax.dot_general(
        normed_mid, logit_grad, (((0,), (0,)), ((), ())), preferred_element_type=jnp.float32
    )
    mid_part, moe_gain_grad = rms_back(mid_norm_grad, gain_two, normal_two, inverse_two)
    mid_grad = grad_out + mid_part
    branch_grad = mid_grad.astype(jnp.bfloat16)
    out_weight_grad = lax.dot_general(
        branch_grad, attended, (((0,), (0,)), ((), ())), preferred_element_type=jnp.float32
    )
    attended_grad = (
        jnp.dot(branch_grad, out_full, preferred_element_type=jnp.float32)
        .astype(jnp.bfloat16)
        .reshape(tok_rows, KV_HEADS, groups, HEAD_DIM)
    )

    def dot_step(step_index, row_dot):
        first_row = step_index * span_len
        raw_scores, visible, key_block = block_scores(first_row, keys_back)
        prob_full = probs_of(raw_scores, visible)
        prob_grad = jnp.einsum(
            "tgrd,kgd->tgrk",
            attended_grad,
            value_block_at(first_row, values_back),
            preferred_element_type=jnp.float32,
        )
        return row_dot + jnp.sum(prob_full * prob_grad, -1)

    row_dot = lax.fori_loop(0, span_count, dot_step, jnp.zeros(stat_shape, jnp.float32))

    def grad_step(step_index, carry):
        query_grad, key_terms, value_terms = carry
        first_row = step_index * span_len
        raw_scores, visible, key_block = block_scores(first_row, keys_back)
        prob_full = probs_of(raw_scores, visible)
        prob_grad = jnp.einsum(
            "tgrd,kgd->tgrk",
            attended_grad,
            value_block_at(first_row, values_back),
            preferred_element_type=jnp.float32,
        )
        score_grad = (prob_full * (prob_grad - row_dot[..., None])).astype(jnp.bfloat16)
        query_grad = query_grad + jnp.einsum(
            "tgrk,kgd->tgrd", score_grad, key_block, preferred_element_type=jnp.float32
        )
        key_part = (
            jnp.einsum(
                "tgrk,tgrd->kgd", score_grad, queries, preferred_element_type=jnp.float32
            ).reshape(span_len, kv_width)
            * score_scale
        )
        value_part = jnp.einsum(
            "tgrk,tgrd->kgd",
            prob_full.astype(jnp.bfloat16),
            attended_grad,
            preferred_element_type=jnp.float32,
        ).reshape(span_len, kv_width)
        key_terms = lax.dynamic_update_slice_in_dim(key_terms, key_part, first_row, 0)
        value_terms = lax.dynamic_update_slice_in_dim(value_terms, value_part, first_row, 0)
        return (query_grad, key_terms, value_terms)

    query_grad, key_terms, value_terms = lax.fori_loop(
        0,
        span_count,
        grad_step,
        (
            jnp.zeros((tok_rows, KV_HEADS, groups, HEAD_DIM), jnp.float32),
            jnp.zeros((seq_len, kv_width), jnp.float32),
            jnp.zeros((seq_len, kv_width), jnp.float32),
        ),
    )
    key_grad, value_grad = (
        lax.psum_scatter(
            key_terms.astype(jnp.bfloat16), "shard", scatter_dimension=0, tiled=True
        ).astype(jnp.float32),
        lax.psum_scatter(
            value_terms.astype(jnp.bfloat16), "shard", scatter_dimension=0, tiled=True
        ).astype(jnp.float32),
    )
    query_back = rotate_back(
        (query_grad * score_scale).reshape(tok_rows, HEADS, HEAD_DIM), cosine, sine_table
    ).reshape(tok_rows, q_width)
    key_back = rotate_back(
        key_grad.reshape(tok_rows, KV_HEADS, HEAD_DIM), cosine, sine_table
    ).reshape(tok_rows, kv_width)
    qkv_grad_rows = jnp.concatenate([query_back, key_back, value_grad], 1).astype(jnp.bfloat16)
    qkv_weight_grad = lax.dot_general(
        normed_in, qkv_grad_rows, (((0,), (0,)), ((), ())), preferred_element_type=jnp.float32
    )
    in_norm_grad = lax.dot_general(
        qkv_grad_rows, qkv_full, (((1,), (1,)), ((), ())), preferred_element_type=jnp.float32
    )
    in_part, attn_gain_grad = rms_back(in_norm_grad, gain_one, normal_one, inverse_one)
    input_grad = (mid_grad + in_part).astype(jnp.bfloat16)
    dense_sums = (
        lax.psum_scatter(
            qkv_weight_grad.astype(jnp.bfloat16), "shard", scatter_dimension=0, tiled=True
        ).astype(jnp.float32),
        lax.psum_scatter(
            out_weight_grad.astype(jnp.bfloat16), "shard", scatter_dimension=0, tiled=True
        ).astype(jnp.float32),
        lax.psum_scatter(
            router_grad.astype(jnp.bfloat16), "shard", scatter_dimension=0, tiled=True
        ).astype(jnp.float32),
        lax.psum_scatter(
            attn_gain_grad.astype(jnp.bfloat16), "shard", scatter_dimension=0, tiled=True
        ).astype(jnp.float32),
        lax.psum_scatter(
            moe_gain_grad.astype(jnp.bfloat16), "shard", scatter_dimension=0, tiled=True
        ).astype(jnp.float32),
    )
    dense_totals = (
        lax.psum(dense_sums[0].astype(jnp.bfloat16), "expert").astype(jnp.float32),
        lax.psum(dense_sums[1].astype(jnp.bfloat16), "expert").astype(jnp.float32),
        lax.psum(dense_sums[2].astype(jnp.bfloat16), "expert").astype(jnp.float32),
        lax.psum(dense_sums[3].astype(jnp.bfloat16), "expert").astype(jnp.float32),
        lax.psum(dense_sums[4].astype(jnp.bfloat16), "expert").astype(jnp.float32),
    )
    return (
        output,
        input_grad,
        dense_totals[0],
        dense_totals[1],
        dense_totals[2],
        dense_totals[3],
        dense_totals[4],
        gate_up_grad,
        down_grad,
    )


GROUPS = 4
SHARDS = 8
rows_by_cols = ((1,), (0,))
rows_by_rows = ((1,), (1,))
cols_by_cols = ((0,), (0,))


def dot(one, two, dims):
    return lax.dot_general(one, two, (dims, ((), ())), preferred_element_type=jnp.float32)


def whole_spec(shape):
    return pl.BlockSpec(shape, lambda i, ids: (0,) * len(shape), pipeline_mode=pl.Buffered(1))


def block_spec(shape, index):
    return pl.BlockSpec(shape, lambda i, ids: index, pipeline_mode=pl.Buffered(1))


def out_spec(shape, index):
    return pl.BlockSpec(shape, lambda i, ids: index)


in_place = pl.BlockSpec(memory_space=pl.ANY)


def shaped(shape, dtype=jnp.bfloat16):
    return jax.ShapeDtypeStruct(shape, dtype)


def call(kernel, name, out_shape, in_specs, out_specs, args, scratch=(), aliases=None, flops=0, steps=1):
    moved = sum(a.size * a.dtype.itemsize for a in args[1:])
    return pl.pallas_call(
        kernel,
        name=name,
        out_shape=out_shape,
        grid_spec=pltpu.PrefetchScalarGridSpec(
            num_scalar_prefetch=1,
            grid=(steps,),
            in_specs=in_specs,
            out_specs=out_specs,
            scratch_shapes=list(scratch),
        ),
        input_output_aliases=aliases or {},
        compiler_params=pltpu.CompilerParams(
            vmem_limit_bytes=58 * 1024 * 1024, dimension_semantics=("arbitrary",)
        ),
        cost_estimate=pl.CostEstimate(flops=flops, transcendentals=0, bytes_accessed=moved),
    )(*args)


def place_rows(offsets, parts, height):
    count, fine, width = parts[0].shape

    def kernel(at, *refs):
        sources, target, done = refs[: len(parts)], refs[len(parts)], refs[-1]
        copies = []
        for n, source in enumerate(sources):
            for i in range(count):
                row = pl.multiple_of(at[n * count + i], 16)
                copies.append(
                    pltpu.make_async_copy(
                        source.at[i], target.at[pl.ds(row, fine)], done.at[n * count + i]
                    )
                )
        for copy in copies:
            copy.start()
        for copy in copies:
            copy.wait()

    return call(
        kernel,
        "place_rows",
        shaped((height, width), parts[0].dtype),
        [in_place] * len(parts),
        out_spec((height, width), (0, 0)),
        (offsets,) + tuple(parts),
        scratch=[pltpu.SemaphoreType.DMA((len(parts) * count,))],
    )


def dense_terms(offsets, products, parts, count, fine):
    height = products[0][0].shape[1]
    width = max(first + two.shape[1] for _, two, first in products)
    firsts = [first for _, _, first in products]

    def kernel(at, *refs):
        sources, targets, held = refs[: 2 * len(firsts)], refs[2 * len(firsts) : -1], refs[-1]
        total = {}
        for n, first in enumerate(firsts):
            found = dot(sources[2 * n][...], sources[2 * n + 1][...], cols_by_cols)
            total[first] = total[first] + found if first in total else found
        for first, found in total.items():
            held[:, first : first + found.shape[1]] = found.astype(jnp.bfloat16)
        for n, target in enumerate(targets):
            for i in range(count):
                row = pl.multiple_of(at[n * count + i], 16)
                target[i] = held[pl.ds(row, fine)]

    operands = [array for one, two, _ in products for array in (one, two)]
    return call(
        kernel,
        "dense_terms",
        [shaped((count, fine, width))] * parts,
        [whole_spec(array.shape) for array in operands],
        [out_spec((count, fine, width), (0, 0, 0))] * parts,
        (offsets,) + tuple(operands),
        scratch=[pltpu.VMEM((height, width), jnp.bfloat16)],
        flops=2 * height * width * products[0][0].shape[0],
    )


def pack_kernel(ids, up, gate_part, up_part, down, down_part, gain, *packs):
    width = down.shape[1]
    scale = gain[...]
    step = pl.program_id(0)

    def scaled(rows):
        return (rows.astype(jnp.float32) * scale).astype(jnp.bfloat16)

    for k in range(SHARDS):

        @pl.when(step == k)
        def _(k=k):
            downs, ups = packs[2 * k : 2 * k + 2]
            downs[0, :, :width] = down[...]
            downs[0, :, width:] = down_part[...]
            ups[0, :, : 2 * width] = scaled(up[...])
            part = down_part.shape[1]
            ups[0, :, 2 * width : 2 * width + part] = scaled(gate_part[...])
            ups[0, :, 2 * width + part :] = scaled(up_part[...])


def unpack_kernel(ids, *refs):
    pieces, gain, up_grad, down_grad = refs[: SHARDS + 2], refs[-3], refs[-2], refs[-1]
    scale = gain[...]
    step = pl.program_id(0)
    share = SHARDS // (pl.num_programs(0) - SHARDS)
    part = pieces[0].shape[2] // 3 - H
    edge = pieces[6].shape[2]

    def columns(k, first, count):
        if k < 6:
            found = pieces[k][0, :, first : first + count]
        elif first < edge:
            found = pieces[2 * k - 6][0, :, first : first + count]
        else:
            found = pieces[2 * k - 5][0, :, first - edge : first - edge + count]
        return found.astype(jnp.float32)

    for k in range(SHARDS):
        source = ids[2] ^ k

        @pl.when(step == k)
        def _(k=k):
            down_grad[...] = columns(k, 0, H)
            up_grad[:, :H] = columns(k, H, H) * scale
            up_grad[:, H:] = columns(k, 2 * H, H) * scale

        @pl.when(step == SHARDS + source // share)
        def _(k=k, source=source):
            at = pl.multiple_of(source % share * part, part)
            at_up = pl.multiple_of(H + source % share * part, part)
            down_grad[:, pl.ds(at, part)] = columns(k, 3 * H, part)
            up_grad[:, pl.ds(at, part)] = columns(k, 3 * H + part, part) * scale
            up_grad[:, pl.ds(at_up, part)] = columns(k, 3 * H + 2 * part, part) * scale


def turn(rows, cosine, sine):
    width = rows.shape[1]
    lanes = lax.broadcasted_iota(jnp.int32, (rows.shape[0], 128), 1)
    first = lanes % HEAD_DIM < HEAD_DIM // 2
    turned = []
    for at in range(0, width, 128):
        piece = rows[:, at : at + 128]
        swapped = jnp.where(
            first,
            pltpu.roll(piece, 128 - HEAD_DIM // 2, 1),
            pltpu.roll(piece, HEAD_DIM // 2, 1),
        )
        turned.append(piece * cosine + swapped * sine)
    return jnp.concatenate(turned, 1)


def qkv_kernel(ids, normed, weight, cosine, sine, queries, key_value):
    step = pl.program_id(0)
    found = dot(normed[...], weight[...], rows_by_cols)

    @pl.when(step < 3)
    def _():
        queries[...] = turn(found, cosine[...], sine[...]).astype(jnp.bfloat16)

    @pl.when(step == 3)
    def _():
        key_value[...] = turn(found, cosine[...], sine[...]).astype(jnp.bfloat16)

    @pl.when(step == 4)
    def _():
        key_value[...] = found.astype(jnp.bfloat16)


def attend_kernel(ids, queries, key_line, key_other, value_line, value_other, bias, attended, logs):
    scale = HEAD_DIM ** (-0.5)
    groups = HEADS // KV_HEADS
    hidden = bias[...]
    keys = jnp.concatenate([key_line[...], key_other[...]], 0)
    values = jnp.concatenate([value_line[...], value_other[...]], 0)
    lanes = lax.broadcasted_iota(jnp.int32, (queries.shape[0], 128), 1)
    totals = jnp.zeros((queries.shape[0], 128), jnp.float32)
    found = []
    for n in range(2 * groups):
        at = n // groups * HEAD_DIM
        scores = dot(
            queries[:, n * HEAD_DIM : (n + 1) * HEAD_DIM], keys[:, at : at + HEAD_DIM], rows_by_rows
        )
        scores = scores * scale + hidden
        top = jnp.max(scores, 1, keepdims=True)
        raised = jnp.exp(scores - top)
        total = jnp.sum(raised, 1, keepdims=True)
        probs = (raised / total).astype(jnp.bfloat16)
        found.append(dot(probs, values[:, at : at + HEAD_DIM], rows_by_cols))
        totals = jnp.where(lanes == n, top + jnp.log(total), totals)
    attended[...] = jnp.concatenate(found, 1).astype(jnp.bfloat16)
    logs[0] = totals


def attend_back_kernel(
    ids, queries, grads, key_line, key_other, value_line, value_other, bias, logs, cosine, sine,
    query_grad, key_mine, key_theirs, value_mine, value_theirs,
):
    scale = HEAD_DIM ** (-0.5)
    groups = HEADS // KV_HEADS
    hidden = bias[...]
    keys = jnp.concatenate([key_line[...], key_other[...]], 0)
    values = jnp.concatenate([value_line[...], value_other[...]], 0)
    half = key_line.shape[0]
    found = []
    key_found, value_found = [], []
    for n in range(2 * groups):
        own = n // groups
        at = own * HEAD_DIM
        head = slice(n * HEAD_DIM, (n + 1) * HEAD_DIM)
        query = queries[:, head]
        grad = grads[:, head]
        scores = dot(query, keys[:, at : at + HEAD_DIM], rows_by_rows) * scale + hidden
        probs = jnp.exp(scores - lane_value(logs[0], n))
        prob_grad = dot(grad, values[:, at : at + HEAD_DIM], rows_by_rows)
        row_dot = jnp.sum(probs * prob_grad, 1, keepdims=True)
        score_grad = (probs * (prob_grad - row_dot)).astype(jnp.bfloat16)
        found.append(dot(score_grad, keys[:, at : at + HEAD_DIM], rows_by_cols))
        key_part = dot(score_grad, query, cols_by_cols)
        value_part = dot(probs.astype(jnp.bfloat16), grad, cols_by_cols)
        if n % groups:
            key_found[own] = key_found[own] + key_part
            value_found[own] = value_found[own] + value_part
        else:
            key_found.append(key_part)
            value_found.append(value_part)
    found = jnp.concatenate(found, 1) * scale
    query_grad[...] = turn(found, cosine[...], -sine[...]).astype(jnp.bfloat16)
    key_found = (jnp.concatenate(key_found, 1) * scale).astype(jnp.bfloat16)
    value_found = jnp.concatenate(value_found, 1).astype(jnp.bfloat16)
    key_mine[...] = key_found[:half]
    key_theirs[...] = key_found[half:]
    value_mine[...] = value_found[:half]
    value_theirs[...] = value_found[half:]


def lane_value(rows, index):
    lanes = lax.broadcasted_iota(jnp.int32, rows.shape, 1)
    return jnp.sum(jnp.where(lanes == index, rows, 0.0), 1, keepdims=True)


def picks_of(extra, one, two):
    extra = extra.astype(jnp.float32)
    lanes = lax.broadcasted_iota(jnp.int32, (extra.shape[0], 2 * CAP), 1)
    wanted = jnp.where(lanes < CAP, lane_value(extra, one), lane_value(extra, two))
    place = jnp.where(lanes < CAP, lanes, lanes - CAP).astype(jnp.float32)
    return jnp.where(wanted == place, 1.0, 0.0).astype(jnp.bfloat16)


def grad_side_kernel(ids, half, other, down_one, down_two, *refs):
    gs, plain = refs[-2:]
    count = half.shape[0]
    for i in range(2 * count):
        source = half if i < count else other
        pick = picks_of(source[i % count, :, D:], ids[0], ids[1])
        found = dot(pick, source[i % count, :, :D], cols_by_cols).astype(jnp.bfloat16)
        gs[0, i * CAP : (i + 1) * CAP] = found[:CAP]
        gs[1, i * CAP : (i + 1) * CAP] = found[CAP:]
    width = down_one.shape[1]
    plain[:, :width] = dot(gs[0], down_one[...], rows_by_cols)
    plain[:, width:] = dot(gs[1], down_two[...], rows_by_cols)


def combine_rows(ids, rows, slots_half, slots_other, back_half, back_other):
    count = slots_half.shape[0]
    for i in range(2 * count):
        target = back_half if i < count else back_other
        slots = slots_half if i < count else slots_other
        pick = picks_of(slots[i % count], ids[0], ids[1])
        at = slice(i * CAP, (i + 1) * CAP)
        both = jnp.concatenate([rows[0, at], rows[1, at]], 0)
        target[i % count] = dot(pick, both, rows_by_cols).astype(jnp.bfloat16)


def row_side_kernel(
    ids, half, other, slots_half, slots_other, plain, gate_one, gate_two, up_one, up_two, *refs
):
    back_half, back_other, xs, hid, pg, gates, tokens, back_rows = refs[-8:]
    total = xs.shape[1]
    count = half.shape[0]
    for i in range(2 * count):
        source = half if i < count else other
        slots = slots_half if i < count else slots_other
        pick = picks_of(slots[i % count], ids[0], ids[1])
        found = dot(pick, source[i % count], cols_by_cols)
        extra = found[:, D:]
        found = found.astype(jnp.bfloat16)
        at = slice(i * CAP, (i + 1) * CAP)
        for n in range(2):
            xs[n, at] = found[n * CAP : (n + 1) * CAP, :D]
            own = extra[n * CAP : (n + 1) * CAP]
            gates[n, at] = lane_value(own, ids[n]) + lane_value(own, ids[n] + EXPERTS)
    first = 0
    second = hid.shape[1]
    for n, gate_weight, up_weight in ((0, gate_one, up_one), (1, gate_two, up_two)):
        width = up_weight.shape[1]
        gate_part = dot(xs[n], gate_weight[...], rows_by_cols)
        up_part = dot(xs[n], up_weight[...], rows_by_cols)
        at = slice(first, first + width)
        at_up = slice(second + first, second + first + width)
        own_plain = plain[:, at]
        sigma = 1.0 / (1.0 + jnp.exp(-gate_part))
        silu_value = gate_part * sigma
        hidden = silu_value * up_part
        tokens[n] = jnp.sum(hidden * own_plain, 1, keepdims=True)
        hid[:, at] = (hidden * gates[n]).astype(jnp.bfloat16)
        hidden_grad = own_plain * gates[n]
        slope = sigma * (1.0 + gate_part * (1.0 - sigma))
        pg[:, at] = (hidden_grad * up_part * slope).astype(jnp.bfloat16)
        pg[:, at_up] = (hidden_grad * silu_value).astype(jnp.bfloat16)
        row_grad = dot(pg[:, at], gate_weight[...], rows_by_rows)
        row_grad = row_grad + dot(pg[:, at_up], up_weight[...], rows_by_rows)
        back_rows[n, :, :D] = row_grad.astype(jnp.bfloat16)
        lanes = lax.broadcasted_iota(jnp.int32, (total, 128), 1)
        back_rows[n, :, D:] = jnp.where(lanes == ids[n], tokens[n], 0.0).astype(jnp.bfloat16)
        first += width
    combine_rows(ids, back_rows, slots_half, slots_other, back_half, back_other)


def out_side_kernel(ids, hid, *refs):
    slots, (down_one, down_two), (mine, theirs, out_rows) = refs[:4], refs[4:6], refs[6:]
    width = down_one.shape[1]
    count = slots[0].shape[0]
    out_rows[0] = dot(hid[:, :width], down_one[...], rows_by_rows).astype(jnp.bfloat16)
    out_rows[1] = dot(hid[:, width:], down_two[...], rows_by_rows).astype(jnp.bfloat16)
    for n, own in enumerate(slots):
        target = theirs if n % 2 else mine
        for i in range(count):
            pick = picks_of(own[i], ids[0], ids[1])
            at = slice((n * count + i) * CAP, (n * count + i + 1) * CAP)
            both = jnp.concatenate([out_rows[0, at], out_rows[1, at]], 0)
            place = i // 2 * 4 + n // 2 * 2 + i % 2
            target[place] = dot(pick, both, rows_by_cols).astype(jnp.bfloat16)


def terms_kernel(ids, xs, gs, pg, hid, terms):
    depth = terms.shape[1]
    width = hid.shape[1]
    for one, two, n, shift, first, count in (
        (gs, hid, 0, 0, 0, H),
        (xs, pg, 0, 0, H, H),
        (xs, pg, 0, width, 2 * H, H),
        (gs, hid, 1, H, 3 * H, width - H),
        (xs, pg, 1, H, 2 * H + width, width - H),
        (xs, pg, 1, width + H, H + 2 * width, width - H),
    ):
        found = dot(one[n], two[:, shift : shift + count], cols_by_cols).astype(jnp.bfloat16)
        for i in range(2):
            at = i ^ ids[2] % 2
            terms[pl.ds(at, 1), :, first : first + count] = found[i * depth : (i + 1) * depth][None]


def hop(values, pairs):
    return lax.ppermute(values, ("expert", "shard"), pairs)


def hop_pairs(step):
    return [
        (e * SHARDS + s, step(e, s)[0] * SHARDS + step(e, s)[1])
        for e in range(GROUPS)
        for s in range(SHARDS)
    ]


to_core = hop_pairs(lambda e, s: (e, s ^ 1))
to_line = [hop_pairs(lambda e, s, k=k: (e, s ^ (2 * k))) for k in range(4)]
over_middle = [
    (e * SHARDS + s, e * SHARDS + (s ^ 6)) for e in range(GROUPS) for s in range(2, 6)
]
from_middle = [
    (e * SHARDS + s, e * SHARDS + (s ^ 2)) for e in range(GROUPS) for s in range(2, 6)
]
to_middle = [(there, here) for here, there in from_middle]
to_first = hop_pairs(lambda e, s: (e ^ (1 + s % 2), s))
to_second = hop_pairs(lambda e, s: (e ^ (2 - s % 2), s))


def add_low(one, two):
    return (one.astype(jnp.float32) + two.astype(jnp.float32)).astype(jnp.bfloat16)


def total_of(line):
    return sum(piece.astype(jnp.float32) for piece in line)


class Flow:
    def __init__(self, steps):
        self.steps = steps
        self.result = None
        self.feed(None)

    def feed(self, values):
        try:
            self.want = self.steps.send(values)
        except StopIteration as stop:
            self.want = None
            self.result = stop.value


class Order:
    def __init__(self, mark):
        self.mark = mark

    def tie(self, values):
        values, self.mark = lax.optimization_barrier((values, self.mark))
        return values

    def round(self, flows, work=None):
        values, self.mark = lax.optimization_barrier(([f.want[0] for f in flows], self.mark))
        found = [hop(v, f.want[1]) for v, f in zip(values, flows)]
        found, work, self.mark = lax.optimization_barrier((found, work, self.mark))
        for flow, values in zip(flows, found):
            flow.feed(values)
        return work


def one_hop(values, pairs):
    found = yield values, pairs
    return found


def line_flows(own):
    return [Flow(one_hop(own, to_line[k])) for k in (1, 2, 3)]


def line_spread(own, marks):
    near = yield own, to_line[1]
    marks.append(near)
    two = jnp.stack([own, near])
    crossed = yield two, over_middle
    passed = yield crossed, from_middle
    at = lax.axis_index("shard") // 2
    return jnp.where((at == 1) | (at == 2), crossed, passed)


def line_collect(near, far):
    passed = yield jnp.stack(far), to_middle
    far = add_low(jnp.stack(far), passed)
    crossed = yield far, over_middle
    at = lax.axis_index("shard") // 2
    middle = (at == 1) | (at == 2)
    both = jnp.stack(near).astype(jnp.float32) + jnp.where(middle, crossed, 0).astype(jnp.float32)
    back = yield both[1].astype(jnp.bfloat16), to_line[1]
    return both[0] + back.astype(jnp.float32)


def by_distance(far):
    at = lax.axis_index("shard") // 2
    middle = (at == 1) | (at == 2)
    return [jnp.where(middle, far[1 - i], far[i]) for i in range(2)]


def spread_pair(pieces):
    two = jnp.stack(pieces) if isinstance(pieces, list) else pieces
    first = yield two, to_first
    four = jnp.concatenate([two, first])
    second = yield four, to_second
    eight = jnp.concatenate([four, second])
    other = yield eight, to_core
    return eight, other


def spread_all(line):
    four = jnp.stack(line)
    first = yield four, to_first
    eight = jnp.concatenate([four, first])
    second = yield eight, to_second
    half = jnp.concatenate([eight, second])
    other = yield half, to_core
    return half, other


def collect_pair(mine, theirs):
    found = yield theirs, to_core
    keep, give = add_low(mine[:4], found[:4]), add_low(mine[4:], found[4:])
    found = yield give, to_second
    keep, give = add_low(keep[:2], found[:2]), add_low(keep[2:], found[2:])
    found = yield give, to_first
    return [add_low(keep[i], found[i]) for i in range(2)]


def collect_all(mine, theirs):
    found = yield theirs, to_core
    keep, give = add_low(mine[:8], found[:8]), add_low(mine[8:], found[8:])
    found = yield give, to_second
    keep, give = add_low(keep[:4], found[:4]), add_low(keep[4:], found[4:])
    found = yield give, to_first
    return [add_low(keep[i], found[i]) for i in range(4)]


def share_flow(own, places):
    first = yield own, to_first
    pair = jnp.stack([own, first])
    second = yield pair, to_second
    quarters = jnp.concatenate([pair, second])
    return jnp.concatenate(
        [lax.dynamic_index_in_dim(quarters, place, 0, keepdims=False) for place in places]
    )


def local_hops(
    tokens_in,
    output_cotangent,
    routes,
    doc_ids,
    picture_starts,
    qkv_weight,
    out_weight,
    router_weight,
    attn_gain,
    moe_gain,
    gate_up_weight,
    down_weight,
):
    low = jnp.bfloat16
    full = jnp.float32
    rows = tokens_in.shape[0]
    seq_len = doc_ids.shape[1]
    q_width = HEADS * HEAD_DIM
    kv_width = KV_HEADS * HEAD_DIM
    qkv_width = q_width + 2 * kv_width
    group_at = lax.axis_index("expert")
    shard_at = lax.axis_index("shard")
    own_experts = EXPERTS // GROUPS
    whole = own_experts // SHARDS * SHARDS
    split = own_experts - whole
    share = SHARDS // split
    part = H // share
    hid_width = H + part
    depth = gate_up_weight.shape[0]
    height = SHARDS * depth
    fine = depth // GROUPS
    pad = 128 - EXPERTS
    gain_one = attn_gain.astype(full)[:, None]
    gain_two = moe_gain.astype(full)[:, None]
    expert_one = group_at * own_experts + shard_at
    expert_two = group_at * own_experts + whole + shard_at // share
    ids = jnp.stack([expert_one, expert_two, shard_at])
    order = Order(jnp.zeros((8, 128), full))

    spot = jnp.arange(GROUPS * SHARDS, dtype=jnp.int32)
    spot_core = spot // 8 % 2
    spot_mate = 1 + (shard_at % 2 ^ spot_core)
    spot_q = spot % 8 // 2
    spot_group = jnp.where(spot_q == 1, spot_mate, jnp.where(spot_q == 2, 3 - spot_mate, spot_q))
    spot_line = spot // 16 * 2 + spot % 2
    fine_at = (shard_at ^ (2 * spot_line + spot_core)) * depth + (group_at ^ spot_group) * fine
    half_core = spot // 16
    half_mate = 1 + (shard_at % 2 ^ half_core)
    half_q = spot % 16 // 4
    half_group = jnp.where(half_q == 1, half_mate, jnp.where(half_q == 2, 3 - half_mate, half_q))
    half_at = (shard_at ^ (2 * (spot % 4) + half_core)) * depth + (group_at ^ half_group) * fine

    expert_ids = jnp.arange(EXPERTS, dtype=jnp.int32)
    hits = jnp.any(routes[:, :, None] == expert_ids[None, None, :], 1)
    earlier = jnp.arange(rows)[:, None] > jnp.arange(rows)[None, :]
    before = dot(earlier.astype(low), hits.astype(low), rows_by_cols)
    slots = jnp.where(hits & (before < CAP), before, -1.0)
    kept = slots >= 0
    grad_pay = jnp.concatenate(
        [output_cotangent, jnp.pad(slots.astype(low), ((0, 0), (0, pad)))], 1
    )

    def fine_rows(array):
        return lax.dynamic_slice_in_dim(array, group_at * fine, fine, 0)

    qkv_own = fine_rows(qkv_weight).astype(full) * fine_rows(gain_one)
    router_own = fine_rows(router_weight).astype(full) * fine_rows(gain_two)
    dense_own = jnp.concatenate([qkv_own, jnp.pad(router_own, ((0, 0), (0, pad)))], 1).astype(low)
    out_own = fine_rows(out_weight)

    def column_spec(width, index):
        return pl.BlockSpec((depth, width), lambda k, ids: (0, index(ids[2] ^ k)))

    to_parts = H // part
    packs = call(
        pack_kernel,
        "pack",
        [shaped((1, depth, hid_width)), shaped((1, depth, 2 * hid_width))] * SHARDS,
        [
            column_spec(2 * H, lambda d: d),
            column_spec(part, lambda d: (whole + d // share) * 2 * to_parts + d % share),
            column_spec(part, lambda d: (whole + d // share) * 2 * to_parts + to_parts + d % share),
            column_spec(H, lambda d: d),
            column_spec(part, lambda d: (whole + d // share) * to_parts + d % share),
            pl.BlockSpec((depth, 1), lambda d, ids: (0, 0)),
        ],
        [
            out_spec((1, depth, hid_width), (0, 0, 0)),
            out_spec((1, depth, 2 * hid_width), (0, 0, 0)),
        ]
        * SHARDS,
        (ids, gate_up_weight, gate_up_weight, gate_up_weight, down_weight, down_weight, gain_two),
        steps=SHARDS,
    )

    to_shard = [hop_pairs(lambda e, s, k=k: (e, s ^ k)) for k in range(SHARDS)]
    shard_rows = (shard_at ^ jnp.arange(SHARDS, dtype=jnp.int32)) * depth

    def exchange(pieces):
        flows = [[Flow(one_hop(piece, to_shard[k])) for piece in pieces[k]] for k in range(1, SHARDS)]
        near = [flows[k - 1][n] for n in range(len(pieces[0])) for k in (2, 3)]
        far = [flows[k - 1][n] for n in range(len(pieces[0])) for k in (4, 5, 6, 7)]
        return flows, flows[0], near, far

    def exchanged(pieces, flows, n):
        parts = [pieces[0][n]] + [flow[n].result for flow in flows]
        return place_rows(shard_rows, parts, height)

    s_pieces = [packs[2 * k : 2 * k + 2] for k in range(SHARDS)]
    s_flows, core, near, far = exchange(s_pieces)

    def some(flows, count):
        taken = flows[:count]
        del flows[:count]
        return taken

    w = line_flows(dense_own)
    o = line_flows(out_own)
    g_marks, x_marks = [], []
    g_line = Flow(line_spread(grad_pay, g_marks))
    order.round(w[:2])
    w_near = Flow(spread_pair([dense_own, w[0].result]))
    order.round([w[2], w_near, g_line])
    w_far = Flow(spread_pair([w[1].result, w[2].result]))
    g_near = Flow(spread_pair([grad_pay, g_marks[0]]))
    order.round([w_near, w_far] + some(far, 1) + some(near, 1) + core)
    order.round([w_near, w_far] + o)
    o_all = Flow(spread_all([out_own] + [flow.result for flow in o]))
    order.round([w_far, o_all])
    dense_full = place_rows(fine_at, w_near.result + w_far.result, height)
    router_full = dense_full[:, qkv_width:]

    tokens_f = tokens_in.astype(full)
    inverse_one = lax.rsqrt(jnp.mean(tokens_f * tokens_f, -1, keepdims=True) + norm_eps)
    normal_one = tokens_f * inverse_one
    normed_in = normal_one.astype(low)
    query_pos = shard_at * rows + jnp.arange(rows, dtype=jnp.int32)
    cosine, sine = rope_tables(query_pos, HEAD_DIM)
    cosine = jnp.tile(cosine[:, 0], (1, 4))
    sine = jnp.tile(jnp.concatenate([-sine[:, 0], sine[:, 0]], 1), (1, 2))
    tile = 512
    queries, key_value = call(
        qkv_kernel,
        "qkv",
        (shaped((rows, q_width)), shaped((rows, 2 * kv_width))),
        [
            whole_spec((rows, D)),
            pl.BlockSpec((D, tile), lambda j, ids: (0, j)),
            whole_spec((rows, 128)),
            whole_spec((rows, 128)),
        ],
        [
            pl.BlockSpec((rows, tile), lambda j, ids: (0, jnp.minimum(j, 2))),
            pl.BlockSpec((rows, tile), lambda j, ids: (0, jnp.maximum(j - 3, 0))),
        ],
        (ids, normed_in, dense_full, cosine, sine),
        flops=2 * rows * D * qkv_width,
        steps=qkv_width // tile,
    )
    queries, key_value = order.round(
        [o_all, g_near, g_line] + some(near, 1), (queries, key_value)
    )
    kv = line_flows(key_value)
    order.round(kv + [o_all, g_near])
    kv_line = jnp.concatenate([key_value] + [flow.result for flow in kv])
    kv_core = Flow(one_hop(kv_line, to_core))
    out_full = place_rows(half_at, o_all.result, height)
    out_full = order.round([kv_core], out_full)
    kv_other = kv_core.result
    block_order = jnp.arange(SHARDS, dtype=jnp.int32)
    block_order = shard_at ^ (block_order % 4 * 2 + block_order // 4)
    key_pos = (
        block_order[:, None] * rows + jnp.arange(rows, dtype=jnp.int32)[None, :]
    ).reshape(seq_len)
    doc_blocks = doc_ids[0].reshape(SHARDS, rows)
    block_hits = block_order[:, None] == jnp.arange(SHARDS)[None, :]
    key_doc = jnp.sum(
        jnp.where(block_hits[:, :, None], doc_blocks[None], 0), 1
    ).reshape(seq_len)
    query_doc = key_doc[:rows]
    key_pic = picture_ids(key_pos, picture_starts[0], SLOT, PIECE)
    query_pic = key_pic[:rows]
    visible = allowed(query_pos, key_pos, query_doc, key_doc, query_pic, key_pic)
    bias = jnp.where(visible, 0.0, masked_score)
    pairs = KV_HEADS // 2
    q_tile = q_width // pairs
    kv_tile = kv_width // pairs
    half_len = seq_len // 2

    def kv_specs(first):
        return [pl.BlockSpec((half_len, kv_tile), lambda j, ids: (0, first + j))] * 2

    q_spec = pl.BlockSpec((rows, q_tile), lambda j, ids: (0, j))
    log_spec = pl.BlockSpec((1, rows, 128), lambda j, ids: (j, 0, 0))
    attended, logs = call(
        attend_kernel,
        "attend",
        (shaped((rows, q_width)), shaped((pairs, rows, 128), full)),
        [q_spec] + kv_specs(0) + kv_specs(pairs) + [whole_spec((rows, seq_len))],
        [q_spec, log_spec],
        (ids, queries, kv_line, kv_other, kv_line, kv_other, bias),
        flops=4 * rows * seq_len * q_width,
        steps=pairs,
    )
    branch = dot(attended, out_full, rows_by_rows)
    middle = tokens_f + branch
    inverse_two = lax.rsqrt(jnp.mean(middle * middle, -1, keepdims=True) + norm_eps)
    normal_two = middle * inverse_two
    normed_mid = normal_two.astype(low)
    logits = dot(normed_mid, router_full, rows_by_cols)[:, :EXPERTS]
    logits = jnp.where(hits, logits, masked_score)
    gates = jnp.exp(logits - jnp.max(logits, -1, keepdims=True))
    gates = jnp.where(hits, gates, 0.0)
    gates = gates / jnp.sum(gates, -1, keepdims=True)
    gate_low = gates.astype(low)
    gate_rest = (gates - gate_low.astype(full)).astype(low)
    row_pay = jnp.concatenate(
        [normed_mid, gate_low, gate_rest, jnp.zeros((rows, 128 - 2 * EXPERTS), low)], 1
    )

    slot_rows = GROUPS * SHARDS * CAP
    step_rows = slot_rows // 2
    blocks = 2 * GROUPS
    pay_spec = whole_spec((blocks, rows, D + 128))
    pay_out = out_spec((blocks, rows, D + 128), (0, 0, 0))
    slot_spec = block_spec((blocks, rows, 128), (0, 0, D // 128))
    up_specs = [
        block_spec((height, H), (0, 0)),
        block_spec((height, part), (0, 2 * to_parts)),
        block_spec((height, H), (0, 1)),
        block_spec((height, part), (0, 2 * to_parts + 1)),
    ]
    down_specs = [
        block_spec((height, H), (0, 0)),
        block_spec((height, part), (0, H // part)),
    ]
    back_shape = shaped((blocks, rows, D + 128))
    gs_shape = shaped((2, slot_rows, D))
    kept_shapes = (gs_shape, shaped((slot_rows, hid_width)), shaped((slot_rows, 2 * hid_width)))
    kept_rows = ()

    gs, plain = (), []

    def grad_side(k):
        nonlocal gs
        gs_next, found = call(
            grad_side_kernel,
            "grad_side",
            (gs_shape, shaped((step_rows, hid_width), full)),
            [pay_spec, pay_spec] + down_specs + [in_place] * len(gs),
            [
                out_spec((2, step_rows, D), (0, k, 0)),
                out_spec((step_rows, hid_width), (0, 0)),
            ],
            (ids,) + (g_near, g_far)[k].result + (owned_down, owned_down) + gs,
            aliases={5: 0} if gs else None,
            flops=2 * step_rows * D * (hid_width + 2 * rows),
        )
        gs = (gs_next,)
        return found

    def row_side(k):
        nonlocal kept_rows
        half_back, other_back, *kept_next = call(
            row_side_kernel,
            "row_side",
            (back_shape, back_shape) + kept_shapes,
            [pay_spec, pay_spec, slot_spec, slot_spec, whole_spec((step_rows, hid_width))]
            + up_specs
            + [in_place] * len(kept_rows),
            [
                pay_out,
                pay_out,
                out_spec((2, step_rows, D), (0, k, 0)),
                out_spec((step_rows, hid_width), (k, 0)),
                out_spec((step_rows, 2 * hid_width), (k, 0)),
            ],
            (ids,)
            + (x_near, x_far)[k].result
            + (g_near, g_far)[k].result
            + (plain[k],)
            + (owned_up,) * 4
            + kept_rows,
            scratch=[
                pltpu.VMEM((2, step_rows, 1), full),
                pltpu.VMEM((2, step_rows, 1), full),
                pltpu.VMEM((2, step_rows, D + 128), low),
            ],
            aliases={10: 2, 11: 3, 12: 4} if kept_rows else None,
            flops=8 * step_rows * D * (hid_width + rows),
        )
        kept_rows = tuple(kept_next)
        return half_back, other_back

    row_pay = order.round([g_near, g_line] + some(far, 3), row_pay)
    x_line = Flow(line_spread(row_pay, x_marks))
    g_far = Flow(spread_pair(g_line.result))
    order.round([x_line, g_far] + some(far, 1))
    x_near = Flow(spread_pair([row_pay, x_marks[0]]))
    owned_down = exchanged(s_pieces, s_flows, 0)
    owned_down = order.round([x_line, x_near, g_far] + some(near, 1), owned_down)
    plain = [order.round([x_line, x_near, g_far] + some(far, 1), grad_side(0))]
    x_far = Flow(spread_pair(x_line.result))
    plain.append(order.round([x_near, x_far] + some(far, 1) + near, grad_side(1)))
    order.round([x_far] + far)
    owned_up = exchanged(s_pieces, s_flows, 1)
    back_near = order.round([x_far], row_side(0))
    b_near = Flow(collect_pair(*back_near))
    back_far = order.round([b_near], row_side(1))
    b_far = Flow(collect_pair(*back_far))

    xs, hid, pg = kept_rows

    def lane_block(i, ids):
        return (0, 0, i ^ ids[2] // 2)

    terms = call(
        terms_kernel,
        "terms",
        shaped((SHARDS, depth, 3 * hid_width)),
        [
            pl.BlockSpec((2, slot_rows, 2 * depth), lane_block),
            pl.BlockSpec((2, slot_rows, 2 * depth), lane_block),
            whole_spec((slot_rows, 2 * hid_width)),
            whole_spec((slot_rows, hid_width)),
        ],
        pl.BlockSpec((2, depth, 3 * hid_width), lambda i, ids: (i, 0, 0)),
        (ids, xs, gs[0], pg, hid),
        flops=2 * slot_rows * D * 3 * hid_width,
        steps=4,
    )
    terms = order.round([b_near, b_far], terms)
    t_edge = 2 * H
    t_pieces = [[terms[k][None]] for k in range(6)]
    t_pieces += [[terms[k, :, :t_edge][None], terms[k, :, t_edge:][None]] for k in (6, 7)]
    t_flows = [[Flow(one_hop(piece, to_shard[k])) for piece in t_pieces[k]] for k in range(1, SHARDS)]
    core, near = t_flows[0], t_flows[1] + t_flows[2]
    far = t_flows[5][:1] + t_flows[3] + t_flows[4] + t_flows[5][1:] + t_flows[6]

    moe_blocks = call(
        out_side_kernel,
        "out_side",
        (shaped((2 * blocks, rows, D)),) * 2,
        [whole_spec((slot_rows, hid_width))] + [slot_spec] * 4 + down_specs,
        [out_spec((2 * blocks, rows, D), (0, 0, 0))] * 2,
        (ids, hid) + g_near.result + g_far.result + (owned_down, owned_down),
        scratch=[pltpu.VMEM((2, slot_rows, D), low)],
        flops=2 * slot_rows * D * (hid_width + 2 * rows),
    )
    moe_blocks = order.round([b_near, b_far] + some(far, 1), moe_blocks)
    moe = Flow(collect_all(*moe_blocks))
    b_line = [Flow(one_hop(b_near.result[1], to_line[1]))]
    order.round([b_far, moe] + b_line + core)
    b_line += [
        Flow(one_hop(piece, to_line[2 + i])) for i, piece in enumerate(by_distance(b_far.result))
    ]
    order.round(b_line[1:] + [moe] + some(near, 1))
    grad_sum = total_of([b_near.result[0]] + [flow.result for flow in b_line])

    gate_grad = jnp.where(kept, grad_sum[:, D : D + EXPERTS], 0.0)
    logit_grad = gates * (gate_grad - jnp.sum(gates * gate_grad, -1, keepdims=True))
    logit_grad = jnp.pad(logit_grad.astype(low), ((0, 0), (0, pad)))
    scaled_two = grad_sum[:, :D] + dot(logit_grad, router_full, rows_by_rows)
    grad_out = output_cotangent.astype(full)
    mean_two = jnp.mean(scaled_two * normal_two, -1, keepdims=True)
    mid_grad = grad_out + inverse_two * (scaled_two - normal_two * mean_two)
    branch_grad = mid_grad.astype(low)
    attended_grad = dot(branch_grad, out_full, rows_by_cols).astype(low)

    kv_out = pl.BlockSpec((half_len, kv_tile), lambda j, ids: (0, j))
    query_back, key_mine, key_theirs, value_mine, value_theirs = call(
        attend_back_kernel,
        "attend_back",
        (shaped((rows, q_width)),) + (shaped((half_len, kv_width)),) * 4,
        [q_spec, q_spec]
        + kv_specs(0)
        + kv_specs(pairs)
        + [whole_spec((rows, seq_len)), log_spec, whole_spec((rows, 128)), whole_spec((rows, 128))],
        [q_spec] + [kv_out] * 4,
        (ids, queries, attended_grad, kv_line, kv_other, kv_line, kv_other, bias, logs, cosine, sine),
        flops=10 * rows * seq_len * q_width,
        steps=pairs,
    )
    kv_theirs = jnp.concatenate([key_theirs, value_theirs], 1)
    kv_mine = jnp.concatenate([key_mine, value_mine], 1)
    def dense_flow(products):
        return dense_terms(half_at, products, 2, 4 * GROUPS, fine)

    early_blocks = dense_flow([(branch_grad, attended, 0), (normed_in, query_back, q_width)])
    kv_theirs, kv_mine, early_blocks = order.round(
        [moe] + some(far, 2) + near, (kv_theirs, kv_mine, early_blocks)
    )
    kv_core = Flow(one_hop(kv_theirs, to_core))
    early = Flow(collect_all(*early_blocks))
    order.round([kv_core, early])
    kv_half = add_low(kv_mine, kv_core.result).reshape(4, rows, 2 * kv_width)
    kv = [Flow(one_hop(kv_half[k], to_line[k])) for k in (1, 2, 3)]
    order.round(kv + [early])
    m_line = Flow(line_collect(moe.result[:2], moe.result[2:]))
    kv_grad = total_of([kv_half[0]] + [flow.result for flow in kv])

    def line_of(blocks):
        return [Flow(one_hop(blocks[k], to_line[k])) for k in (1, 2, 3)]

    def swapped(values):
        lanes = jnp.arange(values.shape[1]) % HEAD_DIM < HEAD_DIM // 2
        return jnp.where(
            lanes[None], jnp.roll(values, -HEAD_DIM // 2, 1), jnp.roll(values, HEAD_DIM // 2, 1)
        )

    key_grad = kv_grad[:, :kv_width]
    key_back = key_grad * jnp.tile(cosine, (1, pairs)) - swapped(key_grad) * jnp.tile(sine, (1, pairs))
    kv_rows = jnp.concatenate([key_back, kv_grad[:, kv_width:]], 1).astype(low)
    scaled_one = dot(query_back, dense_full[:, :q_width], rows_by_rows) + dot(
        kv_rows, dense_full[:, q_width:qkv_width], rows_by_rows
    )
    mean_one = jnp.mean(scaled_one * normal_one, -1, keepdims=True)
    input_grad = mid_grad + inverse_one * (scaled_one - normal_one * mean_one)
    pad_lanes = jnp.arange(128)[None, :]

    def marker(lane):
        return jnp.broadcast_to(jnp.where(pad_lanes == lane, 1.0, 0.0), (rows, 128)).astype(low)

    late_blocks = dense_flow(
        [
            (normed_in, kv_rows, 0),
            (normed_mid, logit_grad, 2 * kv_width),
            ((scaled_two * normal_two).astype(low), marker(EXPERTS), 2 * kv_width),
        ]
    )
    late_blocks = order.round([early, m_line] + some(far, 2), late_blocks)
    late = Flow(collect_all(*late_blocks))
    input_grad = order.round(
        [late, m_line], input_grad.astype(low)
    )
    early_line = line_of(early.result)
    order.round([late, m_line] + early_line)
    order.round([late] + far)
    late_line = line_of(late.result)
    spots = jnp.arange(GROUPS, dtype=jnp.int32) ^ group_at
    mate = 1 + shard_at % 2
    spots = jnp.where(spots == mate, 1, jnp.where(spots == 3 - mate, 2, spots))
    places = [spots[i] for i in range(GROUPS)]

    t_parts = t_pieces[0] + [flow.result for flows in t_flows for flow in flows]

    def to_expert(k, ids):
        return (0, jnp.where(k < SHARDS, ids[2] ^ k, k))

    gate_up_grad, down_grad = call(
        unpack_kernel,
        "unpack",
        (shaped(gate_up_weight.shape, full), shaped(down_weight.shape, full)),
        [whole_spec(piece.shape) for piece in t_parts] + [whole_spec((depth, 1))],
        [pl.BlockSpec((depth, 2 * H), to_expert), pl.BlockSpec((depth, H), to_expert)],
        (ids,) + tuple(t_parts) + (gain_two,),
        steps=own_experts,
    )
    gate_up_grad, down_grad = order.round(late_line, (gate_up_grad, down_grad))
    own_sum = jnp.concatenate(
        [
            total_of([flow.result[0]] + [piece.result for piece in line]).astype(low)
            for flow, line in ((early, early_line), (late, late_line))
        ],
        1,
    )
    share_all = Flow(share_flow(own_sum, places))
    order.round([share_all])
    order.round([share_all])
    output = (middle + m_line.result).astype(low)
    dense_sums = share_all.result.astype(full)
    early_sum, late_sum = dense_sums[:, : 2 * q_width], dense_sums[:, 2 * q_width :]
    out_sum, query_sum = early_sum[:, :q_width], early_sum[:, q_width:]

    qkv_sum = jnp.concatenate([query_sum, late_sum[:, : 2 * kv_width]], 1)
    return (
        output,
        input_grad,
        qkv_sum * gain_one,
        out_sum,
        late_sum[:, 2 * kv_width : 2 * kv_width + EXPERTS] * gain_two,
        jnp.sum(qkv_sum * qkv_weight.astype(full), 1),
        late_sum[:, 2 * kv_width + EXPERTS] / gain_two[:, 0],
        gate_up_grad,
        down_grad,
    )


def solution(mesh):
    body = local
    if mesh.shape["expert"] == GROUPS and mesh.shape["shard"] == SHARDS:
        body = local_hops
    return jax.shard_map(
        body,
        mesh=mesh,
        in_specs=(
            P(("expert", "shard"), None),
            P(("expert", "shard"), None),
            P(("expert", "shard"), None),
            P("expert", None),
            P("expert", None),
            P("shard", None),
            P("shard", None),
            P("shard", None),
            P("shard"),
            P("shard"),
            P("shard", "expert"),
            P("shard", "expert"),
        ),
        out_specs=(
            P(("expert", "shard"), None),
            P(("expert", "shard"), None),
            P("shard", None),
            P("shard", None),
            P("shard", None),
            P("shard"),
            P("shard"),
            P("shard", "expert"),
            P("shard", "expert"),
        ),
        check_vma=False,
    )
```

```python
import jax
import jax.numpy as jnp
from jax import lax
from jax.experimental import pallas as pl
from jax.experimental.pallas import tpu as pltpu
from jax.sharding import PartitionSpec as P

D = 1536
HEADS = 24
KV_HEADS = 8
HEAD_DIM = 64
H = 512
EXPERTS = 40
TOP = 8
PIECE = 256
SLOT = 512
CAP = 32


norm_eps = 1e-06
rope_base = 10000.0
masked_score = -1e30


def rope_tables(positions, head_dim):
    half_dim = head_dim // 2
    frequency = rope_base ** (-2.0 * jnp.arange(half_dim, dtype=jnp.float32) / head_dim)
    angles = positions.astype(jnp.float32)[:, None] * frequency[None, :]
    return (jnp.cos(angles)[:, None, :], jnp.sin(angles)[:, None, :])


def rotate(values, cosine, sine_table):
    half_dim = values.shape[-1] // 2
    first_half = values[..., :half_dim]
    second = values[..., half_dim:]
    return jnp.concatenate(
        [first_half * cosine - second * sine_table, second * cosine + first_half * sine_table], -1
    )


def rotate_back(grad_rows, cosine, sine_table):
    half_dim = grad_rows.shape[-1] // 2
    first_half = grad_rows[..., :half_dim]
    second = grad_rows[..., half_dim:]
    return jnp.concatenate(
        [first_half * cosine + second * sine_table, second * cosine - first_half * sine_table], -1
    )


def rms_norm(values, gain):
    inverse = lax.rsqrt(jnp.mean(values * values, -1, keepdims=True) + norm_eps)
    normal = values * inverse
    return (normal * gain, normal, inverse)


def rms_back(grad_rows, gain, normal, inverse):
    scaled = grad_rows * gain
    grad_in = inverse * (scaled - normal * jnp.mean(scaled * normal, -1, keepdims=True))
    return (grad_in, jnp.sum(grad_rows * normal, 0))


def picture_ids(positions, starts, slot_len, piece_len):
    slot_index = positions // slot_len
    picked_slot = slot_index[:, None] == jnp.arange(starts.shape[0], dtype=jnp.int32)[None, :]
    piece_begin = jnp.sum(jnp.where(picked_slot, starts[None, :], 0), axis=1)
    inside = (positions >= piece_begin) & (positions < piece_begin + piece_len)
    return jnp.where(inside, slot_index, -1)


def allowed(query_pos, key_pos, query_doc, key_doc, query_pic, key_pic):
    same_doc = query_doc[:, None] == key_doc[None, :]
    earlier = key_pos[None, :] <= query_pos[:, None]
    same_pic = (query_pic[:, None] == key_pic[None, :]) & (query_pic[:, None] >= 0)
    return same_doc & (earlier | same_pic)


def local(
    tokens_in,
    output_cotangent,
    routes,
    doc_ids,
    picture_starts,
    qkv_weight,
    out_weight,
    router_weight,
    attn_gain,
    moe_gain,
    gate_up_weight,
    down_weight,
):
    qkv_full, out_full, router_full, gain_first, gain_second = (
        lax.all_gather(qkv_weight, "shard", axis=0, tiled=True),
        lax.all_gather(out_weight, "shard", axis=0, tiled=True),
        lax.all_gather(router_weight, "shard", axis=0, tiled=True),
        lax.all_gather(attn_gain, "shard", axis=0, tiled=True),
        lax.all_gather(moe_gain, "shard", axis=0, tiled=True),
    )
    gain_one = gain_first.astype(jnp.float32)
    gain_two = gain_second.astype(jnp.float32)
    tok_rows = tokens_in.shape[0]
    seq_len = doc_ids.shape[1]
    groups = HEADS // KV_HEADS
    q_width = HEADS * HEAD_DIM
    kv_width = KV_HEADS * HEAD_DIM
    score_scale = HEAD_DIM ** (-0.5)
    shard_at = lax.axis_index("shard")
    query_pos = shard_at * tok_rows + jnp.arange(tok_rows, dtype=jnp.int32)
    key_pos = jnp.arange(seq_len, dtype=jnp.int32)
    key_doc = doc_ids[0]
    key_pic = picture_ids(key_pos, picture_starts[0], SLOT, PIECE)
    query_doc = lax.dynamic_slice_in_dim(key_doc, shard_at * tok_rows, tok_rows)
    query_pic = lax.dynamic_slice_in_dim(key_pic, shard_at * tok_rows, tok_rows)
    tokens_f = tokens_in.astype(jnp.float32)
    normed_one, normal_one, inverse_one = rms_norm(tokens_f, gain_one)
    normed_in = normed_one.astype(jnp.bfloat16)
    qkv_rows = jnp.dot(normed_in, qkv_full, preferred_element_type=jnp.float32)
    cosine, sine_table = rope_tables(query_pos, HEAD_DIM)
    queries = (
        rotate(qkv_rows[:, :q_width].reshape(tok_rows, HEADS, HEAD_DIM), cosine, sine_table)
        .astype(jnp.bfloat16)
        .reshape(tok_rows, KV_HEADS, groups, HEAD_DIM)
    )
    key_local = (
        rotate(
            qkv_rows[:, q_width : q_width + kv_width].reshape(tok_rows, KV_HEADS, HEAD_DIM),
            cosine,
            sine_table,
        )
        .astype(jnp.bfloat16)
        .reshape(tok_rows, kv_width)
    )
    value_local = qkv_rows[:, q_width + kv_width :].astype(jnp.bfloat16)
    all_keys, all_values = (
        lax.all_gather(key_local, "shard", axis=0, tiled=True),
        lax.all_gather(value_local, "shard", axis=0, tiled=True),
    )
    span_len = min(512, seq_len)
    span_count = seq_len // span_len

    def block_scores(first_row, key_rows):
        key_block = lax.dynamic_slice_in_dim(key_rows, first_row, span_len, 0).reshape(
            span_len, KV_HEADS, HEAD_DIM
        )
        raw_scores = (
            jnp.einsum("tgrd,kgd->tgrk", queries, key_block, preferred_element_type=jnp.float32)
            * score_scale
        )
        block_pos = lax.dynamic_slice_in_dim(key_pos, first_row, span_len)
        block_doc = lax.dynamic_slice_in_dim(key_doc, first_row, span_len)
        block_pic = lax.dynamic_slice_in_dim(key_pic, first_row, span_len)
        visible = allowed(query_pos, block_pos, query_doc, block_doc, query_pic, block_pic)[
            :, None, None, :
        ]
        return (raw_scores, visible, key_block)

    def value_block_at(first_row, value_rows):
        return lax.dynamic_slice_in_dim(value_rows, first_row, span_len, 0).reshape(
            span_len, KV_HEADS, HEAD_DIM
        )

    def max_step(step_index, carry):
        run_max, run_sum = carry
        raw_scores, visible, key_block = block_scores(step_index * span_len, all_keys)
        masked = jnp.where(visible, raw_scores, masked_score)
        new_max = jnp.maximum(run_max, jnp.max(masked, -1))
        shifted = jnp.where(visible, jnp.exp(masked - new_max[..., None]), 0.0)
        return (new_max, run_sum * jnp.exp(run_max - new_max) + jnp.sum(shifted, -1))

    stat_shape = (tok_rows, KV_HEADS, groups)
    run_max, run_sum = lax.fori_loop(
        0,
        span_count,
        max_step,
        (jnp.full(stat_shape, masked_score, jnp.float32), jnp.zeros(stat_shape, jnp.float32)),
    )
    log_total = run_max + jnp.log(run_sum)

    def probs_of(raw_scores, visible):
        return jnp.exp(jnp.where(visible, raw_scores - log_total[..., None], masked_score))

    def value_step(step_index, summed):
        first_row = step_index * span_len
        raw_scores, visible, key_block = block_scores(first_row, all_keys)
        probs = probs_of(raw_scores, visible).astype(jnp.bfloat16)
        return summed + jnp.einsum(
            "tgrk,kgd->tgrd",
            probs,
            value_block_at(first_row, all_values),
            preferred_element_type=jnp.float32,
        )

    summed = lax.fori_loop(
        0, span_count, value_step, jnp.zeros((tok_rows, KV_HEADS, groups, HEAD_DIM), jnp.float32)
    )
    attended = summed.reshape(tok_rows, q_width).astype(jnp.bfloat16)
    branch = lax.dot_general(
        attended, out_full, (((1,), (1,)), ((), ())), preferred_element_type=jnp.float32
    )
    middle = tokens_f + branch
    normed_two, normal_two, inverse_two = rms_norm(middle, gain_two)
    normed_mid = normed_two.astype(jnp.bfloat16)
    logits = jnp.dot(normed_mid, router_full, preferred_element_type=jnp.float32)
    gates = jax.nn.softmax(jnp.take_along_axis(logits, routes, 1), axis=-1)
    route_hits = routes[:, :, None] == jnp.arange(EXPERTS, dtype=jnp.int32)[None, None, :]
    hit_count = jnp.sum(route_hits.astype(jnp.int32), 1)
    before = jnp.cumsum(hit_count, 0) - hit_count
    slot_index = jnp.take_along_axis(before, routes, 1)
    kept_pair = slot_index < CAP
    flat_slot = routes * CAP + slot_index
    capacity_rows = EXPERTS * CAP
    target = jnp.where(kept_pair, flat_slot, capacity_rows)
    token_ids = jnp.broadcast_to(jnp.arange(tok_rows, dtype=jnp.int32)[:, None], (tok_rows, TOP))
    owner_row = (
        jnp.full((capacity_rows + 1,), -1, jnp.int32)
        .at[target.reshape(-1)]
        .set(token_ids.reshape(-1))[:capacity_rows]
    )
    filled = owner_row >= 0
    source_row = jnp.maximum(owner_row, 0)
    expert_groups = lax.axis_size("expert")
    local_experts = EXPERTS // expert_groups
    send_rows = jnp.where(
        filled[:, None], normed_mid[source_row], jnp.zeros((), jnp.bfloat16)
    ).reshape(expert_groups, local_experts, CAP, D)
    received = lax.all_to_all(send_rows, "expert", split_axis=0, concat_axis=0, tiled=True)
    gate_up_full, down_full = (
        lax.all_gather(gate_up_weight, "shard", axis=0, tiled=True),
        lax.all_gather(down_weight, "shard", axis=0, tiled=True),
    )
    gate_up3 = gate_up_full.reshape(D, local_experts, 2 * H)
    down3 = down_full.reshape(D, local_experts, H)
    projected = jnp.einsum("secd,dej->secj", received, gate_up3, preferred_element_type=jnp.float32)
    gate_part = projected[..., :H]
    up_part = projected[..., H:]
    sigma = jax.nn.sigmoid(gate_part)
    silu_value = gate_part * sigma
    hidden = (silu_value * up_part).astype(jnp.bfloat16)
    expert_out = jnp.einsum(
        "secj,dej->secd", hidden, down3, preferred_element_type=jnp.float32
    ).astype(jnp.bfloat16)
    returned = lax.all_to_all(
        expert_out, "expert", split_axis=0, concat_axis=0, tiled=True
    ).reshape(capacity_rows, D)
    safe_flat = jnp.where(kept_pair, flat_slot, 0)
    picked = returned[safe_flat].astype(jnp.float32)
    pair_weight = jnp.where(kept_pair, gates, 0.0)
    moe_sum = jnp.einsum("tk,tkd->td", pair_weight, picked)
    output = (middle + moe_sum).astype(jnp.bfloat16)
    grad_out = output_cotangent.astype(jnp.float32)
    gate_grad = jnp.where(kept_pair, jnp.einsum("td,tkd->tk", grad_out, picked), 0.0)
    slot_gate = (
        jnp.zeros((capacity_rows + 1,), jnp.float32)
        .at[target.reshape(-1)]
        .set(gates.reshape(-1))[:capacity_rows]
    )
    grad_send = (
        jnp.where(filled[:, None], slot_gate[:, None] * grad_out[source_row], 0.0)
        .astype(jnp.bfloat16)
        .reshape(expert_groups, local_experts, CAP, D)
    )
    grad_received = lax.all_to_all(grad_send, "expert", split_axis=0, concat_axis=0, tiled=True)
    keys_back, values_back = (
        lax.all_gather(key_local, "shard", axis=0, tiled=True),
        lax.all_gather(value_local, "shard", axis=0, tiled=True),
    )
    again_up, again_down = (
        lax.all_gather(gate_up_weight, "shard", axis=0, tiled=True),
        lax.all_gather(down_weight, "shard", axis=0, tiled=True),
    )
    gate_up_back = again_up.reshape(D, local_experts, 2 * H)
    down_back = again_down.reshape(D, local_experts, H)
    hidden_grad = jnp.einsum(
        "secd,dej->secj", grad_received, down_back, preferred_element_type=jnp.float32
    )
    silu_slope = sigma * (1.0 + gate_part * (1.0 - sigma))
    proj_grad = jnp.concatenate(
        [hidden_grad * up_part * silu_slope, hidden_grad * silu_value], -1
    ).astype(jnp.bfloat16)
    row_grad = jnp.einsum(
        "secj,dej->secd", proj_grad, gate_up_back, preferred_element_type=jnp.float32
    ).astype(jnp.bfloat16)
    grad_back = lax.all_to_all(row_grad, "expert", split_axis=0, concat_axis=0, tiled=True).reshape(
        capacity_rows, D
    )
    row_count = gate_up_weight.shape[0] * lax.axis_size("shard")
    up_terms = jnp.einsum(
        "secd,secj->dej", received, proj_grad, preferred_element_type=jnp.float32
    ).reshape(row_count, local_experts * 2 * H)
    down_terms = jnp.einsum(
        "secd,secj->dej", grad_received, hidden, preferred_element_type=jnp.float32
    ).reshape(row_count, local_experts * H)
    expert_sums = lax.psum_scatter(
        jnp.concatenate([up_terms, down_terms], 1).astype(jnp.bfloat16),
        "shard",
        scatter_dimension=0,
        tiled=True,
    ).astype(jnp.float32)
    gate_up_grad = expert_sums[:, : local_experts * 2 * H]
    down_grad = expert_sums[:, local_experts * 2 * H :]
    mid_norm_grad = jnp.einsum(
        "tk,tkd->td", kept_pair.astype(jnp.float32), grad_back[safe_flat].astype(jnp.float32)
    )
    chosen_grad = gates * (gate_grad - jnp.sum(gates * gate_grad, -1, keepdims=True))
    logit_grad = jnp.sum(jnp.where(route_hits, chosen_grad[:, :, None], 0.0), 1).astype(
        jnp.bfloat16
    )
    mid_norm_grad = mid_norm_grad + lax.dot_general(
        logit_grad, router_full, (((1,), (1,)), ((), ())), preferred_element_type=jnp.float32
    )
    router_grad = lax.dot_general(
        normed_mid, logit_grad, (((0,), (0,)), ((), ())), preferred_element_type=jnp.float32
    )
    mid_part, moe_gain_grad = rms_back(mid_norm_grad, gain_two, normal_two, inverse_two)
    mid_grad = grad_out + mid_part
    branch_grad = mid_grad.astype(jnp.bfloat16)
    out_weight_grad = lax.dot_general(
        branch_grad, attended, (((0,), (0,)), ((), ())), preferred_element_type=jnp.float32
    )
    attended_grad = (
        jnp.dot(branch_grad, out_full, preferred_element_type=jnp.float32)
        .astype(jnp.bfloat16)
        .reshape(tok_rows, KV_HEADS, groups, HEAD_DIM)
    )

    def dot_step(step_index, row_dot):
        first_row = step_index * span_len
        raw_scores, visible, key_block = block_scores(first_row, keys_back)
        prob_full = probs_of(raw_scores, visible)
        prob_grad = jnp.einsum(
            "tgrd,kgd->tgrk",
            attended_grad,
            value_block_at(first_row, values_back),
            preferred_element_type=jnp.float32,
        )
        return row_dot + jnp.sum(prob_full * prob_grad, -1)

    row_dot = lax.fori_loop(0, span_count, dot_step, jnp.zeros(stat_shape, jnp.float32))

    def grad_step(step_index, carry):
        query_grad, key_terms, value_terms = carry
        first_row = step_index * span_len
        raw_scores, visible, key_block = block_scores(first_row, keys_back)
        prob_full = probs_of(raw_scores, visible)
        prob_grad = jnp.einsum(
            "tgrd,kgd->tgrk",
            attended_grad,
            value_block_at(first_row, values_back),
            preferred_element_type=jnp.float32,
        )
        score_grad = (prob_full * (prob_grad - row_dot[..., None])).astype(jnp.bfloat16)
        query_grad = query_grad + jnp.einsum(
            "tgrk,kgd->tgrd", score_grad, key_block, preferred_element_type=jnp.float32
        )
        key_part = (
            jnp.einsum(
                "tgrk,tgrd->kgd", score_grad, queries, preferred_element_type=jnp.float32
            ).reshape(span_len, kv_width)
            * score_scale
        )
        value_part = jnp.einsum(
            "tgrk,tgrd->kgd",
            prob_full.astype(jnp.bfloat16),
            attended_grad,
            preferred_element_type=jnp.float32,
        ).reshape(span_len, kv_width)
        key_terms = lax.dynamic_update_slice_in_dim(key_terms, key_part, first_row, 0)
        value_terms = lax.dynamic_update_slice_in_dim(value_terms, value_part, first_row, 0)
        return (query_grad, key_terms, value_terms)

    query_grad, key_terms, value_terms = lax.fori_loop(
        0,
        span_count,
        grad_step,
        (
            jnp.zeros((tok_rows, KV_HEADS, groups, HEAD_DIM), jnp.float32),
            jnp.zeros((seq_len, kv_width), jnp.float32),
            jnp.zeros((seq_len, kv_width), jnp.float32),
        ),
    )
    key_grad, value_grad = (
        lax.psum_scatter(
            key_terms.astype(jnp.bfloat16), "shard", scatter_dimension=0, tiled=True
        ).astype(jnp.float32),
        lax.psum_scatter(
            value_terms.astype(jnp.bfloat16), "shard", scatter_dimension=0, tiled=True
        ).astype(jnp.float32),
    )
    query_back = rotate_back(
        (query_grad * score_scale).reshape(tok_rows, HEADS, HEAD_DIM), cosine, sine_table
    ).reshape(tok_rows, q_width)
    key_back = rotate_back(
        key_grad.reshape(tok_rows, KV_HEADS, HEAD_DIM), cosine, sine_table
    ).reshape(tok_rows, kv_width)
    qkv_grad_rows = jnp.concatenate([query_back, key_back, value_grad], 1).astype(jnp.bfloat16)
    qkv_weight_grad = lax.dot_general(
        normed_in, qkv_grad_rows, (((0,), (0,)), ((), ())), preferred_element_type=jnp.float32
    )
    in_norm_grad = lax.dot_general(
        qkv_grad_rows, qkv_full, (((1,), (1,)), ((), ())), preferred_element_type=jnp.float32
    )
    in_part, attn_gain_grad = rms_back(in_norm_grad, gain_one, normal_one, inverse_one)
    input_grad = (mid_grad + in_part).astype(jnp.bfloat16)
    dense_sums = (
        lax.psum_scatter(
            qkv_weight_grad.astype(jnp.bfloat16), "shard", scatter_dimension=0, tiled=True
        ).astype(jnp.float32),
        lax.psum_scatter(
            out_weight_grad.astype(jnp.bfloat16), "shard", scatter_dimension=0, tiled=True
        ).astype(jnp.float32),
        lax.psum_scatter(
            router_grad.astype(jnp.bfloat16), "shard", scatter_dimension=0, tiled=True
        ).astype(jnp.float32),
        lax.psum_scatter(
            attn_gain_grad.astype(jnp.bfloat16), "shard", scatter_dimension=0, tiled=True
        ).astype(jnp.float32),
        lax.psum_scatter(
            moe_gain_grad.astype(jnp.bfloat16), "shard", scatter_dimension=0, tiled=True
        ).astype(jnp.float32),
    )
    dense_totals = (
        lax.psum(dense_sums[0].astype(jnp.bfloat16), "expert").astype(jnp.float32),
        lax.psum(dense_sums[1].astype(jnp.bfloat16), "expert").astype(jnp.float32),
        lax.psum(dense_sums[2].astype(jnp.bfloat16), "expert").astype(jnp.float32),
        lax.psum(dense_sums[3].astype(jnp.bfloat16), "expert").astype(jnp.float32),
        lax.psum(dense_sums[4].astype(jnp.bfloat16), "expert").astype(jnp.float32),
    )
    return (
        output,
        input_grad,
        dense_totals[0],
        dense_totals[1],
        dense_totals[2],
        dense_totals[3],
        dense_totals[4],
        gate_up_grad,
        down_grad,
    )


GROUPS = 4
SHARDS = 8
rows_by_cols = ((1,), (0,))
rows_by_rows = ((1,), (1,))
cols_by_cols = ((0,), (0,))


def dot(one, two, dims):
    return lax.dot_general(one, two, (dims, ((), ())), preferred_element_type=jnp.float32)


def whole_spec(shape):
    return pl.BlockSpec(shape, lambda i, ids: (0,) * len(shape), pipeline_mode=pl.Buffered(1))


def block_spec(shape, index):
    return pl.BlockSpec(shape, lambda i, ids: index, pipeline_mode=pl.Buffered(1))


def out_spec(shape, index):
    return pl.BlockSpec(shape, lambda i, ids: index)


in_place = pl.BlockSpec(memory_space=pl.ANY)


def shaped(shape, dtype=jnp.bfloat16):
    return jax.ShapeDtypeStruct(shape, dtype)


def call(kernel, name, out_shape, in_specs, out_specs, args, scratch=(), aliases=None, flops=0, steps=1):
    moved = sum(a.size * a.dtype.itemsize for a in args[1:])
    return pl.pallas_call(
        kernel,
        name=name,
        out_shape=out_shape,
        grid_spec=pltpu.PrefetchScalarGridSpec(
            num_scalar_prefetch=1,
            grid=(steps,),
            in_specs=in_specs,
            out_specs=out_specs,
            scratch_shapes=list(scratch),
        ),
        input_output_aliases=aliases or {},
        compiler_params=pltpu.CompilerParams(
            vmem_limit_bytes=58 * 1024 * 1024, dimension_semantics=("arbitrary",)
        ),
        cost_estimate=pl.CostEstimate(flops=flops, transcendentals=0, bytes_accessed=moved),
    )(*args)


def place_rows(offsets, parts, height):
    count, fine, width = parts[0].shape

    def kernel(at, *refs):
        sources, target, done = refs[: len(parts)], refs[len(parts)], refs[-1]
        copies = []
        for n, source in enumerate(sources):
            for i in range(count):
                row = pl.multiple_of(at[n * count + i], 16)
                copies.append(
                    pltpu.make_async_copy(
                        source.at[i], target.at[pl.ds(row, fine)], done.at[n * count + i]
                    )
                )
        for copy in copies:
            copy.start()
        for copy in copies:
            copy.wait()

    return call(
        kernel,
        "place_rows",
        shaped((height, width), parts[0].dtype),
        [in_place] * len(parts),
        out_spec((height, width), (0, 0)),
        (offsets,) + tuple(parts),
        scratch=[pltpu.SemaphoreType.DMA((len(parts) * count,))],
    )


def dense_terms(offsets, products, parts, count, fine):
    height = products[0][0].shape[1]
    width = max(first + two.shape[1] for _, two, first in products)
    firsts = [first for _, _, first in products]

    def kernel(at, *refs):
        sources, targets, held = refs[: 2 * len(firsts)], refs[2 * len(firsts) : -1], refs[-1]
        total = {}
        for n, first in enumerate(firsts):
            found = dot(sources[2 * n][...], sources[2 * n + 1][...], cols_by_cols)
            total[first] = total[first] + found if first in total else found
        for first, found in total.items():
            held[:, first : first + found.shape[1]] = found.astype(jnp.bfloat16)
        for n, target in enumerate(targets):
            for i in range(count):
                row = pl.multiple_of(at[n * count + i], 16)
                target[i] = held[pl.ds(row, fine)]

    operands = [array for one, two, _ in products for array in (one, two)]
    return call(
        kernel,
        "dense_terms",
        [shaped((count, fine, width))] * parts,
        [whole_spec(array.shape) for array in operands],
        [out_spec((count, fine, width), (0, 0, 0))] * parts,
        (offsets,) + tuple(operands),
        scratch=[pltpu.VMEM((height, width), jnp.bfloat16)],
        flops=2 * height * width * products[0][0].shape[0],
    )


def pack_kernel(ids, up, gate_part, up_part, down, down_part, gain, *packs):
    width = down.shape[1]
    scale = gain[...]
    step = pl.program_id(0)

    def scaled(rows):
        return (rows.astype(jnp.float32) * scale).astype(jnp.bfloat16)

    for k in range(SHARDS):

        @pl.when(step == k)
        def _(k=k):
            downs, ups = packs[2 * k : 2 * k + 2]
            downs[0, :, :width] = down[...]
            downs[0, :, width:] = down_part[...]
            ups[0, :, : 2 * width] = scaled(up[...])
            part = down_part.shape[1]
            ups[0, :, 2 * width : 2 * width + part] = scaled(gate_part[...])
            ups[0, :, 2 * width + part :] = scaled(up_part[...])


def unpack_kernel(ids, *refs):
    pieces, gain, up_grad, down_grad = refs[: SHARDS + 2], refs[-3], refs[-2], refs[-1]
    scale = gain[...]
    step = pl.program_id(0)
    share = SHARDS // (pl.num_programs(0) - SHARDS)
    part = pieces[0].shape[2] // 3 - H
    edge = pieces[6].shape[2]

    def columns(k, first, count):
        if k < 6:
            found = pieces[k][0, :, first : first + count]
        elif first < edge:
            found = pieces[2 * k - 6][0, :, first : first + count]
        else:
            found = pieces[2 * k - 5][0, :, first - edge : first - edge + count]
        return found.astype(jnp.float32)

    for k in range(SHARDS):
        source = ids[2] ^ k

        @pl.when(step == k)
        def _(k=k):
            down_grad[...] = columns(k, 0, H)
            up_grad[:, :H] = columns(k, H, H) * scale
            up_grad[:, H:] = columns(k, 2 * H, H) * scale

        @pl.when(step == SHARDS + source // share)
        def _(k=k, source=source):
            at = pl.multiple_of(source % share * part, part)
            at_up = pl.multiple_of(H + source % share * part, part)
            down_grad[:, pl.ds(at, part)] = columns(k, 3 * H, part)
            up_grad[:, pl.ds(at, part)] = columns(k, 3 * H + part, part) * scale
            up_grad[:, pl.ds(at_up, part)] = columns(k, 3 * H + 2 * part, part) * scale


def turn(rows, cosine, sine):
    width = rows.shape[1]
    lanes = lax.broadcasted_iota(jnp.int32, (rows.shape[0], 128), 1)
    first = lanes % HEAD_DIM < HEAD_DIM // 2
    turned = []
    for at in range(0, width, 128):
        piece = rows[:, at : at + 128]
        swapped = jnp.where(
            first,
            pltpu.roll(piece, 128 - HEAD_DIM // 2, 1),
            pltpu.roll(piece, HEAD_DIM // 2, 1),
        )
        turned.append(piece * cosine + swapped * sine)
    return jnp.concatenate(turned, 1)


def qkv_kernel(ids, normed, weight, cosine, sine, queries, key_value):
    step = pl.program_id(0)
    found = dot(normed[...], weight[...], rows_by_cols)

    @pl.when(step < 3)
    def _():
        queries[...] = turn(found, cosine[...], sine[...]).astype(jnp.bfloat16)

    @pl.when(step == 3)
    def _():
        key_value[...] = turn(found, cosine[...], sine[...]).astype(jnp.bfloat16)

    @pl.when(step == 4)
    def _():
        key_value[...] = found.astype(jnp.bfloat16)


def attend_kernel(ids, queries, key_line, key_other, value_line, value_other, bias, attended, logs):
    scale = HEAD_DIM ** (-0.5)
    groups = HEADS // KV_HEADS
    hidden = bias[...]
    keys = jnp.concatenate([key_line[...], key_other[...]], 0)
    values = jnp.concatenate([value_line[...], value_other[...]], 0)
    lanes = lax.broadcasted_iota(jnp.int32, (queries.shape[0], 128), 1)
    totals = jnp.zeros((queries.shape[0], 128), jnp.float32)
    found = []
    for n in range(2 * groups):
        at = n // groups * HEAD_DIM
        scores = dot(
            queries[:, n * HEAD_DIM : (n + 1) * HEAD_DIM], keys[:, at : at + HEAD_DIM], rows_by_rows
        )
        scores = scores * scale + hidden
        top = jnp.max(scores, 1, keepdims=True)
        raised = jnp.exp(scores - top)
        total = jnp.sum(raised, 1, keepdims=True)
        probs = (raised / total).astype(jnp.bfloat16)
        found.append(dot(probs, values[:, at : at + HEAD_DIM], rows_by_cols))
        totals = jnp.where(lanes == n, top + jnp.log(total), totals)
    attended[...] = jnp.concatenate(found, 1).astype(jnp.bfloat16)
    logs[0] = totals


def attend_back_kernel(
    ids, queries, grads, key_line, key_other, value_line, value_other, bias, logs, cosine, sine,
    query_grad, key_mine, key_theirs, value_mine, value_theirs,
):
    scale = HEAD_DIM ** (-0.5)
    groups = HEADS // KV_HEADS
    hidden = bias[...]
    keys = jnp.concatenate([key_line[...], key_other[...]], 0)
    values = jnp.concatenate([value_line[...], value_other[...]], 0)
    half = key_line.shape[0]
    found = []
    key_found, value_found = [], []
    for n in range(2 * groups):
        own = n // groups
        at = own * HEAD_DIM
        head = slice(n * HEAD_DIM, (n + 1) * HEAD_DIM)
        query = queries[:, head]
        grad = grads[:, head]
        scores = dot(query, keys[:, at : at + HEAD_DIM], rows_by_rows) * scale + hidden
        probs = jnp.exp(scores - lane_value(logs[0], n))
        prob_grad = dot(grad, values[:, at : at + HEAD_DIM], rows_by_rows)
        row_dot = jnp.sum(probs * prob_grad, 1, keepdims=True)
        score_grad = (probs * (prob_grad - row_dot)).astype(jnp.bfloat16)
        found.append(dot(score_grad, keys[:, at : at + HEAD_DIM], rows_by_cols))
        key_part = dot(score_grad, query, cols_by_cols)
        value_part = dot(probs.astype(jnp.bfloat16), grad, cols_by_cols)
        if n % groups:
            key_found[own] = key_found[own] + key_part
            value_found[own] = value_found[own] + value_part
        else:
            key_found.append(key_part)
            value_found.append(value_part)
    found = jnp.concatenate(found, 1) * scale
    query_grad[...] = turn(found, cosine[...], -sine[...]).astype(jnp.bfloat16)
    key_found = (jnp.concatenate(key_found, 1) * scale).astype(jnp.bfloat16)
    value_found = jnp.concatenate(value_found, 1).astype(jnp.bfloat16)
    key_mine[...] = key_found[:half]
    key_theirs[...] = key_found[half:]
    value_mine[...] = value_found[:half]
    value_theirs[...] = value_found[half:]


def lane_value(rows, index):
    lanes = lax.broadcasted_iota(jnp.int32, rows.shape, 1)
    return jnp.sum(jnp.where(lanes == index, rows, 0.0), 1, keepdims=True)


def picks_of(extra, one, two):
    extra = extra.astype(jnp.float32)
    lanes = lax.broadcasted_iota(jnp.int32, (extra.shape[0], 2 * CAP), 1)
    wanted = jnp.where(lanes < CAP, lane_value(extra, one), lane_value(extra, two))
    place = jnp.where(lanes < CAP, lanes, lanes - CAP).astype(jnp.float32)
    return jnp.where(wanted == place, 1.0, 0.0).astype(jnp.bfloat16)


def grad_side_kernel(ids, half, other, down_one, down_two, *refs):
    gs, plain = refs[-2:]
    count = half.shape[0]
    for i in range(2 * count):
        source = half if i < count else other
        pick = picks_of(source[i % count, :, D:], ids[0], ids[1])
        found = dot(pick, source[i % count, :, :D], cols_by_cols).astype(jnp.bfloat16)
        gs[0, i * CAP : (i + 1) * CAP] = found[:CAP]
        gs[1, i * CAP : (i + 1) * CAP] = found[CAP:]
    width = down_one.shape[1]
    plain[:, :width] = dot(gs[0], down_one[...], rows_by_cols)
    plain[:, width:] = dot(gs[1], down_two[...], rows_by_cols)


def combine_rows(ids, rows, slots_half, slots_other, back_half, back_other):
    count = slots_half.shape[0]
    for i in range(2 * count):
        target = back_half if i < count else back_other
        slots = slots_half if i < count else slots_other
        pick = picks_of(slots[i % count], ids[0], ids[1])
        at = slice(i * CAP, (i + 1) * CAP)
        both = jnp.concatenate([rows[0, at], rows[1, at]], 0)
        target[i % count] = dot(pick, both, rows_by_cols).astype(jnp.bfloat16)


def row_side_kernel(
    ids, half, other, slots_half, slots_other, plain, gate_one, gate_two, up_one, up_two, *refs
):
    back_half, back_other, xs, hid, pg, gates, tokens, back_rows = refs[-8:]
    total = xs.shape[1]
    count = half.shape[0]
    for i in range(2 * count):
        source = half if i < count else other
        slots = slots_half if i < count else slots_other
        pick = picks_of(slots[i % count], ids[0], ids[1])
        found = dot(pick, source[i % count], cols_by_cols)
        extra = found[:, D:]
        found = found.astype(jnp.bfloat16)
        at = slice(i * CAP, (i + 1) * CAP)
        for n in range(2):
            xs[n, at] = found[n * CAP : (n + 1) * CAP, :D]
            own = extra[n * CAP : (n + 1) * CAP]
            gates[n, at] = lane_value(own, ids[n]) + lane_value(own, ids[n] + EXPERTS)
    first = 0
    second = hid.shape[1]
    for n, gate_weight, up_weight in ((0, gate_one, up_one), (1, gate_two, up_two)):
        width = up_weight.shape[1]
        gate_part = dot(xs[n], gate_weight[...], rows_by_cols)
        up_part = dot(xs[n], up_weight[...], rows_by_cols)
        at = slice(first, first + width)
        at_up = slice(second + first, second + first + width)
        own_plain = plain[:, at]
        sigma = 1.0 / (1.0 + jnp.exp(-gate_part))
        silu_value = gate_part * sigma
        hidden = silu_value * up_part
        tokens[n] = jnp.sum(hidden * own_plain, 1, keepdims=True)
        hid[:, at] = (hidden * gates[n]).astype(jnp.bfloat16)
        hidden_grad = own_plain * gates[n]
        slope = sigma * (1.0 + gate_part * (1.0 - sigma))
        pg[:, at] = (hidden_grad * up_part * slope).astype(jnp.bfloat16)
        pg[:, at_up] = (hidden_grad * silu_value).astype(jnp.bfloat16)
        row_grad = dot(pg[:, at], gate_weight[...], rows_by_rows)
        row_grad = row_grad + dot(pg[:, at_up], up_weight[...], rows_by_rows)
        back_rows[n, :, :D] = row_grad.astype(jnp.bfloat16)
        lanes = lax.broadcasted_iota(jnp.int32, (total, 128), 1)
        back_rows[n, :, D:] = jnp.where(lanes == ids[n], tokens[n], 0.0).astype(jnp.bfloat16)
        first += width
    combine_rows(ids, back_rows, slots_half, slots_other, back_half, back_other)


def out_side_kernel(ids, hid, *refs):
    slots, (down_one, down_two), (mine, theirs, out_rows) = refs[:4], refs[4:6], refs[6:]
    width = down_one.shape[1]
    count = slots[0].shape[0]
    out_rows[0] = dot(hid[:, :width], down_one[...], rows_by_rows).astype(jnp.bfloat16)
    out_rows[1] = dot(hid[:, width:], down_two[...], rows_by_rows).astype(jnp.bfloat16)
    for n, own in enumerate(slots):
        target = theirs if n % 2 else mine
        for i in range(count):
            pick = picks_of(own[i], ids[0], ids[1])
            at = slice((n * count + i) * CAP, (n * count + i + 1) * CAP)
            both = jnp.concatenate([out_rows[0, at], out_rows[1, at]], 0)
            place = i // 2 * 4 + n // 2 * 2 + i % 2
            target[place] = dot(pick, both, rows_by_cols).astype(jnp.bfloat16)


def terms_kernel(ids, xs, gs, pg, hid, terms):
    depth = terms.shape[1]
    width = hid.shape[1]
    for one, two, n, shift, first, count in (
        (gs, hid, 0, 0, 0, H),
        (xs, pg, 0, 0, H, H),
        (xs, pg, 0, width, 2 * H, H),
        (gs, hid, 1, H, 3 * H, width - H),
        (xs, pg, 1, H, 2 * H + width, width - H),
        (xs, pg, 1, width + H, H + 2 * width, width - H),
    ):
        found = dot(one[n], two[:, shift : shift + count], cols_by_cols).astype(jnp.bfloat16)
        for i in range(2):
            at = i ^ ids[2] % 2
            terms[pl.ds(at, 1), :, first : first + count] = found[i * depth : (i + 1) * depth][None]


def hop(values, pairs):
    return lax.ppermute(values, ("expert", "shard"), pairs)


def hop_pairs(step):
    return [
        (e * SHARDS + s, step(e, s)[0] * SHARDS + step(e, s)[1])
        for e in range(GROUPS)
        for s in range(SHARDS)
    ]


to_core = hop_pairs(lambda e, s: (e, s ^ 1))
to_line = [hop_pairs(lambda e, s, k=k: (e, s ^ (2 * k))) for k in range(4)]
over_middle = [
    (e * SHARDS + s, e * SHARDS + (s ^ 6)) for e in range(GROUPS) for s in range(2, 6)
]
from_middle = [
    (e * SHARDS + s, e * SHARDS + (s ^ 2)) for e in range(GROUPS) for s in range(2, 6)
]
to_middle = [(there, here) for here, there in from_middle]
to_first = hop_pairs(lambda e, s: (e ^ (1 + s % 2), s))
to_second = hop_pairs(lambda e, s: (e ^ (2 - s % 2), s))


def add_low(one, two):
    return (one.astype(jnp.float32) + two.astype(jnp.float32)).astype(jnp.bfloat16)


def total_of(line):
    return sum(piece.astype(jnp.float32) for piece in line)


class Flow:
    def __init__(self, steps):
        self.steps = steps
        self.result = None
        self.feed(None)

    def feed(self, values):
        try:
            self.want = self.steps.send(values)
        except StopIteration as stop:
            self.want = None
            self.result = stop.value


class Order:
    def __init__(self, mark):
        self.mark = mark

    def tie(self, values):
        values, self.mark = lax.optimization_barrier((values, self.mark))
        return values

    def round(self, flows, work=None):
        values, self.mark = lax.optimization_barrier(([f.want[0] for f in flows], self.mark))
        found = [hop(v, f.want[1]) for v, f in zip(values, flows)]
        found, work, self.mark = lax.optimization_barrier((found, work, self.mark))
        for flow, values in zip(flows, found):
            flow.feed(values)
        return work


def one_hop(values, pairs):
    found = yield values, pairs
    return found


def line_flows(own):
    return [Flow(one_hop(own, to_line[k])) for k in (1, 2, 3)]


def line_spread(own, marks):
    near = yield own, to_line[1]
    marks.append(near)
    two = jnp.stack([own, near])
    crossed = yield two, over_middle
    passed = yield crossed, from_middle
    at = lax.axis_index("shard") // 2
    return jnp.where((at == 1) | (at == 2), crossed, passed)


def line_collect(near, far):
    passed = yield jnp.stack(far), to_middle
    far = add_low(jnp.stack(far), passed)
    crossed = yield far, over_middle
    at = lax.axis_index("shard") // 2
    middle = (at == 1) | (at == 2)
    both = jnp.stack(near).astype(jnp.float32) + jnp.where(middle, crossed, 0).astype(jnp.float32)
    back = yield both[1].astype(jnp.bfloat16), to_line[1]
    return both[0] + back.astype(jnp.float32)


def by_distance(far):
    at = lax.axis_index("shard") // 2
    middle = (at == 1) | (at == 2)
    return [jnp.where(middle, far[1 - i], far[i]) for i in range(2)]


def spread_pair(pieces):
    two = jnp.stack(pieces) if isinstance(pieces, list) else pieces
    first = yield two, to_first
    four = jnp.concatenate([two, first])
    second = yield four, to_second
    eight = jnp.concatenate([four, second])
    other = yield eight, to_core
    return eight, other


def spread_all(line):
    four = jnp.stack(line)
    first = yield four, to_first
    eight = jnp.concatenate([four, first])
    second = yield eight, to_second
    half = jnp.concatenate([eight, second])
    other = yield half, to_core
    return half, other


def collect_pair(mine, theirs):
    found = yield theirs, to_core
    keep, give = add_low(mine[:4], found[:4]), add_low(mine[4:], found[4:])
    found = yield give, to_second
    keep, give = add_low(keep[:2], found[:2]), add_low(keep[2:], found[2:])
    found = yield give, to_first
    return [add_low(keep[i], found[i]) for i in range(2)]


def collect_all(mine, theirs):
    found = yield theirs, to_core
    keep, give = add_low(mine[:8], found[:8]), add_low(mine[8:], found[8:])
    found = yield give, to_second
    keep, give = add_low(keep[:4], found[:4]), add_low(keep[4:], found[4:])
    found = yield give, to_first
    return [add_low(keep[i], found[i]) for i in range(4)]


def share_flow(own, places):
    first = yield own, to_first
    pair = jnp.stack([own, first])
    second = yield pair, to_second
    quarters = jnp.concatenate([pair, second])
    return jnp.concatenate(
        [lax.dynamic_index_in_dim(quarters, place, 0, keepdims=False) for place in places]
    )


def local_hops(
    tokens_in,
    output_cotangent,
    routes,
    doc_ids,
    picture_starts,
    qkv_weight,
    out_weight,
    router_weight,
    attn_gain,
    moe_gain,
    gate_up_weight,
    down_weight,
):
    low = jnp.bfloat16
    full = jnp.float32
    rows = tokens_in.shape[0]
    seq_len = doc_ids.shape[1]
    q_width = HEADS * HEAD_DIM
    kv_width = KV_HEADS * HEAD_DIM
    qkv_width = q_width + 2 * kv_width
    group_at = lax.axis_index("expert")
    shard_at = lax.axis_index("shard")
    own_experts = EXPERTS // GROUPS
    whole = own_experts // SHARDS * SHARDS
    split = own_experts - whole
    share = SHARDS // split
    part = H // share
    hid_width = H + part
    depth = gate_up_weight.shape[0]
    height = SHARDS * depth
    fine = depth // GROUPS
    pad = 128 - EXPERTS
    gain_one = attn_gain.astype(full)[:, None]
    gain_two = moe_gain.astype(full)[:, None]
    expert_one = group_at * own_experts + shard_at
    expert_two = group_at * own_experts + whole + shard_at // share
    ids = jnp.stack([expert_one, expert_two, shard_at])
    order = Order(jnp.zeros((8, 128), full))

    spot = jnp.arange(GROUPS * SHARDS, dtype=jnp.int32)
    spot_core = spot // 8 % 2
    spot_mate = 1 + (shard_at % 2 ^ spot_core)
    spot_q = spot % 8 // 2
    spot_group = jnp.where(spot_q == 1, spot_mate, jnp.where(spot_q == 2, 3 - spot_mate, spot_q))
    spot_line = spot // 16 * 2 + spot % 2
    fine_at = (shard_at ^ (2 * spot_line + spot_core)) * depth + (group_at ^ spot_group) * fine
    half_core = spot // 16
    half_mate = 1 + (shard_at % 2 ^ half_core)
    half_q = spot % 16 // 4
    half_group = jnp.where(half_q == 1, half_mate, jnp.where(half_q == 2, 3 - half_mate, half_q))
    half_at = (shard_at ^ (2 * (spot % 4) + half_core)) * depth + (group_at ^ half_group) * fine

    expert_ids = jnp.arange(EXPERTS, dtype=jnp.int32)
    hits = jnp.any(routes[:, :, None] == expert_ids[None, None, :], 1)
    earlier = jnp.arange(rows)[:, None] > jnp.arange(rows)[None, :]
    before = dot(earlier.astype(low), hits.astype(low), rows_by_cols)
    slots = jnp.where(hits & (before < CAP), before, -1.0)
    kept = slots >= 0
    grad_pay = jnp.concatenate(
        [output_cotangent, jnp.pad(slots.astype(low), ((0, 0), (0, pad)))], 1
    )

    def fine_rows(array):
        return lax.dynamic_slice_in_dim(array, group_at * fine, fine, 0)

    qkv_own = fine_rows(qkv_weight).astype(full) * fine_rows(gain_one)
    router_own = fine_rows(router_weight).astype(full) * fine_rows(gain_two)
    dense_own = jnp.concatenate([qkv_own, jnp.pad(router_own, ((0, 0), (0, pad)))], 1).astype(low)
    out_own = fine_rows(out_weight)

    def column_spec(width, index):
        return pl.BlockSpec((depth, width), lambda k, ids: (0, index(ids[2] ^ k)))

    to_parts = H // part
    packs = call(
        pack_kernel,
        "pack",
        [shaped((1, depth, hid_width)), shaped((1, depth, 2 * hid_width))] * SHARDS,
        [
            column_spec(2 * H, lambda d: d),
            column_spec(part, lambda d: (whole + d // share) * 2 * to_parts + d % share),
            column_spec(part, lambda d: (whole + d // share) * 2 * to_parts + to_parts + d % share),
            column_spec(H, lambda d: d),
            column_spec(part, lambda d: (whole + d // share) * to_parts + d % share),
            pl.BlockSpec((depth, 1), lambda d, ids: (0, 0)),
        ],
        [
            out_spec((1, depth, hid_width), (0, 0, 0)),
            out_spec((1, depth, 2 * hid_width), (0, 0, 0)),
        ]
        * SHARDS,
        (ids, gate_up_weight, gate_up_weight, gate_up_weight, down_weight, down_weight, gain_two),
        steps=SHARDS,
    )

    to_shard = [hop_pairs(lambda e, s, k=k: (e, s ^ k)) for k in range(SHARDS)]
    shard_rows = (shard_at ^ jnp.arange(SHARDS, dtype=jnp.int32)) * depth

    def exchange(pieces):
        flows = [[Flow(one_hop(piece, to_shard[k])) for piece in pieces[k]] for k in range(1, SHARDS)]
        near = [flows[k - 1][n] for n in range(len(pieces[0])) for k in (2, 3)]
        far = [flows[k - 1][n] for n in range(len(pieces[0])) for k in (4, 5, 6, 7)]
        return flows, flows[0], near, far

    def exchanged(pieces, flows, n):
        parts = [pieces[0][n]] + [flow[n].result for flow in flows]
        return place_rows(shard_rows, parts, height)

    s_pieces = [packs[2 * k : 2 * k + 2] for k in range(SHARDS)]
    s_flows, core, near, far = exchange(s_pieces)

    def some(flows, count):
        taken = flows[:count]
        del flows[:count]
        return taken

    w = line_flows(dense_own)
    o = line_flows(out_own)
    g_marks, x_marks = [], []
    g_line = Flow(line_spread(grad_pay, g_marks))
    order.round(w[:2])
    w_near = Flow(spread_pair([dense_own, w[0].result]))
    order.round([w[2], w_near, g_line])
    w_far = Flow(spread_pair([w[1].result, w[2].result]))
    g_near = Flow(spread_pair([grad_pay, g_marks[0]]))
    order.round([w_near, w_far] + some(far, 1) + some(near, 1) + core)
    order.round([w_near, w_far] + o)
    o_all = Flow(spread_all([out_own] + [flow.result for flow in o]))
    order.round([w_far, o_all])
    dense_full = place_rows(fine_at, w_near.result + w_far.result, height)
    router_full = dense_full[:, qkv_width:]

    tokens_f = tokens_in.astype(full)
    inverse_one = lax.rsqrt(jnp.mean(tokens_f * tokens_f, -1, keepdims=True) + norm_eps)
    normal_one = tokens_f * inverse_one
    normed_in = normal_one.astype(low)
    query_pos = shard_at * rows + jnp.arange(rows, dtype=jnp.int32)
    cosine, sine = rope_tables(query_pos, HEAD_DIM)
    cosine = jnp.tile(cosine[:, 0], (1, 4))
    sine = jnp.tile(jnp.concatenate([-sine[:, 0], sine[:, 0]], 1), (1, 2))
    tile = 512
    queries, key_value = call(
        qkv_kernel,
        "qkv",
        (shaped((rows, q_width)), shaped((rows, 2 * kv_width))),
        [
            whole_spec((rows, D)),
            pl.BlockSpec((D, tile), lambda j, ids: (0, j)),
            whole_spec((rows, 128)),
            whole_spec((rows, 128)),
        ],
        [
            pl.BlockSpec((rows, tile), lambda j, ids: (0, jnp.minimum(j, 2))),
            pl.BlockSpec((rows, tile), lambda j, ids: (0, jnp.maximum(j - 3, 0))),
        ],
        (ids, normed_in, dense_full, cosine, sine),
        flops=2 * rows * D * qkv_width,
        steps=qkv_width // tile,
    )
    queries, key_value = order.round(
        [o_all, g_near, g_line], (queries, key_value)
    )
    kv = line_flows(key_value)
    order.round(kv + [o_all, g_near])
    kv_line = jnp.concatenate([key_value] + [flow.result for flow in kv])
    kv_core = Flow(one_hop(kv_line, to_core))
    out_full = place_rows(half_at, o_all.result, height)
    out_full = order.round([kv_core], out_full)
    kv_other = kv_core.result
    block_order = jnp.arange(SHARDS, dtype=jnp.int32)
    block_order = shard_at ^ (block_order % 4 * 2 + block_order // 4)
    key_pos = (
        block_order[:, None] * rows + jnp.arange(rows, dtype=jnp.int32)[None, :]
    ).reshape(seq_len)
    doc_blocks = doc_ids[0].reshape(SHARDS, rows)
    block_hits = block_order[:, None] == jnp.arange(SHARDS)[None, :]
    key_doc = jnp.sum(
        jnp.where(block_hits[:, :, None], doc_blocks[None], 0), 1
    ).reshape(seq_len)
    query_doc = key_doc[:rows]
    key_pic = picture_ids(key_pos, picture_starts[0], SLOT, PIECE)
    query_pic = key_pic[:rows]
    visible = allowed(query_pos, key_pos, query_doc, key_doc, query_pic, key_pic)
    bias = jnp.where(visible, 0.0, masked_score)
    pairs = KV_HEADS // 2
    q_tile = q_width // pairs
    kv_tile = kv_width // pairs
    half_len = seq_len // 2

    def kv_specs(first):
        return [pl.BlockSpec((half_len, kv_tile), lambda j, ids: (0, first + j))] * 2

    q_spec = pl.BlockSpec((rows, q_tile), lambda j, ids: (0, j))
    log_spec = pl.BlockSpec((1, rows, 128), lambda j, ids: (j, 0, 0))
    attended, logs = call(
        attend_kernel,
        "attend",
        (shaped((rows, q_width)), shaped((pairs, rows, 128), full)),
        [q_spec] + kv_specs(0) + kv_specs(pairs) + [whole_spec((rows, seq_len))],
        [q_spec, log_spec],
        (ids, queries, kv_line, kv_other, kv_line, kv_other, bias),
        flops=4 * rows * seq_len * q_width,
        steps=pairs,
    )
    branch = dot(attended, out_full, rows_by_rows)
    middle = tokens_f + branch
    inverse_two = lax.rsqrt(jnp.mean(middle * middle, -1, keepdims=True) + norm_eps)
    normal_two = middle * inverse_two
    normed_mid = normal_two.astype(low)
    logits = dot(normed_mid, router_full, rows_by_cols)[:, :EXPERTS]
    logits = jnp.where(hits, logits, masked_score)
    gates = jnp.exp(logits - jnp.max(logits, -1, keepdims=True))
    gates = jnp.where(hits, gates, 0.0)
    gates = gates / jnp.sum(gates, -1, keepdims=True)
    gate_low = gates.astype(low)
    gate_rest = (gates - gate_low.astype(full)).astype(low)
    row_pay = jnp.concatenate(
        [normed_mid, gate_low, gate_rest, jnp.zeros((rows, 128 - 2 * EXPERTS), low)], 1
    )

    slot_rows = GROUPS * SHARDS * CAP
    step_rows = slot_rows // 2
    blocks = 2 * GROUPS
    pay_spec = whole_spec((blocks, rows, D + 128))
    pay_out = out_spec((blocks, rows, D + 128), (0, 0, 0))
    slot_spec = block_spec((blocks, rows, 128), (0, 0, D // 128))
    up_specs = [
        block_spec((height, H), (0, 0)),
        block_spec((height, part), (0, 2 * to_parts)),
        block_spec((height, H), (0, 1)),
        block_spec((height, part), (0, 2 * to_parts + 1)),
    ]
    down_specs = [
        block_spec((height, H), (0, 0)),
        block_spec((height, part), (0, H // part)),
    ]
    back_shape = shaped((blocks, rows, D + 128))
    gs_shape = shaped((2, slot_rows, D))
    kept_shapes = (gs_shape, shaped((slot_rows, hid_width)), shaped((slot_rows, 2 * hid_width)))
    kept_rows = ()

    gs, plain = (), []

    def grad_side(k):
        nonlocal gs
        gs_next, found = call(
            grad_side_kernel,
            "grad_side",
            (gs_shape, shaped((step_rows, hid_width), full)),
            [pay_spec, pay_spec] + down_specs + [in_place] * len(gs),
            [
                out_spec((2, step_rows, D), (0, k, 0)),
                out_spec((step_rows, hid_width), (0, 0)),
            ],
            (ids,) + (g_near, g_far)[k].result + (owned_down, owned_down) + gs,
            aliases={5: 0} if gs else None,
            flops=2 * step_rows * D * (hid_width + 2 * rows),
        )
        gs = (gs_next,)
        return found

    def row_side(k):
        nonlocal kept_rows
        half_back, other_back, *kept_next = call(
            row_side_kernel,
            "row_side",
            (back_shape, back_shape) + kept_shapes,
            [pay_spec, pay_spec, slot_spec, slot_spec, whole_spec((step_rows, hid_width))]
            + up_specs
            + [in_place] * len(kept_rows),
            [
                pay_out,
                pay_out,
                out_spec((2, step_rows, D), (0, k, 0)),
                out_spec((step_rows, hid_width), (k, 0)),
                out_spec((step_rows, 2 * hid_width), (k, 0)),
            ],
            (ids,)
            + (x_near, x_far)[k].result
            + (g_near, g_far)[k].result
            + (plain[k],)
            + (owned_up,) * 4
            + kept_rows,
            scratch=[
                pltpu.VMEM((2, step_rows, 1), full),
                pltpu.VMEM((2, step_rows, 1), full),
                pltpu.VMEM((2, step_rows, D + 128), low),
            ],
            aliases={10: 2, 11: 3, 12: 4} if kept_rows else None,
            flops=8 * step_rows * D * (hid_width + rows),
        )
        kept_rows = tuple(kept_next)
        return half_back, other_back

    row_pay = order.round([g_near, g_line] + some(far, 3), row_pay)
    x_line = Flow(line_spread(row_pay, x_marks))
    g_far = Flow(spread_pair(g_line.result))
    order.round([x_line, g_far] + some(far, 1) + some(near, 1))
    x_near = Flow(spread_pair([row_pay, x_marks[0]]))
    owned_down = exchanged(s_pieces, s_flows, 0)
    owned_down = order.round([x_line, x_near, g_far] + some(near, 1), owned_down)
    plain = [order.round([x_line, x_near, g_far] + some(far, 1), grad_side(0))]
    x_far = Flow(spread_pair(x_line.result))
    plain.append(order.round([x_near, x_far] + some(far, 1) + near, grad_side(1)))
    order.round([x_far] + far)
    owned_up = exchanged(s_pieces, s_flows, 1)
    back_near = order.round([x_far], row_side(0))
    b_near = Flow(collect_pair(*back_near))
    back_far = order.round([b_near], row_side(1))
    b_far = Flow(collect_pair(*back_far))

    xs, hid, pg = kept_rows

    def lane_block(i, ids):
        return (0, 0, i ^ ids[2] // 2)

    terms = call(
        terms_kernel,
        "terms",
        shaped((SHARDS, depth, 3 * hid_width)),
        [
            pl.BlockSpec((2, slot_rows, 2 * depth), lane_block),
            pl.BlockSpec((2, slot_rows, 2 * depth), lane_block),
            whole_spec((slot_rows, 2 * hid_width)),
            whole_spec((slot_rows, hid_width)),
        ],
        pl.BlockSpec((2, depth, 3 * hid_width), lambda i, ids: (i, 0, 0)),
        (ids, xs, gs[0], pg, hid),
        flops=2 * slot_rows * D * 3 * hid_width,
        steps=4,
    )
    terms = order.round([b_near, b_far], terms)
    t_edge = 2 * H
    t_pieces = [[terms[k][None]] for k in range(6)]
    t_pieces += [[terms[k, :, :t_edge][None], terms[k, :, t_edge:][None]] for k in (6, 7)]
    t_flows = [[Flow(one_hop(piece, to_shard[k])) for piece in t_pieces[k]] for k in range(1, SHARDS)]
    core, near = t_flows[0], t_flows[1] + t_flows[2]
    far = t_flows[5][:1] + t_flows[6][:1] + t_flows[3] + t_flows[4] + t_flows[5][1:] + t_flows[6][1:]

    moe_blocks = call(
        out_side_kernel,
        "out_side",
        (shaped((2 * blocks, rows, D)),) * 2,
        [whole_spec((slot_rows, hid_width))] + [slot_spec] * 4 + down_specs,
        [out_spec((2 * blocks, rows, D), (0, 0, 0))] * 2,
        (ids, hid) + g_near.result + g_far.result + (owned_down, owned_down),
        scratch=[pltpu.VMEM((2, slot_rows, D), low)],
        flops=2 * slot_rows * D * (hid_width + 2 * rows),
    )
    moe_blocks = order.round([b_near, b_far] + some(far, 1), moe_blocks)
    moe = Flow(collect_all(*moe_blocks))
    b_line = [Flow(one_hop(b_near.result[1], to_line[1]))]
    order.round([b_far, moe] + b_line + core + some(far, 1))
    b_line += [
        Flow(one_hop(piece, to_line[2 + i])) for i, piece in enumerate(by_distance(b_far.result))
    ]
    order.round(b_line[1:] + [moe] + some(near, 1))
    grad_sum = total_of([b_near.result[0]] + [flow.result for flow in b_line])

    gate_grad = jnp.where(kept, grad_sum[:, D : D + EXPERTS], 0.0)
    logit_grad = gates * (gate_grad - jnp.sum(gates * gate_grad, -1, keepdims=True))
    logit_grad = jnp.pad(logit_grad.astype(low), ((0, 0), (0, pad)))
    scaled_two = grad_sum[:, :D] + dot(logit_grad, router_full, rows_by_rows)
    grad_out = output_cotangent.astype(full)
    mean_two = jnp.mean(scaled_two * normal_two, -1, keepdims=True)
    mid_grad = grad_out + inverse_two * (scaled_two - normal_two * mean_two)
    branch_grad = mid_grad.astype(low)
    attended_grad = dot(branch_grad, out_full, rows_by_cols).astype(low)

    kv_out = pl.BlockSpec((half_len, kv_tile), lambda j, ids: (0, j))
    query_back, key_mine, key_theirs, value_mine, value_theirs = call(
        attend_back_kernel,
        "attend_back",
        (shaped((rows, q_width)),) + (shaped((half_len, kv_width)),) * 4,
        [q_spec, q_spec]
        + kv_specs(0)
        + kv_specs(pairs)
        + [whole_spec((rows, seq_len)), log_spec, whole_spec((rows, 128)), whole_spec((rows, 128))],
        [q_spec] + [kv_out] * 4,
        (ids, queries, attended_grad, kv_line, kv_other, kv_line, kv_other, bias, logs, cosine, sine),
        flops=10 * rows * seq_len * q_width,
        steps=pairs,
    )
    kv_theirs = jnp.concatenate([key_theirs, value_theirs], 1)
    kv_mine = jnp.concatenate([key_mine, value_mine], 1)
    def dense_flow(products):
        return dense_terms(half_at, products, 2, 4 * GROUPS, fine)

    early_blocks = dense_flow([(branch_grad, attended, 0), (normed_in, query_back, q_width)])
    kv_theirs, kv_mine, early_blocks = order.round(
        [moe] + some(far, 2) + near, (kv_theirs, kv_mine, early_blocks)
    )
    kv_core = Flow(one_hop(kv_theirs, to_core))
    early = Flow(collect_all(*early_blocks))
    order.round([kv_core, early])
    kv_half = add_low(kv_mine, kv_core.result).reshape(4, rows, 2 * kv_width)
    kv = [Flow(one_hop(kv_half[k], to_line[k])) for k in (1, 2, 3)]
    order.round(kv + [early])
    m_line = Flow(line_collect(moe.result[:2], moe.result[2:]))
    kv_grad = total_of([kv_half[0]] + [flow.result for flow in kv])

    def line_of(blocks):
        return [Flow(one_hop(blocks[k], to_line[k])) for k in (1, 2, 3)]

    def swapped(values):
        lanes = jnp.arange(values.shape[1]) % HEAD_DIM < HEAD_DIM // 2
        return jnp.where(
            lanes[None], jnp.roll(values, -HEAD_DIM // 2, 1), jnp.roll(values, HEAD_DIM // 2, 1)
        )

    key_grad = kv_grad[:, :kv_width]
    key_back = key_grad * jnp.tile(cosine, (1, pairs)) - swapped(key_grad) * jnp.tile(sine, (1, pairs))
    kv_rows = jnp.concatenate([key_back, kv_grad[:, kv_width:]], 1).astype(low)
    scaled_one = dot(query_back, dense_full[:, :q_width], rows_by_rows) + dot(
        kv_rows, dense_full[:, q_width:qkv_width], rows_by_rows
    )
    mean_one = jnp.mean(scaled_one * normal_one, -1, keepdims=True)
    input_grad = mid_grad + inverse_one * (scaled_one - normal_one * mean_one)
    pad_lanes = jnp.arange(128)[None, :]

    def marker(lane):
        return jnp.broadcast_to(jnp.where(pad_lanes == lane, 1.0, 0.0), (rows, 128)).astype(low)

    late_blocks = dense_flow(
        [
            (normed_in, kv_rows, 0),
            (normed_mid, logit_grad, 2 * kv_width),
            ((scaled_two * normal_two).astype(low), marker(EXPERTS), 2 * kv_width),
        ]
    )
    late_blocks = order.round([early, m_line] + some(far, 1), late_blocks)
    late = Flow(collect_all(*late_blocks))
    input_grad = order.round(
        [late, m_line], input_grad.astype(low)
    )
    early_line = line_of(early.result)
    order.round([late, m_line] + early_line)
    order.round([late] + far)
    late_line = line_of(late.result)
    spots = jnp.arange(GROUPS, dtype=jnp.int32) ^ group_at
    mate = 1 + shard_at % 2
    spots = jnp.where(spots == mate, 1, jnp.where(spots == 3 - mate, 2, spots))
    places = [spots[i] for i in range(GROUPS)]

    t_parts = t_pieces[0] + [flow.result for flows in t_flows for flow in flows]

    def to_expert(k, ids):
        return (0, jnp.where(k < SHARDS, ids[2] ^ k, k))

    gate_up_grad, down_grad = call(
        unpack_kernel,
        "unpack",
        (shaped(gate_up_weight.shape, full), shaped(down_weight.shape, full)),
        [whole_spec(piece.shape) for piece in t_parts] + [whole_spec((depth, 1))],
        [pl.BlockSpec((depth, 2 * H), to_expert), pl.BlockSpec((depth, H), to_expert)],
        (ids,) + tuple(t_parts) + (gain_two,),
        steps=own_experts,
    )
    gate_up_grad, down_grad = order.round(late_line, (gate_up_grad, down_grad))
    own_sum = jnp.concatenate(
        [
            total_of([flow.result[0]] + [piece.result for piece in line]).astype(low)
            for flow, line in ((early, early_line), (late, late_line))
        ],
        1,
    )
    share_all = Flow(share_flow(own_sum, places))
    order.round([share_all])
    order.round([share_all])
    output = (middle + m_line.result).astype(low)
    dense_sums = share_all.result.astype(full)
    early_sum, late_sum = dense_sums[:, : 2 * q_width], dense_sums[:, 2 * q_width :]
    out_sum, query_sum = early_sum[:, :q_width], early_sum[:, q_width:]

    qkv_sum = jnp.concatenate([query_sum, late_sum[:, : 2 * kv_width]], 1)
    return (
        output,
        input_grad,
        qkv_sum * gain_one,
        out_sum,
        late_sum[:, 2 * kv_width : 2 * kv_width + EXPERTS] * gain_two,
        jnp.sum(qkv_sum * qkv_weight.astype(full), 1),
        late_sum[:, 2 * kv_width + EXPERTS] / gain_two[:, 0],
        gate_up_grad,
        down_grad,
    )


def solution(mesh):
    body = local
    if mesh.shape["expert"] == GROUPS and mesh.shape["shard"] == SHARDS:
        body = local_hops
    return jax.shard_map(
        body,
        mesh=mesh,
        in_specs=(
            P(("expert", "shard"), None),
            P(("expert", "shard"), None),
            P(("expert", "shard"), None),
            P("expert", None),
            P("expert", None),
            P("shard", None),
            P("shard", None),
            P("shard", None),
            P("shard"),
            P("shard"),
            P("shard", "expert"),
            P("shard", "expert"),
        ),
        out_specs=(
            P(("expert", "shard"), None),
            P(("expert", "shard"), None),
            P("shard", None),
            P("shard", None),
            P("shard", None),
            P("shard"),
            P("shard"),
            P("shard", "expert"),
            P("shard", "expert"),
        ),
        check_vma=False,
    )
```

```python
import jax
import jax.numpy as jnp
from jax import lax
from jax.experimental import pallas as pl
from jax.experimental.pallas import tpu as pltpu
from jax.sharding import PartitionSpec as P

D = 1536
HEADS = 24
KV_HEADS = 8
HEAD_DIM = 64
H = 512
EXPERTS = 40
TOP = 8
PIECE = 256
SLOT = 512
CAP = 32


norm_eps = 1e-06
rope_base = 10000.0
masked_score = -1e30


def rope_tables(positions, head_dim):
    half_dim = head_dim // 2
    frequency = rope_base ** (-2.0 * jnp.arange(half_dim, dtype=jnp.float32) / head_dim)
    angles = positions.astype(jnp.float32)[:, None] * frequency[None, :]
    return (jnp.cos(angles)[:, None, :], jnp.sin(angles)[:, None, :])


def rotate(values, cosine, sine_table):
    half_dim = values.shape[-1] // 2
    first_half = values[..., :half_dim]
    second = values[..., half_dim:]
    return jnp.concatenate(
        [first_half * cosine - second * sine_table, second * cosine + first_half * sine_table], -1
    )


def rotate_back(grad_rows, cosine, sine_table):
    half_dim = grad_rows.shape[-1] // 2
    first_half = grad_rows[..., :half_dim]
    second = grad_rows[..., half_dim:]
    return jnp.concatenate(
        [first_half * cosine + second * sine_table, second * cosine - first_half * sine_table], -1
    )


def rms_norm(values, gain):
    inverse = lax.rsqrt(jnp.mean(values * values, -1, keepdims=True) + norm_eps)
    normal = values * inverse
    return (normal * gain, normal, inverse)


def rms_back(grad_rows, gain, normal, inverse):
    scaled = grad_rows * gain
    grad_in = inverse * (scaled - normal * jnp.mean(scaled * normal, -1, keepdims=True))
    return (grad_in, jnp.sum(grad_rows * normal, 0))


def picture_ids(positions, starts, slot_len, piece_len):
    slot_index = positions // slot_len
    picked_slot = slot_index[:, None] == jnp.arange(starts.shape[0], dtype=jnp.int32)[None, :]
    piece_begin = jnp.sum(jnp.where(picked_slot, starts[None, :], 0), axis=1)
    inside = (positions >= piece_begin) & (positions < piece_begin + piece_len)
    return jnp.where(inside, slot_index, -1)


def allowed(query_pos, key_pos, query_doc, key_doc, query_pic, key_pic):
    same_doc = query_doc[:, None] == key_doc[None, :]
    earlier = key_pos[None, :] <= query_pos[:, None]
    same_pic = (query_pic[:, None] == key_pic[None, :]) & (query_pic[:, None] >= 0)
    return same_doc & (earlier | same_pic)


def local(
    tokens_in,
    output_cotangent,
    routes,
    doc_ids,
    picture_starts,
    qkv_weight,
    out_weight,
    router_weight,
    attn_gain,
    moe_gain,
    gate_up_weight,
    down_weight,
):
    qkv_full, out_full, router_full, gain_first, gain_second = (
        lax.all_gather(qkv_weight, "shard", axis=0, tiled=True),
        lax.all_gather(out_weight, "shard", axis=0, tiled=True),
        lax.all_gather(router_weight, "shard", axis=0, tiled=True),
        lax.all_gather(attn_gain, "shard", axis=0, tiled=True),
        lax.all_gather(moe_gain, "shard", axis=0, tiled=True),
    )
    gain_one = gain_first.astype(jnp.float32)
    gain_two = gain_second.astype(jnp.float32)
    tok_rows = tokens_in.shape[0]
    seq_len = doc_ids.shape[1]
    groups = HEADS // KV_HEADS
    q_width = HEADS * HEAD_DIM
    kv_width = KV_HEADS * HEAD_DIM
    score_scale = HEAD_DIM ** (-0.5)
    shard_at = lax.axis_index("shard")
    query_pos = shard_at * tok_rows + jnp.arange(tok_rows, dtype=jnp.int32)
    key_pos = jnp.arange(seq_len, dtype=jnp.int32)
    key_doc = doc_ids[0]
    key_pic = picture_ids(key_pos, picture_starts[0], SLOT, PIECE)
    query_doc = lax.dynamic_slice_in_dim(key_doc, shard_at * tok_rows, tok_rows)
    query_pic = lax.dynamic_slice_in_dim(key_pic, shard_at * tok_rows, tok_rows)
    tokens_f = tokens_in.astype(jnp.float32)
    normed_one, normal_one, inverse_one = rms_norm(tokens_f, gain_one)
    normed_in = normed_one.astype(jnp.bfloat16)
    qkv_rows = jnp.dot(normed_in, qkv_full, preferred_element_type=jnp.float32)
    cosine, sine_table = rope_tables(query_pos, HEAD_DIM)
    queries = (
        rotate(qkv_rows[:, :q_width].reshape(tok_rows, HEADS, HEAD_DIM), cosine, sine_table)
        .astype(jnp.bfloat16)
        .reshape(tok_rows, KV_HEADS, groups, HEAD_DIM)
    )
    key_local = (
        rotate(
            qkv_rows[:, q_width : q_width + kv_width].reshape(tok_rows, KV_HEADS, HEAD_DIM),
            cosine,
            sine_table,
        )
        .astype(jnp.bfloat16)
        .reshape(tok_rows, kv_width)
    )
    value_local = qkv_rows[:, q_width + kv_width :].astype(jnp.bfloat16)
    all_keys, all_values = (
        lax.all_gather(key_local, "shard", axis=0, tiled=True),
        lax.all_gather(value_local, "shard", axis=0, tiled=True),
    )
    span_len = min(512, seq_len)
    span_count = seq_len // span_len

    def block_scores(first_row, key_rows):
        key_block = lax.dynamic_slice_in_dim(key_rows, first_row, span_len, 0).reshape(
            span_len, KV_HEADS, HEAD_DIM
        )
        raw_scores = (
            jnp.einsum("tgrd,kgd->tgrk", queries, key_block, preferred_element_type=jnp.float32)
            * score_scale
        )
        block_pos = lax.dynamic_slice_in_dim(key_pos, first_row, span_len)
        block_doc = lax.dynamic_slice_in_dim(key_doc, first_row, span_len)
        block_pic = lax.dynamic_slice_in_dim(key_pic, first_row, span_len)
        visible = allowed(query_pos, block_pos, query_doc, block_doc, query_pic, block_pic)[
            :, None, None, :
        ]
        return (raw_scores, visible, key_block)

    def value_block_at(first_row, value_rows):
        return lax.dynamic_slice_in_dim(value_rows, first_row, span_len, 0).reshape(
            span_len, KV_HEADS, HEAD_DIM
        )

    def max_step(step_index, carry):
        run_max, run_sum = carry
        raw_scores, visible, key_block = block_scores(step_index * span_len, all_keys)
        masked = jnp.where(visible, raw_scores, masked_score)
        new_max = jnp.maximum(run_max, jnp.max(masked, -1))
        shifted = jnp.where(visible, jnp.exp(masked - new_max[..., None]), 0.0)
        return (new_max, run_sum * jnp.exp(run_max - new_max) + jnp.sum(shifted, -1))

    stat_shape = (tok_rows, KV_HEADS, groups)
    run_max, run_sum = lax.fori_loop(
        0,
        span_count,
        max_step,
        (jnp.full(stat_shape, masked_score, jnp.float32), jnp.zeros(stat_shape, jnp.float32)),
    )
    log_total = run_max + jnp.log(run_sum)

    def probs_of(raw_scores, visible):
        return jnp.exp(jnp.where(visible, raw_scores - log_total[..., None], masked_score))

    def value_step(step_index, summed):
        first_row = step_index * span_len
        raw_scores, visible, key_block = block_scores(first_row, all_keys)
        probs = probs_of(raw_scores, visible).astype(jnp.bfloat16)
        return summed + jnp.einsum(
            "tgrk,kgd->tgrd",
            probs,
            value_block_at(first_row, all_values),
            preferred_element_type=jnp.float32,
        )

    summed = lax.fori_loop(
        0, span_count, value_step, jnp.zeros((tok_rows, KV_HEADS, groups, HEAD_DIM), jnp.float32)
    )
    attended = summed.reshape(tok_rows, q_width).astype(jnp.bfloat16)
    branch = lax.dot_general(
        attended, out_full, (((1,), (1,)), ((), ())), preferred_element_type=jnp.float32
    )
    middle = tokens_f + branch
    normed_two, normal_two, inverse_two = rms_norm(middle, gain_two)
    normed_mid = normed_two.astype(jnp.bfloat16)
    logits = jnp.dot(normed_mid, router_full, preferred_element_type=jnp.float32)
    gates = jax.nn.softmax(jnp.take_along_axis(logits, routes, 1), axis=-1)
    route_hits = routes[:, :, None] == jnp.arange(EXPERTS, dtype=jnp.int32)[None, None, :]
    hit_count = jnp.sum(route_hits.astype(jnp.int32), 1)
    before = jnp.cumsum(hit_count, 0) - hit_count
    slot_index = jnp.take_along_axis(before, routes, 1)
    kept_pair = slot_index < CAP
    flat_slot = routes * CAP + slot_index
    capacity_rows = EXPERTS * CAP
    target = jnp.where(kept_pair, flat_slot, capacity_rows)
    token_ids = jnp.broadcast_to(jnp.arange(tok_rows, dtype=jnp.int32)[:, None], (tok_rows, TOP))
    owner_row = (
        jnp.full((capacity_rows + 1,), -1, jnp.int32)
        .at[target.reshape(-1)]
        .set(token_ids.reshape(-1))[:capacity_rows]
    )
    filled = owner_row >= 0
    source_row = jnp.maximum(owner_row, 0)
    expert_groups = lax.axis_size("expert")
    local_experts = EXPERTS // expert_groups
    send_rows = jnp.where(
        filled[:, None], normed_mid[source_row], jnp.zeros((), jnp.bfloat16)
    ).reshape(expert_groups, local_experts, CAP, D)
    received = lax.all_to_all(send_rows, "expert", split_axis=0, concat_axis=0, tiled=True)
    gate_up_full, down_full = (
        lax.all_gather(gate_up_weight, "shard", axis=0, tiled=True),
        lax.all_gather(down_weight, "shard", axis=0, tiled=True),
    )
    gate_up3 = gate_up_full.reshape(D, local_experts, 2 * H)
    down3 = down_full.reshape(D, local_experts, H)
    projected = jnp.einsum("secd,dej->secj", received, gate_up3, preferred_element_type=jnp.float32)
    gate_part = projected[..., :H]
    up_part = projected[..., H:]
    sigma = jax.nn.sigmoid(gate_part)
    silu_value = gate_part * sigma
    hidden = (silu_value * up_part).astype(jnp.bfloat16)
    expert_out = jnp.einsum(
        "secj,dej->secd", hidden, down3, preferred_element_type=jnp.float32
    ).astype(jnp.bfloat16)
    returned = lax.all_to_all(
        expert_out, "expert", split_axis=0, concat_axis=0, tiled=True
    ).reshape(capacity_rows, D)
    safe_flat = jnp.where(kept_pair, flat_slot, 0)
    picked = returned[safe_flat].astype(jnp.float32)
    pair_weight = jnp.where(kept_pair, gates, 0.0)
    moe_sum = jnp.einsum("tk,tkd->td", pair_weight, picked)
    output = (middle + moe_sum).astype(jnp.bfloat16)
    grad_out = output_cotangent.astype(jnp.float32)
    gate_grad = jnp.where(kept_pair, jnp.einsum("td,tkd->tk", grad_out, picked), 0.0)
    slot_gate = (
        jnp.zeros((capacity_rows + 1,), jnp.float32)
        .at[target.reshape(-1)]
        .set(gates.reshape(-1))[:capacity_rows]
    )
    grad_send = (
        jnp.where(filled[:, None], slot_gate[:, None] * grad_out[source_row], 0.0)
        .astype(jnp.bfloat16)
        .reshape(expert_groups, local_experts, CAP, D)
    )
    grad_received = lax.all_to_all(grad_send, "expert", split_axis=0, concat_axis=0, tiled=True)
    keys_back, values_back = (
        lax.all_gather(key_local, "shard", axis=0, tiled=True),
        lax.all_gather(value_local, "shard", axis=0, tiled=True),
    )
    again_up, again_down = (
        lax.all_gather(gate_up_weight, "shard", axis=0, tiled=True),
        lax.all_gather(down_weight, "shard", axis=0, tiled=True),
    )
    gate_up_back = again_up.reshape(D, local_experts, 2 * H)
    down_back = again_down.reshape(D, local_experts, H)
    hidden_grad = jnp.einsum(
        "secd,dej->secj", grad_received, down_back, preferred_element_type=jnp.float32
    )
    silu_slope = sigma * (1.0 + gate_part * (1.0 - sigma))
    proj_grad = jnp.concatenate(
        [hidden_grad * up_part * silu_slope, hidden_grad * silu_value], -1
    ).astype(jnp.bfloat16)
    row_grad = jnp.einsum(
        "secj,dej->secd", proj_grad, gate_up_back, preferred_element_type=jnp.float32
    ).astype(jnp.bfloat16)
    grad_back = lax.all_to_all(row_grad, "expert", split_axis=0, concat_axis=0, tiled=True).reshape(
        capacity_rows, D
    )
    row_count = gate_up_weight.shape[0] * lax.axis_size("shard")
    up_terms = jnp.einsum(
        "secd,secj->dej", received, proj_grad, preferred_element_type=jnp.float32
    ).reshape(row_count, local_experts * 2 * H)
    down_terms = jnp.einsum(
        "secd,secj->dej", grad_received, hidden, preferred_element_type=jnp.float32
    ).reshape(row_count, local_experts * H)
    expert_sums = lax.psum_scatter(
        jnp.concatenate([up_terms, down_terms], 1).astype(jnp.bfloat16),
        "shard",
        scatter_dimension=0,
        tiled=True,
    ).astype(jnp.float32)
    gate_up_grad = expert_sums[:, : local_experts * 2 * H]
    down_grad = expert_sums[:, local_experts * 2 * H :]
    mid_norm_grad = jnp.einsum(
        "tk,tkd->td", kept_pair.astype(jnp.float32), grad_back[safe_flat].astype(jnp.float32)
    )
    chosen_grad = gates * (gate_grad - jnp.sum(gates * gate_grad, -1, keepdims=True))
    logit_grad = jnp.sum(jnp.where(route_hits, chosen_grad[:, :, None], 0.0), 1).astype(
        jnp.bfloat16
    )
    mid_norm_grad = mid_norm_grad + lax.dot_general(
        logit_grad, router_full, (((1,), (1,)), ((), ())), preferred_element_type=jnp.float32
    )
    router_grad = lax.dot_general(
        normed_mid, logit_grad, (((0,), (0,)), ((), ())), preferred_element_type=jnp.float32
    )
    mid_part, moe_gain_grad = rms_back(mid_norm_grad, gain_two, normal_two, inverse_two)
    mid_grad = grad_out + mid_part
    branch_grad = mid_grad.astype(jnp.bfloat16)
    out_weight_grad = lax.dot_general(
        branch_grad, attended, (((0,), (0,)), ((), ())), preferred_element_type=jnp.float32
    )
    attended_grad = (
        jnp.dot(branch_grad, out_full, preferred_element_type=jnp.float32)
        .astype(jnp.bfloat16)
        .reshape(tok_rows, KV_HEADS, groups, HEAD_DIM)
    )

    def dot_step(step_index, row_dot):
        first_row = step_index * span_len
        raw_scores, visible, key_block = block_scores(first_row, keys_back)
        prob_full = probs_of(raw_scores, visible)
        prob_grad = jnp.einsum(
            "tgrd,kgd->tgrk",
            attended_grad,
            value_block_at(first_row, values_back),
            preferred_element_type=jnp.float32,
        )
        return row_dot + jnp.sum(prob_full * prob_grad, -1)

    row_dot = lax.fori_loop(0, span_count, dot_step, jnp.zeros(stat_shape, jnp.float32))

    def grad_step(step_index, carry):
        query_grad, key_terms, value_terms = carry
        first_row = step_index * span_len
        raw_scores, visible, key_block = block_scores(first_row, keys_back)
        prob_full = probs_of(raw_scores, visible)
        prob_grad = jnp.einsum(
            "tgrd,kgd->tgrk",
            attended_grad,
            value_block_at(first_row, values_back),
            preferred_element_type=jnp.float32,
        )
        score_grad = (prob_full * (prob_grad - row_dot[..., None])).astype(jnp.bfloat16)
        query_grad = query_grad + jnp.einsum(
            "tgrk,kgd->tgrd", score_grad, key_block, preferred_element_type=jnp.float32
        )
        key_part = (
            jnp.einsum(
                "tgrk,tgrd->kgd", score_grad, queries, preferred_element_type=jnp.float32
            ).reshape(span_len, kv_width)
            * score_scale
        )
        value_part = jnp.einsum(
            "tgrk,tgrd->kgd",
            prob_full.astype(jnp.bfloat16),
            attended_grad,
            preferred_element_type=jnp.float32,
        ).reshape(span_len, kv_width)
        key_terms = lax.dynamic_update_slice_in_dim(key_terms, key_part, first_row, 0)
        value_terms = lax.dynamic_update_slice_in_dim(value_terms, value_part, first_row, 0)
        return (query_grad, key_terms, value_terms)

    query_grad, key_terms, value_terms = lax.fori_loop(
        0,
        span_count,
        grad_step,
        (
            jnp.zeros((tok_rows, KV_HEADS, groups, HEAD_DIM), jnp.float32),
            jnp.zeros((seq_len, kv_width), jnp.float32),
            jnp.zeros((seq_len, kv_width), jnp.float32),
        ),
    )
    key_grad, value_grad = (
        lax.psum_scatter(
            key_terms.astype(jnp.bfloat16), "shard", scatter_dimension=0, tiled=True
        ).astype(jnp.float32),
        lax.psum_scatter(
            value_terms.astype(jnp.bfloat16), "shard", scatter_dimension=0, tiled=True
        ).astype(jnp.float32),
    )
    query_back = rotate_back(
        (query_grad * score_scale).reshape(tok_rows, HEADS, HEAD_DIM), cosine, sine_table
    ).reshape(tok_rows, q_width)
    key_back = rotate_back(
        key_grad.reshape(tok_rows, KV_HEADS, HEAD_DIM), cosine, sine_table
    ).reshape(tok_rows, kv_width)
    qkv_grad_rows = jnp.concatenate([query_back, key_back, value_grad], 1).astype(jnp.bfloat16)
    qkv_weight_grad = lax.dot_general(
        normed_in, qkv_grad_rows, (((0,), (0,)), ((), ())), preferred_element_type=jnp.float32
    )
    in_norm_grad = lax.dot_general(
        qkv_grad_rows, qkv_full, (((1,), (1,)), ((), ())), preferred_element_type=jnp.float32
    )
    in_part, attn_gain_grad = rms_back(in_norm_grad, gain_one, normal_one, inverse_one)
    input_grad = (mid_grad + in_part).astype(jnp.bfloat16)
    dense_sums = (
        lax.psum_scatter(
            qkv_weight_grad.astype(jnp.bfloat16), "shard", scatter_dimension=0, tiled=True
        ).astype(jnp.float32),
        lax.psum_scatter(
            out_weight_grad.astype(jnp.bfloat16), "shard", scatter_dimension=0, tiled=True
        ).astype(jnp.float32),
        lax.psum_scatter(
            router_grad.astype(jnp.bfloat16), "shard", scatter_dimension=0, tiled=True
        ).astype(jnp.float32),
        lax.psum_scatter(
            attn_gain_grad.astype(jnp.bfloat16), "shard", scatter_dimension=0, tiled=True
        ).astype(jnp.float32),
        lax.psum_scatter(
            moe_gain_grad.astype(jnp.bfloat16), "shard", scatter_dimension=0, tiled=True
        ).astype(jnp.float32),
    )
    dense_totals = (
        lax.psum(dense_sums[0].astype(jnp.bfloat16), "expert").astype(jnp.float32),
        lax.psum(dense_sums[1].astype(jnp.bfloat16), "expert").astype(jnp.float32),
        lax.psum(dense_sums[2].astype(jnp.bfloat16), "expert").astype(jnp.float32),
        lax.psum(dense_sums[3].astype(jnp.bfloat16), "expert").astype(jnp.float32),
        lax.psum(dense_sums[4].astype(jnp.bfloat16), "expert").astype(jnp.float32),
    )
    return (
        output,
        input_grad,
        dense_totals[0],
        dense_totals[1],
        dense_totals[2],
        dense_totals[3],
        dense_totals[4],
        gate_up_grad,
        down_grad,
    )


GROUPS = 4
SHARDS = 8
rows_by_cols = ((1,), (0,))
rows_by_rows = ((1,), (1,))
cols_by_cols = ((0,), (0,))


def dot(one, two, dims):
    return lax.dot_general(one, two, (dims, ((), ())), preferred_element_type=jnp.float32)


def whole_spec(shape):
    return pl.BlockSpec(shape, lambda i, ids: (0,) * len(shape), pipeline_mode=pl.Buffered(1))


def block_spec(shape, index):
    return pl.BlockSpec(shape, lambda i, ids: index, pipeline_mode=pl.Buffered(1))


def out_spec(shape, index):
    return pl.BlockSpec(shape, lambda i, ids: index)


in_place = pl.BlockSpec(memory_space=pl.ANY)


def shaped(shape, dtype=jnp.bfloat16):
    return jax.ShapeDtypeStruct(shape, dtype)


def call(kernel, name, out_shape, in_specs, out_specs, args, scratch=(), aliases=None, flops=0, steps=1):
    moved = sum(a.size * a.dtype.itemsize for a in args[1:])
    return pl.pallas_call(
        kernel,
        name=name,
        out_shape=out_shape,
        grid_spec=pltpu.PrefetchScalarGridSpec(
            num_scalar_prefetch=1,
            grid=(steps,),
            in_specs=in_specs,
            out_specs=out_specs,
            scratch_shapes=list(scratch),
        ),
        input_output_aliases=aliases or {},
        compiler_params=pltpu.CompilerParams(
            vmem_limit_bytes=58 * 1024 * 1024, dimension_semantics=("arbitrary",)
        ),
        cost_estimate=pl.CostEstimate(flops=flops, transcendentals=0, bytes_accessed=moved),
    )(*args)


def place_rows(offsets, parts, height):
    count, fine, width = parts[0].shape

    def kernel(at, *refs):
        sources, target, done = refs[: len(parts)], refs[len(parts)], refs[-1]
        copies = []
        for n, source in enumerate(sources):
            for i in range(count):
                row = pl.multiple_of(at[n * count + i], 16)
                copies.append(
                    pltpu.make_async_copy(
                        source.at[i], target.at[pl.ds(row, fine)], done.at[n * count + i]
                    )
                )
        for copy in copies:
            copy.start()
        for copy in copies:
            copy.wait()

    return call(
        kernel,
        "place_rows",
        shaped((height, width), parts[0].dtype),
        [in_place] * len(parts),
        out_spec((height, width), (0, 0)),
        (offsets,) + tuple(parts),
        scratch=[pltpu.SemaphoreType.DMA((len(parts) * count,))],
    )


def dense_terms(offsets, products, parts, count, fine):
    height = products[0][0].shape[1]
    width = max(first + two.shape[1] for _, two, first in products)
    firsts = [first for _, _, first in products]

    def kernel(at, *refs):
        sources, targets, held = refs[: 2 * len(firsts)], refs[2 * len(firsts) : -1], refs[-1]
        total = {}
        for n, first in enumerate(firsts):
            found = dot(sources[2 * n][...], sources[2 * n + 1][...], cols_by_cols)
            total[first] = total[first] + found if first in total else found
        for first, found in total.items():
            held[:, first : first + found.shape[1]] = found.astype(jnp.bfloat16)
        for n, target in enumerate(targets):
            for i in range(count):
                row = pl.multiple_of(at[n * count + i], 16)
                target[i] = held[pl.ds(row, fine)]

    operands = [array for one, two, _ in products for array in (one, two)]
    return call(
        kernel,
        "dense_terms",
        [shaped((count, fine, width))] * parts,
        [whole_spec(array.shape) for array in operands],
        [out_spec((count, fine, width), (0, 0, 0))] * parts,
        (offsets,) + tuple(operands),
        scratch=[pltpu.VMEM((height, width), jnp.bfloat16)],
        flops=2 * height * width * products[0][0].shape[0],
    )


def pack_kernel(ids, up, gate_part, up_part, down, down_part, gain, *packs):
    width = down.shape[1]
    scale = gain[...]
    step = pl.program_id(0)

    def scaled(rows):
        return (rows.astype(jnp.float32) * scale).astype(jnp.bfloat16)

    for k in range(SHARDS):

        @pl.when(step == k)
        def _(k=k):
            downs, ups = packs[2 * k : 2 * k + 2]
            downs[0, :, :width] = down[...]
            downs[0, :, width:] = down_part[...]
            ups[0, :, : 2 * width] = scaled(up[...])
            part = down_part.shape[1]
            ups[0, :, 2 * width : 2 * width + part] = scaled(gate_part[...])
            ups[0, :, 2 * width + part :] = scaled(up_part[...])


def unpack_kernel(ids, *refs):
    pieces, gain, up_grad, down_grad = refs[: SHARDS + 2], refs[-3], refs[-2], refs[-1]
    scale = gain[...]
    step = pl.program_id(0)
    share = SHARDS // (pl.num_programs(0) - SHARDS)
    part = pieces[0].shape[2] // 3 - H
    edge = pieces[6].shape[2]

    def columns(k, first, count):
        if k < 6:
            found = pieces[k][0, :, first : first + count]
        elif first < edge:
            found = pieces[2 * k - 6][0, :, first : first + count]
        else:
            found = pieces[2 * k - 5][0, :, first - edge : first - edge + count]
        return found.astype(jnp.float32)

    for k in range(SHARDS):
        source = ids[2] ^ k

        @pl.when(step == k)
        def _(k=k):
            down_grad[...] = columns(k, 0, H)
            up_grad[:, :H] = columns(k, H, H) * scale
            up_grad[:, H:] = columns(k, 2 * H, H) * scale

        @pl.when(step == SHARDS + source // share)
        def _(k=k, source=source):
            at = pl.multiple_of(source % share * part, part)
            at_up = pl.multiple_of(H + source % share * part, part)
            down_grad[:, pl.ds(at, part)] = columns(k, 3 * H, part)
            up_grad[:, pl.ds(at, part)] = columns(k, 3 * H + part, part) * scale
            up_grad[:, pl.ds(at_up, part)] = columns(k, 3 * H + 2 * part, part) * scale


def turn(rows, cosine, sine):
    width = rows.shape[1]
    lanes = lax.broadcasted_iota(jnp.int32, (rows.shape[0], 128), 1)
    first = lanes % HEAD_DIM < HEAD_DIM // 2
    turned = []
    for at in range(0, width, 128):
        piece = rows[:, at : at + 128]
        swapped = jnp.where(
            first,
            pltpu.roll(piece, 128 - HEAD_DIM // 2, 1),
            pltpu.roll(piece, HEAD_DIM // 2, 1),
        )
        turned.append(piece * cosine + swapped * sine)
    return jnp.concatenate(turned, 1)


def qkv_kernel(ids, normed, weight, cosine, sine, queries, key_value):
    step = pl.program_id(0)
    found = dot(normed[...], weight[...], rows_by_cols)

    @pl.when(step < 3)
    def _():
        queries[...] = turn(found, cosine[...], sine[...]).astype(jnp.bfloat16)

    @pl.when(step == 3)
    def _():
        key_value[...] = turn(found, cosine[...], sine[...]).astype(jnp.bfloat16)

    @pl.when(step == 4)
    def _():
        key_value[...] = found.astype(jnp.bfloat16)


def attend_kernel(ids, queries, key_line, key_other, value_line, value_other, bias, attended, logs):
    scale = HEAD_DIM ** (-0.5)
    groups = HEADS // KV_HEADS
    hidden = bias[...]
    keys = jnp.concatenate([key_line[...], key_other[...]], 0)
    values = jnp.concatenate([value_line[...], value_other[...]], 0)
    lanes = lax.broadcasted_iota(jnp.int32, (queries.shape[0], 128), 1)
    totals = jnp.zeros((queries.shape[0], 128), jnp.float32)
    found = []
    for n in range(2 * groups):
        at = n // groups * HEAD_DIM
        scores = dot(
            queries[:, n * HEAD_DIM : (n + 1) * HEAD_DIM], keys[:, at : at + HEAD_DIM], rows_by_rows
        )
        scores = scores * scale + hidden
        top = jnp.max(scores, 1, keepdims=True)
        raised = jnp.exp(scores - top)
        total = jnp.sum(raised, 1, keepdims=True)
        probs = (raised / total).astype(jnp.bfloat16)
        found.append(dot(probs, values[:, at : at + HEAD_DIM], rows_by_cols))
        totals = jnp.where(lanes == n, top + jnp.log(total), totals)
    attended[...] = jnp.concatenate(found, 1).astype(jnp.bfloat16)
    logs[0] = totals


def attend_back_kernel(
    ids, queries, grads, key_line, key_other, value_line, value_other, bias, logs, cosine, sine,
    query_grad, key_mine, key_theirs, value_mine, value_theirs,
):
    scale = HEAD_DIM ** (-0.5)
    groups = HEADS // KV_HEADS
    hidden = bias[...]
    keys = jnp.concatenate([key_line[...], key_other[...]], 0)
    values = jnp.concatenate([value_line[...], value_other[...]], 0)
    half = key_line.shape[0]
    found = []
    key_found, value_found = [], []
    for n in range(2 * groups):
        own = n // groups
        at = own * HEAD_DIM
        head = slice(n * HEAD_DIM, (n + 1) * HEAD_DIM)
        query = queries[:, head]
        grad = grads[:, head]
        scores = dot(query, keys[:, at : at + HEAD_DIM], rows_by_rows) * scale + hidden
        probs = jnp.exp(scores - lane_value(logs[0], n))
        prob_grad = dot(grad, values[:, at : at + HEAD_DIM], rows_by_rows)
        row_dot = jnp.sum(probs * prob_grad, 1, keepdims=True)
        score_grad = (probs * (prob_grad - row_dot)).astype(jnp.bfloat16)
        found.append(dot(score_grad, keys[:, at : at + HEAD_DIM], rows_by_cols))
        key_part = dot(score_grad, query, cols_by_cols)
        value_part = dot(probs.astype(jnp.bfloat16), grad, cols_by_cols)
        if n % groups:
            key_found[own] = key_found[own] + key_part
            value_found[own] = value_found[own] + value_part
        else:
            key_found.append(key_part)
            value_found.append(value_part)
    found = jnp.concatenate(found, 1) * scale
    query_grad[...] = turn(found, cosine[...], -sine[...]).astype(jnp.bfloat16)
    key_found = (jnp.concatenate(key_found, 1) * scale).astype(jnp.bfloat16)
    value_found = jnp.concatenate(value_found, 1).astype(jnp.bfloat16)
    key_mine[...] = key_found[:half]
    key_theirs[...] = key_found[half:]
    value_mine[...] = value_found[:half]
    value_theirs[...] = value_found[half:]


def lane_value(rows, index):
    lanes = lax.broadcasted_iota(jnp.int32, rows.shape, 1)
    return jnp.sum(jnp.where(lanes == index, rows, 0.0), 1, keepdims=True)


def picks_of(extra, one, two):
    extra = extra.astype(jnp.float32)
    lanes = lax.broadcasted_iota(jnp.int32, (extra.shape[0], 2 * CAP), 1)
    wanted = jnp.where(lanes < CAP, lane_value(extra, one), lane_value(extra, two))
    place = jnp.where(lanes < CAP, lanes, lanes - CAP).astype(jnp.float32)
    return jnp.where(wanted == place, 1.0, 0.0).astype(jnp.bfloat16)


def grad_side_kernel(ids, half, other, down_one, down_two, *refs):
    gs, plain = refs[-2:]
    count = half.shape[0]
    for i in range(2 * count):
        source = half if i < count else other
        pick = picks_of(source[i % count, :, D:], ids[0], ids[1])
        found = dot(pick, source[i % count, :, :D], cols_by_cols).astype(jnp.bfloat16)
        gs[0, i * CAP : (i + 1) * CAP] = found[:CAP]
        gs[1, i * CAP : (i + 1) * CAP] = found[CAP:]
    width = down_one.shape[1]
    plain[:, :width] = dot(gs[0], down_one[...], rows_by_cols)
    plain[:, width:] = dot(gs[1], down_two[...], rows_by_cols)


def combine_rows(ids, rows, slots_half, slots_other, back_half, back_other):
    count = slots_half.shape[0]
    for i in range(2 * count):
        target = back_half if i < count else back_other
        slots = slots_half if i < count else slots_other
        pick = picks_of(slots[i % count], ids[0], ids[1])
        at = slice(i * CAP, (i + 1) * CAP)
        both = jnp.concatenate([rows[0, at], rows[1, at]], 0)
        target[i % count] = dot(pick, both, rows_by_cols).astype(jnp.bfloat16)


def row_side_kernel(
    ids, half, other, slots_half, slots_other, plain, gate_one, gate_two, up_one, up_two, *refs
):
    back_half, back_other, xs, hid, pg, gates, tokens, back_rows = refs[-8:]
    total = xs.shape[1]
    count = half.shape[0]
    for i in range(2 * count):
        source = half if i < count else other
        slots = slots_half if i < count else slots_other
        pick = picks_of(slots[i % count], ids[0], ids[1])
        found = dot(pick, source[i % count], cols_by_cols)
        extra = found[:, D:]
        found = found.astype(jnp.bfloat16)
        at = slice(i * CAP, (i + 1) * CAP)
        for n in range(2):
            xs[n, at] = found[n * CAP : (n + 1) * CAP, :D]
            own = extra[n * CAP : (n + 1) * CAP]
            gates[n, at] = lane_value(own, ids[n]) + lane_value(own, ids[n] + EXPERTS)
    first = 0
    second = hid.shape[1]
    for n, gate_weight, up_weight in ((0, gate_one, up_one), (1, gate_two, up_two)):
        width = up_weight.shape[1]
        gate_part = dot(xs[n], gate_weight[...], rows_by_cols)
        up_part = dot(xs[n], up_weight[...], rows_by_cols)
        at = slice(first, first + width)
        at_up = slice(second + first, second + first + width)
        own_plain = plain[:, at]
        sigma = 1.0 / (1.0 + jnp.exp(-gate_part))
        silu_value = gate_part * sigma
        hidden = silu_value * up_part
        tokens[n] = jnp.sum(hidden * own_plain, 1, keepdims=True)
        hid[:, at] = (hidden * gates[n]).astype(jnp.bfloat16)
        hidden_grad = own_plain * gates[n]
        slope = sigma * (1.0 + gate_part * (1.0 - sigma))
        pg[:, at] = (hidden_grad * up_part * slope).astype(jnp.bfloat16)
        pg[:, at_up] = (hidden_grad * silu_value).astype(jnp.bfloat16)
        row_grad = dot(pg[:, at], gate_weight[...], rows_by_rows)
        row_grad = row_grad + dot(pg[:, at_up], up_weight[...], rows_by_rows)
        back_rows[n, :, :D] = row_grad.astype(jnp.bfloat16)
        lanes = lax.broadcasted_iota(jnp.int32, (total, 128), 1)
        back_rows[n, :, D:] = jnp.where(lanes == ids[n], tokens[n], 0.0).astype(jnp.bfloat16)
        first += width
    combine_rows(ids, back_rows, slots_half, slots_other, back_half, back_other)


def out_side_kernel(ids, hid, *refs):
    slots, (down_one, down_two), (mine, theirs, out_rows) = refs[:4], refs[4:6], refs[6:]
    width = down_one.shape[1]
    count = slots[0].shape[0]
    out_rows[0] = dot(hid[:, :width], down_one[...], rows_by_rows).astype(jnp.bfloat16)
    out_rows[1] = dot(hid[:, width:], down_two[...], rows_by_rows).astype(jnp.bfloat16)
    for n, own in enumerate(slots):
        target = theirs if n % 2 else mine
        for i in range(count):
            pick = picks_of(own[i], ids[0], ids[1])
            at = slice((n * count + i) * CAP, (n * count + i + 1) * CAP)
            both = jnp.concatenate([out_rows[0, at], out_rows[1, at]], 0)
            place = i // 2 * 4 + n // 2 * 2 + i % 2
            target[place] = dot(pick, both, rows_by_cols).astype(jnp.bfloat16)


def terms_kernel(ids, xs, gs, pg, hid, terms):
    depth = terms.shape[1]
    width = hid.shape[1]
    for one, two, n, shift, first, count in (
        (gs, hid, 0, 0, 0, H),
        (xs, pg, 0, 0, H, H),
        (xs, pg, 0, width, 2 * H, H),
        (gs, hid, 1, H, 3 * H, width - H),
        (xs, pg, 1, H, 2 * H + width, width - H),
        (xs, pg, 1, width + H, H + 2 * width, width - H),
    ):
        found = dot(one[n], two[:, shift : shift + count], cols_by_cols).astype(jnp.bfloat16)
        for i in range(2):
            at = i ^ ids[2] % 2
            terms[pl.ds(at, 1), :, first : first + count] = found[i * depth : (i + 1) * depth][None]


def hop(values, pairs):
    return lax.ppermute(values, ("expert", "shard"), pairs)


def hop_pairs(step):
    return [
        (e * SHARDS + s, step(e, s)[0] * SHARDS + step(e, s)[1])
        for e in range(GROUPS)
        for s in range(SHARDS)
    ]


to_core = hop_pairs(lambda e, s: (e, s ^ 1))
to_line = [hop_pairs(lambda e, s, k=k: (e, s ^ (2 * k))) for k in range(4)]
over_middle = [
    (e * SHARDS + s, e * SHARDS + (s ^ 6)) for e in range(GROUPS) for s in range(2, 6)
]
from_middle = [
    (e * SHARDS + s, e * SHARDS + (s ^ 2)) for e in range(GROUPS) for s in range(2, 6)
]
to_middle = [(there, here) for here, there in from_middle]
to_first = hop_pairs(lambda e, s: (e ^ (1 + s % 2), s))
to_second = hop_pairs(lambda e, s: (e ^ (2 - s % 2), s))


def add_low(one, two):
    return (one.astype(jnp.float32) + two.astype(jnp.float32)).astype(jnp.bfloat16)


def total_of(line):
    return sum(piece.astype(jnp.float32) for piece in line)


class Flow:
    def __init__(self, steps):
        self.steps = steps
        self.result = None
        self.feed(None)

    def feed(self, values):
        try:
            self.want = self.steps.send(values)
        except StopIteration as stop:
            self.want = None
            self.result = stop.value


class Order:
    def __init__(self, mark):
        self.mark = mark

    def tie(self, values):
        values, self.mark = lax.optimization_barrier((values, self.mark))
        return values

    def round(self, flows, work=None):
        values, self.mark = lax.optimization_barrier(([f.want[0] for f in flows], self.mark))
        found = [hop(v, f.want[1]) for v, f in zip(values, flows)]
        found, work, self.mark = lax.optimization_barrier((found, work, self.mark))
        for flow, values in zip(flows, found):
            flow.feed(values)
        return work


def one_hop(values, pairs):
    found = yield values, pairs
    return found


def line_flows(own):
    return [Flow(one_hop(own, to_line[k])) for k in (1, 2, 3)]


def line_spread(own, marks):
    near = yield own, to_line[1]
    marks.append(near)
    two = jnp.stack([own, near])
    crossed = yield two, over_middle
    passed = yield crossed, from_middle
    at = lax.axis_index("shard") // 2
    return jnp.where((at == 1) | (at == 2), crossed, passed)


def line_collect(near, far):
    passed = yield jnp.stack(far), to_middle
    far = add_low(jnp.stack(far), passed)
    crossed = yield far, over_middle
    at = lax.axis_index("shard") // 2
    middle = (at == 1) | (at == 2)
    both = jnp.stack(near).astype(jnp.float32) + jnp.where(middle, crossed, 0).astype(jnp.float32)
    back = yield both[1].astype(jnp.bfloat16), to_line[1]
    return both[0] + back.astype(jnp.float32)


def by_distance(far):
    at = lax.axis_index("shard") // 2
    middle = (at == 1) | (at == 2)
    return [jnp.where(middle, far[1 - i], far[i]) for i in range(2)]


def spread_pair(pieces):
    two = jnp.stack(pieces) if isinstance(pieces, list) else pieces
    first = yield two, to_first
    four = jnp.concatenate([two, first])
    second = yield four, to_second
    eight = jnp.concatenate([four, second])
    other = yield eight, to_core
    return eight, other


def spread_all(line):
    four = jnp.stack(line)
    first = yield four, to_first
    eight = jnp.concatenate([four, first])
    second = yield eight, to_second
    half = jnp.concatenate([eight, second])
    other = yield half, to_core
    return half, other


def collect_pair(mine, theirs):
    found = yield theirs, to_core
    keep, give = add_low(mine[:4], found[:4]), add_low(mine[4:], found[4:])
    found = yield give, to_second
    keep, give = add_low(keep[:2], found[:2]), add_low(keep[2:], found[2:])
    found = yield give, to_first
    return [add_low(keep[i], found[i]) for i in range(2)]


def collect_all(mine, theirs):
    found = yield theirs, to_core
    keep, give = add_low(mine[:8], found[:8]), add_low(mine[8:], found[8:])
    found = yield give, to_second
    keep, give = add_low(keep[:4], found[:4]), add_low(keep[4:], found[4:])
    found = yield give, to_first
    return [add_low(keep[i], found[i]) for i in range(4)]


def share_flow(own, places):
    first = yield own, to_first
    pair = jnp.stack([own, first])
    second = yield pair, to_second
    quarters = jnp.concatenate([pair, second])
    return jnp.concatenate(
        [lax.dynamic_index_in_dim(quarters, place, 0, keepdims=False) for place in places]
    )


def local_hops(
    tokens_in,
    output_cotangent,
    routes,
    doc_ids,
    picture_starts,
    qkv_weight,
    out_weight,
    router_weight,
    attn_gain,
    moe_gain,
    gate_up_weight,
    down_weight,
):
    low = jnp.bfloat16
    full = jnp.float32
    rows = tokens_in.shape[0]
    seq_len = doc_ids.shape[1]
    q_width = HEADS * HEAD_DIM
    kv_width = KV_HEADS * HEAD_DIM
    qkv_width = q_width + 2 * kv_width
    group_at = lax.axis_index("expert")
    shard_at = lax.axis_index("shard")
    own_experts = EXPERTS // GROUPS
    whole = own_experts // SHARDS * SHARDS
    split = own_experts - whole
    share = SHARDS // split
    part = H // share
    hid_width = H + part
    depth = gate_up_weight.shape[0]
    height = SHARDS * depth
    fine = depth // GROUPS
    pad = 128 - EXPERTS
    gain_one = attn_gain.astype(full)[:, None]
    gain_two = moe_gain.astype(full)[:, None]
    expert_one = group_at * own_experts + shard_at
    expert_two = group_at * own_experts + whole + shard_at // share
    ids = jnp.stack([expert_one, expert_two, shard_at])
    order = Order(jnp.zeros((8, 128), full))

    spot = jnp.arange(GROUPS * SHARDS, dtype=jnp.int32)
    spot_core = spot // 8 % 2
    spot_mate = 1 + (shard_at % 2 ^ spot_core)
    spot_q = spot % 8 // 2
    spot_group = jnp.where(spot_q == 1, spot_mate, jnp.where(spot_q == 2, 3 - spot_mate, spot_q))
    spot_line = spot // 16 * 2 + spot % 2
    fine_at = (shard_at ^ (2 * spot_line + spot_core)) * depth + (group_at ^ spot_group) * fine
    half_core = spot // 16
    half_mate = 1 + (shard_at % 2 ^ half_core)
    half_q = spot % 16 // 4
    half_group = jnp.where(half_q == 1, half_mate, jnp.where(half_q == 2, 3 - half_mate, half_q))
    half_at = (shard_at ^ (2 * (spot % 4) + half_core)) * depth + (group_at ^ half_group) * fine

    expert_ids = jnp.arange(EXPERTS, dtype=jnp.int32)
    hits = jnp.any(routes[:, :, None] == expert_ids[None, None, :], 1)
    earlier = jnp.arange(rows)[:, None] > jnp.arange(rows)[None, :]
    before = dot(earlier.astype(low), hits.astype(low), rows_by_cols)
    slots = jnp.where(hits & (before < CAP), before, -1.0)
    kept = slots >= 0
    grad_pay = jnp.concatenate(
        [output_cotangent, jnp.pad(slots.astype(low), ((0, 0), (0, pad)))], 1
    )

    def fine_rows(array):
        return lax.dynamic_slice_in_dim(array, group_at * fine, fine, 0)

    qkv_own = fine_rows(qkv_weight).astype(full) * fine_rows(gain_one)
    router_own = fine_rows(router_weight).astype(full) * fine_rows(gain_two)
    dense_own = jnp.concatenate([qkv_own, jnp.pad(router_own, ((0, 0), (0, pad)))], 1).astype(low)
    out_own = fine_rows(out_weight)

    def column_spec(width, index):
        return pl.BlockSpec((depth, width), lambda k, ids: (0, index(ids[2] ^ k)))

    to_parts = H // part
    packs = call(
        pack_kernel,
        "pack",
        [shaped((1, depth, hid_width)), shaped((1, depth, 2 * hid_width))] * SHARDS,
        [
            column_spec(2 * H, lambda d: d),
            column_spec(part, lambda d: (whole + d // share) * 2 * to_parts + d % share),
            column_spec(part, lambda d: (whole + d // share) * 2 * to_parts + to_parts + d % share),
            column_spec(H, lambda d: d),
            column_spec(part, lambda d: (whole + d // share) * to_parts + d % share),
            pl.BlockSpec((depth, 1), lambda d, ids: (0, 0)),
        ],
        [
            out_spec((1, depth, hid_width), (0, 0, 0)),
            out_spec((1, depth, 2 * hid_width), (0, 0, 0)),
        ]
        * SHARDS,
        (ids, gate_up_weight, gate_up_weight, gate_up_weight, down_weight, down_weight, gain_two),
        steps=SHARDS,
    )

    to_shard = [hop_pairs(lambda e, s, k=k: (e, s ^ k)) for k in range(SHARDS)]
    shard_rows = (shard_at ^ jnp.arange(SHARDS, dtype=jnp.int32)) * depth

    def exchange(pieces):
        flows = [[Flow(one_hop(piece, to_shard[k])) for piece in pieces[k]] for k in range(1, SHARDS)]
        near = [flows[k - 1][n] for n in range(len(pieces[0])) for k in (2, 3)]
        far = [flows[k - 1][n] for n in range(len(pieces[0])) for k in (4, 5, 6, 7)]
        return flows, flows[0], near, far

    def exchanged(pieces, flows, n):
        parts = [pieces[0][n]] + [flow[n].result for flow in flows]
        return place_rows(shard_rows, parts, height)

    s_pieces = [packs[2 * k : 2 * k + 2] for k in range(SHARDS)]
    s_flows, core, near, far = exchange(s_pieces)

    def some(flows, count):
        taken = flows[:count]
        del flows[:count]
        return taken

    w = line_flows(dense_own)
    o = line_flows(out_own)
    g_marks, x_marks = [], []
    g_line = Flow(line_spread(grad_pay, g_marks))
    order.round(w[:2])
    w_near = Flow(spread_pair([dense_own, w[0].result]))
    order.round([w[2], w_near, g_line])
    w_far = Flow(spread_pair([w[1].result, w[2].result]))
    g_near = Flow(spread_pair([grad_pay, g_marks[0]]))
    order.round([w_near, w_far] + some(far, 1) + some(near, 1) + core)
    order.round([w_near, w_far] + o)
    o_all = Flow(spread_all([out_own] + [flow.result for flow in o]))
    order.round([w_far, o_all])
    dense_full = place_rows(fine_at, w_near.result + w_far.result, height)
    router_full = dense_full[:, qkv_width:]

    tokens_f = tokens_in.astype(full)
    inverse_one = lax.rsqrt(jnp.mean(tokens_f * tokens_f, -1, keepdims=True) + norm_eps)
    normal_one = tokens_f * inverse_one
    normed_in = normal_one.astype(low)
    query_pos = shard_at * rows + jnp.arange(rows, dtype=jnp.int32)
    cosine, sine = rope_tables(query_pos, HEAD_DIM)
    cosine = jnp.tile(cosine[:, 0], (1, 4))
    sine = jnp.tile(jnp.concatenate([-sine[:, 0], sine[:, 0]], 1), (1, 2))
    tile = 512
    queries, key_value = call(
        qkv_kernel,
        "qkv",
        (shaped((rows, q_width)), shaped((rows, 2 * kv_width))),
        [
            whole_spec((rows, D)),
            pl.BlockSpec((D, tile), lambda j, ids: (0, j)),
            whole_spec((rows, 128)),
            whole_spec((rows, 128)),
        ],
        [
            pl.BlockSpec((rows, tile), lambda j, ids: (0, jnp.minimum(j, 2))),
            pl.BlockSpec((rows, tile), lambda j, ids: (0, jnp.maximum(j - 3, 0))),
        ],
        (ids, normed_in, dense_full, cosine, sine),
        flops=2 * rows * D * qkv_width,
        steps=qkv_width // tile,
    )
    queries, key_value = order.round(
        [o_all, g_near, g_line] + some(near, 1), (queries, key_value)
    )
    kv = line_flows(key_value)
    order.round(kv + [o_all, g_near])
    kv_line = jnp.concatenate([key_value] + [flow.result for flow in kv])
    kv_core = Flow(one_hop(kv_line, to_core))
    out_full = place_rows(half_at, o_all.result, height)
    out_full = order.round([kv_core], out_full)
    kv_other = kv_core.result
    block_order = jnp.arange(SHARDS, dtype=jnp.int32)
    block_order = shard_at ^ (block_order % 4 * 2 + block_order // 4)
    key_pos = (
        block_order[:, None] * rows + jnp.arange(rows, dtype=jnp.int32)[None, :]
    ).reshape(seq_len)
    doc_blocks = doc_ids[0].reshape(SHARDS, rows)
    block_hits = block_order[:, None] == jnp.arange(SHARDS)[None, :]
    key_doc = jnp.sum(
        jnp.where(block_hits[:, :, None], doc_blocks[None], 0), 1
    ).reshape(seq_len)
    query_doc = key_doc[:rows]
    key_pic = picture_ids(key_pos, picture_starts[0], SLOT, PIECE)
    query_pic = key_pic[:rows]
    visible = allowed(query_pos, key_pos, query_doc, key_doc, query_pic, key_pic)
    bias = jnp.where(visible, 0.0, masked_score)
    pairs = KV_HEADS // 2
    q_tile = q_width // pairs
    kv_tile = kv_width // pairs
    half_len = seq_len // 2

    def kv_specs(first):
        return [pl.BlockSpec((half_len, kv_tile), lambda j, ids: (0, first + j))] * 2

    q_spec = pl.BlockSpec((rows, q_tile), lambda j, ids: (0, j))
    log_spec = pl.BlockSpec((1, rows, 128), lambda j, ids: (j, 0, 0))
    attended, logs = call(
        attend_kernel,
        "attend",
        (shaped((rows, q_width)), shaped((pairs, rows, 128), full)),
        [q_spec] + kv_specs(0) + kv_specs(pairs) + [whole_spec((rows, seq_len))],
        [q_spec, log_spec],
        (ids, queries, kv_line, kv_other, kv_line, kv_other, bias),
        flops=4 * rows * seq_len * q_width,
        steps=pairs,
    )
    branch = dot(attended, out_full, rows_by_rows)
    middle = tokens_f + branch
    inverse_two = lax.rsqrt(jnp.mean(middle * middle, -1, keepdims=True) + norm_eps)
    normal_two = middle * inverse_two
    normed_mid = normal_two.astype(low)
    logits = dot(normed_mid, router_full, rows_by_cols)[:, :EXPERTS]
    logits = jnp.where(hits, logits, masked_score)
    gates = jnp.exp(logits - jnp.max(logits, -1, keepdims=True))
    gates = jnp.where(hits, gates, 0.0)
    gates = gates / jnp.sum(gates, -1, keepdims=True)
    gate_low = gates.astype(low)
    gate_rest = (gates - gate_low.astype(full)).astype(low)
    row_pay = jnp.concatenate(
        [normed_mid, gate_low, gate_rest, jnp.zeros((rows, 128 - 2 * EXPERTS), low)], 1
    )

    slot_rows = GROUPS * SHARDS * CAP
    step_rows = slot_rows // 2
    blocks = 2 * GROUPS
    pay_spec = whole_spec((blocks, rows, D + 128))
    pay_out = out_spec((blocks, rows, D + 128), (0, 0, 0))
    slot_spec = block_spec((blocks, rows, 128), (0, 0, D // 128))
    up_specs = [
        block_spec((height, H), (0, 0)),
        block_spec((height, part), (0, 2 * to_parts)),
        block_spec((height, H), (0, 1)),
        block_spec((height, part), (0, 2 * to_parts + 1)),
    ]
    down_specs = [
        block_spec((height, H), (0, 0)),
        block_spec((height, part), (0, H // part)),
    ]
    back_shape = shaped((blocks, rows, D + 128))
    gs_shape = shaped((2, slot_rows, D))
    kept_shapes = (gs_shape, shaped((slot_rows, hid_width)), shaped((slot_rows, 2 * hid_width)))
    kept_rows = ()

    gs, plain = (), []

    def grad_side(k):
        nonlocal gs
        gs_next, found = call(
            grad_side_kernel,
            "grad_side",
            (gs_shape, shaped((step_rows, hid_width), full)),
            [pay_spec, pay_spec] + down_specs + [in_place] * len(gs),
            [
                out_spec((2, step_rows, D), (0, k, 0)),
                out_spec((step_rows, hid_width), (0, 0)),
            ],
            (ids,) + (g_near, g_far)[k].result + (owned_down, owned_down) + gs,
            aliases={5: 0} if gs else None,
            flops=2 * step_rows * D * (hid_width + 2 * rows),
        )
        gs = (gs_next,)
        return found

    def row_side(k):
        nonlocal kept_rows
        half_back, other_back, *kept_next = call(
            row_side_kernel,
            "row_side",
            (back_shape, back_shape) + kept_shapes,
            [pay_spec, pay_spec, slot_spec, slot_spec, whole_spec((step_rows, hid_width))]
            + up_specs
            + [in_place] * len(kept_rows),
            [
                pay_out,
                pay_out,
                out_spec((2, step_rows, D), (0, k, 0)),
                out_spec((step_rows, hid_width), (k, 0)),
                out_spec((step_rows, 2 * hid_width), (k, 0)),
            ],
            (ids,)
            + (x_near, x_far)[k].result
            + (g_near, g_far)[k].result
            + (plain[k],)
            + (owned_up,) * 4
            + kept_rows,
            scratch=[
                pltpu.VMEM((2, step_rows, 1), full),
                pltpu.VMEM((2, step_rows, 1), full),
                pltpu.VMEM((2, step_rows, D + 128), low),
            ],
            aliases={10: 2, 11: 3, 12: 4} if kept_rows else None,
            flops=8 * step_rows * D * (hid_width + rows),
        )
        kept_rows = tuple(kept_next)
        return half_back, other_back

    row_pay = order.round([g_near, g_line] + some(far, 2), row_pay)
    x_line = Flow(line_spread(row_pay, x_marks))
    g_far = Flow(spread_pair(g_line.result))
    order.round([x_line, g_far] + some(far, 2))
    x_near = Flow(spread_pair([row_pay, x_marks[0]]))
    owned_down = exchanged(s_pieces, s_flows, 0)
    owned_down = order.round([x_line, x_near, g_far] + some(near, 1), owned_down)
    plain = [order.round([x_line, x_near, g_far] + some(far, 1), grad_side(0))]
    x_far = Flow(spread_pair(x_line.result))
    plain.append(order.round([x_near, x_far] + some(far, 1) + near, grad_side(1)))
    order.round([x_far] + far)
    owned_up = exchanged(s_pieces, s_flows, 1)
    back_near = order.round([x_far], row_side(0))
    b_near = Flow(collect_pair(*back_near))
    back_far = order.round([b_near], row_side(1))
    b_far = Flow(collect_pair(*back_far))

    xs, hid, pg = kept_rows

    def lane_block(i, ids):
        return (0, 0, i ^ ids[2] // 2)

    terms = call(
        terms_kernel,
        "terms",
        shaped((SHARDS, depth, 3 * hid_width)),
        [
            pl.BlockSpec((2, slot_rows, 2 * depth), lane_block),
            pl.BlockSpec((2, slot_rows, 2 * depth), lane_block),
            whole_spec((slot_rows, 2 * hid_width)),
            whole_spec((slot_rows, hid_width)),
        ],
        pl.BlockSpec((2, depth, 3 * hid_width), lambda i, ids: (i, 0, 0)),
        (ids, xs, gs[0], pg, hid),
        flops=2 * slot_rows * D * 3 * hid_width,
        steps=4,
    )
    terms = order.round([b_near, b_far], terms)
    t_edge = 2 * H
    t_pieces = [[terms[k][None]] for k in range(6)]
    t_pieces += [[terms[k, :, :t_edge][None], terms[k, :, t_edge:][None]] for k in (6, 7)]
    t_flows = [[Flow(one_hop(piece, to_shard[k])) for piece in t_pieces[k]] for k in range(1, SHARDS)]
    core, near = t_flows[0], t_flows[1] + t_flows[2]
    far = t_flows[5][:1] + t_flows[3] + t_flows[4] + t_flows[5][1:] + t_flows[6]

    moe_blocks = call(
        out_side_kernel,
        "out_side",
        (shaped((2 * blocks, rows, D)),) * 2,
        [whole_spec((slot_rows, hid_width))] + [slot_spec] * 4 + down_specs,
        [out_spec((2 * blocks, rows, D), (0, 0, 0))] * 2,
        (ids, hid) + g_near.result + g_far.result + (owned_down, owned_down),
        scratch=[pltpu.VMEM((2, slot_rows, D), low)],
        flops=2 * slot_rows * D * (hid_width + 2 * rows),
    )
    moe_blocks = order.round([b_near, b_far] + some(far, 1), moe_blocks)
    moe = Flow(collect_all(*moe_blocks))
    b_line = [Flow(one_hop(b_near.result[1], to_line[1]))]
    order.round([b_far, moe] + b_line + core)
    b_line += [
        Flow(one_hop(piece, to_line[2 + i])) for i, piece in enumerate(by_distance(b_far.result))
    ]
    order.round(b_line[1:] + [moe] + some(near, 1))
    grad_sum = total_of([b_near.result[0]] + [flow.result for flow in b_line])

    gate_grad = jnp.where(kept, grad_sum[:, D : D + EXPERTS], 0.0)
    logit_grad = gates * (gate_grad - jnp.sum(gates * gate_grad, -1, keepdims=True))
    logit_grad = jnp.pad(logit_grad.astype(low), ((0, 0), (0, pad)))
    scaled_two = grad_sum[:, :D] + dot(logit_grad, router_full, rows_by_rows)
    grad_out = output_cotangent.astype(full)
    mean_two = jnp.mean(scaled_two * normal_two, -1, keepdims=True)
    mid_grad = grad_out + inverse_two * (scaled_two - normal_two * mean_two)
    branch_grad = mid_grad.astype(low)
    attended_grad = dot(branch_grad, out_full, rows_by_cols).astype(low)

    kv_out = pl.BlockSpec((half_len, kv_tile), lambda j, ids: (0, j))
    query_back, key_mine, key_theirs, value_mine, value_theirs = call(
        attend_back_kernel,
        "attend_back",
        (shaped((rows, q_width)),) + (shaped((half_len, kv_width)),) * 4,
        [q_spec, q_spec]
        + kv_specs(0)
        + kv_specs(pairs)
        + [whole_spec((rows, seq_len)), log_spec, whole_spec((rows, 128)), whole_spec((rows, 128))],
        [q_spec] + [kv_out] * 4,
        (ids, queries, attended_grad, kv_line, kv_other, kv_line, kv_other, bias, logs, cosine, sine),
        flops=10 * rows * seq_len * q_width,
        steps=pairs,
    )
    kv_theirs = jnp.concatenate([key_theirs, value_theirs], 1)
    kv_mine = jnp.concatenate([key_mine, value_mine], 1)
    def dense_flow(products):
        return dense_terms(half_at, products, 2, 4 * GROUPS, fine)

    early_blocks = dense_flow([(branch_grad, attended, 0), (normed_in, query_back, q_width)])
    kv_theirs, kv_mine, early_blocks = order.round(
        [moe] + some(far, 2) + near, (kv_theirs, kv_mine, early_blocks)
    )
    kv_core = Flow(one_hop(kv_theirs, to_core))
    early = Flow(collect_all(*early_blocks))
    order.round([kv_core, early])
    kv_half = add_low(kv_mine, kv_core.result).reshape(4, rows, 2 * kv_width)
    kv = [Flow(one_hop(kv_half[k], to_line[k])) for k in (1, 2, 3)]
    order.round(kv + [early])
    m_line = Flow(line_collect(moe.result[:2], moe.result[2:]))
    kv_grad = total_of([kv_half[0]] + [flow.result for flow in kv])

    def line_of(blocks):
        return [Flow(one_hop(blocks[k], to_line[k])) for k in (1, 2, 3)]

    def swapped(values):
        lanes = jnp.arange(values.shape[1]) % HEAD_DIM < HEAD_DIM // 2
        return jnp.where(
            lanes[None], jnp.roll(values, -HEAD_DIM // 2, 1), jnp.roll(values, HEAD_DIM // 2, 1)
        )

    key_grad = kv_grad[:, :kv_width]
    key_back = key_grad * jnp.tile(cosine, (1, pairs)) - swapped(key_grad) * jnp.tile(sine, (1, pairs))
    kv_rows = jnp.concatenate([key_back, kv_grad[:, kv_width:]], 1).astype(low)
    scaled_one = dot(query_back, dense_full[:, :q_width], rows_by_rows) + dot(
        kv_rows, dense_full[:, q_width:qkv_width], rows_by_rows
    )
    mean_one = jnp.mean(scaled_one * normal_one, -1, keepdims=True)
    input_grad = mid_grad + inverse_one * (scaled_one - normal_one * mean_one)
    pad_lanes = jnp.arange(128)[None, :]

    def marker(lane):
        return jnp.broadcast_to(jnp.where(pad_lanes == lane, 1.0, 0.0), (rows, 128)).astype(low)

    late_blocks = dense_flow(
        [
            (normed_in, kv_rows, 0),
            (normed_mid, logit_grad, 2 * kv_width),
            ((scaled_two * normal_two).astype(low), marker(EXPERTS), 2 * kv_width),
        ]
    )
    late_blocks = order.round([early, m_line] + some(far, 2), late_blocks)
    late = Flow(collect_all(*late_blocks))
    input_grad = order.round(
        [late, m_line], input_grad.astype(low)
    )
    early_line = line_of(early.result)
    order.round([late, m_line] + early_line)
    order.round([late] + far)
    late_line = line_of(late.result)
    spots = jnp.arange(GROUPS, dtype=jnp.int32) ^ group_at
    mate = 1 + shard_at % 2
    spots = jnp.where(spots == mate, 1, jnp.where(spots == 3 - mate, 2, spots))
    places = [spots[i] for i in range(GROUPS)]

    t_parts = t_pieces[0] + [flow.result for flows in t_flows for flow in flows]

    def to_expert(k, ids):
        return (0, jnp.where(k < SHARDS, ids[2] ^ k, k))

    gate_up_grad, down_grad = call(
        unpack_kernel,
        "unpack",
        (shaped(gate_up_weight.shape, full), shaped(down_weight.shape, full)),
        [whole_spec(piece.shape) for piece in t_parts] + [whole_spec((depth, 1))],
        [pl.BlockSpec((depth, 2 * H), to_expert), pl.BlockSpec((depth, H), to_expert)],
        (ids,) + tuple(t_parts) + (gain_two,),
        steps=own_experts,
    )
    gate_up_grad, down_grad = order.round(late_line, (gate_up_grad, down_grad))
    own_sum = jnp.concatenate(
        [
            total_of([flow.result[0]] + [piece.result for piece in line]).astype(low)
            for flow, line in ((early, early_line), (late, late_line))
        ],
        1,
    )
    share_all = Flow(share_flow(own_sum, places))
    order.round([share_all])
    order.round([share_all])
    output = (middle + m_line.result).astype(low)
    dense_sums = share_all.result.astype(full)
    early_sum, late_sum = dense_sums[:, : 2 * q_width], dense_sums[:, 2 * q_width :]
    out_sum, query_sum = early_sum[:, :q_width], early_sum[:, q_width:]

    qkv_sum = jnp.concatenate([query_sum, late_sum[:, : 2 * kv_width]], 1)
    return (
        output,
        input_grad,
        qkv_sum * gain_one,
        out_sum,
        late_sum[:, 2 * kv_width : 2 * kv_width + EXPERTS] * gain_two,
        jnp.sum(qkv_sum * qkv_weight.astype(full), 1),
        late_sum[:, 2 * kv_width + EXPERTS] / gain_two[:, 0],
        gate_up_grad,
        down_grad,
    )


def solution(mesh):
    body = local
    if mesh.shape["expert"] == GROUPS and mesh.shape["shard"] == SHARDS:
        body = local_hops
    return jax.shard_map(
        body,
        mesh=mesh,
        in_specs=(
            P(("expert", "shard"), None),
            P(("expert", "shard"), None),
            P(("expert", "shard"), None),
            P("expert", None),
            P("expert", None),
            P("shard", None),
            P("shard", None),
            P("shard", None),
            P("shard"),
            P("shard"),
            P("shard", "expert"),
            P("shard", "expert"),
        ),
        out_specs=(
            P(("expert", "shard"), None),
            P(("expert", "shard"), None),
            P("shard", None),
            P("shard", None),
            P("shard", None),
            P("shard"),
            P("shard"),
            P("shard", "expert"),
            P("shard", "expert"),
        ),
        check_vma=False,
    )
```
